32 devices in a mesh: dp: 16 (over z, y, core), tensor: 2 (over x).
Axes of the slice: x: 2, y: 2, z: 4, core: 2. Of those that a mesh axis runs over, the one named last changes fastest.
Arguments:
- residual: bfloat16 [16384, 1536], P(('dp', 'tensor')), may hold values from -6 to 6
- norm_gain: float32 [1536], replicated, may hold values from 0.25 to 1.75
- w_gate_inner: bfloat16 [2, 1536, 3072], P(None, 'dp', 'tensor'), may hold values from -0.15625 to 0.15625
- w_state_io: bfloat16 [1536, 256], P('dp'), may hold values from -0.15625 to 0.15625
- w_step: bfloat16 [1536, 48], P('dp', 'tensor'), may hold values from -0.15625 to 0.15625
- conv_inner: float32 [5, 3072], P(None, 'tensor'), may hold values from -0.5 to 0.5
- conv_state: float32 [5, 256], replicated, may hold values from -0.5 to 0.5
- step_bias: float32 [48], P('tensor'), may hold values from -6 to -2
- decay_log: float32 [48], P('tensor'), may hold values from 0 to 2.5
- skip_gain: float32 [48], P('tensor'), may hold values from 0.5 to 1.5
- gate_gain: float32 [3072], P('tensor'), may hold values from 0.25 to 1.75
- w_output: bfloat16 [3072, 1536], P('tensor', 'dp'), may hold values from -0.109375 to 0.109375
- cotangent: bfloat16 [16384, 1536], P(('dp', 'tensor')), may hold values from -6 to 6
Outputs:
- output: bfloat16 [16384, 1536], P(('dp', 'tensor'))
- grad_residual: float32 [16384, 1536], P(('dp', 'tensor'))
- grad_norm_gain: float32 [1536], P(('dp', 'tensor'))
- grad_gate_inner: float32 [2, 1536, 3072], P(None, 'dp', 'tensor')
- grad_state_io: float32 [1536, 256], P('dp', 'tensor')
- grad_w_step: float32 [1536, 48], P('dp', 'tensor')
- grad_conv_inner: float32 [5, 3072], P(None, 'tensor')
- grad_conv_state: float32 [5, 256], P(None, 'tensor')
- grad_step_bias: float32 [48], P('tensor')
- grad_decay_log: float32 [48], P('tensor')
- grad_skip_gain: float32 [48], P('tensor')
- grad_gate_gain: float32 [3072], P('tensor')
- grad_w_output: float32 [3072, 1536], P('tensor', 'dp')
The draws below stay inside these ranges and needn't reach their ends.
All inputs are finite; a program needn't handle non-finite values.
Results may differ from the reference program's by a relative error of at most 0.0099.
Values may be sent and summed in bfloat16 or wider, within the bound.
A program may use at most 256 MiB of HBM per device.

```python
import jax
import jax.numpy as jnp
from jax import lax

D = 1536
H = 48
P_SIZE = 64
N = 128
K = 4
Q = 256
LEN = 1024
DI = 3072
HG = 24
TOKENS = 16384
N_TENSOR = 2


def with_spikes(array, rng, source, target, shards_of, factor):
    def block_of(axis_at):
        return (jnp.arange(array.shape[axis_at]) // (array.shape[axis_at] // shards_of)).reshape((-1,) + (1,) * (array.ndim - 1 - axis_at))

    one_side = jax.random.permutation(rng, shards_of)[block_of(target)]
    far = (block_of(target) + shards_of // 2) % shards_of
    return jnp.where((block_of(source) == one_side) | (block_of(source) == far), factor * array, array)


def level_of(key, extent, cuts, least, high):
    gain, own = 1.0, jax.random.fold_in(key, 6)
    for dim, parts in cuts:
        heights = jnp.exp(jax.random.uniform(jax.random.fold_in(own, dim), (parts,), jnp.float32, least / len(cuts), high / len(cuts)))
        gain = gain * jnp.repeat(heights, extent[dim] // parts).reshape([-1 if axis == dim else 1 for axis in range(len(extent))])
    return gain


def gaussian(rng, extent, spread, reach, pieces=(), held_as=jnp.bfloat16):
    level = level_of(rng, extent, pieces, -0.22, 0.18) if pieces else 1.0
    array = jax.random.normal(rng, extent, jnp.float32) * spread * level
    return jnp.minimum(jnp.maximum(array, -reach), reach).astype(held_as)


def heavy_noise(rng, extent, spread, bound, cuts, heavy, kind=jnp.bfloat16):
    entries = spread * jax.random.normal(rng, extent, jnp.float32)
    if cuts:
        entries = entries * level_of(rng, extent, cuts, -0.22, 0.18)
    return jnp.clip(with_spikes(entries, jax.random.fold_in(rng, 3), *heavy), -bound, bound).astype(kind)


def setup_inputs(seed: int = 0) -> dict:
    streams_of = jax.random.split(jax.random.key(seed), 14)
    residual = heavy_noise(streams_of[0], (TOKENS, D), 1.0, 6.0, ((0, 32),), (0, 1, 32, 2.75))
    norm_gain = jnp.clip(1.0 + 0.15 * jax.random.normal(streams_of[1], (D,), jnp.float32), 0.25, 1.75)
    w_gate_inner = gaussian(streams_of[2], (2, D, DI), D ** -0.5, 0.15625, ((1, 16), (2, 2)))
    w_state_io = gaussian(streams_of[3], (D, 2 * N), D ** -0.5, 0.15625, ((0, 16),))
    w_step = gaussian(streams_of[4], (D, H), D ** -0.5, 0.15625, ((0, 16), (1, 2)))
    conv_inner = jnp.clip(jax.random.uniform(streams_of[5], (K + 1, DI), jnp.float32, -0.5, 0.5) * level_of(streams_of[5], (K + 1, DI), ((1, 2),), -0.4, 0.0), -0.5, 0.5)
    conv_state = jnp.clip(jax.random.uniform(streams_of[6], (K + 1, 2 * N), jnp.float32, -0.5, 0.5), -0.5, 0.5)
    step_bias = jnp.clip(-6.0 + 4.0 * jax.random.uniform(streams_of[7], (H,), jnp.float32) ** level_of(streams_of[7], (H,), ((0, 2),), -0.2, 0.2), -6.0, -2.0)
    decay_log = jnp.clip(2.5 * jax.random.uniform(streams_of[8], (H,), jnp.float32) ** level_of(streams_of[8], (H,), ((0, 2),), -0.2, 0.2), 0.0, 2.5)
    skip_gain = jnp.clip(0.5 + 1.0 * jax.random.uniform(streams_of[9], (H,), jnp.float32) ** level_of(streams_of[9], (H,), ((0, 2),), -0.2, 0.2), 0.5, 1.5)
    gate_gain = jnp.clip(1.0 + 0.15 * jax.random.normal(streams_of[10], (DI,), jnp.float32), 0.25, 1.75)
    w_output = gaussian(streams_of[11], (DI, D), DI ** -0.5, 0.109375, ((0, 2), (1, 16)))
    cotangent = heavy_noise(streams_of[12], (TOKENS, D), 1.0, 6.0, ((0, 32),), (0, 1, 32, 2.75))
    return dict(residual=residual, norm_gain=norm_gain, w_gate_inner=w_gate_inner, w_state_io=w_state_io, w_step=w_step, conv_inner=conv_inner, conv_state=conv_state, step_bias=step_bias, decay_log=decay_log, skip_gain=skip_gain, gate_gain=gate_gain, w_output=w_output, cotangent=cotangent)


@jax.custom_vjp
def low(v):
    return lax.optimization_barrier(v.astype(jnp.bfloat16)).astype(jnp.float32)

@jax.custom_vjp
def low_back(v):
    return v

def low_keep(v):
    return (low(v), None)

def low_pass(kept, grad):
    return (grad,)

def back_keep(v):
    return (v, None)

def back_low(kept, grad):
    return (low(grad),)
low.defvjp(low_keep, low_pass)
low_back.defvjp(back_keep, back_low)
norm_eps = 1e-05

def matmul(left_mat, right_mat):
    return jnp.dot(left_mat, right_mat, precision=lax.Precision.HIGHEST, preferred_element_type=jnp.float32)

def causal_conv(signal, kernel):
    tap_count = kernel.shape[0] - 1
    length = signal.shape[0]
    padded = jnp.pad(signal, ((tap_count - 1, 0), (0, 0)))
    result = kernel[tap_count] + kernel[0] * padded[0:length]
    for offset in range(1, tap_count):
        result = result + kernel[offset] * padded[offset:offset + length]
    return result

def ssd_group(xs_part, b_matrix, c_matrix, step_size, decay_rate, skip_part):
    length, head_count, head_width = xs_part.shape
    span_count = length // Q
    xs_spans = xs_part.reshape(span_count, Q, head_count, head_width)
    x_low = low(xs_part).reshape(span_count, Q, head_count, head_width)
    b_low = low(b_matrix).reshape(span_count, Q, N)
    c_low = low(c_matrix).reshape(span_count, Q, N)
    step_spans = jnp.transpose(step_size.reshape(span_count, Q, head_count), (0, 2, 1))
    cumulative = jnp.cumsum(step_spans * decay_rate[None, :, None], axis=2)
    span_total = cumulative[:, :, -1]
    gram_mat = low_back(jnp.einsum('cqn,crn->cqr', c_low, b_low, precision=lax.Precision.HIGHEST))
    causal = jnp.arange(Q)[:, None] >= jnp.arange(Q)[None, :]
    log_gaps = cumulative[:, :, :, None] - cumulative[:, :, None, :]
    decays = jnp.where(causal, jnp.exp(jnp.where(causal, log_gaps, 0.0)), 0.0)
    mixing = low(gram_mat[:, None] * decays * step_spans[:, :, None, :])
    intra_out = jnp.einsum('chtr,crhp->cthp', mixing, x_low, precision=lax.Precision.HIGHEST)
    write_weight = jnp.exp(span_total[:, :, None] - cumulative) * step_spans
    xw_low = low(xs_spans * jnp.swapaxes(write_weight, 1, 2)[..., None])
    span_state = low_back(jnp.einsum('cqhp,cqn->chpn', xw_low, b_low, precision=lax.Precision.HIGHEST))

    def carry_state(state_in, inputs):
        fade_log, local_state = inputs
        return (jnp.exp(fade_log)[:, None, None] * state_in + local_state, state_in)
    start_state = jnp.zeros((head_count, head_width, N), dtype=xs_part.dtype)
    last_state, entering = lax.scan(carry_state, start_state, (span_total, span_state))
    readout = low_back(jnp.einsum('cqn,chpn->cqhp', c_low, low(entering), precision=lax.Precision.HIGHEST))
    inter_out = jnp.swapaxes(jnp.exp(cumulative), 1, 2)[..., None] * readout
    ssd_out = low_back(intra_out + inter_out + skip_part[None, None, :, None] * xs_spans)
    return ssd_out.reshape(length, head_count * head_width)

def layer(params, residual):
    norm_gain, w_gate_inner, w_state_io, w_step, conv_inner, conv_state, step_bias, decay_log, skip_gain, gate_gain, w_output = params
    rstd_in = lax.rsqrt(lax.optimization_barrier(jnp.mean(residual * residual, axis=1, keepdims=True)) + norm_eps)
    normed = low(residual * rstd_in * norm_gain)
    gate_proj = low_back(matmul(normed, w_gate_inner[0]))
    inner_proj = low_back(matmul(normed, w_gate_inner[1]))
    state_proj = matmul(normed, w_state_io)
    step_raw = low_back(matmul(normed, w_step))
    step_size = jax.nn.softplus(step_raw + step_bias)
    decay_rate = -jnp.exp(decay_log)
    length = residual.shape[0]
    group_width = HG * P_SIZE
    outputs_list = []
    for member in range(N_TENSOR):
        start_col = member * group_width
        stop_col = start_col + group_width
        state_copy = low_back(state_proj)
        conv_in = jnp.concatenate([inner_proj[:, start_col:stop_col], state_copy], axis=1)
        kernel = jnp.concatenate([conv_inner[:, start_col:stop_col], conv_state], axis=1)
        active = jax.nn.silu(causal_conv(conv_in, kernel))
        xs_part = active[:, :group_width].reshape(length, HG, P_SIZE)
        b_matrix = active[:, group_width:group_width + N]
        c_matrix = active[:, group_width + N:]
        head_start = member * HG
        outputs_list.append(ssd_group(xs_part, b_matrix, c_matrix, step_size[:, head_start:head_start + HG], decay_rate[head_start:head_start + HG], skip_gain[head_start:head_start + HG]))
    duality_full_output = jnp.concatenate(outputs_list, axis=1)
    gated_out = duality_full_output * jax.nn.silu(gate_proj)
    gate_rstd = lax.rsqrt(lax.optimization_barrier(jnp.mean(gated_out * gated_out, axis=1, keepdims=True)) + norm_eps)
    normed_gate = low(gated_out * gate_rstd * gate_gain)
    return residual + matmul(normed_gate, w_output)

def reference(residual, norm_gain, w_gate_inner, w_state_io, w_step, conv_inner, conv_state, step_bias, decay_log, skip_gain, gate_gain, w_output, cotangent):
    params = (norm_gain, w_gate_inner.astype(jnp.float32), w_state_io.astype(jnp.float32), w_step.astype(jnp.float32), conv_inner, conv_state, step_bias, decay_log, skip_gain, gate_gain, w_output.astype(jnp.float32))
    seq_rows = residual.astype(jnp.float32).reshape(TOKENS // LEN, LEN, D)
    seq_cots = cotangent.astype(jnp.float32).reshape(TOKENS // LEN, LEN, D)

    def one_sequence(totals, inputs):
        rows_in, cot_in = inputs
        layer_out, pullback = jax.vjp(layer, params, rows_in)
        grad_params, grad_rows = pullback(cot_in)
        totals = jax.tree.map(jnp.add, totals, grad_params)
        return (totals, (layer_out.astype(jnp.bfloat16), grad_rows))
    zero_grads = jax.tree.map(jnp.zeros_like, params)
    totals, (out_rows, grad_rows) = lax.scan(one_sequence, zero_grads, (seq_rows, seq_cots))
    grad_norm, grad_zx, grad_bc, grad_stepw, grad_cinner, grad_cstate, grad_bias, grad_decay, grad_skip, grad_ggain, grad_wout = totals
    return (out_rows.reshape(TOKENS, D), grad_rows.reshape(TOKENS, D), grad_norm, grad_zx, grad_bc, grad_stepw, grad_cinner, grad_cstate, grad_bias, grad_decay, grad_skip, grad_ggain, grad_wout)
```

```python
import functools

import jax
import jax.numpy as jnp
from jax import lax
from jax.experimental import pallas as pl
from jax.experimental.pallas import tpu as pltpu
from jax.sharding import PartitionSpec as P

Q = 256
LEN = 1024
HEAD = 64
BW = 256
HB = BW // HEAD
LOG2E = 1.4426950408889634
FAR = -1e30
norm_eps = 1e-05
f32 = jnp.float32
bf16 = jnp.bfloat16


def mm(a, b, ca=1, cb=0):
    return lax.dot_general(a, b, (((ca,), (cb,)), ((), ())), preferred_element_type=f32)


def sigmoid(v):
    return 1.0 / (1.0 + jnp.exp(-v))


def split3(a):
    hi = a.astype(bf16)
    rest = a - hi.astype(f32)
    mid = rest.astype(bf16)
    low = (rest - mid.astype(f32)).astype(bf16)
    return hi, mid, low


def split2(a):
    hi = a.astype(bf16)
    return hi, (a - hi.astype(f32)).astype(bf16)


def iota(shape, axis):
    return lax.broadcasted_iota(jnp.int32, shape, axis)


def expand(cols):
    rows = cols.shape[0]
    left = iota((rows, 128), 1) < HEAD
    return jnp.concatenate(
        [jnp.where(left, cols[:, 2 * q : 2 * q + 1], cols[:, 2 * q + 1 : 2 * q + 2]) for q in range(2)],
        axis=1,
    )


def conv_taps(window, kernel):
    out = kernel[4:5] + kernel[3:4] * window[8:]
    for k in range(3):
        out = out + kernel[k : k + 1] * pltpu.roll(window, 3 - k, 0)[8:]
    return out


def head_masks():
    lane = iota((1, BW), 1) // HEAD
    return [(lane == j).astype(f32).astype(bf16) for j in range(HB)]


def quads():
    for r in range(0, Q, 64):
        for half in range(2):
            if half * 128 <= r:
                yield r, half, r < half * 128 + 128


def decay_chunk(col, row, r, half, diag):
    gap = col[r : r + 64] - row[:, half * 128 : half * 128 + 128]
    if diag:
        keep = iota((64, 128), 0) + (r - half * 128) >= iota((64, 128), 1)
        gap = jnp.where(keep, gap, FAR)
    return jnp.exp2(gap)


def mixer_forward(
    normed, wi, wsx, kin, kst, hp,
    inner_out, ssd_out, states_out, cst_out, bc_out, step_out, cum_out, stepT_out, cumT_out, preT_out,
    buf, gram, colc, cols, rowp, mst, xst, state,
):
    i = pl.program_id(0)
    tokens = normed.shape[0]
    spans = tokens // Q

    @pl.when(i == 0)
    def _():
        proj = mm(normed[...], wsx[...])
        buf[0:8] = jnp.zeros((8, BW), f32)
        cst_out[...] = proj[:, :BW]
        buf[8 : 8 + tokens] = proj[:, :BW]
        tri = (iota((Q, Q), 0) >= iota((Q, Q), 1)).astype(f32).astype(bf16)
        pre = proj[:, BW:] + hp[0:1]
        step = jnp.maximum(pre, 0.0) + jnp.log1p(jnp.exp(-jnp.abs(pre)))
        step_out[...] = step
        scaled = step * (hp[1:2] * LOG2E)
        for s in range(spans):
            parts = split3(scaled[s * Q : s * Q + Q])
            cum_out[s * Q : s * Q + Q] = mm(tri, parts[0]) + mm(tri, parts[1]) + mm(tri, parts[2])
            conv = conv_taps(buf[s * Q : s * Q + Q + 8], kst[...])
            bc = (conv * sigmoid(conv)).astype(bf16)
            bc_out[s * Q : s * Q + Q] = bc
            gram[s] = mm(bc[:, 128:], bc[:, :128], 1, 1)
        preT_out[...] = jnp.transpose(pre)[:48]
        stepT_out[...] = jnp.transpose(step)[:48]
        cumT_out[...] = jnp.transpose(cum_out[...])[:48]
        mst[...] = jnp.zeros(mst.shape, bf16)

    inner = mm(normed[...], wi[...])
    inner_out[...] = inner
    buf[8 : 8 + tokens] = inner
    turn = lax.rem(128 - 8 * i, 128)
    colc[...] = pltpu.roll(cum_out[...], turn, 1)
    cols[...] = pltpu.roll(step_out[...], turn, 1)
    rows8 = pl.ds(pl.multiple_of(8 * i, 8), 8)
    rowp[...] = cumT_out[rows8] - jnp.log2(stepT_out[rows8])
    state[...] = jnp.zeros(state.shape, f32)
    masks = head_masks()

    def span(s, carry):
        at = pl.multiple_of(s * Q, Q)
        rows = pl.ds(at, Q)
        conv = conv_taps(buf[pl.ds(at, Q + 8)], kin[...])
        xs = conv * sigmoid(conv)
        x_low = xs.astype(bf16)
        col = colc[rows]
        total = col[Q - 1 : Q]
        growth = expand(jnp.exp2(col[:, :8]))
        weight = expand(jnp.exp2(total[:, :8] - col[:, :8]) * cols[rows][:, :8])
        xw_low = (xs * weight).astype(bf16)
        for j in range(HB):
            xst[j * Q : j * Q + Q] = x_low * masks[j]
            row = rowp[j : j + 1, rows]
            for r, half, diag in quads():
                part = gram[s, r : r + 64, half * 128 : half * 128 + 128]
                dec = decay_chunk(col[:, j : j + 1], row, r, half, diag)
                mst[r : r + 64, j * Q + half * 128 : j * Q + half * 128 + 128] = (part * dec).astype(bf16)
        intra = mm(mst[...], xst[...])
        state_in = state[...]
        states_out[s] = state_in
        bc = bc_out[rows]
        readout = mm(bc[:, 128:], state_in.astype(bf16), 1, 1)
        ssd_out[rows] = intra + growth * readout + kin[5:6] * xs
        local = mm(xw_low, bc[:, :128], 0, 0)
        fade = jnp.exp2(total)
        for j in range(HB):
            at_j = slice(j * HEAD, j * HEAD + HEAD)
            state[at_j] = fade[:, j : j + 1] * state_in[at_j] + local[at_j]
        return carry

    lax.fori_loop(0, spans, span, 0)


def gate_forward(normed, cot, wg, wo, ssd, gain, gate_out, ggo_out, stats_out, sq, gi):
    i = pl.program_id(0)

    @pl.when(i == 0)
    def _():
        sq[...] = jnp.zeros(sq.shape, f32)
        gi[...] = jnp.zeros(gi.shape, f32)

    gate = mm(normed[...], wg[...])
    gate_out[...] = gate
    ggo = mm(cot[...], wo[...])
    ggo_out[...] = ggo
    gated = ssd[...] * (gate * sigmoid(gate))
    squares = gated * gated
    sq[...] += squares[:, :128] + squares[:, 128:]
    inner = ggo * gain[0:1] * gated
    gi[...] += inner[:, :128] + inner[:, 128:]

    @pl.when(i == pl.num_programs(0) - 1)
    def _():
        lane = iota(sq.shape, 1)
        both = jnp.where(
            lane == 0,
            jnp.sum(sq[...], axis=1, keepdims=True),
            jnp.where(lane == 1, jnp.sum(gi[...], axis=1, keepdims=True), 0.0),
        )
        stats_out[...] = jnp.transpose(both)[:8]


def gate_backward(unit_total, stats, gate, ssd, ggo, gain, dy_out, dgate_out, ng_out, gg_out, cols):
    @pl.when(pl.program_id(0) == 0)
    def _():
        full = jnp.concatenate([stats[...], jnp.zeros((120, stats.shape[1]), f32)], axis=0)
        cols[...] = jnp.transpose(full)

    rstd = lax.rsqrt(cols[:, 0:1] / unit_total + norm_eps)
    pull = rstd * rstd * rstd * (cols[:, 1:2] / unit_total)
    v = gate[...]
    sig = sigmoid(v)
    act = v * sig
    y = ssd[...]
    gated = y * act
    scaled = gated * rstd
    ng_out[...] = (scaled * gain[0:1]).astype(bf16)
    gg = ggo[...]
    gg_out[...] = jnp.broadcast_to(jnp.sum(gg * scaled, axis=0, keepdims=True), gg_out.shape)
    grad = rstd * (gg * gain[0:1]) - gated * pull
    dy_out[...] = (grad * act).astype(bf16)
    dgate_out[...] = (grad * y * (sig * (1.0 + v * (1.0 - sig)))).astype(bf16)


def mixer_backward(
    inner, dy, states, kin, kst, hp, cst, bc_in, step_in, cum_in, stepT, cumT, preT, rateT,
    dinner_out, gk_out, dsd_out, gks_out, hs_out,
    buf, dbuf, gram, gg, gb, gc, colc, cols, rowp, mst, dyst, gmix, sgrad, rs_t, cs_t, dr_t, wg_t, gt_t, gtaps,
):
    i = pl.program_id(0)
    tokens = inner.shape[0]
    spans = tokens // Q
    masks = head_masks()

    @pl.when(i == 0)
    def _():
        buf[0:8] = jnp.zeros((8, BW), f32)
        dbuf[tokens : tokens + 8] = jnp.zeros((8, BW), f32)
        for s in range(spans):
            bc = bc_in[s * Q : s * Q + Q]
            gram[s] = mm(bc[:, 128:], bc[:, :128], 1, 1)
        for ref in (gg, gb, gc, rs_t, cs_t, dr_t, wg_t, gt_t):
            ref[...] = jnp.zeros(ref.shape, f32)
        mst[...] = jnp.zeros(mst.shape, bf16)

    buf[8 : 8 + tokens] = inner[...]
    turn = lax.rem(128 - 8 * i, 128)
    colc[...] = pltpu.roll(cum_in[...], turn, 1)
    cols[...] = pltpu.roll(step_in[...], turn, 1)
    rows8 = pl.ds(pl.multiple_of(8 * i, 8), 8)
    rowp[...] = cumT[rows8] - jnp.log2(stepT[rows8])
    sgrad[...] = jnp.zeros(sgrad.shape, f32)
    gtaps[...] = jnp.zeros(gtaps.shape, f32)
    pick = (iota((8, BW), 1) // HEAD == iota((8, BW), 0)).astype(f32).astype(bf16)

    def conv_rows(at, kernel, grad_act):
        window = buf[pl.ds(at, Q + 8)]
        conv = conv_taps(window, kernel)
        sig = sigmoid(conv)
        gco = grad_act * (sig * (1.0 + conv * (1.0 - sig)))
        dbuf[pl.ds(at, Q)] = gco
        for k in range(4):
            prod = gco * (window[8:] if k == 3 else pltpu.roll(window, 3 - k, 0)[8:])
            gtaps[k : k + 1] += jnp.sum(prod, axis=0, keepdims=True)
        gtaps[4:5] += jnp.sum(gco, axis=0, keepdims=True)
        after = dbuf[pl.ds(at, Q + 8)]
        grad_in = kernel[3:4] * gco
        for k in range(3):
            grad_in = grad_in + kernel[k : k + 1] * pltpu.roll(after, Q + 8 - (3 - k), 0)[:Q]
        return grad_in

    def span(back, carry):
        s = spans - 1 - back
        at = pl.multiple_of(s * Q, Q)
        rows = pl.ds(at, Q)
        conv = conv_taps(buf[pl.ds(at, Q + 8)], kin[...])
        xs = conv * sigmoid(conv)
        x_low = xs.astype(bf16)
        dy_s = dy[rows]
        dy_f = dy_s.astype(f32)
        bc = bc_in[rows]
        b_low, c_low = bc[:, :128], bc[:, 128:]
        col = colc[rows]
        total = col[Q - 1 : Q]
        for j in range(HB):
            dyst[j * Q : j * Q + Q] = dy_s * masks[j]
        gmix[...] = mm(dyst[...], x_low, 1, 1)
        lane = iota((Q, 128), 1)
        row_sums = jnp.zeros((Q, 128), f32)
        for j in range(HB):
            row = rowp[j : j + 1, rows]
            col_sum = [jnp.zeros((1, 128), f32), jnp.zeros((1, 128), f32)]
            row_parts = []
            for r, half, diag in quads():
                here = slice(half * 128, half * 128 + 128)
                dec = decay_chunk(col[:, j : j + 1], row, r, half, diag)
                part = gram[s, r : r + 64, here]
                p = gmix[j * Q + r : j * Q + r + 64, here] * dec
                gg[s, r : r + 64, here] += p
                q = p * part
                mst[j * Q + r : j * Q + r + 64, here] = (part * dec).astype(bf16)
                col_sum[half] = col_sum[half] + jnp.sum(q, axis=0, keepdims=True)
                if half == 0:
                    row_parts.append(q)
                else:
                    row_parts[-1] = row_parts[-1] + q
            sums = jnp.concatenate([jnp.sum(q, axis=1, keepdims=True) for q in row_parts], axis=0)
            row_sums = jnp.where(lane == j, sums, row_sums)
            cs_t[pl.ds(8 * i + j, 1), rows] = jnp.concatenate(col_sum, axis=1)
        rs_t[rows8, rows] = jnp.transpose(row_sums)[:8]
        grad_xs = mm(mst[...], dyst[...], 0, 0) + kin[5:6] * dy_f

        growth = expand(jnp.exp2(col[:, :8]))
        weight = expand(jnp.exp2(total[:, :8] - col[:, :8]) * cols[rows][:, :8])
        state_in = states[s]
        state_low = state_in.astype(bf16)
        state_grad = sgrad[...]
        carry_low = state_grad.astype(bf16)
        readout = mm(c_low, state_low, 1, 1)
        read_low = (dy_f * growth).astype(bf16)
        hi, low = split2(dy_f * readout)
        dr_t[rows8, rows] = mm(pick, hi, 1, 1) + mm(pick, low, 1, 1)
        gc[rows] += mm(read_low, state_low)
        grad_xw = mm(b_low, carry_low, 1, 1)
        xw_low = (xs * weight).astype(bf16)
        gb[rows] += mm(xw_low, carry_low)
        hi, low = split2(grad_xw * xs)
        wg_t[rows8, rows] = mm(pick, hi, 1, 1) + mm(pick, low, 1, 1)
        hi, low = split2(state_grad * state_in)
        sums = jnp.sum(mm(pick, hi) + mm(pick, low), axis=1, keepdims=True)
        gt_t[rows8] = jnp.where(iota((8, 128), 1) == s, sums, gt_t[rows8])
        grad_xs = grad_xs + grad_xw * weight
        local = mm(read_low, c_low, 0, 0)
        fade = jnp.exp2(total)
        for j in range(HB):
            at_j = slice(j * HEAD, j * HEAD + HEAD)
            sgrad[at_j] = fade[:, j : j + 1] * state_grad[at_j] + local[at_j]
        gtaps[5:6] += jnp.sum(dy_f * xs, axis=0, keepdims=True)
        dinner_out[rows] = conv_rows(at, kin[...], grad_xs).astype(bf16)
        return carry

    lax.fori_loop(0, spans, span, 0)
    gk_out[...] = gtaps[...]

    @pl.when(i == pl.num_programs(0) - 1)
    def _():
        buf[8 : 8 + tokens] = cst[...]
        gtaps[...] = jnp.zeros(gtaps.shape, f32)
        rate = rateT[:, 0:1]
        later = (iota((Q, Q), 0) >= iota((Q, Q), 1)).astype(f32).astype(bf16)
        last = iota((48, Q), 1) == Q - 1
        bias_sum = jnp.zeros((48, 1), f32)
        decay_sum = jnp.zeros((48, 1), f32)
        for back in range(spans):
            s = spans - 1 - back
            rows = slice(s * Q, s * Q + Q)
            bc = bc_in[rows]
            gl = gg[s].astype(bf16)
            grad_c = gc[rows] + mm(gl, bc[:, :128])
            grad_b = gb[rows] + mm(gl, bc[:, 128:], 0, 0)
            both = jnp.concatenate([grad_b, grad_c], axis=1)
            dsd_out[rows, :BW] = conv_rows(s * Q, kst[...], both).astype(bf16)

            cum, step, pre = cumT[:, rows], stepT[:, rows], preT[:, rows]
            total = cum[:, Q - 1 : Q]
            rate_w = jnp.exp2(total - cum)
            wg = wg_t[:, rows]
            cs = cs_t[:, rows]
            moved = wg * (rate_w * step)
            grad_cum = rs_t[:, rows] - cs + jnp.exp2(cum) * dr_t[:, rows] - moved
            grad_total = jnp.exp2(total) * gt_t[:, s : s + 1] + jnp.sum(moved, axis=1, keepdims=True)
            grad_cum = grad_cum + jnp.where(last, grad_total, 0.0)
            parts = split3(grad_cum)
            grad_rate = mm(parts[0], later) + mm(parts[1], later) + mm(parts[2], later)
            sig = sigmoid(pre)
            ratio = jnp.where(pre < -15.0, 1.0, sig / step)
            grad_pre = (wg * rate_w + grad_rate * rate) * sig + cs * ratio
            bias_sum = bias_sum + jnp.sum(grad_pre, axis=1, keepdims=True)
            decay_sum = decay_sum + jnp.sum(grad_rate * step, axis=1, keepdims=True)
            full = jnp.concatenate([grad_pre, jnp.zeros((80, Q), f32)], axis=0)
            dsd_out[rows, BW:] = jnp.transpose(full).astype(bf16)
        gks_out[...] = gtaps[...]
        lane = iota((48, 128), 1)
        hs_out[...] = jnp.where(lane == 0, bias_sum, jnp.where(lane == 1, decay_sum * rate, 0.0))


def const(shape):
    return pl.BlockSpec(shape, lambda i: (0,) * len(shape))


def once(shape, at=None):
    where = at or (0,) * len(shape)
    return pl.BlockSpec(shape, lambda i: where, pipeline_mode=pl.Buffered(1))


def by_cols(rows, offset=0):
    return pl.BlockSpec((rows, BW), lambda i: (0, i + offset))


def params():
    return pltpu.CompilerParams(dimension_semantics=("arbitrary",), vmem_limit_bytes=60 * 1024 * 1024)


def spread(v):
    lead = v.shape[:-1]
    v = v.reshape(lead + (v.shape[-1] // HB, HB))
    v = jnp.pad(v, [(0, 0)] * len(lead) + [(0, 0), (0, 8 - HB)]).reshape(lead + (-1,))
    return jnp.pad(v, [(0, 0)] * len(lead) + [(0, 128 - v.shape[-1])])


def gathered_heads(v, heads):
    return v[..., : heads * 2].reshape(v.shape[:-1] + (heads // HB, 8))[..., :HB].reshape(v.shape[:-1] + (heads,))


def sds(shape, dtype=f32):
    return jax.ShapeDtypeStruct(shape, dtype)


def on_device(
    residual, norm_gain, w_gate_inner, w_state_io, w_step, conv_inner, conv_state,
    step_bias, decay_log, skip_gain, gate_gain, w_output, cotangent,
):
    width = residual.shape[1]
    units = w_gate_inner.shape[2]
    heads = w_step.shape[1]
    blocks = units // BW
    unit_total = units * lax.axis_size("tensor")
    rows_in = residual.astype(f32)
    rstd_in = lax.rsqrt(jnp.mean(rows_in * rows_in, axis=1, keepdims=True) + norm_eps)
    scaled = rows_in * rstd_in
    normed_local = (scaled * norm_gain).astype(bf16)
    pack_a = jnp.concatenate([w_gate_inner[1], w_state_io, spread(w_step)], axis=1)
    pack_b = jnp.concatenate([w_gate_inner[0], w_output.T], axis=1)
    wa = lax.all_gather(pack_a, "dp", axis=0, tiled=True)
    normed = lax.all_gather(normed_local, "tensor", axis=0, tiled=True)
    wb = lax.all_gather(pack_b, "dp", axis=0, tiled=True)
    cot = lax.all_gather(cotangent, "tensor", axis=0, tiled=True)
    tokens = normed.shape[0]
    spans = tokens // Q
    rate = -jnp.exp(decay_log)
    kin = jnp.concatenate([conv_inner, jnp.repeat(skip_gain, HEAD)[None], jnp.zeros((2, units), f32)], axis=0)
    kst = jnp.concatenate([conv_state, jnp.zeros((3, BW), f32)], axis=0)
    hp = jnp.concatenate([spread(step_bias)[None], spread(rate)[None], jnp.zeros((6, 128), f32)], axis=0)
    rate_t = jnp.broadcast_to(spread(rate)[:48, None], (48, 128))
    gain8 = jnp.broadcast_to(gate_gain[None], (8, units))

    inner, ssd, states, cst, bc, step, cum, step_t, cum_t, pre_t = pl.pallas_call(
        mixer_forward,
        name="mixer_forward",
        grid=(blocks,),
        in_specs=[
            once((tokens, width)), by_cols(width), once((width, 384), (0, units // 384)),
            by_cols(8), once((8, BW)), once((8, 128)),
        ],
        out_specs=[
            by_cols(tokens), by_cols(tokens), pl.BlockSpec((spans, BW, 128), lambda i: (0, i, 0)),
            once((tokens, BW)), once((tokens, BW)), once((tokens, 128)), once((tokens, 128)),
            once((48, tokens)), once((48, tokens)), once((48, tokens)),
        ],
        out_shape=[
            sds((tokens, units)), sds((tokens, units)), sds((spans, units, 128)),
            sds((tokens, BW)), sds((tokens, BW), bf16), sds((tokens, 128)), sds((tokens, 128)),
            sds((48, tokens)), sds((48, tokens)), sds((48, tokens)),
        ],
        scratch_shapes=[
            pltpu.VMEM((tokens + 8, BW), f32), pltpu.VMEM((spans, Q, Q), f32),
            pltpu.VMEM((tokens, 128), f32), pltpu.VMEM((tokens, 128), f32), pltpu.VMEM((8, tokens), f32),
            pltpu.VMEM((Q, HB * Q), bf16), pltpu.VMEM((HB * Q, BW), bf16), pltpu.VMEM((BW, 128), f32),
        ],
        compiler_params=params(),
        cost_estimate=pl.CostEstimate(flops=2 * tokens * width * (units + 384) + 4 * tokens * 256 * units, bytes_accessed=30_000_000, transcendentals=heads * spans * Q * Q),
    )(normed, wa, wa, kin, kst, hp)

    gate, ggo, stats = pl.pallas_call(
        gate_forward,
        name="gate_forward",
        grid=(blocks,),
        in_specs=[
            once((tokens, width)), once((tokens, width)), by_cols(width), by_cols(width, blocks),
            by_cols(tokens), by_cols(8),
        ],
        out_specs=[by_cols(tokens), by_cols(tokens), once((8, tokens))],
        out_shape=[sds((tokens, units)), sds((tokens, units)), sds((8, tokens))],
        scratch_shapes=[pltpu.VMEM((tokens, 128), f32), pltpu.VMEM((tokens, 128), f32)],
        compiler_params=params(),
        cost_estimate=pl.CostEstimate(flops=4 * tokens * width * units, bytes_accessed=35_000_000, transcendentals=tokens * units),
    )(normed, cot, wb, wb, ssd, gain8)
    stats = lax.psum(stats, "tensor")

    dy, dgate, ng, ggg = pl.pallas_call(
        functools.partial(gate_backward, float(unit_total)),
        name="gate_backward",
        grid=(blocks,),
        in_specs=[once((8, tokens)), by_cols(tokens), by_cols(tokens), by_cols(tokens), by_cols(8)],
        out_specs=[by_cols(tokens), by_cols(tokens), by_cols(tokens), by_cols(8)],
        out_shape=[sds((tokens, units), bf16), sds((tokens, units), bf16), sds((tokens, units), bf16), sds((8, units))],
        scratch_shapes=[pltpu.VMEM((tokens, 128), f32)],
        compiler_params=params(),
        cost_estimate=pl.CostEstimate(flops=20 * tokens * units, bytes_accessed=30_000_000, transcendentals=tokens * units),
    )(stats, gate, ssd, ggo, gain8)

    grad_wo = mm(cot, ng, 0, 0).astype(bf16)
    grad_wg = mm(normed, dgate, 0, 0).astype(bf16)
    wo_shard = lax.psum_scatter(grad_wo, "dp", scatter_dimension=0, tiled=True)
    wg_shard = lax.psum_scatter(grad_wg, "dp", scatter_dimension=0, tiled=True)
    mixed = lax.psum_scatter(mm(ng, wb[:, units:], 1, 1).astype(bf16), "tensor", scatter_dimension=0, tiled=True)
    output = (rows_in + mixed.astype(f32)).astype(bf16)

    dinner, gk, dsd, gks, hs = pl.pallas_call(
        mixer_backward,
        name="mixer_backward",
        grid=(blocks,),
        in_specs=[
            by_cols(tokens), by_cols(tokens), pl.BlockSpec((spans, BW, 128), lambda i: (0, i, 0)),
            by_cols(8), once((8, BW)), once((8, 128)),
            once((tokens, BW)), once((tokens, BW)), once((tokens, 128)), once((tokens, 128)),
            once((48, tokens)), once((48, tokens)), once((48, tokens)), once((48, 128)),
        ],
        out_specs=[by_cols(tokens), by_cols(8), once((tokens, 384)), once((8, BW)), once((48, 128))],
        out_shape=[sds((tokens, units), bf16), sds((8, units)), sds((tokens, 384), bf16), sds((8, BW)), sds((48, 128))],
        scratch_shapes=[
            pltpu.VMEM((tokens + 8, BW), f32), pltpu.VMEM((tokens + 8, BW), f32),
            pltpu.VMEM((spans, Q, Q), f32), pltpu.VMEM((spans, Q, Q), f32),
            pltpu.VMEM((tokens, 128), f32), pltpu.VMEM((tokens, 128), f32),
            pltpu.VMEM((tokens, 128), f32), pltpu.VMEM((tokens, 128), f32), pltpu.VMEM((8, tokens), f32),
            pltpu.VMEM((HB * Q, Q), bf16), pltpu.VMEM((HB * Q, BW), bf16), pltpu.VMEM((HB * Q, Q), f32),
            pltpu.VMEM((BW, 128), f32),
            pltpu.VMEM((48, tokens), f32), pltpu.VMEM((48, tokens), f32), pltpu.VMEM((48, tokens), f32),
            pltpu.VMEM((48, tokens), f32), pltpu.VMEM((48, 128), f32), pltpu.VMEM((8, BW), f32),
        ],
        compiler_params=params(),
        cost_estimate=pl.CostEstimate(flops=40_000_000_000, bytes_accessed=30_000_000, transcendentals=heads * spans * Q * Q),
    )(inner, dy, states, kin, kst, hp, cst, bc, step, cum, step_t, cum_t, pre_t, rate_t)

    grad_wi = mm(normed, dinner, 0, 0).astype(bf16)
    grad_ws = mm(normed, dsd, 0, 0).astype(bf16)
    wa_shard = lax.psum_scatter(jnp.concatenate([grad_wi, grad_ws], axis=1), "dp", scatter_dimension=0, tiled=True)
    grad_normed = (
        mm(dgate, wb[:, :units], 1, 1) + mm(dinner, wa[:, :units], 1, 1) + mm(dsd, wa[:, units:], 1, 1)
    ).astype(bf16)
    grad_normed = lax.psum_scatter(grad_normed, "tensor", scatter_dimension=0, tiled=True).astype(f32)
    grad_v = grad_normed * norm_gain
    grad_residual = cotangent.astype(f32) + rstd_in * (
        grad_v - scaled * jnp.mean(grad_v * scaled, axis=1, keepdims=True)
    )

    small = jnp.concatenate([gk, ggg, jnp.pad(gks, ((0, 0), (0, units - BW)))], axis=0)
    small = jnp.concatenate([small.reshape(-1), hs[:, 0], hs[:, 1]])
    small = lax.psum(small, "dp")
    table = small[: 24 * units].reshape(24, units)
    bias_sum = gathered_heads(small[24 * units : 24 * units + 48], heads)
    decay_sum = gathered_heads(small[24 * units + 48 : 24 * units + 96], heads)
    skip_sum = jnp.sum(table[5].reshape(heads, HEAD), axis=1)

    wg_f, wa_f, wo_f = wg_shard.astype(f32), wa_shard.astype(f32), wo_shard.astype(f32)
    gain_rows = jnp.sum(wg_f * w_gate_inner[0].astype(f32), axis=1) + jnp.sum(wa_f * pack_a.astype(f32), axis=1)
    gain_own = gain_rows / lax.dynamic_slice_in_dim(
        norm_gain, lax.axis_index("dp") * gain_rows.shape[0], gain_rows.shape[0]
    )
    state_own = wa_f[:, units : units + BW]
    conv_state_part, state_part, gain_part = (
        lax.psum_scatter(table[16:21, :BW], "tensor", scatter_dimension=1, tiled=True),
        lax.psum_scatter(state_own, "tensor", scatter_dimension=1, tiled=True),
        lax.psum_scatter(gain_own, "tensor", scatter_dimension=0, tiled=True),
    )
    return (
        output,
        grad_residual,
        gain_part,
        jnp.stack([wg_f, wa_f[:, :units]]),
        state_part,
        gathered_heads(wa_f[:, units + BW :], heads),
        table[0:5],
        conv_state_part,
        bias_sum,
        decay_sum,
        skip_sum,
        table[8],
        wo_f.T,
    )


def solution(mesh):
    return jax.shard_map(
        on_device,
        mesh=mesh,
        in_specs=(
            P(("dp", "tensor"), None),
            P(),
            P(None, "dp", "tensor"),
            P("dp", None),
            P("dp", "tensor"),
            P(None, "tensor"),
            P(),
            P("tensor"),
            P("tensor"),
            P("tensor"),
            P("tensor"),
            P("tensor", "dp"),
            P(("dp", "tensor"), None),
        ),
        out_specs=(
            P(("dp", "tensor"), None),
            P(("dp", "tensor"), None),
            P(("dp", "tensor")),
            P(None, "dp", "tensor"),
            P("dp", "tensor"),
            P("dp", "tensor"),
            P(None, "tensor"),
            P(None, "tensor"),
            P("tensor"),
            P("tensor"),
            P("tensor"),
            P("tensor"),
            P("tensor", "dp"),
        ),
        check_vma=False,
    )
```

```python
import functools

import jax
import jax.numpy as jnp
from jax import lax
from jax.experimental import pallas as pl
from jax.experimental.pallas import tpu as pltpu
from jax.sharding import PartitionSpec as P

Q = 256
LEN = 1024
HEAD = 64
BW = 256
HB = BW // HEAD
LOG2E = 1.4426950408889634
FAR = -1e30
norm_eps = 1e-05
MESH = pl.DeviceIdType.MESH
f32 = jnp.float32
bf16 = jnp.bfloat16


def mm(a, b, ca=1, cb=0):
    return lax.dot_general(a, b, (((ca,), (cb,)), ((), ())), preferred_element_type=f32)


def sigmoid(v):
    return 1.0 / (1.0 + jnp.exp(-v))


def split3(a):
    hi = a.astype(bf16)
    rest = a - hi.astype(f32)
    mid = rest.astype(bf16)
    low = (rest - mid.astype(f32)).astype(bf16)
    return hi, mid, low


def split2(a):
    hi = a.astype(bf16)
    return hi, (a - hi.astype(f32)).astype(bf16)


def iota(shape, axis):
    return lax.broadcasted_iota(jnp.int32, shape, axis)


def expand(cols):
    rows = cols.shape[0]
    left = iota((rows, 128), 1) < HEAD
    return jnp.concatenate(
        [jnp.where(left, cols[:, 2 * q : 2 * q + 1], cols[:, 2 * q + 1 : 2 * q + 2]) for q in range(2)],
        axis=1,
    )


def conv_taps(window, kernel):
    out = kernel[4:5] + kernel[3:4] * window[8:]
    for k in range(3):
        out = out + kernel[k : k + 1] * pltpu.roll(window, 3 - k, 0)[8:]
    return out


def head_masks():
    lane = iota((1, BW), 1) // HEAD
    return [(lane == j).astype(f32).astype(bf16) for j in range(HB)]


def quads():
    for r in range(0, Q, 64):
        for half in range(2):
            if half * 128 <= r:
                yield r, half, r < half * 128 + 128


def decay_chunk(col, row, r, half, diag):
    gap = col[r : r + 64] - row[:, half * 128 : half * 128 + 128]
    if diag:
        keep = iota((64, 128), 0) + (r - half * 128) >= iota((64, 128), 1)
        gap = jnp.where(keep, gap, FAR)
    return jnp.exp2(gap)


def mixer_forward(
    normed, wi, wsx, kin, kst, hp,
    inner_out, ssd_out, states_out, cst_out, bc_out, step_out, cum_out, stepT_out, cumT_out, preT_out,
    buf, gram, colc, cols, rowp, mst, xst, state,
):
    i = pl.program_id(0)
    tokens = normed.shape[0]
    spans = tokens // Q

    @pl.when(i == 0)
    def _():
        proj = mm(normed[...], wsx[...])
        buf[0:8] = jnp.zeros((8, BW), f32)
        cst_out[...] = proj[:, :BW]
        buf[8 : 8 + tokens] = proj[:, :BW]
        tri = (iota((Q, Q), 0) >= iota((Q, Q), 1)).astype(f32).astype(bf16)
        pre = proj[:, BW:] + hp[0:1]
        step = jnp.maximum(pre, 0.0) + jnp.log1p(jnp.exp(-jnp.abs(pre)))
        step_out[...] = step
        scaled = step * (hp[1:2] * LOG2E)
        for s in range(spans):
            parts = split3(scaled[s * Q : s * Q + Q])
            cum_out[s * Q : s * Q + Q] = mm(tri, parts[0]) + mm(tri, parts[1]) + mm(tri, parts[2])
            conv = conv_taps(buf[s * Q : s * Q + Q + 8], kst[...])
            bc = (conv * sigmoid(conv)).astype(bf16)
            bc_out[s * Q : s * Q + Q] = bc
            gram[s] = mm(bc[:, 128:], bc[:, :128], 1, 1)
        preT_out[...] = jnp.transpose(pre)[:48]
        stepT_out[...] = jnp.transpose(step)[:48]
        cumT_out[...] = jnp.transpose(cum_out[...])[:48]
        mst[...] = jnp.zeros(mst.shape, bf16)

    inner = mm(normed[...], wi[...])
    inner_out[...] = inner
    buf[8 : 8 + tokens] = inner
    turn = lax.rem(128 - 8 * i, 128)
    colc[...] = pltpu.roll(cum_out[...], turn, 1)
    cols[...] = pltpu.roll(step_out[...], turn, 1)
    rows8 = pl.ds(pl.multiple_of(8 * i, 8), 8)
    rowp[...] = cumT_out[rows8] - jnp.log2(stepT_out[rows8])
    state[...] = jnp.zeros(state.shape, f32)
    masks = head_masks()

    def span(s, carry):
        at = pl.multiple_of(s * Q, Q)
        rows = pl.ds(at, Q)
        conv = conv_taps(buf[pl.ds(at, Q + 8)], kin[...])
        xs = conv * sigmoid(conv)
        x_low = xs.astype(bf16)
        col = colc[rows]
        total = col[Q - 1 : Q]
        growth = expand(jnp.exp2(col[:, :8]))
        weight = expand(jnp.exp2(total[:, :8] - col[:, :8]) * cols[rows][:, :8])
        xw_low = (xs * weight).astype(bf16)
        for j in range(HB):
            xst[j * Q : j * Q + Q] = x_low * masks[j]
            row = rowp[j : j + 1, rows]
            for r, half, diag in quads():
                part = gram[s, r : r + 64, half * 128 : half * 128 + 128]
                dec = decay_chunk(col[:, j : j + 1], row, r, half, diag)
                mst[r : r + 64, j * Q + half * 128 : j * Q + half * 128 + 128] = (part * dec).astype(bf16)
        intra = mm(mst[...], xst[...])
        state_in = state[...]
        states_out[s] = state_in
        bc = bc_out[rows]
        readout = mm(bc[:, 128:], state_in.astype(bf16), 1, 1)
        ssd_out[rows] = intra + growth * readout + kin[5:6] * xs
        local = mm(xw_low, bc[:, :128], 0, 0)
        fade = jnp.exp2(total)
        for j in range(HB):
            at_j = slice(j * HEAD, j * HEAD + HEAD)
            state[at_j] = fade[:, j : j + 1] * state_in[at_j] + local[at_j]
        return carry

    lax.fori_loop(0, spans, span, 0)


def gate_forward(normed, cot, wg, wo, ssd, gain, gate_out, ggo_out, stats_out, sq, gi):
    i = pl.program_id(0)

    @pl.when(i == 0)
    def _():
        sq[...] = jnp.zeros(sq.shape, f32)
        gi[...] = jnp.zeros(gi.shape, f32)

    gate = mm(normed[...], wg[...])
    gate_out[...] = gate
    ggo = mm(cot[...], wo[...])
    ggo_out[...] = ggo
    gated = ssd[...] * (gate * sigmoid(gate))
    squares = gated * gated
    sq[...] += squares[:, :128] + squares[:, 128:]
    inner = ggo * gain[0:1] * gated
    gi[...] += inner[:, :128] + inner[:, 128:]

    @pl.when(i == pl.num_programs(0) - 1)
    def _():
        lane = iota(sq.shape, 1)
        both = jnp.where(
            lane == 0,
            jnp.sum(sq[...], axis=1, keepdims=True),
            jnp.where(lane == 1, jnp.sum(gi[...], axis=1, keepdims=True), 0.0),
        )
        stats_out[...] = jnp.transpose(both)[:8]


def gate_backward(unit_total, stats, gate, ssd, ggo, gain, dy_out, dgate_out, ng_out, gg_out, cols):
    @pl.when(pl.program_id(0) == 0)
    def _():
        full = jnp.concatenate([stats[...], jnp.zeros((120, stats.shape[1]), f32)], axis=0)
        cols[...] = jnp.transpose(full)

    rstd = lax.rsqrt(cols[:, 0:1] / unit_total + norm_eps)
    pull = rstd * rstd * rstd * (cols[:, 1:2] / unit_total)
    v = gate[...]
    sig = sigmoid(v)
    act = v * sig
    y = ssd[...]
    gated = y * act
    scaled = gated * rstd
    ng_out[...] = (scaled * gain[0:1]).astype(bf16)
    gg = ggo[...]
    gg_out[...] = jnp.broadcast_to(jnp.sum(gg * scaled, axis=0, keepdims=True), gg_out.shape)
    grad = rstd * (gg * gain[0:1]) - gated * pull
    dy_out[...] = (grad * act).astype(bf16)
    dgate_out[...] = (grad * y * (sig * (1.0 + v * (1.0 - sig)))).astype(bf16)


def mixer_backward(
    inner, dy, states, kin, kst, hp, cst, bc_in, step_in, cum_in, stepT, cumT, preT, rateT,
    dinner_out, gk_out, dsd_out, gks_out, hs_out,
    buf, dbuf, gram, gg, gb, gc, colc, cols, rowp, mst, dyst, gmix, sgrad, rs_t, cs_t, dr_t, wg_t, gt_t, gtaps,
):
    i = pl.program_id(0)
    tokens = inner.shape[0]
    spans = tokens // Q
    masks = head_masks()

    @pl.when(i == 0)
    def _():
        buf[0:8] = jnp.zeros((8, BW), f32)
        dbuf[tokens : tokens + 8] = jnp.zeros((8, BW), f32)
        for s in range(spans):
            bc = bc_in[s * Q : s * Q + Q]
            gram[s] = mm(bc[:, 128:], bc[:, :128], 1, 1)
        for ref in (gg, gb, gc, rs_t, cs_t, dr_t, wg_t, gt_t):
            ref[...] = jnp.zeros(ref.shape, f32)
        mst[...] = jnp.zeros(mst.shape, bf16)

    buf[8 : 8 + tokens] = inner[...]
    turn = lax.rem(128 - 8 * i, 128)
    colc[...] = pltpu.roll(cum_in[...], turn, 1)
    cols[...] = pltpu.roll(step_in[...], turn, 1)
    rows8 = pl.ds(pl.multiple_of(8 * i, 8), 8)
    rowp[...] = cumT[rows8] - jnp.log2(stepT[rows8])
    sgrad[...] = jnp.zeros(sgrad.shape, f32)
    gtaps[...] = jnp.zeros(gtaps.shape, f32)
    pick = (iota((8, BW), 1) // HEAD == iota((8, BW), 0)).astype(f32).astype(bf16)

    def conv_rows(at, kernel, grad_act):
        window = buf[pl.ds(at, Q + 8)]
        conv = conv_taps(window, kernel)
        sig = sigmoid(conv)
        gco = grad_act * (sig * (1.0 + conv * (1.0 - sig)))
        dbuf[pl.ds(at, Q)] = gco
        for k in range(4):
            prod = gco * (window[8:] if k == 3 else pltpu.roll(window, 3 - k, 0)[8:])
            gtaps[k : k + 1] += jnp.sum(prod, axis=0, keepdims=True)
        gtaps[4:5] += jnp.sum(gco, axis=0, keepdims=True)
        after = dbuf[pl.ds(at, Q + 8)]
        grad_in = kernel[3:4] * gco
        for k in range(3):
            grad_in = grad_in + kernel[k : k + 1] * pltpu.roll(after, Q + 8 - (3 - k), 0)[:Q]
        return grad_in

    def span(back, carry):
        s = spans - 1 - back
        at = pl.multiple_of(s * Q, Q)
        rows = pl.ds(at, Q)
        conv = conv_taps(buf[pl.ds(at, Q + 8)], kin[...])
        xs = conv * sigmoid(conv)
        x_low = xs.astype(bf16)
        dy_s = dy[rows]
        dy_f = dy_s.astype(f32)
        bc = bc_in[rows]
        b_low, c_low = bc[:, :128], bc[:, 128:]
        col = colc[rows]
        total = col[Q - 1 : Q]
        for j in range(HB):
            dyst[j * Q : j * Q + Q] = dy_s * masks[j]
        gmix[...] = mm(dyst[...], x_low, 1, 1)
        lane = iota((Q, 128), 1)
        row_sums = jnp.zeros((Q, 128), f32)
        for j in range(HB):
            row = rowp[j : j + 1, rows]
            col_sum = [jnp.zeros((1, 128), f32), jnp.zeros((1, 128), f32)]
            row_parts = []
            for r, half, diag in quads():
                here = slice(half * 128, half * 128 + 128)
                dec = decay_chunk(col[:, j : j + 1], row, r, half, diag)
                part = gram[s, r : r + 64, here]
                p = gmix[j * Q + r : j * Q + r + 64, here] * dec
                gg[s, r : r + 64, here] += p
                q = p * part
                mst[j * Q + r : j * Q + r + 64, here] = (part * dec).astype(bf16)
                col_sum[half] = col_sum[half] + jnp.sum(q, axis=0, keepdims=True)
                if half == 0:
                    row_parts.append(q)
                else:
                    row_parts[-1] = row_parts[-1] + q
            sums = jnp.concatenate([jnp.sum(q, axis=1, keepdims=True) for q in row_parts], axis=0)
            row_sums = jnp.where(lane == j, sums, row_sums)
            cs_t[pl.ds(8 * i + j, 1), rows] = jnp.concatenate(col_sum, axis=1)
        rs_t[rows8, rows] = jnp.transpose(row_sums)[:8]
        grad_xs = mm(mst[...], dyst[...], 0, 0) + kin[5:6] * dy_f

        growth = expand(jnp.exp2(col[:, :8]))
        weight = expand(jnp.exp2(total[:, :8] - col[:, :8]) * cols[rows][:, :8])
        state_in = states[s]
        state_low = state_in.astype(bf16)
        state_grad = sgrad[...]
        carry_low = state_grad.astype(bf16)
        readout = mm(c_low, state_low, 1, 1)
        read_low = (dy_f * growth).astype(bf16)
        hi, low = split2(dy_f * readout)
        dr_t[rows8, rows] = mm(pick, hi, 1, 1) + mm(pick, low, 1, 1)
        gc[rows] += mm(read_low, state_low)
        grad_xw = mm(b_low, carry_low, 1, 1)
        xw_low = (xs * weight).astype(bf16)
        gb[rows] += mm(xw_low, carry_low)
        hi, low = split2(grad_xw * xs)
        wg_t[rows8, rows] = mm(pick, hi, 1, 1) + mm(pick, low, 1, 1)
        hi, low = split2(state_grad * state_in)
        sums = jnp.sum(mm(pick, hi) + mm(pick, low), axis=1, keepdims=True)
        gt_t[rows8] = jnp.where(iota((8, 128), 1) == s, sums, gt_t[rows8])
        grad_xs = grad_xs + grad_xw * weight
        local = mm(read_low, c_low, 0, 0)
        fade = jnp.exp2(total)
        for j in range(HB):
            at_j = slice(j * HEAD, j * HEAD + HEAD)
            sgrad[at_j] = fade[:, j : j + 1] * state_grad[at_j] + local[at_j]
        gtaps[5:6] += jnp.sum(dy_f * xs, axis=0, keepdims=True)
        dinner_out[rows] = conv_rows(at, kin[...], grad_xs).astype(bf16)
        return carry

    lax.fori_loop(0, spans, span, 0)
    gk_out[...] = gtaps[...]

    @pl.when(i == pl.num_programs(0) - 1)
    def _():
        buf[8 : 8 + tokens] = cst[...]
        gtaps[...] = jnp.zeros(gtaps.shape, f32)
        rate = rateT[:, 0:1]
        later = (iota((Q, Q), 0) >= iota((Q, Q), 1)).astype(f32).astype(bf16)
        last = iota((48, Q), 1) == Q - 1
        bias_sum = jnp.zeros((48, 1), f32)
        decay_sum = jnp.zeros((48, 1), f32)
        for back in range(spans):
            s = spans - 1 - back
            rows = slice(s * Q, s * Q + Q)
            bc = bc_in[rows]
            gl = gg[s].astype(bf16)
            grad_c = gc[rows] + mm(gl, bc[:, :128])
            grad_b = gb[rows] + mm(gl, bc[:, 128:], 0, 0)
            both = jnp.concatenate([grad_b, grad_c], axis=1)
            dsd_out[rows, :BW] = conv_rows(s * Q, kst[...], both).astype(bf16)

            cum, step, pre = cumT[:, rows], stepT[:, rows], preT[:, rows]
            total = cum[:, Q - 1 : Q]
            rate_w = jnp.exp2(total - cum)
            wg = wg_t[:, rows]
            cs = cs_t[:, rows]
            moved = wg * (rate_w * step)
            grad_cum = rs_t[:, rows] - cs + jnp.exp2(cum) * dr_t[:, rows] - moved
            grad_total = jnp.exp2(total) * gt_t[:, s : s + 1] + jnp.sum(moved, axis=1, keepdims=True)
            grad_cum = grad_cum + jnp.where(last, grad_total, 0.0)
            parts = split3(grad_cum)
            grad_rate = mm(parts[0], later) + mm(parts[1], later) + mm(parts[2], later)
            sig = sigmoid(pre)
            ratio = jnp.where(pre < -15.0, 1.0, sig / step)
            grad_pre = (wg * rate_w + grad_rate * rate) * sig + cs * ratio
            bias_sum = bias_sum + jnp.sum(grad_pre, axis=1, keepdims=True)
            decay_sum = decay_sum + jnp.sum(grad_rate * step, axis=1, keepdims=True)
            full = jnp.concatenate([grad_pre, jnp.zeros((80, Q), f32)], axis=0)
            dsd_out[rows, BW:] = jnp.transpose(full).astype(bf16)
        gks_out[...] = gtaps[...]
        lane = iota((48, 128), 1)
        hs_out[...] = jnp.where(lane == 0, bias_sum, jnp.where(lane == 1, decay_sum * rate, 0.0))


class Place:
    def __init__(self):
        me = lax.axis_index("dp")
        self.me = me
        self.c, self.y, self.z = me % 2, (me // 2) % 2, me // 4

    def at(self, z, y, c):
        return (z * 2 + y) * 2 + c

    def core(self):
        return self.at(self.z, self.y, 1 - self.c)

    def side(self):
        return self.at(self.z, 1 - self.y, self.c)

    def up(self):
        return self.me + 4

    def down(self):
        return self.me - 4


def greet(here, across):
    barrier = pltpu.get_barrier_semaphore()

    def signal(**device):
        pl.semaphore_signal(barrier, 1, device_id=device, device_id_type=MESH)

    signal(dp=here.core())
    signal(dp=here.side())
    pl.when(here.z < 3)(lambda: signal(dp=here.up()))
    pl.when(here.z > 0)(lambda: signal(dp=here.down()))
    if across:
        signal(tensor=1 - lax.axis_index("tensor"))
    ends = (here.z == 0).astype(jnp.int32) + (here.z == 3).astype(jnp.int32)
    pl.semaphore_wait(barrier, 4 + int(across) - ends)


def remote(src, dst, send_sem, recv_sem, **device):
    return pltpu.make_async_remote_copy(
        src_ref=src, dst_ref=dst, send_sem=send_sem, recv_sem=recv_sem, device_id=device, device_id_type=MESH
    )


class Gather:
    def __init__(self, here, own, full, ss, rs):
        self.here, self.own, self.full, self.ss, self.rs = here, own, full, ss, rs
        self.rows = own.shape[0]

    def slot(self, origin):
        return self.full.at[pl.ds(pl.multiple_of(origin * self.rows, self.rows), self.rows)]

    def copy(self, origin, way, src=None):
        here = self.here
        target = (here.up, here.down, here.side, here.core)[way]()
        slot = self.slot(origin)
        return remote(slot if src is None else src, slot, self.ss.at[origin, way], self.rs.at[origin], dp=target)

    def arrived(self, origin):
        self.copy(origin, 3).wait_recv()

    def each_send(self, act):
        here = self.here
        for hops in range(4):
            for way, origin_z in ((0, here.z - hops), (1, here.z + hops)):
                if hops == 0:
                    if way == 1:
                        continue
                    origin = here.me
                    pl.when(here.z < 3)(lambda o=origin: act(o, 0))
                    pl.when(here.z > 0)(lambda o=origin: act(o, 1))
                    act(origin, 2)
                    act(origin, 3)
                    continue
                origin = here.at(origin_z, here.y, here.c)

                def go(o=origin, way=way):
                    pl.when((here.z < 3) if way == 0 else (here.z > 0))(lambda: act(o, way))
                    act(o, 2)
                    act(o, 3)

                pl.when((origin_z >= 0) & (origin_z <= 3))(go)

    def start(self):
        here = self.here
        pl.when(here.z < 3)(lambda: self.copy(here.me, 0, self.own).start())
        pl.when(here.z > 0)(lambda: self.copy(here.me, 1, self.own).start())
        self.copy(here.me, 2, self.own).start()
        self.copy(here.me, 3, self.own).start()

    def hop(self, hops):
        here = self.here
        for way, origin_z in ((0, here.z - hops), (1, here.z + hops)):

            def go(way=way, origin_z=origin_z):
                origin = here.at(origin_z, here.y, here.c)
                self.arrived(origin)
                pl.when((here.z < 3) if way == 0 else (here.z > 0))(lambda: self.copy(origin, way).start())
                self.copy(origin, 2).start()
                self.copy(origin, 3).start()

            pl.when((origin_z >= 0) & (origin_z <= 3))(go)

    def sides(self, hops):
        here = self.here
        for way, origin_z in ((0, here.z - hops), (1, here.z + hops)):
            if hops == 0 and way == 1:
                continue

            def go(origin_z=origin_z):
                origin = here.at(origin_z, 1 - here.y, here.c)
                self.arrived(origin)
                self.copy(origin, 3).start()

            pl.when((origin_z >= 0) & (origin_z <= 3))(go)

    def finish(self):
        here = self.here
        for z in range(4):
            for y in range(2):
                self.arrived(here.at(z, y, 1 - here.c))
        self.each_send(lambda origin, way: self.copy(origin, way).wait_send())
        for z in range(4):
            self.copy(here.at(z, 1 - here.y, here.c), 3).wait_send()


def gather_kernel(tokens_in, gain, pack, tokens_out, full, low, ss, rs, xs, xr, ls, norm):
    here = Place()
    half = lax.axis_index("tensor")
    rows = tokens_in.shape[0]
    greet(here, True)
    moves = Gather(here, pack, full, ss, rs)
    moves.start()
    own = pltpu.make_async_copy(pack, moves.slot(here.me), ls.at[0])
    own.start()
    part = rows // 4
    across, local = [], []
    for n in range(4):
        piece = slice(n * part, n * part + part)
        if norm:
            v = tokens_in[piece].astype(f32)
            scale = lax.rsqrt(jnp.mean(v * v, axis=1, keepdims=True) + norm_eps)
            low[piece] = (v * scale * gain[...]).astype(bf16)
        else:
            low[piece] = tokens_in[piece]
        slot = tokens_out.at[pl.ds(pl.multiple_of(half * rows + n * part, part), part)]
        across.append(remote(low.at[piece], slot, xs.at[n], xr.at[n], tensor=1 - half))
        across[-1].start()
        local.append(pltpu.make_async_copy(low.at[piece], slot, ls.at[n + 1]))
        local[-1].start()
    moves.hop(1)
    moves.sides(0)
    moves.hop(2)
    moves.sides(1)
    moves.hop(3)
    moves.sides(2)
    moves.sides(3)
    own.wait()
    for n in range(4):
        local[n].wait()
        across[n].wait()
    moves.finish()


def gather_rows(tokens_in, gain, pack, ways, norm, collective_id):
    rows, width = tokens_in.shape
    vmem = pl.BlockSpec(memory_space=pltpu.VMEM)
    hbm = pl.BlockSpec(memory_space=pl.ANY)
    return pl.pallas_call(
        functools.partial(gather_kernel, norm=norm),
        name="gather_rows",
        in_specs=[vmem, vmem, vmem],
        out_specs=[hbm, hbm],
        out_shape=[sds((2 * rows, width), bf16), sds((ways * pack.shape[0], pack.shape[1]), bf16)],
        scratch_shapes=[
            pltpu.VMEM((rows, width), bf16),
            pltpu.SemaphoreType.DMA((16, 4)), pltpu.SemaphoreType.DMA((16,)),
            pltpu.SemaphoreType.DMA((4,)), pltpu.SemaphoreType.DMA((4,)), pltpu.SemaphoreType.DMA((5,)),
        ],
        compiler_params=pltpu.CompilerParams(
            collective_id=collective_id, has_side_effects=True, vmem_limit_bytes=60 * 1024 * 1024
        ),
    )(tokens_in, gain, pack)


class Reduce:
    def __init__(self, here, grads, out, bufs, sems):
        self.here, self.grads, self.out = here, grads, out
        self.mine, self.buf_a, self.buf_b, self.buf_up, self.buf_dn = bufs
        self.local, self.send_a, self.recv_a, self.send_b, self.recv_b, self.send_c, self.recv_up, self.recv_dn = sems
        self.rows = out.shape[0]
        z = here.z
        self.order = (3 * (1 - z // 2), (3 * z + 2) % 5, 1 + z % 2, z)

    def block(self, z, y, c):
        at = pl.multiple_of(self.here.at(z, y, c) * self.rows, self.rows)
        return self.grads.at[pl.ds(at, self.rows)]

    def copy_a(self, z, y):
        here, at = self.here, z * 2 + y
        return remote(self.block(z, y, 1 - here.c), self.buf_a.at[at], self.send_a.at[at], self.recv_a.at[at], dp=here.core())

    def take(self, z, y):
        at = z * 2 + y
        return pltpu.make_async_copy(self.block(z, y, self.here.c), self.mine.at[at], self.local.at[at])

    def copy_b(self, z):
        here = self.here
        return remote(self.mine.at[z * 2 + 1 - here.y], self.buf_b.at[z], self.send_b.at[z], self.recv_b.at[z], dp=here.side())

    def copy_up(self, z):
        return remote(self.mine.at[z * 2 + self.here.y], self.buf_up.at[z], self.send_c.at[z], self.recv_up.at[z], dp=self.here.up())

    def copy_dn(self, z):
        return remote(self.mine.at[z * 2 + self.here.y], self.buf_dn.at[z], self.send_c.at[z], self.recv_dn.at[z], dp=self.here.down())

    def add(self, at, buf, slot):
        def rows(n, carry):
            piece = pl.ds(pl.multiple_of(n * 16, 16), 16)
            self.mine[at, piece] = (self.mine[at, piece].astype(f32) + buf[slot, piece].astype(f32)).astype(bf16)
            return carry

        lax.fori_loop(0, self.rows // 16, rows, 0)

    def start(self):
        here = self.here
        for side in (1 - here.y, here.y):
            for z in self.order:
                self.copy_a(z, side).start()
                self.take(z, side).start()

    def cores(self, n):
        here = self.here
        z = self.order[n]
        at = z * 2 + 1 - here.y
        self.take(z, 1 - here.y).wait()
        self.copy_a(z, 1 - here.y).wait_recv()
        self.add(at, self.buf_a, at)
        self.copy_b(z).start()

    def stay(self, n):
        here = self.here
        z = self.order[n]
        at = z * 2 + here.y
        self.take(z, here.y).wait()
        self.copy_a(z, here.y).wait_recv()
        self.add(at, self.buf_a, at)

    def sides(self, n):
        z = self.order[n]
        self.copy_b(z).wait_recv()
        self.add(z * 2 + self.here.y, self.buf_b, z)

    def pass_on(self, n):
        here = self.here
        z = self.order[n]
        at = z * 2 + here.y

        def up():
            def below():
                self.copy_up(z).wait_recv()
                self.add(at, self.buf_up, z)

            pl.when(here.z > 0)(below)
            self.copy_up(z).start()

        def down():
            def above():
                self.copy_dn(z).wait_recv()
                self.add(at, self.buf_dn, z)

            pl.when(here.z < 3)(above)
            self.copy_dn(z).start()

        pl.when(z > here.z)(up)
        pl.when(z < here.z)(down)

    def finish(self):
        here = self.here
        z = here.z
        at = z * 2 + here.y
        pl.when(z > 0)(lambda: self.copy_up(z).wait_recv())
        pl.when(z < 3)(lambda: self.copy_dn(z).wait_recv())

        def rows(n, carry):
            piece = pl.ds(pl.multiple_of(n * 16, 16), 16)
            below = jnp.where(z > 0, self.buf_up[z, piece].astype(f32), 0.0)
            above = jnp.where(z < 3, self.buf_dn[z, piece].astype(f32), 0.0)
            self.out[piece] = self.mine[at, piece].astype(f32) + below + above
            return carry

        lax.fori_loop(0, self.rows // 16, rows, 0)
        for n in range(4):
            zn = self.order[n]
            self.copy_a(zn, 0).wait_send()
            self.copy_a(zn, 1).wait_send()
            self.copy_b(zn).wait_send()
            pl.when(zn > z)(lambda zn=zn: self.copy_up(zn).wait_send())
            pl.when(zn < z)(lambda zn=zn: self.copy_dn(zn).wait_send())

    def all(self):
        self.start()
        for n in range(4):
            self.cores(n)
        for n in range(4):
            self.stay(n)
        for n in range(3):
            self.sides(n)
            self.pass_on(n)
        self.sides(3)


def reduce_scratch(rows, cols):
    sem = pltpu.SemaphoreType.DMA
    return [
        pltpu.VMEM((8, rows, cols), bf16), pltpu.VMEM((8, rows, cols), bf16), pltpu.VMEM((4, rows, cols), bf16),
        pltpu.VMEM((4, rows, cols), bf16), pltpu.VMEM((4, rows, cols), bf16),
        sem((8,)), sem((8,)), sem((8,)), sem((4,)), sem((4,)), sem((4,)), sem((4,)), sem((4,)),
    ]


def reduce_kernel(grads, out, *scratch):
    here = Place()
    greet(here, False)
    work = Reduce(here, grads, out, scratch[:5], scratch[5:])
    work.all()
    work.finish()


def reduce_small_kernel(grads, small, out, small_out, *scratch):
    here = Place()
    far = pltpu.get_barrier_semaphore()
    partners = [here.me + bit - 2 * bit * ((here.me // bit) % 2) for bit in (1, 2, 4, 8)]
    for partner in partners:
        pl.semaphore_signal(far, 1, device_id={"dp": partner}, device_id_type=MESH)
    middle = (here.z == 1) | (here.z == 2)
    pl.when(here.z == 1)(lambda: pl.semaphore_signal(far, 1, device_id={"dp": here.up()}, device_id_type=MESH))
    pl.when(here.z == 2)(lambda: pl.semaphore_signal(far, 1, device_id={"dp": here.down()}, device_id_type=MESH))
    pl.semaphore_wait(far, 4 + middle.astype(jnp.int32))
    work = Reduce(here, grads, out, scratch[:5], scratch[5:13])
    total, landed, send, recv = scratch[13:]
    total[0] = small[...]
    for k in range(4):
        if k == 0:
            work.start()
        swap = remote(total.at[k], landed.at[k], send.at[k], recv.at[k], dp=partners[k])
        swap.start()
        if k == 0:
            for n in range(4):
                work.cores(n)
            for n in range(4):
                work.stay(n)
        else:
            work.sides(k - 1)
            work.pass_on(k - 1)
        swap.wait()
        total[k + 1] = total[k] + landed[k]
    small_out[...] = total[4]
    work.sides(3)
    work.finish()


def reduce_rows(grads, ways, collective_id, small=None):
    rows, cols = grads.shape[0] // ways, grads.shape[1]
    vmem = pl.BlockSpec(memory_space=pltpu.VMEM)
    hbm = pl.BlockSpec(memory_space=pl.ANY)
    settings = pltpu.CompilerParams(
        collective_id=collective_id, has_side_effects=True, vmem_limit_bytes=60 * 1024 * 1024
    )
    if small is None:
        return pl.pallas_call(
            reduce_kernel, name="reduce_rows", in_specs=[hbm], out_specs=vmem, out_shape=sds((rows, cols)),
            scratch_shapes=reduce_scratch(rows, cols), compiler_params=settings,
        )(grads)
    return pl.pallas_call(
        reduce_small_kernel, name="reduce_rows_small", in_specs=[hbm, vmem], out_specs=[vmem, vmem],
        out_shape=[sds((rows, cols)), sds(small.shape)],
        scratch_shapes=reduce_scratch(rows, cols) + [
            pltpu.VMEM((5,) + small.shape, f32), pltpu.VMEM((4,) + small.shape, f32),
            pltpu.SemaphoreType.DMA((4,)), pltpu.SemaphoreType.DMA((4,)),
        ],
        compiler_params=settings,
    )(grads, small)


def swap(v):
    return lax.ppermute(v, "tensor", [(0, 1), (1, 0)])


def halves(v, axis):
    size = v.shape[axis] // 2
    me = lax.axis_index("tensor")
    return (
        lax.dynamic_slice_in_dim(v, me * size, size, axis),
        lax.dynamic_slice_in_dim(v, (1 - me) * size, size, axis),
    )


def once(shape, at=None):
    where = at or (0,) * len(shape)
    return pl.BlockSpec(shape, lambda i: where, pipeline_mode=pl.Buffered(1))


def by_cols(rows, offset=0):
    return pl.BlockSpec((rows, BW), lambda i: (0, i + offset))


def params():
    return pltpu.CompilerParams(dimension_semantics=("arbitrary",), vmem_limit_bytes=60 * 1024 * 1024)


def spread(v):
    lead = v.shape[:-1]
    v = v.reshape(lead + (v.shape[-1] // HB, HB))
    v = jnp.pad(v, [(0, 0)] * len(lead) + [(0, 0), (0, 8 - HB)]).reshape(lead + (-1,))
    return jnp.pad(v, [(0, 0)] * len(lead) + [(0, 128 - v.shape[-1])])


def gathered_heads(v, heads):
    return v[..., : heads * 2].reshape(v.shape[:-1] + (heads // HB, 8))[..., :HB].reshape(v.shape[:-1] + (heads,))


def sds(shape, dtype=f32):
    return jax.ShapeDtypeStruct(shape, dtype)


def on_device(
    residual, norm_gain, w_gate_inner, w_state_io, w_step, conv_inner, conv_state,
    step_bias, decay_log, skip_gain, gate_gain, w_output, cotangent,
):
    width = residual.shape[1]
    units = w_gate_inner.shape[2]
    heads = w_step.shape[1]
    blocks = units // BW
    unit_total = units * lax.axis_size("tensor")
    ways = lax.axis_size("dp")
    own_links = ways == 16
    rows_in = residual.astype(f32)
    rstd_in = lax.rsqrt(jnp.mean(rows_in * rows_in, axis=1, keepdims=True) + norm_eps)
    scaled = rows_in * rstd_in
    pack_a = jnp.concatenate([w_gate_inner[1], w_state_io, spread(w_step)], axis=1)
    pack_b = jnp.concatenate([w_gate_inner[0], w_output.T], axis=1)
    if own_links:
        normed, wa = gather_rows(residual, norm_gain[None], pack_a, ways, True, 1)
    else:
        wa = lax.all_gather(pack_a, "dp", axis=0, tiled=True)
        normed = lax.all_gather((scaled * norm_gain).astype(bf16), "tensor", axis=0, tiled=True)
    tokens = normed.shape[0]
    spans = tokens // Q
    rate = -jnp.exp(decay_log)
    kin = jnp.concatenate([conv_inner, jnp.repeat(skip_gain, HEAD)[None], jnp.zeros((2, units), f32)], axis=0)
    kst = jnp.concatenate([conv_state, jnp.zeros((3, BW), f32)], axis=0)
    hp = jnp.concatenate([spread(step_bias)[None], spread(rate)[None], jnp.zeros((6, 128), f32)], axis=0)
    rate_t = jnp.broadcast_to(spread(rate)[:48, None], (48, 128))
    gain8 = jnp.broadcast_to(gate_gain[None], (8, units))

    inner, ssd, states, cst, bc, step, cum, step_t, cum_t, pre_t = pl.pallas_call(
        mixer_forward,
        name="mixer_forward",
        grid=(blocks,),
        in_specs=[
            once((tokens, width)), by_cols(width), once((width, 384), (0, units // 384)),
            by_cols(8), once((8, BW)), once((8, 128)),
        ],
        out_specs=[
            by_cols(tokens), by_cols(tokens), pl.BlockSpec((spans, BW, 128), lambda i: (0, i, 0)),
            once((tokens, BW)), once((tokens, BW)), once((tokens, 128)), once((tokens, 128)),
            once((48, tokens)), once((48, tokens)), once((48, tokens)),
        ],
        out_shape=[
            sds((tokens, units)), sds((tokens, units)), sds((spans, units, 128)),
            sds((tokens, BW)), sds((tokens, BW), bf16), sds((tokens, 128)), sds((tokens, 128)),
            sds((48, tokens)), sds((48, tokens)), sds((48, tokens)),
        ],
        scratch_shapes=[
            pltpu.VMEM((tokens + 8, BW), f32), pltpu.VMEM((spans, Q, Q), f32),
            pltpu.VMEM((tokens, 128), f32), pltpu.VMEM((tokens, 128), f32), pltpu.VMEM((8, tokens), f32),
            pltpu.VMEM((Q, HB * Q), bf16), pltpu.VMEM((HB * Q, BW), bf16), pltpu.VMEM((BW, 128), f32),
        ],
        compiler_params=params(),
        cost_estimate=pl.CostEstimate(flops=2 * tokens * width * (units + 384) + 4 * tokens * 256 * units, bytes_accessed=30_000_000, transcendentals=heads * spans * Q * Q),
    )(normed, wa, wa, kin, kst, hp)

    if own_links:
        cot, wb = gather_rows(cotangent, norm_gain[None], pack_b, ways, False, 2)
    else:
        wb = lax.all_gather(pack_b, "dp", axis=0, tiled=True)
        cot = lax.all_gather(cotangent, "tensor", axis=0, tiled=True)

    gate, ggo, stats = pl.pallas_call(
        gate_forward,
        name="gate_forward",
        grid=(blocks,),
        in_specs=[
            once((tokens, width)), once((tokens, width)), by_cols(width), by_cols(width, blocks),
            by_cols(tokens), by_cols(8),
        ],
        out_specs=[by_cols(tokens), by_cols(tokens), once((8, tokens))],
        out_shape=[sds((tokens, units)), sds((tokens, units)), sds((8, tokens))],
        scratch_shapes=[pltpu.VMEM((tokens, 128), f32), pltpu.VMEM((tokens, 128), f32)],
        compiler_params=params(),
        cost_estimate=pl.CostEstimate(flops=4 * tokens * width * units, bytes_accessed=35_000_000, transcendentals=tokens * units),
    )(normed, cot, wb, wb, ssd, gain8)
    stats = stats + swap(stats)

    dy, dgate, ng, ggg = pl.pallas_call(
        functools.partial(gate_backward, float(unit_total)),
        name="gate_backward",
        grid=(blocks,),
        in_specs=[once((8, tokens)), by_cols(tokens), by_cols(tokens), by_cols(tokens), by_cols(8)],
        out_specs=[by_cols(tokens), by_cols(tokens), by_cols(tokens), by_cols(8)],
        out_shape=[sds((tokens, units), bf16), sds((tokens, units), bf16), sds((tokens, units), bf16), sds((8, units))],
        scratch_shapes=[pltpu.VMEM((tokens, 128), f32)],
        compiler_params=params(),
        cost_estimate=pl.CostEstimate(flops=20 * tokens * units, bytes_accessed=30_000_000, transcendentals=tokens * units),
    )(stats, gate, ssd, ggo, gain8)

    grad_wo = mm(cot, ng, 0, 0).astype(bf16)
    grad_wg = mm(normed, dgate, 0, 0).astype(bf16)
    grad_b = jnp.concatenate([grad_wg, grad_wo], axis=1)
    if own_links:
        wb_shard = reduce_rows(grad_b, ways, 3)
    else:
        wb_shard = lax.psum_scatter(grad_b, "dp", scatter_dimension=0, tiled=True).astype(f32)
    mixed, mixed_far = halves(mm(ng, wb[:, units:], 1, 1).astype(bf16), 0)
    output = (rows_in + mixed.astype(f32) + swap(mixed_far).astype(f32)).astype(bf16)

    dinner, gk, dsd, gks, hs = pl.pallas_call(
        mixer_backward,
        name="mixer_backward",
        grid=(blocks,),
        in_specs=[
            by_cols(tokens), by_cols(tokens), pl.BlockSpec((spans, BW, 128), lambda i: (0, i, 0)),
            by_cols(8), once((8, BW)), once((8, 128)),
            once((tokens, BW)), once((tokens, BW)), once((tokens, 128)), once((tokens, 128)),
            once((48, tokens)), once((48, tokens)), once((48, tokens)), once((48, 128)),
        ],
        out_specs=[by_cols(tokens), by_cols(8), once((tokens, 384)), once((8, BW)), once((48, 128))],
        out_shape=[sds((tokens, units), bf16), sds((8, units)), sds((tokens, 384), bf16), sds((8, BW)), sds((48, 128))],
        scratch_shapes=[
            pltpu.VMEM((tokens + 8, BW), f32), pltpu.VMEM((tokens + 8, BW), f32),
            pltpu.VMEM((spans, Q, Q), f32), pltpu.VMEM((spans, Q, Q), f32),
            pltpu.VMEM((tokens, 128), f32), pltpu.VMEM((tokens, 128), f32),
            pltpu.VMEM((tokens, 128), f32), pltpu.VMEM((tokens, 128), f32), pltpu.VMEM((8, tokens), f32),
            pltpu.VMEM((HB * Q, Q), bf16), pltpu.VMEM((HB * Q, BW), bf16), pltpu.VMEM((HB * Q, Q), f32),
            pltpu.VMEM((BW, 128), f32),
            pltpu.VMEM((48, tokens), f32), pltpu.VMEM((48, tokens), f32), pltpu.VMEM((48, tokens), f32),
            pltpu.VMEM((48, tokens), f32), pltpu.VMEM((48, 128), f32), pltpu.VMEM((8, BW), f32),
        ],
        compiler_params=params(),
        cost_estimate=pl.CostEstimate(flops=40_000_000_000, bytes_accessed=30_000_000, transcendentals=heads * spans * Q * Q),
    )(inner, dy, states, kin, kst, hp, cst, bc, step, cum, step_t, cum_t, pre_t, rate_t)

    grad_wi = mm(normed, dinner, 0, 0).astype(bf16)
    grad_ws = mm(normed, dsd, 0, 0).astype(bf16)
    grad_a = jnp.concatenate([grad_wi, grad_ws], axis=1)
    tail = jnp.concatenate([gks[:5].reshape(-1), hs[:, 0], hs[:, 1], jnp.zeros((units - 5 * BW - 96,), f32)])
    small = jnp.concatenate([gk[:6], ggg[:1], tail[None]], axis=0)
    if own_links:
        wa_shard, small = reduce_rows(grad_a, ways, 4, small)
    else:
        wa_shard = lax.psum_scatter(grad_a, "dp", scatter_dimension=0, tiled=True).astype(f32)
        small = lax.psum(small, "dp")
    near, far = halves(
        (mm(dgate, wb[:, :units], 1, 1) + mm(dinner, wa[:, :units], 1, 1) + mm(dsd, wa[:, units:], 1, 1)).astype(bf16),
        0,
    )
    grad_normed = near.astype(f32) + swap(far).astype(f32)
    grad_v = grad_normed * norm_gain
    grad_residual = cotangent.astype(f32) + rstd_in * (
        grad_v - scaled * jnp.mean(grad_v * scaled, axis=1, keepdims=True)
    )

    conv_state_sum = small[7, : 5 * BW].reshape(5, BW)
    bias_sum = gathered_heads(small[7, 5 * BW : 5 * BW + 48], heads)
    decay_sum = gathered_heads(small[7, 5 * BW + 48 : 5 * BW + 96], heads)
    skip_sum = jnp.sum(small[5].reshape(heads, HEAD), axis=1)

    gain_rows = jnp.sum(wb_shard[:, :units] * w_gate_inner[0].astype(f32), axis=1) + jnp.sum(
        wa_shard * pack_a.astype(f32), axis=1
    )
    count = gain_rows.shape[0]
    gain_own = gain_rows / lax.dynamic_slice_in_dim(norm_gain, lax.axis_index("dp") * count, count)
    near_s, far_s = halves(jnp.concatenate([wa_shard[:, units : units + BW], conv_state_sum], axis=0), 1)
    near_g, far_g = halves(gain_own, 0)
    far_all = jnp.concatenate([far_s.reshape(-1), far_g])
    got = swap(far_all)
    both = near_s + got[: far_s.size].reshape(far_s.shape)
    gain_part = near_g + got[far_s.size :]
    return (
        output,
        grad_residual,
        gain_part,
        jnp.stack([wb_shard[:, :units], wa_shard[:, :units]]),
        both[:count],
        gathered_heads(wa_shard[:, units + BW :], heads),
        small[0:5],
        both[count:],
        bias_sum,
        decay_sum,
        skip_sum,
        small[6],
        wb_shard[:, units:].T,
    )


def solution(mesh):
    return jax.shard_map(
        on_device,
        mesh=mesh,
        in_specs=(
            P(("dp", "tensor"), None),
            P(),
            P(None, "dp", "tensor"),
            P("dp", None),
            P("dp", "tensor"),
            P(None, "tensor"),
            P(),
            P("tensor"),
            P("tensor"),
            P("tensor"),
            P("tensor"),
            P("tensor", "dp"),
            P(("dp", "tensor"), None),
        ),
        out_specs=(
            P(("dp", "tensor"), None),
            P(("dp", "tensor"), None),
            P(("dp", "tensor")),
            P(None, "dp", "tensor"),
            P("dp", "tensor"),
            P("dp", "tensor"),
            P(None, "tensor"),
            P(None, "tensor"),
            P("tensor"),
            P("tensor"),
            P("tensor"),
            P("tensor"),
            P("tensor", "dp"),
        ),
        check_vma=False,
    )
```

```python
import functools

import jax
import jax.numpy as jnp
from jax import lax
from jax.experimental import pallas as pl
from jax.experimental.pallas import tpu as pltpu
from jax.sharding import PartitionSpec as P

Q = 256
LEN = 1024
HEAD = 64
BW = 256
HB = BW // HEAD
LOG2E = 1.4426950408889634
FAR = -1e30
norm_eps = 1e-05
MESH = pl.DeviceIdType.MESH
f32 = jnp.float32
bf16 = jnp.bfloat16


def mm(a, b, ca=1, cb=0):
    return lax.dot_general(a, b, (((ca,), (cb,)), ((), ())), preferred_element_type=f32)


def sigmoid(v):
    return 1.0 / (1.0 + jnp.exp(-v))


def split3(a):
    hi = a.astype(bf16)
    rest = a - hi.astype(f32)
    mid = rest.astype(bf16)
    low = (rest - mid.astype(f32)).astype(bf16)
    return hi, mid, low


def split2(a):
    hi = a.astype(bf16)
    return hi, (a - hi.astype(f32)).astype(bf16)


def iota(shape, axis):
    return lax.broadcasted_iota(jnp.int32, shape, axis)


def expand(cols):
    rows = cols.shape[0]
    left = iota((rows, 128), 1) < HEAD
    return jnp.concatenate(
        [jnp.where(left, cols[:, 2 * q : 2 * q + 1], cols[:, 2 * q + 1 : 2 * q + 2]) for q in range(2)],
        axis=1,
    )


def conv_taps(window, kernel):
    out = kernel[4:5] + kernel[3:4] * window[8:]
    for k in range(3):
        out = out + kernel[k : k + 1] * pltpu.roll(window, 3 - k, 0)[8:]
    return out


def head_masks():
    lane = iota((1, BW), 1) // HEAD
    return [(lane == j).astype(f32).astype(bf16) for j in range(HB)]


def quads():
    for r in range(0, Q, 64):
        for half in range(2):
            if half * 128 <= r:
                yield r, half, r < half * 128 + 128


def decay_chunk(col, row, r, half, diag):
    gap = col[r : r + 64] - row[:, half * 128 : half * 128 + 128]
    if diag:
        keep = iota((64, 128), 0) + (r - half * 128) >= iota((64, 128), 1)
        gap = jnp.where(keep, gap, FAR)
    return jnp.exp2(gap)


def mixer_forward(links, normed, wi, wsx, kin, kst, hp, *refs):
    refs = list(refs)
    if links:
        cot, pack = refs[:2]
        cot_out, wb = refs[12:14]
        refs = refs[2:12] + refs[14:]
    inner_out, ssd_out, states_out, cst_out, bc_out, step_out, cum_out, stepT_out, cumT_out, preT_out = refs[:10]
    buf, gram, colc, cols, rowp, mst, xst, state = refs[10:18]
    i = pl.program_id(0)
    tokens = normed.shape[0]
    spans = tokens // Q
    work = BesideForward(cot, pack, cot_out, wb, *refs[18:]) if links else None

    if links:
        pl.when(i == 0)(work.start)

    @pl.when(i == 0)
    def _():
        proj = mm(normed[...], wsx[...])
        buf[0:8] = jnp.zeros((8, BW), f32)
        cst_out[...] = proj[:, :BW]
        buf[8 : 8 + tokens] = proj[:, :BW]
        tri = (iota((Q, Q), 0) >= iota((Q, Q), 1)).astype(f32).astype(bf16)
        pre = proj[:, BW:] + hp[0:1]
        step = jnp.maximum(pre, 0.0) + jnp.log1p(jnp.exp(-jnp.abs(pre)))
        step_out[...] = step
        scaled = step * (hp[1:2] * LOG2E)
        for s in range(spans):
            parts = split3(scaled[s * Q : s * Q + Q])
            cum_out[s * Q : s * Q + Q] = mm(tri, parts[0]) + mm(tri, parts[1]) + mm(tri, parts[2])
            conv = conv_taps(buf[s * Q : s * Q + Q + 8], kst[...])
            bc = (conv * sigmoid(conv)).astype(bf16)
            bc_out[s * Q : s * Q + Q] = bc
            gram[s] = mm(bc[:, 128:], bc[:, :128], 1, 1)
        preT_out[...] = jnp.transpose(pre)[:48]
        stepT_out[...] = jnp.transpose(step)[:48]
        cumT_out[...] = jnp.transpose(cum_out[...])[:48]
        mst[...] = jnp.zeros(mst.shape, bf16)

    inner = mm(normed[...], wi[...])
    inner_out[...] = inner
    buf[8 : 8 + tokens] = inner
    turn = lax.rem(128 - 8 * i, 128)
    colc[...] = pltpu.roll(cum_out[...], turn, 1)
    cols[...] = pltpu.roll(step_out[...], turn, 1)
    rows8 = pl.ds(pl.multiple_of(8 * i, 8), 8)
    rowp[...] = cumT_out[rows8] - jnp.log2(stepT_out[rows8])
    state[...] = jnp.zeros(state.shape, f32)
    masks = head_masks()

    def span(s, carry):
        at = pl.multiple_of(s * Q, Q)
        rows = pl.ds(at, Q)
        conv = conv_taps(buf[pl.ds(at, Q + 8)], kin[...])
        xs = conv * sigmoid(conv)
        x_low = xs.astype(bf16)
        col = colc[rows]
        total = col[Q - 1 : Q]
        growth = expand(jnp.exp2(col[:, :8]))
        weight = expand(jnp.exp2(total[:, :8] - col[:, :8]) * cols[rows][:, :8])
        xw_low = (xs * weight).astype(bf16)
        for j in range(HB):
            xst[j * Q : j * Q + Q] = x_low * masks[j]
            row = rowp[j : j + 1, rows]
            for r, half, diag in quads():
                part = gram[s, r : r + 64, half * 128 : half * 128 + 128]
                dec = decay_chunk(col[:, j : j + 1], row, r, half, diag)
                mst[r : r + 64, j * Q + half * 128 : j * Q + half * 128 + 128] = (part * dec).astype(bf16)
        intra = mm(mst[...], xst[...])
        state_in = state[...]
        states_out[s] = state_in
        bc = bc_out[rows]
        readout = mm(bc[:, 128:], state_in.astype(bf16), 1, 1)
        ssd_out[rows] = intra + growth * readout + kin[5:6] * xs
        local = mm(xw_low, bc[:, :128], 0, 0)
        fade = jnp.exp2(total)
        for j in range(HB):
            at_j = slice(j * HEAD, j * HEAD + HEAD)
            state[at_j] = fade[:, j : j + 1] * state_in[at_j] + local[at_j]
        if links:
            work.step(i * spans + s)
        return carry

    lax.fori_loop(0, spans, span, 0)
    if links:
        pl.when(i == pl.num_programs(0) - 1)(work.finish)


class BesideForward:
    def __init__(self, cot, pack, cot_out, wb, ss, rs, xs, xr, ls):
        self.here = Place()
        self.moves = gathers(self.here, pack, wb, ss, rs)
        self.own = own_rows(self.here, pack, wb, ls.at[0])
        half = lax.axis_index("tensor")
        rows = cot.shape[0]
        slot = cot_out.at[pl.ds(pl.multiple_of(half * rows, rows), rows)]
        self.across = remote(cot, slot, xs, xr, tensor=1 - half)
        self.local = pltpu.make_async_copy(cot, slot, ls.at[1])

    def start(self):
        greet(self.here, True)
        for move in self.moves:
            move.start()
        self.across.start()
        self.own.start()
        self.local.start()

    def step(self, at):
        for when, chunk, hops in ((7, 0, 1), (11, 1, 1), (15, 0, 2), (19, 1, 2)):

            def go(move=self.moves[chunk], hops=hops):
                move.hop(hops)
                move.sides(hops - 1)

            pl.when(at == when)(go)

    def finish(self):
        for hops in (3, 4):
            for move in self.moves:
                if hops < 4:
                    move.hop(hops)
                move.sides(hops - 1)
        self.own.wait()
        self.local.wait()
        self.across.wait()
        for move in self.moves:
            move.finish()


def gate_forward(normed, cot, wg, wo, ssd, gain, gate_out, ggo_out, stats_out, sq, gi):
    i = pl.program_id(0)

    @pl.when(i == 0)
    def _():
        sq[...] = jnp.zeros(sq.shape, f32)
        gi[...] = jnp.zeros(gi.shape, f32)

    gate = mm(normed[...], wg[...])
    gate_out[...] = gate
    ggo = mm(cot[...], wo[...])
    ggo_out[...] = ggo
    gated = ssd[...] * (gate * sigmoid(gate))
    squares = gated * gated
    sq[...] += squares[:, :128] + squares[:, 128:]
    inner = ggo * gain[0:1] * gated
    gi[...] += inner[:, :128] + inner[:, 128:]

    @pl.when(i == pl.num_programs(0) - 1)
    def _():
        lane = iota(sq.shape, 1)
        both = jnp.where(
            lane == 0,
            jnp.sum(sq[...], axis=1, keepdims=True),
            jnp.where(lane == 1, jnp.sum(gi[...], axis=1, keepdims=True), 0.0),
        )
        stats_out[...] = jnp.transpose(both)[:8]


def gate_backward(unit_total, stats, gate, ssd, ggo, gain, dy_out, dgate_out, ng_out, gg_out, cols):
    @pl.when(pl.program_id(0) == 0)
    def _():
        full = jnp.concatenate([stats[...], jnp.zeros((120, stats.shape[1]), f32)], axis=0)
        cols[...] = jnp.transpose(full)

    rstd = lax.rsqrt(cols[:, 0:1] / unit_total + norm_eps)
    pull = rstd * rstd * rstd * (cols[:, 1:2] / unit_total)
    v = gate[...]
    sig = sigmoid(v)
    act = v * sig
    y = ssd[...]
    gated = y * act
    scaled = gated * rstd
    ng_out[...] = (scaled * gain[0:1]).astype(bf16)
    gg = ggo[...]
    gg_out[...] = jnp.broadcast_to(jnp.sum(gg * scaled, axis=0, keepdims=True), gg_out.shape)
    grad = rstd * (gg * gain[0:1]) - gated * pull
    dy_out[...] = (grad * act).astype(bf16)
    dgate_out[...] = (grad * y * (sig * (1.0 + v * (1.0 - sig)))).astype(bf16)


def mixer_backward(
    inner, dy, states, kin, kst, hp, cst, bc_in, step_in, cum_in, stepT, cumT, preT, rateT,
    dinner_out, gk_out, dsd_out, gks_out, hs_out,
    buf, dbuf, gram, gg, gb, gc, colc, cols, rowp, mst, dyst, gmix, sgrad, rs_t, cs_t, dr_t, wg_t, gt_t, gtaps,
):
    i = pl.program_id(0)
    tokens = inner.shape[0]
    spans = tokens // Q
    masks = head_masks()

    @pl.when(i == 0)
    def _():
        buf[0:8] = jnp.zeros((8, BW), f32)
        dbuf[tokens : tokens + 8] = jnp.zeros((8, BW), f32)
        for s in range(spans):
            bc = bc_in[s * Q : s * Q + Q]
            gram[s] = mm(bc[:, 128:], bc[:, :128], 1, 1)
        for ref in (gg, gb, gc, rs_t, cs_t, dr_t, wg_t, gt_t):
            ref[...] = jnp.zeros(ref.shape, f32)
        mst[...] = jnp.zeros(mst.shape, bf16)

    buf[8 : 8 + tokens] = inner[...]
    turn = lax.rem(128 - 8 * i, 128)
    colc[...] = pltpu.roll(cum_in[...], turn, 1)
    cols[...] = pltpu.roll(step_in[...], turn, 1)
    rows8 = pl.ds(pl.multiple_of(8 * i, 8), 8)
    rowp[...] = cumT[rows8] - jnp.log2(stepT[rows8])
    sgrad[...] = jnp.zeros(sgrad.shape, f32)
    gtaps[...] = jnp.zeros(gtaps.shape, f32)
    pick = (iota((8, BW), 1) // HEAD == iota((8, BW), 0)).astype(f32).astype(bf16)

    def conv_rows(at, kernel, grad_act):
        window = buf[pl.ds(at, Q + 8)]
        conv = conv_taps(window, kernel)
        sig = sigmoid(conv)
        gco = grad_act * (sig * (1.0 + conv * (1.0 - sig)))
        dbuf[pl.ds(at, Q)] = gco
        for k in range(4):
            prod = gco * (window[8:] if k == 3 else pltpu.roll(window, 3 - k, 0)[8:])
            gtaps[k : k + 1] += jnp.sum(prod, axis=0, keepdims=True)
        gtaps[4:5] += jnp.sum(gco, axis=0, keepdims=True)
        after = dbuf[pl.ds(at, Q + 8)]
        grad_in = kernel[3:4] * gco
        for k in range(3):
            grad_in = grad_in + kernel[k : k + 1] * pltpu.roll(after, Q + 8 - (3 - k), 0)[:Q]
        return grad_in

    def span(back, carry):
        s = spans - 1 - back
        at = pl.multiple_of(s * Q, Q)
        rows = pl.ds(at, Q)
        conv = conv_taps(buf[pl.ds(at, Q + 8)], kin[...])
        xs = conv * sigmoid(conv)
        x_low = xs.astype(bf16)
        dy_s = dy[rows]
        dy_f = dy_s.astype(f32)
        bc = bc_in[rows]
        b_low, c_low = bc[:, :128], bc[:, 128:]
        col = colc[rows]
        total = col[Q - 1 : Q]
        for j in range(HB):
            dyst[j * Q : j * Q + Q] = dy_s * masks[j]
        gmix[...] = mm(dyst[...], x_low, 1, 1)
        lane = iota((Q, 128), 1)
        row_sums = jnp.zeros((Q, 128), f32)
        for j in range(HB):
            row = rowp[j : j + 1, rows]
            col_sum = [jnp.zeros((1, 128), f32), jnp.zeros((1, 128), f32)]
            row_parts = []
            for r, half, diag in quads():
                here = slice(half * 128, half * 128 + 128)
                dec = decay_chunk(col[:, j : j + 1], row, r, half, diag)
                part = gram[s, r : r + 64, here]
                p = gmix[j * Q + r : j * Q + r + 64, here] * dec
                gg[s, r : r + 64, here] += p
                q = p * part
                mst[j * Q + r : j * Q + r + 64, here] = (part * dec).astype(bf16)
                col_sum[half] = col_sum[half] + jnp.sum(q, axis=0, keepdims=True)
                if half == 0:
                    row_parts.append(q)
                else:
                    row_parts[-1] = row_parts[-1] + q
            sums = jnp.concatenate([jnp.sum(q, axis=1, keepdims=True) for q in row_parts], axis=0)
            row_sums = jnp.where(lane == j, sums, row_sums)
            cs_t[pl.ds(8 * i + j, 1), rows] = jnp.concatenate(col_sum, axis=1)
        rs_t[rows8, rows] = jnp.transpose(row_sums)[:8]
        grad_xs = mm(mst[...], dyst[...], 0, 0) + kin[5:6] * dy_f

        growth = expand(jnp.exp2(col[:, :8]))
        weight = expand(jnp.exp2(total[:, :8] - col[:, :8]) * cols[rows][:, :8])
        state_in = states[s]
        state_low = state_in.astype(bf16)
        state_grad = sgrad[...]
        carry_low = state_grad.astype(bf16)
        readout = mm(c_low, state_low, 1, 1)
        read_low = (dy_f * growth).astype(bf16)
        hi, low = split2(dy_f * readout)
        dr_t[rows8, rows] = mm(pick, hi, 1, 1) + mm(pick, low, 1, 1)
        gc[rows] += mm(read_low, state_low)
        grad_xw = mm(b_low, carry_low, 1, 1)
        xw_low = (xs * weight).astype(bf16)
        gb[rows] += mm(xw_low, carry_low)
        hi, low = split2(grad_xw * xs)
        wg_t[rows8, rows] = mm(pick, hi, 1, 1) + mm(pick, low, 1, 1)
        hi, low = split2(state_grad * state_in)
        sums = jnp.sum(mm(pick, hi) + mm(pick, low), axis=1, keepdims=True)
        gt_t[rows8] = jnp.where(iota((8, 128), 1) == s, sums, gt_t[rows8])
        grad_xs = grad_xs + grad_xw * weight
        local = mm(read_low, c_low, 0, 0)
        fade = jnp.exp2(total)
        for j in range(HB):
            at_j = slice(j * HEAD, j * HEAD + HEAD)
            sgrad[at_j] = fade[:, j : j + 1] * state_grad[at_j] + local[at_j]
        gtaps[5:6] += jnp.sum(dy_f * xs, axis=0, keepdims=True)
        dinner_out[rows] = conv_rows(at, kin[...], grad_xs).astype(bf16)
        return carry

    lax.fori_loop(0, spans, span, 0)
    gk_out[...] = gtaps[...]

    @pl.when(i == pl.num_programs(0) - 1)
    def _():
        buf[8 : 8 + tokens] = cst[...]
        gtaps[...] = jnp.zeros(gtaps.shape, f32)
        rate = rateT[:, 0:1]
        later = (iota((Q, Q), 0) >= iota((Q, Q), 1)).astype(f32).astype(bf16)
        last = iota((48, Q), 1) == Q - 1
        bias_sum = jnp.zeros((48, 1), f32)
        decay_sum = jnp.zeros((48, 1), f32)
        for back in range(spans):
            s = spans - 1 - back
            rows = slice(s * Q, s * Q + Q)
            bc = bc_in[rows]
            gl = gg[s].astype(bf16)
            grad_c = gc[rows] + mm(gl, bc[:, :128])
            grad_b = gb[rows] + mm(gl, bc[:, 128:], 0, 0)
            both = jnp.concatenate([grad_b, grad_c], axis=1)
            dsd_out[rows, :BW] = conv_rows(s * Q, kst[...], both).astype(bf16)

            cum, step, pre = cumT[:, rows], stepT[:, rows], preT[:, rows]
            total = cum[:, Q - 1 : Q]
            rate_w = jnp.exp2(total - cum)
            wg = wg_t[:, rows]
            cs = cs_t[:, rows]
            moved = wg * (rate_w * step)
            grad_cum = rs_t[:, rows] - cs + jnp.exp2(cum) * dr_t[:, rows] - moved
            grad_total = jnp.exp2(total) * gt_t[:, s : s + 1] + jnp.sum(moved, axis=1, keepdims=True)
            grad_cum = grad_cum + jnp.where(last, grad_total, 0.0)
            parts = split3(grad_cum)
            grad_rate = mm(parts[0], later) + mm(parts[1], later) + mm(parts[2], later)
            sig = sigmoid(pre)
            ratio = jnp.where(pre < -15.0, 1.0, sig / step)
            grad_pre = (wg * rate_w + grad_rate * rate) * sig + cs * ratio
            bias_sum = bias_sum + jnp.sum(grad_pre, axis=1, keepdims=True)
            decay_sum = decay_sum + jnp.sum(grad_rate * step, axis=1, keepdims=True)
            full = jnp.concatenate([grad_pre, jnp.zeros((80, Q), f32)], axis=0)
            dsd_out[rows, BW:] = jnp.transpose(full).astype(bf16)
        gks_out[...] = gtaps[...]
        lane = iota((48, 128), 1)
        hs_out[...] = jnp.where(lane == 0, bias_sum, jnp.where(lane == 1, decay_sum * rate, 0.0))


class Place:
    def __init__(self):
        me = lax.axis_index("dp")
        self.me = me
        self.c, self.y, self.z = me % 2, (me // 2) % 2, me // 4

    def at(self, z, y, c):
        return (z * 2 + y) * 2 + c

    def core(self):
        return self.at(self.z, self.y, 1 - self.c)

    def side(self):
        return self.at(self.z, 1 - self.y, self.c)

    def up(self):
        return self.me + 4

    def down(self):
        return self.me - 4


def greet(here, across):
    barrier = pltpu.get_barrier_semaphore()

    def signal(**device):
        pl.semaphore_signal(barrier, 1, device_id=device, device_id_type=MESH)

    signal(dp=here.core())
    signal(dp=here.side())
    pl.when(here.z < 3)(lambda: signal(dp=here.up()))
    pl.when(here.z > 0)(lambda: signal(dp=here.down()))
    if across:
        signal(tensor=1 - lax.axis_index("tensor"))
    ends = (here.z == 0).astype(jnp.int32) + (here.z == 3).astype(jnp.int32)
    pl.semaphore_wait(barrier, 4 + int(across) - ends)


def remote(src, dst, send_sem, recv_sem, **device):
    return pltpu.make_async_remote_copy(
        src_ref=src, dst_ref=dst, send_sem=send_sem, recv_sem=recv_sem, device_id=device, device_id_type=MESH
    )


class Gather:
    def __init__(self, here, pack, full, ss, rs, chunk, cols):
        self.here, self.full, self.ss, self.rs, self.chunk, self.cols = here, full, ss, rs, chunk, cols
        self.rows = pack.shape[0]
        self.own = pack.at[:, cols]

    def slot(self, origin):
        return self.full.at[pl.ds(pl.multiple_of(origin * self.rows, self.rows), self.rows), self.cols]

    def copy(self, origin, way, src=None):
        here = self.here
        target = (here.up, here.down, here.side, here.core)[way]()
        slot = self.slot(origin)
        sems = self.ss.at[self.chunk, origin, way], self.rs.at[self.chunk, origin]
        return remote(slot if src is None else src, slot, *sems, dp=target)

    def arrived(self, origin):
        self.copy(origin, 3).wait_recv()

    def each_send(self, act):
        here = self.here
        for hops in range(4):
            for way, origin_z in ((0, here.z - hops), (1, here.z + hops)):
                if hops == 0:
                    if way == 1:
                        continue
                    origin = here.me
                    pl.when(here.z < 3)(lambda o=origin: act(o, 0))
                    pl.when(here.z > 0)(lambda o=origin: act(o, 1))
                    act(origin, 2)
                    act(origin, 3)
                    continue
                origin = here.at(origin_z, here.y, here.c)

                def go(o=origin, way=way):
                    pl.when((here.z < 3) if way == 0 else (here.z > 0))(lambda: act(o, way))
                    act(o, 2)
                    act(o, 3)

                pl.when((origin_z >= 0) & (origin_z <= 3))(go)

    def start(self):
        here = self.here
        pl.when(here.z < 3)(lambda: self.copy(here.me, 0, self.own).start())
        pl.when(here.z > 0)(lambda: self.copy(here.me, 1, self.own).start())
        self.copy(here.me, 2, self.own).start()
        self.copy(here.me, 3, self.own).start()

    def hop(self, hops):
        here = self.here
        for way, origin_z in ((0, here.z - hops), (1, here.z + hops)):

            def go(way=way, origin_z=origin_z):
                origin = here.at(origin_z, here.y, here.c)
                self.arrived(origin)
                pl.when((here.z < 3) if way == 0 else (here.z > 0))(lambda: self.copy(origin, way).start())
                self.copy(origin, 2).start()
                self.copy(origin, 3).start()

            pl.when((origin_z >= 0) & (origin_z <= 3))(go)

    def sides(self, hops):
        here = self.here
        for way, origin_z in ((0, here.z - hops), (1, here.z + hops)):
            if hops == 0 and way == 1:
                continue

            def go(origin_z=origin_z):
                origin = here.at(origin_z, 1 - here.y, here.c)
                self.arrived(origin)
                self.copy(origin, 3).start()

            pl.when((origin_z >= 0) & (origin_z <= 3))(go)

    def finish(self):
        here = self.here
        for z in range(4):
            for y in range(2):
                self.arrived(here.at(z, y, 1 - here.c))
        self.each_send(lambda origin, way: self.copy(origin, way).wait_send())
        for z in range(4):
            self.copy(here.at(z, 1 - here.y, here.c), 3).wait_send()


def gathers(here, pack, full, ss, rs):
    cols = pack.shape[1]
    cut = cols // 256 * 128
    return [Gather(here, pack, full, ss, rs, n, c) for n, c in enumerate((slice(0, cut), slice(cut, cols)))]


def own_rows(here, pack, full, sem):
    rows = pack.shape[0]
    return pltpu.make_async_copy(pack, full.at[pl.ds(pl.multiple_of(here.me * rows, rows), rows)], sem)


def gather_scratch():
    sem = pltpu.SemaphoreType.DMA
    return [sem((2, 16, 4)), sem((2, 16))]


def gather_kernel(tokens_in, gain, pack, tokens_out, full, low, ss, rs, xs, xr, ls):
    here = Place()
    half = lax.axis_index("tensor")
    rows = tokens_in.shape[0]
    greet(here, True)
    moves = gathers(here, pack, full, ss, rs)
    for move in moves:
        move.start()
    own = own_rows(here, pack, full, ls.at[0])
    own.start()
    part = rows // 4
    across, local = [], []
    for n in range(4):
        piece = slice(n * part, n * part + part)
        v = tokens_in[piece].astype(f32)
        scale = lax.rsqrt(jnp.mean(v * v, axis=1, keepdims=True) + norm_eps)
        low[piece] = (v * scale * gain[...]).astype(bf16)
        slot = tokens_out.at[pl.ds(pl.multiple_of(half * rows + n * part, part), part)]
        across.append(remote(low.at[piece], slot, xs.at[n], xr.at[n], tensor=1 - half))
        across[-1].start()
        local.append(pltpu.make_async_copy(low.at[piece], slot, ls.at[n + 1]))
        local[-1].start()
    for hops in range(1, 5):
        for move in moves:
            if hops < 4:
                move.hop(hops)
            move.sides(hops - 1)
    own.wait()
    for n in range(4):
        local[n].wait()
        across[n].wait()
    for move in moves:
        move.finish()


def gather_rows(tokens_in, gain, pack, ways, collective_id):
    rows, width = tokens_in.shape
    vmem = pl.BlockSpec(memory_space=pltpu.VMEM)
    hbm = pl.BlockSpec(memory_space=pl.ANY)
    return pl.pallas_call(
        gather_kernel,
        name="gather_rows",
        in_specs=[vmem, vmem, vmem],
        out_specs=[hbm, hbm],
        out_shape=[sds((2 * rows, width), bf16), sds((ways * pack.shape[0], pack.shape[1]), bf16)],
        scratch_shapes=[
            pltpu.VMEM((rows, width), bf16), *gather_scratch(),
            pltpu.SemaphoreType.DMA((4,)), pltpu.SemaphoreType.DMA((4,)), pltpu.SemaphoreType.DMA((5,)),
        ],
        compiler_params=pltpu.CompilerParams(
            collective_id=collective_id, has_side_effects=True, vmem_limit_bytes=60 * 1024 * 1024
        ),
    )(tokens_in, gain, pack)


class Reduce:
    def __init__(self, here, grads, out, bufs, sems):
        self.here, self.grads, self.out = here, grads, out
        self.mine, self.buf_a, self.buf_b, self.buf_up, self.buf_dn = bufs
        self.local, self.send_a, self.recv_a, self.send_b, self.recv_b, self.send_c, self.recv_up, self.recv_dn = sems
        self.rows = out.shape[0]
        z = here.z
        self.order = (3 * (1 - z // 2), (3 * z + 2) % 5, 1 + z % 2, z)

    def block(self, z, y, c):
        at = pl.multiple_of(self.here.at(z, y, c) * self.rows, self.rows)
        return self.grads.at[pl.ds(at, self.rows)]

    def copy_a(self, z, y):
        here, at = self.here, z * 2 + y
        return remote(self.block(z, y, 1 - here.c), self.buf_a.at[at], self.send_a.at[at], self.recv_a.at[at], dp=here.core())

    def take(self, z, y):
        at = z * 2 + y
        return pltpu.make_async_copy(self.block(z, y, self.here.c), self.mine.at[at], self.local.at[at])

    def copy_b(self, z):
        here = self.here
        return remote(self.mine.at[z * 2 + 1 - here.y], self.buf_b.at[z], self.send_b.at[z], self.recv_b.at[z], dp=here.side())

    def copy_up(self, z):
        return remote(self.mine.at[z * 2 + self.here.y], self.buf_up.at[z], self.send_c.at[z], self.recv_up.at[z], dp=self.here.up())

    def copy_dn(self, z):
        return remote(self.mine.at[z * 2 + self.here.y], self.buf_dn.at[z], self.send_c.at[z], self.recv_dn.at[z], dp=self.here.down())

    def add(self, at, buf, slot):
        def rows(n, carry):
            piece = pl.ds(pl.multiple_of(n * 16, 16), 16)
            self.mine[at, piece] = (self.mine[at, piece].astype(f32) + buf[slot, piece].astype(f32)).astype(bf16)
            return carry

        lax.fori_loop(0, self.rows // 16, rows, 0)

    def start(self):
        here = self.here
        for side in (1 - here.y, here.y):
            for z in self.order:
                self.copy_a(z, side).start()
                self.take(z, side).start()

    def cores(self, n):
        here = self.here
        z = self.order[n]
        at = z * 2 + 1 - here.y
        self.take(z, 1 - here.y).wait()
        self.copy_a(z, 1 - here.y).wait_recv()
        self.add(at, self.buf_a, at)
        self.copy_b(z).start()

    def stay(self, n):
        here = self.here
        z = self.order[n]
        at = z * 2 + here.y
        self.take(z, here.y).wait()
        self.copy_a(z, here.y).wait_recv()
        self.add(at, self.buf_a, at)

    def sides(self, n):
        z = self.order[n]
        self.copy_b(z).wait_recv()
        self.add(z * 2 + self.here.y, self.buf_b, z)

    def pass_on(self, n):
        here = self.here
        z = self.order[n]
        at = z * 2 + here.y

        def up():
            def below():
                self.copy_up(z).wait_recv()
                self.add(at, self.buf_up, z)

            pl.when(here.z > 0)(below)
            self.copy_up(z).start()

        def down():
            def above():
                self.copy_dn(z).wait_recv()
                self.add(at, self.buf_dn, z)

            pl.when(here.z < 3)(above)
            self.copy_dn(z).start()

        pl.when(z > here.z)(up)
        pl.when(z < here.z)(down)

    def finish(self):
        here = self.here
        z = here.z
        at = z * 2 + here.y
        pl.when(z > 0)(lambda: self.copy_up(z).wait_recv())
        pl.when(z < 3)(lambda: self.copy_dn(z).wait_recv())

        def rows(n, carry):
            piece = pl.ds(pl.multiple_of(n * 16, 16), 16)
            below = jnp.where(z > 0, self.buf_up[z, piece].astype(f32), 0.0)
            above = jnp.where(z < 3, self.buf_dn[z, piece].astype(f32), 0.0)
            self.out[piece] = self.mine[at, piece].astype(f32) + below + above
            return carry

        lax.fori_loop(0, self.rows // 16, rows, 0)
        for n in range(4):
            zn = self.order[n]
            self.copy_a(zn, 0).wait_send()
            self.copy_a(zn, 1).wait_send()
            self.copy_b(zn).wait_send()
            pl.when(zn > z)(lambda zn=zn: self.copy_up(zn).wait_send())
            pl.when(zn < z)(lambda zn=zn: self.copy_dn(zn).wait_send())

    def all(self):
        self.start()
        for n in range(4):
            self.cores(n)
        for n in range(4):
            self.stay(n)
        for n in range(3):
            self.sides(n)
            self.pass_on(n)
        self.sides(3)


def reduce_scratch(rows, cols):
    sem = pltpu.SemaphoreType.DMA
    return [
        pltpu.VMEM((8, rows, cols), bf16), pltpu.VMEM((8, rows, cols), bf16), pltpu.VMEM((4, rows, cols), bf16),
        pltpu.VMEM((4, rows, cols), bf16), pltpu.VMEM((4, rows, cols), bf16),
        sem((8,)), sem((8,)), sem((8,)), sem((4,)), sem((4,)), sem((4,)), sem((4,)), sem((4,)),
    ]


def reduce_kernel(grads, out, *scratch):
    here = Place()
    greet(here, False)
    work = Reduce(here, grads, out, scratch[:5], scratch[5:])
    work.all()
    work.finish()


def reduce_small_kernel(grads, small, out, small_out, *scratch):
    here = Place()
    far = pltpu.get_barrier_semaphore()
    partners = [here.me + bit - 2 * bit * ((here.me // bit) % 2) for bit in (1, 2, 4, 8)]
    for partner in partners:
        pl.semaphore_signal(far, 1, device_id={"dp": partner}, device_id_type=MESH)
    middle = (here.z == 1) | (here.z == 2)
    pl.when(here.z == 1)(lambda: pl.semaphore_signal(far, 1, device_id={"dp": here.up()}, device_id_type=MESH))
    pl.when(here.z == 2)(lambda: pl.semaphore_signal(far, 1, device_id={"dp": here.down()}, device_id_type=MESH))
    pl.semaphore_wait(far, 4 + middle.astype(jnp.int32))
    work = Reduce(here, grads, out, scratch[:5], scratch[5:13])
    total, landed, send, recv = scratch[13:]
    total[0] = small[...]
    for k in range(4):
        if k == 0:
            work.start()
        swap = remote(total.at[k], landed.at[k], send.at[k], recv.at[k], dp=partners[k])
        swap.start()
        if k == 0:
            for n in range(4):
                work.cores(n)
            for n in range(4):
                work.stay(n)
        else:
            work.sides(k - 1)
            work.pass_on(k - 1)
        swap.wait()
        total[k + 1] = total[k] + landed[k]
    small_out[...] = total[4]
    work.sides(3)
    work.finish()


def reduce_rows(grads, ways, collective_id, small=None):
    rows, cols = grads.shape[0] // ways, grads.shape[1]
    vmem = pl.BlockSpec(memory_space=pltpu.VMEM)
    hbm = pl.BlockSpec(memory_space=pl.ANY)
    settings = pltpu.CompilerParams(
        collective_id=collective_id, has_side_effects=True, vmem_limit_bytes=60 * 1024 * 1024
    )
    if small is None:
        return pl.pallas_call(
            reduce_kernel, name="reduce_rows", in_specs=[hbm], out_specs=vmem, out_shape=sds((rows, cols)),
            scratch_shapes=reduce_scratch(rows, cols), compiler_params=settings,
        )(grads)
    return pl.pallas_call(
        reduce_small_kernel, name="reduce_rows_small", in_specs=[hbm, vmem], out_specs=[vmem, vmem],
        out_shape=[sds((rows, cols)), sds(small.shape)],
        scratch_shapes=reduce_scratch(rows, cols) + [
            pltpu.VMEM((5,) + small.shape, f32), pltpu.VMEM((4,) + small.shape, f32),
            pltpu.SemaphoreType.DMA((4,)), pltpu.SemaphoreType.DMA((4,)),
        ],
        compiler_params=settings,
    )(grads, small)


def swap(v):
    return lax.ppermute(v, "tensor", [(0, 1), (1, 0)])


def halves(v, axis):
    size = v.shape[axis] // 2
    me = lax.axis_index("tensor")
    return (
        lax.dynamic_slice_in_dim(v, me * size, size, axis),
        lax.dynamic_slice_in_dim(v, (1 - me) * size, size, axis),
    )


def once(shape, at=None):
    where = at or (0,) * len(shape)
    return pl.BlockSpec(shape, lambda i: where, pipeline_mode=pl.Buffered(1))


def by_cols(rows, offset=0):
    return pl.BlockSpec((rows, BW), lambda i: (0, i + offset))


def params(collective_id=None):
    return pltpu.CompilerParams(
        dimension_semantics=("arbitrary",), vmem_limit_bytes=60 * 1024 * 1024,
        collective_id=collective_id, has_side_effects=collective_id is not None,
    )


def spread(v):
    lead = v.shape[:-1]
    v = v.reshape(lead + (v.shape[-1] // HB, HB))
    v = jnp.pad(v, [(0, 0)] * len(lead) + [(0, 0), (0, 8 - HB)]).reshape(lead + (-1,))
    return jnp.pad(v, [(0, 0)] * len(lead) + [(0, 128 - v.shape[-1])])


def gathered_heads(v, heads):
    return v[..., : heads * 2].reshape(v.shape[:-1] + (heads // HB, 8))[..., :HB].reshape(v.shape[:-1] + (heads,))


def sds(shape, dtype=f32):
    return jax.ShapeDtypeStruct(shape, dtype)


def on_device(
    residual, norm_gain, w_gate_inner, w_state_io, w_step, conv_inner, conv_state,
    step_bias, decay_log, skip_gain, gate_gain, w_output, cotangent,
):
    width = residual.shape[1]
    units = w_gate_inner.shape[2]
    heads = w_step.shape[1]
    blocks = units // BW
    unit_total = units * lax.axis_size("tensor")
    ways = lax.axis_size("dp")
    own_links = ways == 16
    rows_in = residual.astype(f32)
    rstd_in = lax.rsqrt(jnp.mean(rows_in * rows_in, axis=1, keepdims=True) + norm_eps)
    scaled = rows_in * rstd_in
    pack_a = jnp.concatenate([w_gate_inner[1], w_state_io, spread(w_step)], axis=1)
    pack_b = jnp.concatenate([w_gate_inner[0], w_output.T], axis=1)
    if own_links:
        normed, wa = gather_rows(residual, norm_gain[None], pack_a, ways, 1)
    else:
        wa = lax.all_gather(pack_a, "dp", axis=0, tiled=True)
        normed = lax.all_gather((scaled * norm_gain).astype(bf16), "tensor", axis=0, tiled=True)
    tokens = normed.shape[0]
    spans = tokens // Q
    rate = -jnp.exp(decay_log)
    kin = jnp.concatenate([conv_inner, jnp.repeat(skip_gain, HEAD)[None], jnp.zeros((2, units), f32)], axis=0)
    kst = jnp.concatenate([conv_state, jnp.zeros((3, BW), f32)], axis=0)
    hp = jnp.concatenate([spread(step_bias)[None], spread(rate)[None], jnp.zeros((6, 128), f32)], axis=0)
    rate_t = jnp.broadcast_to(spread(rate)[:48, None], (48, 128))
    gain8 = jnp.broadcast_to(gate_gain[None], (8, units))

    hbm = pl.BlockSpec(memory_space=pl.ANY)
    sem = pltpu.SemaphoreType.DMA
    inner, ssd, states, cst, bc, step, cum, step_t, cum_t, pre_t, *sent = pl.pallas_call(
        functools.partial(mixer_forward, own_links),
        name="mixer_forward",
        grid=(blocks,),
        in_specs=[
            once((tokens, width)), by_cols(width), once((width, 384), (0, units // 384)),
            by_cols(8), once((8, BW)), once((8, 128)),
        ] + [once(cotangent.shape), once(pack_b.shape)] * own_links,
        out_specs=[
            by_cols(tokens), by_cols(tokens), pl.BlockSpec((spans, BW, 128), lambda i: (0, i, 0)),
            once((tokens, BW)), once((tokens, BW)), once((tokens, 128)), once((tokens, 128)),
            once((48, tokens)), once((48, tokens)), once((48, tokens)),
        ] + [hbm, hbm] * own_links,
        out_shape=[
            sds((tokens, units)), sds((tokens, units)), sds((spans, units, 128)),
            sds((tokens, BW)), sds((tokens, BW), bf16), sds((tokens, 128)), sds((tokens, 128)),
            sds((48, tokens)), sds((48, tokens)), sds((48, tokens)),
        ] + [sds((tokens, width), bf16), sds((width, 2 * units), bf16)] * own_links,
        scratch_shapes=[
            pltpu.VMEM((tokens + 8, BW), f32), pltpu.VMEM((spans, Q, Q), f32),
            pltpu.VMEM((tokens, 128), f32), pltpu.VMEM((tokens, 128), f32), pltpu.VMEM((8, tokens), f32),
            pltpu.VMEM((Q, HB * Q), bf16), pltpu.VMEM((HB * Q, BW), bf16), pltpu.VMEM((BW, 128), f32),
        ] + (gather_scratch() + [sem, sem, sem((2,))]) * own_links,
        compiler_params=params(2 if own_links else None),
        cost_estimate=pl.CostEstimate(flops=2 * tokens * width * (units + 384) + 4 * tokens * 256 * units, bytes_accessed=30_000_000, transcendentals=heads * spans * Q * Q),
    )(normed, wa, wa, kin, kst, hp, *[cotangent, pack_b] * own_links)

    if own_links:
        cot, wb = sent
    else:
        wb = lax.all_gather(pack_b, "dp", axis=0, tiled=True)
        cot = lax.all_gather(cotangent, "tensor", axis=0, tiled=True)

    gate, ggo, stats = pl.pallas_call(
        gate_forward,
        name="gate_forward",
        grid=(blocks,),
        in_specs=[
            once((tokens, width)), once((tokens, width)), by_cols(width), by_cols(width, blocks),
            by_cols(tokens), by_cols(8),
        ],
        out_specs=[by_cols(tokens), by_cols(tokens), once((8, tokens))],
        out_shape=[sds((tokens, units)), sds((tokens, units)), sds((8, tokens))],
        scratch_shapes=[pltpu.VMEM((tokens, 128), f32), pltpu.VMEM((tokens, 128), f32)],
        compiler_params=params(),
        cost_estimate=pl.CostEstimate(flops=4 * tokens * width * units, bytes_accessed=35_000_000, transcendentals=tokens * units),
    )(normed, cot, wb, wb, ssd, gain8)
    stats = stats + swap(stats)

    dy, dgate, ng, ggg = pl.pallas_call(
        functools.partial(gate_backward, float(unit_total)),
        name="gate_backward",
        grid=(blocks,),
        in_specs=[once((8, tokens)), by_cols(tokens), by_cols(tokens), by_cols(tokens), by_cols(8)],
        out_specs=[by_cols(tokens), by_cols(tokens), by_cols(tokens), by_cols(8)],
        out_shape=[sds((tokens, units), bf16), sds((tokens, units), bf16), sds((tokens, units), bf16), sds((8, units))],
        scratch_shapes=[pltpu.VMEM((tokens, 128), f32)],
        compiler_params=params(),
        cost_estimate=pl.CostEstimate(flops=20 * tokens * units, bytes_accessed=30_000_000, transcendentals=tokens * units),
    )(stats, gate, ssd, ggo, gain8)

    grad_wo = mm(cot, ng, 0, 0).astype(bf16)
    grad_wg = mm(normed, dgate, 0, 0).astype(bf16)
    grad_b = jnp.concatenate([grad_wg, grad_wo], axis=1)
    if own_links:
        wb_shard = reduce_rows(grad_b, ways, 3)
    else:
        wb_shard = lax.psum_scatter(grad_b, "dp", scatter_dimension=0, tiled=True).astype(f32)
    mixed, mixed_far = halves(mm(ng, wb[:, units:], 1, 1).astype(bf16), 0)
    output = (rows_in + mixed.astype(f32) + swap(mixed_far).astype(f32)).astype(bf16)

    dinner, gk, dsd, gks, hs = pl.pallas_call(
        mixer_backward,
        name="mixer_backward",
        grid=(blocks,),
        in_specs=[
            by_cols(tokens), by_cols(tokens), pl.BlockSpec((spans, BW, 128), lambda i: (0, i, 0)),
            by_cols(8), once((8, BW)), once((8, 128)),
            once((tokens, BW)), once((tokens, BW)), once((tokens, 128)), once((tokens, 128)),
            once((48, tokens)), once((48, tokens)), once((48, tokens)), once((48, 128)),
        ],
        out_specs=[by_cols(tokens), by_cols(8), once((tokens, 384)), once((8, BW)), once((48, 128))],
        out_shape=[sds((tokens, units), bf16), sds((8, units)), sds((tokens, 384), bf16), sds((8, BW)), sds((48, 128))],
        scratch_shapes=[
            pltpu.VMEM((tokens + 8, BW), f32), pltpu.VMEM((tokens + 8, BW), f32),
            pltpu.VMEM((spans, Q, Q), f32), pltpu.VMEM((spans, Q, Q), f32),
            pltpu.VMEM((tokens, 128), f32), pltpu.VMEM((tokens, 128), f32),
            pltpu.VMEM((tokens, 128), f32), pltpu.VMEM((tokens, 128), f32), pltpu.VMEM((8, tokens), f32),
            pltpu.VMEM((HB * Q, Q), bf16), pltpu.VMEM((HB * Q, BW), bf16), pltpu.VMEM((HB * Q, Q), f32),
            pltpu.VMEM((BW, 128), f32),
            pltpu.VMEM((48, tokens), f32), pltpu.VMEM((48, tokens), f32), pltpu.VMEM((48, tokens), f32),
            pltpu.VMEM((48, tokens), f32), pltpu.VMEM((48, 128), f32), pltpu.VMEM((8, BW), f32),
        ],
        compiler_params=params(),
        cost_estimate=pl.CostEstimate(flops=40_000_000_000, bytes_accessed=30_000_000, transcendentals=heads * spans * Q * Q),
    )(inner, dy, states, kin, kst, hp, cst, bc, step, cum, step_t, cum_t, pre_t, rate_t)

    grad_wi = mm(normed, dinner, 0, 0).astype(bf16)
    grad_ws = mm(normed, dsd, 0, 0).astype(bf16)
    grad_a = jnp.concatenate([grad_wi, grad_ws], axis=1)
    tail = jnp.concatenate([gks[:5].reshape(-1), hs[:, 0], hs[:, 1], jnp.zeros((units - 5 * BW - 96,), f32)])
    small = jnp.concatenate([gk[:6], ggg[:1], tail[None]], axis=0)
    if own_links:
        wa_shard, small = reduce_rows(grad_a, ways, 4, small)
    else:
        wa_shard = lax.psum_scatter(grad_a, "dp", scatter_dimension=0, tiled=True).astype(f32)
        small = lax.psum(small, "dp")
    near, far = halves(
        (mm(dgate, wb[:, :units], 1, 1) + mm(dinner, wa[:, :units], 1, 1) + mm(dsd, wa[:, units:], 1, 1)).astype(bf16),
        0,
    )
    grad_normed = near.astype(f32) + swap(far).astype(f32)
    grad_v = grad_normed * norm_gain
    grad_residual = cotangent.astype(f32) + rstd_in * (
        grad_v - scaled * jnp.mean(grad_v * scaled, axis=1, keepdims=True)
    )

    conv_state_sum = small[7, : 5 * BW].reshape(5, BW)
    bias_sum = gathered_heads(small[7, 5 * BW : 5 * BW + 48], heads)
    decay_sum = gathered_heads(small[7, 5 * BW + 48 : 5 * BW + 96], heads)
    skip_sum = jnp.sum(small[5].reshape(heads, HEAD), axis=1)

    gain_rows = jnp.sum(wb_shard[:, :units] * w_gate_inner[0].astype(f32), axis=1) + jnp.sum(
        wa_shard * pack_a.astype(f32), axis=1
    )
    count = gain_rows.shape[0]
    gain_own = gain_rows / lax.dynamic_slice_in_dim(norm_gain, lax.axis_index("dp") * count, count)
    near_s, far_s = halves(jnp.concatenate([wa_shard[:, units : units + BW], conv_state_sum], axis=0), 1)
    near_g, far_g = halves(gain_own, 0)
    far_all = jnp.concatenate([far_s.reshape(-1), far_g])
    got = swap(far_all)
    both = near_s + got[: far_s.size].reshape(far_s.shape)
    gain_part = near_g + got[far_s.size :]
    return (
        output,
        grad_residual,
        gain_part,
        jnp.stack([wb_shard[:, :units], wa_shard[:, :units]]),
        both[:count],
        gathered_heads(wa_shard[:, units + BW :], heads),
        small[0:5],
        both[count:],
        bias_sum,
        decay_sum,
        skip_sum,
        small[6],
        wb_shard[:, units:].T,
    )


def solution(mesh):
    return jax.shard_map(
        on_device,
        mesh=mesh,
        in_specs=(
            P(("dp", "tensor"), None),
            P(),
            P(None, "dp", "tensor"),
            P("dp", None),
            P("dp", "tensor"),
            P(None, "tensor"),
            P(),
            P("tensor"),
            P("tensor"),
            P("tensor"),
            P("tensor"),
            P("tensor", "dp"),
            P(("dp", "tensor"), None),
        ),
        out_specs=(
            P(("dp", "tensor"), None),
            P(("dp", "tensor"), None),
            P(("dp", "tensor")),
            P(None, "dp", "tensor"),
            P("dp", "tensor"),
            P("dp", "tensor"),
            P(None, "tensor"),
            P(None, "tensor"),
            P("tensor"),
            P("tensor"),
            P("tensor"),
            P("tensor"),
            P("tensor", "dp"),
        ),
        check_vma=False,
    )
```

```python
import functools

import jax
import jax.numpy as jnp
from jax import lax
from jax.experimental import pallas as pl
from jax.experimental.pallas import tpu as pltpu
from jax.sharding import PartitionSpec as P

Q = 256
LEN = 1024
HEAD = 64
BW = 256
HB = BW // HEAD
LOG2E = 1.4426950408889634
FAR = -1e30
norm_eps = 1e-05
MESH = pl.DeviceIdType.MESH
f32 = jnp.float32
bf16 = jnp.bfloat16


def mm(a, b, ca=1, cb=0):
    return lax.dot_general(a, b, (((ca,), (cb,)), ((), ())), preferred_element_type=f32)


def sigmoid(v):
    return 1.0 / (1.0 + jnp.exp(-v))


def split3(a):
    hi = a.astype(bf16)
    rest = a - hi.astype(f32)
    mid = rest.astype(bf16)
    low = (rest - mid.astype(f32)).astype(bf16)
    return hi, mid, low


def split2(a):
    hi = a.astype(bf16)
    return hi, (a - hi.astype(f32)).astype(bf16)


def iota(shape, axis):
    return lax.broadcasted_iota(jnp.int32, shape, axis)


def expand(cols):
    rows = cols.shape[0]
    left = iota((rows, 128), 1) < HEAD
    return jnp.concatenate(
        [jnp.where(left, cols[:, 2 * q : 2 * q + 1], cols[:, 2 * q + 1 : 2 * q + 2]) for q in range(2)],
        axis=1,
    )


def conv_taps(window, kernel):
    out = kernel[4:5] + kernel[3:4] * window[8:]
    for k in range(3):
        out = out + kernel[k : k + 1] * pltpu.roll(window, 3 - k, 0)[8:]
    return out


def head_masks():
    lane = iota((1, BW), 1) // HEAD
    return [(lane == j).astype(f32).astype(bf16) for j in range(HB)]


def quads():
    for r in range(0, Q, 64):
        for half in range(2):
            if half * 128 <= r:
                yield r, half, r < half * 128 + 128


def decay_chunk(col, row, r, half, diag):
    gap = col[r : r + 64] - row[:, half * 128 : half * 128 + 128]
    if diag:
        keep = iota((64, 128), 0) + (r - half * 128) >= iota((64, 128), 1)
        gap = jnp.where(keep, gap, FAR)
    return jnp.exp2(gap)


def mixer_forward(links, normed, wi, wsx, kin, kst, hp, *refs):
    refs = list(refs)
    if links:
        cot, pack = refs[:2]
        cot_out, wb = refs[12:14]
        refs = refs[2:12] + refs[14:]
    inner_out, ssd_out, states_out, cst_out, bc_out, step_out, cum_out, stepT_out, cumT_out, preT_out = refs[:10]
    buf, gram, colc, cols, rowp, mst, xst, state = refs[10:18]
    i = pl.program_id(0)
    tokens = normed.shape[0]
    spans = tokens // Q
    work = BesideForward(cot, pack, cot_out, wb, *refs[18:]) if links else None

    if links:
        pl.when(i == 0)(work.start)

    @pl.when(i == 0)
    def _():
        proj = mm(normed[...], wsx[...])
        buf[0:8] = jnp.zeros((8, BW), f32)
        cst_out[...] = proj[:, :BW]
        buf[8 : 8 + tokens] = proj[:, :BW]
        tri = (iota((Q, Q), 0) >= iota((Q, Q), 1)).astype(f32).astype(bf16)
        pre = proj[:, BW:] + hp[0:1]
        step = jnp.maximum(pre, 0.0) + jnp.log1p(jnp.exp(-jnp.abs(pre)))
        step_out[...] = step
        scaled = step * (hp[1:2] * LOG2E)
        for s in range(spans):
            parts = split3(scaled[s * Q : s * Q + Q])
            cum_out[s * Q : s * Q + Q] = mm(tri, parts[0]) + mm(tri, parts[1]) + mm(tri, parts[2])
            conv = conv_taps(buf[s * Q : s * Q + Q + 8], kst[...])
            bc = (conv * sigmoid(conv)).astype(bf16)
            bc_out[s * Q : s * Q + Q] = bc
            gram[s] = mm(bc[:, 128:], bc[:, :128], 1, 1)
        preT_out[...] = jnp.transpose(pre)[:48]
        stepT_out[...] = jnp.transpose(step)[:48]
        cumT_out[...] = jnp.transpose(cum_out[...])[:48]
        mst[...] = jnp.zeros(mst.shape, bf16)

    inner = mm(normed[...], wi[...])
    inner_out[...] = inner
    buf[8 : 8 + tokens] = inner
    turn = lax.rem(128 - 8 * i, 128)
    colc[...] = pltpu.roll(cum_out[...], turn, 1)
    cols[...] = pltpu.roll(step_out[...], turn, 1)
    rows8 = pl.ds(pl.multiple_of(8 * i, 8), 8)
    rowp[...] = cumT_out[rows8] - jnp.log2(stepT_out[rows8])
    state[...] = jnp.zeros(state.shape, f32)
    masks = head_masks()

    def span(s, carry):
        at = pl.multiple_of(s * Q, Q)
        rows = pl.ds(at, Q)
        conv = conv_taps(buf[pl.ds(at, Q + 8)], kin[...])
        xs = conv * sigmoid(conv)
        x_low = xs.astype(bf16)
        col = colc[rows]
        total = col[Q - 1 : Q]
        growth = expand(jnp.exp2(col[:, :8]))
        weight = expand(jnp.exp2(total[:, :8] - col[:, :8]) * cols[rows][:, :8])
        xw_low = (xs * weight).astype(bf16)
        for j in range(HB):
            xst[j * Q : j * Q + Q] = x_low * masks[j]
            row = rowp[j : j + 1, rows]
            for r, half, diag in quads():
                part = gram[s, r : r + 64, half * 128 : half * 128 + 128]
                dec = decay_chunk(col[:, j : j + 1], row, r, half, diag)
                mst[r : r + 64, j * Q + half * 128 : j * Q + half * 128 + 128] = (part * dec).astype(bf16)
        intra = mm(mst[...], xst[...])
        state_in = state[...]
        states_out[s] = state_in
        bc = bc_out[rows]
        readout = mm(bc[:, 128:], state_in.astype(bf16), 1, 1)
        ssd_out[rows] = intra + growth * readout + kin[5:6] * xs
        local = mm(xw_low, bc[:, :128], 0, 0)
        fade = jnp.exp2(total)
        for j in range(HB):
            at_j = slice(j * HEAD, j * HEAD + HEAD)
            state[at_j] = fade[:, j : j + 1] * state_in[at_j] + local[at_j]
        if links:
            work.step(i * spans + s)
        return carry

    lax.fori_loop(0, spans, span, 0)
    if links:
        pl.when(i == pl.num_programs(0) - 1)(work.finish)


class BesideForward:
    def __init__(self, cot, pack, cot_out, wb, ss, rs, xs, xr, ls):
        self.here = Place()
        self.moves = gathers(self.here, pack, wb, ss, rs)
        self.own = own_rows(self.here, pack, wb, ls.at[0])
        half = lax.axis_index("tensor")
        rows = cot.shape[0]
        slot = cot_out.at[pl.ds(pl.multiple_of(half * rows, rows), rows)]
        self.across = remote(cot, slot, xs, xr, tensor=1 - half)
        self.local = pltpu.make_async_copy(cot, slot, ls.at[1])

    def start(self):
        greet(self.here, True)
        for move in self.moves:
            move.start()
        self.across.start()
        self.own.start()
        self.local.start()

    def step(self, at):
        for when, chunk, hops in ((7, 0, 1), (11, 1, 1), (15, 0, 2), (19, 1, 2)):

            def go(move=self.moves[chunk], hops=hops):
                move.hop(hops)
                move.sides(hops - 1)

            pl.when(at == when)(go)

    def finish(self):
        for hops in (3, 4):
            for move in self.moves:
                if hops < 4:
                    move.hop(hops)
                move.sides(hops - 1)
        self.own.wait()
        self.local.wait()
        self.across.wait()
        for move in self.moves:
            move.finish()


def gate_forward(links, normed, cot, wg, wo, ssd, gain, gate_out, ggo_out, stats_out, sq, gi, *refs):
    i = pl.program_id(0)

    @pl.when(i == 0)
    def _():
        if links:
            barrier = pltpu.get_barrier_semaphore()
            other = {"tensor": 1 - lax.axis_index("tensor")}
            pl.semaphore_signal(barrier, 1, device_id=other, device_id_type=MESH)
            pl.semaphore_wait(barrier, 1)
        sq[...] = jnp.zeros(sq.shape, f32)
        gi[...] = jnp.zeros(gi.shape, f32)

    gate = mm(normed[...], wg[...])
    gate_out[...] = gate
    ggo = mm(cot[...], wo[...])
    ggo_out[...] = ggo
    gated = ssd[...] * (gate * sigmoid(gate))
    squares = gated * gated
    sq[...] += squares[:, :128] + squares[:, 128:]
    inner = ggo * gain[0:1] * gated
    gi[...] += inner[:, :128] + inner[:, 128:]

    @pl.when(i == pl.num_programs(0) - 1)
    def _():
        lane = iota(sq.shape, 1)
        both = jnp.where(
            lane == 0,
            jnp.sum(sq[...], axis=1, keepdims=True),
            jnp.where(lane == 1, jnp.sum(gi[...], axis=1, keepdims=True), 0.0),
        )
        if not links:
            stats_out[...] = jnp.transpose(both)[:8]
            return
        mine, landed, send, recv = refs
        mine[...] = jnp.transpose(both)[:8]
        swap = remote(mine, landed, send, recv, tensor=1 - lax.axis_index("tensor"))
        swap.start()
        swap.wait()
        stats_out[...] = mine[...] + landed[...]


def gate_backward(
    unit_total, stats, gate, ssd, ggo, gain, normed, cot, dy_out, dgate_out, ng_out, gg_out, grads_out, cols, normed_t, cot_t
):
    @pl.when(pl.program_id(0) == 0)
    def _():
        full = jnp.concatenate([stats[...], jnp.zeros((120, stats.shape[1]), f32)], axis=0)
        cols[...] = jnp.transpose(full)

        def turn(n, carry):
            here = pl.ds(pl.multiple_of(n * 128, 128), 128)
            normed_t[here] = jnp.transpose(normed[:, here])
            cot_t[here] = jnp.transpose(cot[:, here])
            return carry

        lax.fori_loop(0, normed.shape[1] // 128, turn, 0)

    rstd = lax.rsqrt(cols[:, 0:1] / unit_total + norm_eps)
    pull = rstd * rstd * rstd * (cols[:, 1:2] / unit_total)
    v = gate[...]
    sig = sigmoid(v)
    act = v * sig
    y = ssd[...]
    gated = y * act
    scaled = gated * rstd
    ng = (scaled * gain[0:1]).astype(bf16)
    ng_out[...] = ng
    grads_out[1] = mm(cot_t[...], ng).astype(bf16)
    gg = ggo[...]
    gg_out[...] = jnp.broadcast_to(jnp.sum(gg * scaled, axis=0, keepdims=True), gg_out.shape)
    grad = rstd * (gg * gain[0:1]) - gated * pull
    dy_out[...] = (grad * act).astype(bf16)
    dgate = (grad * y * (sig * (1.0 + v * (1.0 - sig)))).astype(bf16)
    dgate_out[...] = dgate
    grads_out[0] = mm(normed_t[...], dgate).astype(bf16)


class BesideBackward:
    def __init__(self, mixed, grads, far_out, shard_out, scratch):
        self.here = Place()
        half = lax.axis_index("tensor")
        rows = far_out.shape[0]
        other = mixed.at[pl.ds(pl.multiple_of((1 - half) * rows, rows), rows)]
        self.across = remote(other, far_out, scratch[0], scratch[1], tensor=1 - half)
        self.sum = Reduce(self.here, grads, shard_out, scratch[2:7], scratch[7:15])

    def start(self):
        greet(self.here, True)
        self.sum.start()
        self.across.start()

    def step(self, at):
        total = self.sum
        z = self.here.z
        ends = (z == 0) | (z == 3)
        for n in range(4):
            pl.when(at == n)(lambda n=n: total.cores(n))
            pl.when(at == (4, 6, 7, 8)[n])(lambda n=n: total.stay(n))
            pl.when(at == (5, 10, 15, 19)[n])(lambda n=n: total.sides(n))
        for n in range(3):
            when = jnp.where(ends, (5, 10, 15)[n], (11, 16, 17)[n])
            pl.when(at == when)(lambda n=n: total.pass_on(n))

    def finish(self):
        self.sum.finish()
        self.across.wait()


def mixer_backward(links, inner, dy, states, kin, kst, hp, cst, bc_in, step_in, cum_in, stepT, cumT, preT, rateT, *refs):
    refs = list(refs)
    if links:
        beside = refs[:2] + refs[7:9]
        refs = refs[2:7] + refs[9:]
        work = BesideBackward(*beside, refs[24:])
    dinner_out, gk_out, dsd_out, gks_out, hs_out = refs[:5]
    buf, dbuf, gram, gg, gb, gc, colc, cols, rowp, mst, dyst, gmix, sgrad = refs[5:18]
    rs_t, cs_t, dr_t, wg_t, gt_t, gtaps = refs[18:24]
    i = pl.program_id(0)
    if links:
        pl.when(i == 0)(work.start)
    tokens = inner.shape[0]
    spans = tokens // Q
    masks = head_masks()

    @pl.when(i == 0)
    def _():
        buf[0:8] = jnp.zeros((8, BW), f32)
        dbuf[tokens : tokens + 8] = jnp.zeros((8, BW), f32)
        for s in range(spans):
            bc = bc_in[s * Q : s * Q + Q]
            gram[s] = mm(bc[:, 128:], bc[:, :128], 1, 1)
        for ref in (gg, gb, gc, rs_t, cs_t, dr_t, wg_t, gt_t):
            ref[...] = jnp.zeros(ref.shape, f32)
        mst[...] = jnp.zeros(mst.shape, bf16)

    buf[8 : 8 + tokens] = inner[...]
    turn = lax.rem(128 - 8 * i, 128)
    colc[...] = pltpu.roll(cum_in[...], turn, 1)
    cols[...] = pltpu.roll(step_in[...], turn, 1)
    rows8 = pl.ds(pl.multiple_of(8 * i, 8), 8)
    rowp[...] = cumT[rows8] - jnp.log2(stepT[rows8])
    sgrad[...] = jnp.zeros(sgrad.shape, f32)
    gtaps[...] = jnp.zeros(gtaps.shape, f32)
    pick = (iota((8, BW), 1) // HEAD == iota((8, BW), 0)).astype(f32).astype(bf16)

    def conv_rows(at, kernel, grad_act):
        window = buf[pl.ds(at, Q + 8)]
        conv = conv_taps(window, kernel)
        sig = sigmoid(conv)
        gco = grad_act * (sig * (1.0 + conv * (1.0 - sig)))
        dbuf[pl.ds(at, Q)] = gco
        for k in range(4):
            prod = gco * (window[8:] if k == 3 else pltpu.roll(window, 3 - k, 0)[8:])
            gtaps[k : k + 1] += jnp.sum(prod, axis=0, keepdims=True)
        gtaps[4:5] += jnp.sum(gco, axis=0, keepdims=True)
        after = dbuf[pl.ds(at, Q + 8)]
        grad_in = kernel[3:4] * gco
        for k in range(3):
            grad_in = grad_in + kernel[k : k + 1] * pltpu.roll(after, Q + 8 - (3 - k), 0)[:Q]
        return grad_in

    def span(back, carry):
        s = spans - 1 - back
        at = pl.multiple_of(s * Q, Q)
        rows = pl.ds(at, Q)
        conv = conv_taps(buf[pl.ds(at, Q + 8)], kin[...])
        xs = conv * sigmoid(conv)
        x_low = xs.astype(bf16)
        dy_s = dy[rows]
        dy_f = dy_s.astype(f32)
        bc = bc_in[rows]
        b_low, c_low = bc[:, :128], bc[:, 128:]
        col = colc[rows]
        total = col[Q - 1 : Q]
        for j in range(HB):
            dyst[j * Q : j * Q + Q] = dy_s * masks[j]
        gmix[...] = mm(dyst[...], x_low, 1, 1)
        lane = iota((Q, 128), 1)
        row_sums = jnp.zeros((Q, 128), f32)
        for j in range(HB):
            row = rowp[j : j + 1, rows]
            col_sum = [jnp.zeros((1, 128), f32), jnp.zeros((1, 128), f32)]
            row_parts = []
            for r, half, diag in quads():
                here = slice(half * 128, half * 128 + 128)
                dec = decay_chunk(col[:, j : j + 1], row, r, half, diag)
                part = gram[s, r : r + 64, here]
                p = gmix[j * Q + r : j * Q + r + 64, here] * dec
                gg[s, r : r + 64, here] += p
                q = p * part
                mst[j * Q + r : j * Q + r + 64, here] = (part * dec).astype(bf16)
                col_sum[half] = col_sum[half] + jnp.sum(q, axis=0, keepdims=True)
                if half == 0:
                    row_parts.append(q)
                else:
                    row_parts[-1] = row_parts[-1] + q
            sums = jnp.concatenate([jnp.sum(q, axis=1, keepdims=True) for q in row_parts], axis=0)
            row_sums = jnp.where(lane == j, sums, row_sums)
            cs_t[pl.ds(8 * i + j, 1), rows] = jnp.concatenate(col_sum, axis=1)
        rs_t[rows8, rows] = jnp.transpose(row_sums)[:8]
        grad_xs = mm(mst[...], dyst[...], 0, 0) + kin[5:6] * dy_f

        growth = expand(jnp.exp2(col[:, :8]))
        weight = expand(jnp.exp2(total[:, :8] - col[:, :8]) * cols[rows][:, :8])
        state_in = states[s]
        state_low = state_in.astype(bf16)
        state_grad = sgrad[...]
        carry_low = state_grad.astype(bf16)
        readout = mm(c_low, state_low, 1, 1)
        read_low = (dy_f * growth).astype(bf16)
        hi, low = split2(dy_f * readout)
        dr_t[rows8, rows] = mm(pick, hi, 1, 1) + mm(pick, low, 1, 1)
        gc[rows] += mm(read_low, state_low)
        grad_xw = mm(b_low, carry_low, 1, 1)
        xw_low = (xs * weight).astype(bf16)
        gb[rows] += mm(xw_low, carry_low)
        hi, low = split2(grad_xw * xs)
        wg_t[rows8, rows] = mm(pick, hi, 1, 1) + mm(pick, low, 1, 1)
        hi, low = split2(state_grad * state_in)
        sums = jnp.sum(mm(pick, hi) + mm(pick, low), axis=1, keepdims=True)
        gt_t[rows8] = jnp.where(iota((8, 128), 1) == s, sums, gt_t[rows8])
        grad_xs = grad_xs + grad_xw * weight
        local = mm(read_low, c_low, 0, 0)
        fade = jnp.exp2(total)
        for j in range(HB):
            at_j = slice(j * HEAD, j * HEAD + HEAD)
            sgrad[at_j] = fade[:, j : j + 1] * state_grad[at_j] + local[at_j]
        gtaps[5:6] += jnp.sum(dy_f * xs, axis=0, keepdims=True)
        dinner_out[rows] = conv_rows(at, kin[...], grad_xs).astype(bf16)
        if links:
            work.step(i * spans + back)
        return carry

    lax.fori_loop(0, spans, span, 0)
    gk_out[...] = gtaps[...]

    @pl.when(i == pl.num_programs(0) - 1)
    def _():
        buf[8 : 8 + tokens] = cst[...]
        gtaps[...] = jnp.zeros(gtaps.shape, f32)
        rate = rateT[:, 0:1]
        later = (iota((Q, Q), 0) >= iota((Q, Q), 1)).astype(f32).astype(bf16)
        last = iota((48, Q), 1) == Q - 1
        bias_sum = jnp.zeros((48, 1), f32)
        decay_sum = jnp.zeros((48, 1), f32)
        for back in range(spans):
            s = spans - 1 - back
            rows = slice(s * Q, s * Q + Q)
            bc = bc_in[rows]
            gl = gg[s].astype(bf16)
            grad_c = gc[rows] + mm(gl, bc[:, :128])
            grad_b = gb[rows] + mm(gl, bc[:, 128:], 0, 0)
            both = jnp.concatenate([grad_b, grad_c], axis=1)
            dsd_out[rows, :BW] = conv_rows(s * Q, kst[...], both).astype(bf16)

            cum, step, pre = cumT[:, rows], stepT[:, rows], preT[:, rows]
            total = cum[:, Q - 1 : Q]
            rate_w = jnp.exp2(total - cum)
            wg = wg_t[:, rows]
            cs = cs_t[:, rows]
            moved = wg * (rate_w * step)
            grad_cum = rs_t[:, rows] - cs + jnp.exp2(cum) * dr_t[:, rows] - moved
            grad_total = jnp.exp2(total) * gt_t[:, s : s + 1] + jnp.sum(moved, axis=1, keepdims=True)
            grad_cum = grad_cum + jnp.where(last, grad_total, 0.0)
            parts = split3(grad_cum)
            grad_rate = mm(parts[0], later) + mm(parts[1], later) + mm(parts[2], later)
            sig = sigmoid(pre)
            ratio = jnp.where(pre < -15.0, 1.0, sig / step)
            grad_pre = (wg * rate_w + grad_rate * rate) * sig + cs * ratio
            bias_sum = bias_sum + jnp.sum(grad_pre, axis=1, keepdims=True)
            decay_sum = decay_sum + jnp.sum(grad_rate * step, axis=1, keepdims=True)
            full = jnp.concatenate([grad_pre, jnp.zeros((80, Q), f32)], axis=0)
            dsd_out[rows, BW:] = jnp.transpose(full).astype(bf16)
        gks_out[...] = gtaps[...]
        lane = iota((48, 128), 1)
        hs_out[...] = jnp.where(lane == 0, bias_sum, jnp.where(lane == 1, decay_sum * rate, 0.0))
        if links:
            work.finish()


class Place:
    def __init__(self):
        me = lax.axis_index("dp")
        self.me = me
        self.c, self.y, self.z = me % 2, (me // 2) % 2, me // 4

    def at(self, z, y, c):
        return (z * 2 + y) * 2 + c

    def core(self):
        return self.at(self.z, self.y, 1 - self.c)

    def side(self):
        return self.at(self.z, 1 - self.y, self.c)

    def up(self):
        return self.me + 4

    def down(self):
        return self.me - 4


def greet(here, across):
    barrier = pltpu.get_barrier_semaphore()

    def signal(**device):
        pl.semaphore_signal(barrier, 1, device_id=device, device_id_type=MESH)

    signal(dp=here.core())
    signal(dp=here.side())
    pl.when(here.z < 3)(lambda: signal(dp=here.up()))
    pl.when(here.z > 0)(lambda: signal(dp=here.down()))
    if across:
        signal(tensor=1 - lax.axis_index("tensor"))
    ends = (here.z == 0).astype(jnp.int32) + (here.z == 3).astype(jnp.int32)
    pl.semaphore_wait(barrier, 4 + int(across) - ends)


def remote(src, dst, send_sem, recv_sem, **device):
    return pltpu.make_async_remote_copy(
        src_ref=src, dst_ref=dst, send_sem=send_sem, recv_sem=recv_sem, device_id=device, device_id_type=MESH
    )


class Gather:
    def __init__(self, here, pack, full, ss, rs, chunk, cols):
        self.here, self.full, self.ss, self.rs, self.chunk, self.cols = here, full, ss, rs, chunk, cols
        self.rows = pack.shape[0]
        self.own = pack.at[:, cols]

    def slot(self, origin):
        return self.full.at[pl.ds(pl.multiple_of(origin * self.rows, self.rows), self.rows), self.cols]

    def copy(self, origin, way, src=None):
        here = self.here
        target = (here.up, here.down, here.side, here.core)[way]()
        slot = self.slot(origin)
        sems = self.ss.at[self.chunk, origin, way], self.rs.at[self.chunk, origin]
        return remote(slot if src is None else src, slot, *sems, dp=target)

    def arrived(self, origin):
        self.copy(origin, 3).wait_recv()

    def each_send(self, act):
        here = self.here
        for hops in range(4):
            for way, origin_z in ((0, here.z - hops), (1, here.z + hops)):
                if hops == 0:
                    if way == 1:
                        continue
                    origin = here.me
                    pl.when(here.z < 3)(lambda o=origin: act(o, 0))
                    pl.when(here.z > 0)(lambda o=origin: act(o, 1))
                    act(origin, 2)
                    act(origin, 3)
                    continue
                origin = here.at(origin_z, here.y, here.c)

                def go(o=origin, way=way):
                    pl.when((here.z < 3) if way == 0 else (here.z > 0))(lambda: act(o, way))
                    act(o, 2)
                    act(o, 3)

                pl.when((origin_z >= 0) & (origin_z <= 3))(go)

    def start(self):
        here = self.here
        pl.when(here.z < 3)(lambda: self.copy(here.me, 0, self.own).start())
        pl.when(here.z > 0)(lambda: self.copy(here.me, 1, self.own).start())
        self.copy(here.me, 2, self.own).start()
        self.copy(here.me, 3, self.own).start()

    def hop(self, hops):
        here = self.here
        for way, origin_z in ((0, here.z - hops), (1, here.z + hops)):

            def go(way=way, origin_z=origin_z):
                origin = here.at(origin_z, here.y, here.c)
                self.arrived(origin)
                pl.when((here.z < 3) if way == 0 else (here.z > 0))(lambda: self.copy(origin, way).start())
                self.copy(origin, 2).start()
                self.copy(origin, 3).start()

            pl.when((origin_z >= 0) & (origin_z <= 3))(go)

    def sides(self, hops):
        here = self.here
        for way, origin_z in ((0, here.z - hops), (1, here.z + hops)):
            if hops == 0 and way == 1:
                continue

            def go(origin_z=origin_z):
                origin = here.at(origin_z, 1 - here.y, here.c)
                self.arrived(origin)
                self.copy(origin, 3).start()

            pl.when((origin_z >= 0) & (origin_z <= 3))(go)

    def finish(self):
        here = self.here
        for z in range(4):
            for y in range(2):
                self.arrived(here.at(z, y, 1 - here.c))
        self.each_send(lambda origin, way: self.copy(origin, way).wait_send())
        for z in range(4):
            self.copy(here.at(z, 1 - here.y, here.c), 3).wait_send()


def gathers(here, pack, full, ss, rs):
    cols = pack.shape[1]
    cut = cols // 256 * 128
    return [Gather(here, pack, full, ss, rs, n, c) for n, c in enumerate((slice(0, cut), slice(cut, cols)))]


def own_rows(here, pack, full, sem):
    rows = pack.shape[0]
    return pltpu.make_async_copy(pack, full.at[pl.ds(pl.multiple_of(here.me * rows, rows), rows)], sem)


def gather_scratch():
    sem = pltpu.SemaphoreType.DMA
    return [sem((2, 16, 4)), sem((2, 16))]


def gather_kernel(tokens_in, gain, pack, tokens_out, full, low, ss, rs, xs, xr, ls):
    here = Place()
    half = lax.axis_index("tensor")
    rows = tokens_in.shape[0]
    greet(here, True)
    moves = gathers(here, pack, full, ss, rs)
    for move in moves:
        move.start()
    own = own_rows(here, pack, full, ls.at[0])
    own.start()
    part = rows // 4
    across, local = [], []
    for n in range(4):
        piece = slice(n * part, n * part + part)
        v = tokens_in[piece].astype(f32)
        scale = lax.rsqrt(jnp.mean(v * v, axis=1, keepdims=True) + norm_eps)
        low[piece] = (v * scale * gain[...]).astype(bf16)
        slot = tokens_out.at[pl.ds(pl.multiple_of(half * rows + n * part, part), part)]
        across.append(remote(low.at[piece], slot, xs.at[n], xr.at[n], tensor=1 - half))
        across[-1].start()
        local.append(pltpu.make_async_copy(low.at[piece], slot, ls.at[n + 1]))
        local[-1].start()
    for hops in range(1, 5):
        for move in moves:
            if hops < 4:
                move.hop(hops)
            move.sides(hops - 1)
    own.wait()
    for n in range(4):
        local[n].wait()
        across[n].wait()
    for move in moves:
        move.finish()


def gather_rows(tokens_in, gain, pack, ways, collective_id):
    rows, width = tokens_in.shape
    vmem = pl.BlockSpec(memory_space=pltpu.VMEM)
    hbm = pl.BlockSpec(memory_space=pl.ANY)
    return pl.pallas_call(
        gather_kernel,
        name="gather_rows",
        in_specs=[vmem, vmem, vmem],
        out_specs=[hbm, hbm],
        out_shape=[sds((2 * rows, width), bf16), sds((ways * pack.shape[0], pack.shape[1]), bf16)],
        scratch_shapes=[
            pltpu.VMEM((rows, width), bf16), *gather_scratch(),
            pltpu.SemaphoreType.DMA((4,)), pltpu.SemaphoreType.DMA((4,)), pltpu.SemaphoreType.DMA((5,)),
        ],
        compiler_params=pltpu.CompilerParams(
            collective_id=collective_id, has_side_effects=True, vmem_limit_bytes=60 * 1024 * 1024
        ),
    )(tokens_in, gain, pack)


class Reduce:
    def __init__(self, here, grads, out, bufs, sems):
        self.here, self.grads, self.out = here, grads, out
        self.mine, self.buf_a, self.buf_b, self.buf_up, self.buf_dn = bufs
        self.local, self.send_a, self.recv_a, self.send_b, self.recv_b, self.send_c, self.recv_up, self.recv_dn = sems
        self.parts, self.rows = out.shape[:2]
        z = here.z
        self.order = (3 * (1 - z // 2), (3 * z + 2) % 5, 1 + z % 2, z)

    def block(self, z, y, c):
        at = pl.multiple_of(self.here.at(z, y, c) * self.rows, self.rows)
        return self.grads.at[:, pl.ds(at, self.rows)]

    def copy_a(self, z, y):
        here, at = self.here, z * 2 + y
        return remote(self.block(z, y, 1 - here.c), self.buf_a.at[at], self.send_a.at[at], self.recv_a.at[at], dp=here.core())

    def take(self, z, y):
        at = z * 2 + y
        return pltpu.make_async_copy(self.block(z, y, self.here.c), self.mine.at[at], self.local.at[at])

    def copy_b(self, z):
        here = self.here
        return remote(self.mine.at[z * 2 + 1 - here.y], self.buf_b.at[z], self.send_b.at[z], self.recv_b.at[z], dp=here.side())

    def copy_up(self, z):
        return remote(self.mine.at[z * 2 + self.here.y], self.buf_up.at[z], self.send_c.at[z], self.recv_up.at[z], dp=self.here.up())

    def copy_dn(self, z):
        return remote(self.mine.at[z * 2 + self.here.y], self.buf_dn.at[z], self.send_c.at[z], self.recv_dn.at[z], dp=self.here.down())

    def add(self, at, buf, slot):
        def rows(n, carry):
            piece = pl.ds(pl.multiple_of(n * 16, 16), 16)
            for part in range(self.parts):
                total = self.mine[at, part, piece].astype(f32) + buf[slot, part, piece].astype(f32)
                self.mine[at, part, piece] = total.astype(bf16)
            return carry

        lax.fori_loop(0, self.rows // 16, rows, 0)

    def start(self):
        here = self.here
        for side in (1 - here.y, here.y):
            for z in self.order:
                self.copy_a(z, side).start()
                self.take(z, side).start()

    def cores(self, n):
        here = self.here
        z = self.order[n]
        at = z * 2 + 1 - here.y
        self.take(z, 1 - here.y).wait()
        self.copy_a(z, 1 - here.y).wait_recv()
        self.add(at, self.buf_a, at)
        self.copy_b(z).start()

    def stay(self, n):
        here = self.here
        z = self.order[n]
        at = z * 2 + here.y
        self.take(z, here.y).wait()
        self.copy_a(z, here.y).wait_recv()
        self.add(at, self.buf_a, at)

    def sides(self, n):
        z = self.order[n]
        self.copy_b(z).wait_recv()
        self.add(z * 2 + self.here.y, self.buf_b, z)

    def pass_on(self, n):
        here = self.here
        z = self.order[n]
        at = z * 2 + here.y

        def up():
            def below():
                self.copy_up(z).wait_recv()
                self.add(at, self.buf_up, z)

            pl.when(here.z > 0)(below)
            self.copy_up(z).start()

        def down():
            def above():
                self.copy_dn(z).wait_recv()
                self.add(at, self.buf_dn, z)

            pl.when(here.z < 3)(above)
            self.copy_dn(z).start()

        pl.when(z > here.z)(up)
        pl.when(z < here.z)(down)

    def finish(self):
        here = self.here
        z = here.z
        at = z * 2 + here.y
        pl.when(z > 0)(lambda: self.copy_up(z).wait_recv())
        pl.when(z < 3)(lambda: self.copy_dn(z).wait_recv())

        def rows(n, carry):
            piece = pl.ds(pl.multiple_of(n * 16, 16), 16)
            for part in range(self.parts):
                below = jnp.where(z > 0, self.buf_up[z, part, piece].astype(f32), 0.0)
                above = jnp.where(z < 3, self.buf_dn[z, part, piece].astype(f32), 0.0)
                self.out[part, piece] = self.mine[at, part, piece].astype(f32) + below + above
            return carry

        lax.fori_loop(0, self.rows // 16, rows, 0)
        for n in range(4):
            zn = self.order[n]
            self.copy_a(zn, 0).wait_send()
            self.copy_a(zn, 1).wait_send()
            self.copy_b(zn).wait_send()
            pl.when(zn > z)(lambda zn=zn: self.copy_up(zn).wait_send())
            pl.when(zn < z)(lambda zn=zn: self.copy_dn(zn).wait_send())


def reduce_scratch(*block):
    sem = pltpu.SemaphoreType.DMA
    return [
        pltpu.VMEM((8,) + block, bf16), pltpu.VMEM((8,) + block, bf16), pltpu.VMEM((4,) + block, bf16),
        pltpu.VMEM((4,) + block, bf16), pltpu.VMEM((4,) + block, bf16),
        sem((8,)), sem((8,)), sem((8,)), sem((4,)), sem((4,)), sem((4,)), sem((4,)), sem((4,)),
    ]


def tail_kernel(grads, small, mixed, out, small_out, far_out, *scratch):
    here = Place()
    half = lax.axis_index("tensor")
    far = pltpu.get_barrier_semaphore()
    partners = [here.me + bit - 2 * bit * ((here.me // bit) % 2) for bit in (1, 2, 4, 8)]
    for partner in partners:
        pl.semaphore_signal(far, 1, device_id={"dp": partner}, device_id_type=MESH)
    pl.semaphore_signal(far, 1, device_id={"tensor": 1 - half}, device_id_type=MESH)
    middle = (here.z == 1) | (here.z == 2)
    pl.when(here.z == 1)(lambda: pl.semaphore_signal(far, 1, device_id={"dp": here.up()}, device_id_type=MESH))
    pl.when(here.z == 2)(lambda: pl.semaphore_signal(far, 1, device_id={"dp": here.down()}, device_id_type=MESH))
    pl.semaphore_wait(far, 5 + middle.astype(jnp.int32))
    work = Reduce(here, grads, out, scratch[:5], scratch[5:13])
    total, landed, send, recv, send_x, recv_x = scratch[13:]
    rows = far_out.shape[0]
    other = mixed.at[pl.ds(pl.multiple_of((1 - half) * rows, rows), rows)]
    across = remote(other, far_out, send_x, recv_x, tensor=1 - half)
    across.start()
    total[0] = small[...]
    for k in range(4):
        if k == 0:
            work.start()
        swap = remote(total.at[k], landed.at[k], send.at[k], recv.at[k], dp=partners[k])
        swap.start()
        if k == 0:
            for n in range(4):
                work.cores(n)
            for n in range(4):
                work.stay(n)
        else:
            work.sides(k - 1)
            work.pass_on(k - 1)
        swap.wait()
        total[k + 1] = total[k] + landed[k]
    small_out[...] = total[4]
    work.sides(3)
    work.finish()
    across.wait()


def reduce_tail(grads, ways, small, mixed, collective_id):
    parts, rows, cols = grads.shape[0], grads.shape[1] // ways, grads.shape[2]
    tokens, width = mixed.shape
    vmem = pl.BlockSpec(memory_space=pltpu.VMEM)
    hbm = pl.BlockSpec(memory_space=pl.ANY)
    sem = pltpu.SemaphoreType.DMA
    return pl.pallas_call(
        tail_kernel, name="tail", in_specs=[hbm, vmem, hbm], out_specs=[vmem, vmem, hbm],
        out_shape=[sds((parts, rows, cols)), sds(small.shape), sds((tokens // 2, width), bf16)],
        scratch_shapes=reduce_scratch(parts, rows, cols) + [
            pltpu.VMEM((5,) + small.shape, f32), pltpu.VMEM((4,) + small.shape, f32), sem((4,)), sem((4,)), sem, sem,
        ],
        compiler_params=pltpu.CompilerParams(
            collective_id=collective_id, has_side_effects=True, vmem_limit_bytes=60 * 1024 * 1024
        ),
    )(grads, small, mixed)


def swap(v):
    return lax.ppermute(v, "tensor", [(0, 1), (1, 0)])


def halves(v, axis):
    size = v.shape[axis] // 2
    me = lax.axis_index("tensor")
    return (
        lax.dynamic_slice_in_dim(v, me * size, size, axis),
        lax.dynamic_slice_in_dim(v, (1 - me) * size, size, axis),
    )


def once(shape, at=None):
    where = at or (0,) * len(shape)
    return pl.BlockSpec(shape, lambda i: where, pipeline_mode=pl.Buffered(1))


def by_cols(rows, offset=0):
    return pl.BlockSpec((rows, BW), lambda i: (0, i + offset))


def params(collective_id=None):
    return pltpu.CompilerParams(
        dimension_semantics=("arbitrary",), vmem_limit_bytes=60 * 1024 * 1024,
        collective_id=collective_id, has_side_effects=collective_id is not None,
    )


def spread(v):
    lead = v.shape[:-1]
    v = v.reshape(lead + (v.shape[-1] // HB, HB))
    v = jnp.pad(v, [(0, 0)] * len(lead) + [(0, 0), (0, 8 - HB)]).reshape(lead + (-1,))
    return jnp.pad(v, [(0, 0)] * len(lead) + [(0, 128 - v.shape[-1])])


def gathered_heads(v, heads):
    return v[..., : heads * 2].reshape(v.shape[:-1] + (heads // HB, 8))[..., :HB].reshape(v.shape[:-1] + (heads,))


def sds(shape, dtype=f32):
    return jax.ShapeDtypeStruct(shape, dtype)


def on_device(
    residual, norm_gain, w_gate_inner, w_state_io, w_step, conv_inner, conv_state,
    step_bias, decay_log, skip_gain, gate_gain, w_output, cotangent,
):
    width = residual.shape[1]
    units = w_gate_inner.shape[2]
    heads = w_step.shape[1]
    blocks = units // BW
    unit_total = units * lax.axis_size("tensor")
    ways = lax.axis_size("dp")
    own_links = ways == 16
    rows_in = residual.astype(f32)
    rstd_in = lax.rsqrt(jnp.mean(rows_in * rows_in, axis=1, keepdims=True) + norm_eps)
    scaled = rows_in * rstd_in
    pack_a = jnp.concatenate([w_gate_inner[1], w_state_io, spread(w_step)], axis=1)
    pack_b = jnp.concatenate([w_gate_inner[0], w_output.T], axis=1)
    if own_links:
        normed, wa = gather_rows(residual, norm_gain[None], pack_a, ways, 1)
    else:
        wa = lax.all_gather(pack_a, "dp", axis=0, tiled=True)
        normed = lax.all_gather((scaled * norm_gain).astype(bf16), "tensor", axis=0, tiled=True)
    tokens = normed.shape[0]
    spans = tokens // Q
    rate = -jnp.exp(decay_log)
    kin = jnp.concatenate([conv_inner, jnp.repeat(skip_gain, HEAD)[None], jnp.zeros((2, units), f32)], axis=0)
    kst = jnp.concatenate([conv_state, jnp.zeros((3, BW), f32)], axis=0)
    hp = jnp.concatenate([spread(step_bias)[None], spread(rate)[None], jnp.zeros((6, 128), f32)], axis=0)
    rate_t = jnp.broadcast_to(spread(rate)[:48, None], (48, 128))
    gain8 = jnp.broadcast_to(gate_gain[None], (8, units))

    hbm = pl.BlockSpec(memory_space=pl.ANY)
    sem = pltpu.SemaphoreType.DMA
    inner, ssd, states, cst, bc, step, cum, step_t, cum_t, pre_t, *sent = pl.pallas_call(
        functools.partial(mixer_forward, own_links),
        name="mixer_forward",
        grid=(blocks,),
        in_specs=[
            once((tokens, width)), by_cols(width), once((width, 384), (0, units // 384)),
            by_cols(8), once((8, BW)), once((8, 128)),
        ] + [once(cotangent.shape), once(pack_b.shape)] * own_links,
        out_specs=[
            by_cols(tokens), by_cols(tokens), pl.BlockSpec((spans, BW, 128), lambda i: (0, i, 0)),
            once((tokens, BW)), once((tokens, BW)), once((tokens, 128)), once((tokens, 128)),
            once((48, tokens)), once((48, tokens)), once((48, tokens)),
        ] + [hbm, hbm] * own_links,
        out_shape=[
            sds((tokens, units)), sds((tokens, units)), sds((spans, units, 128)),
            sds((tokens, BW)), sds((tokens, BW), bf16), sds((tokens, 128)), sds((tokens, 128)),
            sds((48, tokens)), sds((48, tokens)), sds((48, tokens)),
        ] + [sds((tokens, width), bf16), sds((width, 2 * units), bf16)] * own_links,
        scratch_shapes=[
            pltpu.VMEM((tokens + 8, BW), f32), pltpu.VMEM((spans, Q, Q), f32),
            pltpu.VMEM((tokens, 128), f32), pltpu.VMEM((tokens, 128), f32), pltpu.VMEM((8, tokens), f32),
            pltpu.VMEM((Q, HB * Q), bf16), pltpu.VMEM((HB * Q, BW), bf16), pltpu.VMEM((BW, 128), f32),
        ] + (gather_scratch() + [sem, sem, sem((2,))]) * own_links,
        compiler_params=params(2 if own_links else None),
        cost_estimate=pl.CostEstimate(flops=2 * tokens * width * (units + 384) + 4 * tokens * 256 * units, bytes_accessed=30_000_000, transcendentals=heads * spans * Q * Q),
    )(normed, wa, wa, kin, kst, hp, *[cotangent, pack_b] * own_links)

    if own_links:
        cot, wb = sent
    else:
        wb = lax.all_gather(pack_b, "dp", axis=0, tiled=True)
        cot = lax.all_gather(cotangent, "tensor", axis=0, tiled=True)

    gate, ggo, stats = pl.pallas_call(
        functools.partial(gate_forward, own_links),
        name="gate_forward",
        grid=(blocks,),
        in_specs=[
            once((tokens, width)), once((tokens, width)), by_cols(width), by_cols(width, blocks),
            by_cols(tokens), by_cols(8),
        ],
        out_specs=[by_cols(tokens), by_cols(tokens), once((8, tokens))],
        out_shape=[sds((tokens, units)), sds((tokens, units)), sds((8, tokens))],
        scratch_shapes=[pltpu.VMEM((tokens, 128), f32), pltpu.VMEM((tokens, 128), f32)]
        + [pltpu.VMEM((8, tokens), f32), pltpu.VMEM((8, tokens), f32), sem, sem] * own_links,
        compiler_params=params(3 if own_links else None),
        cost_estimate=pl.CostEstimate(flops=4 * tokens * width * units, bytes_accessed=35_000_000, transcendentals=tokens * units),
    )(normed, cot, wb, wb, ssd, gain8)
    if not own_links:
        stats = stats + swap(stats)

    dy, dgate, ng, ggg, grad_b = pl.pallas_call(
        functools.partial(gate_backward, float(unit_total)),
        name="gate_backward",
        grid=(blocks,),
        in_specs=[
            once((8, tokens)), by_cols(tokens), by_cols(tokens), by_cols(tokens), by_cols(8),
            once((tokens, width)), once((tokens, width)),
        ],
        out_specs=[
            by_cols(tokens), by_cols(tokens), by_cols(tokens), by_cols(8),
            pl.BlockSpec((2, width, BW), lambda i: (0, 0, i)),
        ],
        out_shape=[
            sds((tokens, units), bf16), sds((tokens, units), bf16), sds((tokens, units), bf16), sds((8, units)),
            sds((2, width, units), bf16),
        ],
        scratch_shapes=[pltpu.VMEM((tokens, 128), f32), pltpu.VMEM((width, tokens), bf16), pltpu.VMEM((width, tokens), bf16)],
        compiler_params=params(),
        cost_estimate=pl.CostEstimate(flops=4 * tokens * units * width, bytes_accessed=45_000_000, transcendentals=tokens * units),
    )(stats, gate, ssd, ggo, gain8, normed, cot)

    mixed = mm(ng, wb[:, units:], 1, 1).astype(bf16)
    mixed_near, mixed_far = halves(mixed, 0)

    dinner, gk, dsd, gks, hs, *sent = pl.pallas_call(
        functools.partial(mixer_backward, own_links),
        name="mixer_backward",
        grid=(blocks,),
        in_specs=[
            by_cols(tokens), by_cols(tokens), pl.BlockSpec((spans, BW, 128), lambda i: (0, i, 0)),
            by_cols(8), once((8, BW)), once((8, 128)),
            once((tokens, BW)), once((tokens, BW)), once((tokens, 128)), once((tokens, 128)),
            once((48, tokens)), once((48, tokens)), once((48, tokens)), once((48, 128)),
        ] + [hbm, hbm] * own_links,
        out_specs=[by_cols(tokens), by_cols(8), once((tokens, 384)), once((8, BW)), once((48, 128))]
        + [hbm, once((2, width // ways, units))] * own_links,
        out_shape=[sds((tokens, units), bf16), sds((8, units)), sds((tokens, 384), bf16), sds((8, BW)), sds((48, 128))]
        + [sds((tokens // 2, width), bf16), sds((2, width // ways, units))] * own_links,
        scratch_shapes=[
            pltpu.VMEM((tokens + 8, BW), f32), pltpu.VMEM((tokens + 8, BW), f32),
            pltpu.VMEM((spans, Q, Q), f32), pltpu.VMEM((spans, Q, Q), f32),
            pltpu.VMEM((tokens, 128), f32), pltpu.VMEM((tokens, 128), f32),
            pltpu.VMEM((tokens, 128), f32), pltpu.VMEM((tokens, 128), f32), pltpu.VMEM((8, tokens), f32),
            pltpu.VMEM((HB * Q, Q), bf16), pltpu.VMEM((HB * Q, BW), bf16), pltpu.VMEM((HB * Q, Q), f32),
            pltpu.VMEM((BW, 128), f32),
            pltpu.VMEM((48, tokens), f32), pltpu.VMEM((48, tokens), f32), pltpu.VMEM((48, tokens), f32),
            pltpu.VMEM((48, tokens), f32), pltpu.VMEM((48, 128), f32), pltpu.VMEM((8, BW), f32),
        ] + ([sem, sem] + reduce_scratch(2, width // ways, units)) * own_links,
        compiler_params=params(4 if own_links else None),
        cost_estimate=pl.CostEstimate(flops=40_000_000_000, bytes_accessed=30_000_000, transcendentals=heads * spans * Q * Q),
    )(inner, dy, states, kin, kst, hp, cst, bc, step, cum, step_t, cum_t, pre_t, rate_t, *[mixed, grad_b] * own_links)
    if own_links:
        mixed_got, wb_shard = sent
    else:
        mixed_got = swap(mixed_far)
        wb_shard = lax.psum_scatter(grad_b, "dp", scatter_dimension=1, tiled=True).astype(f32)
    output = (rows_in + mixed_near.astype(f32) + mixed_got.astype(f32)).astype(bf16)

    grad_wi = mm(normed, dinner, 0, 0).astype(bf16)
    grad_ws = mm(normed, dsd, 0, 0).astype(bf16)
    grad_a = jnp.concatenate([grad_wi, grad_ws], axis=1)
    tail = jnp.concatenate([gks[:5].reshape(-1), hs[:, 0], hs[:, 1], jnp.zeros((units - 5 * BW - 96,), f32)])
    small = jnp.concatenate([gk[:6], ggg[:1], tail[None]], axis=0)
    pulled = (mm(dgate, wb[:, :units], 1, 1) + mm(dinner, wa[:, :units], 1, 1) + mm(dsd, wa[:, units:], 1, 1)).astype(bf16)
    near, far = halves(pulled, 0)
    if own_links:
        wa_shard, small, got = reduce_tail(grad_a[None], ways, small, pulled, 5)
        wa_shard = wa_shard[0]
    else:
        wa_shard = lax.psum_scatter(grad_a, "dp", scatter_dimension=0, tiled=True).astype(f32)
        small = lax.psum(small, "dp")
        got = swap(far)
    grad_normed = near.astype(f32) + got.astype(f32)
    grad_v = grad_normed * norm_gain
    grad_residual = cotangent.astype(f32) + rstd_in * (
        grad_v - scaled * jnp.mean(grad_v * scaled, axis=1, keepdims=True)
    )

    conv_state_sum = small[7, : 5 * BW].reshape(5, BW)
    bias_sum = gathered_heads(small[7, 5 * BW : 5 * BW + 48], heads)
    decay_sum = gathered_heads(small[7, 5 * BW + 48 : 5 * BW + 96], heads)
    skip_sum = jnp.sum(small[5].reshape(heads, HEAD), axis=1)

    gain_rows = jnp.sum(wb_shard[0] * w_gate_inner[0].astype(f32), axis=1) + jnp.sum(
        wa_shard * pack_a.astype(f32), axis=1
    )
    count = gain_rows.shape[0]
    gain_own = gain_rows / lax.dynamic_slice_in_dim(norm_gain, lax.axis_index("dp") * count, count)
    near_s, far_s = halves(jnp.concatenate([wa_shard[:, units : units + BW], conv_state_sum], axis=0), 1)
    near_g, far_g = halves(gain_own, 0)
    far_all = jnp.concatenate([far_s.reshape(-1), far_g])
    got = swap(far_all)
    both = near_s + got[: far_s.size].reshape(far_s.shape)
    gain_part = near_g + got[far_s.size :]
    return (
        output,
        grad_residual,
        gain_part,
        jnp.stack([wb_shard[0], wa_shard[:, :units]]),
        both[:count],
        gathered_heads(wa_shard[:, units + BW :], heads),
        small[0:5],
        both[count:],
        bias_sum,
        decay_sum,
        skip_sum,
        small[6],
        wb_shard[1].T,
    )


def solution(mesh):
    return jax.shard_map(
        on_device,
        mesh=mesh,
        in_specs=(
            P(("dp", "tensor"), None),
            P(),
            P(None, "dp", "tensor"),
            P("dp", None),
            P("dp", "tensor"),
            P(None, "tensor"),
            P(),
            P("tensor"),
            P("tensor"),
            P("tensor"),
            P("tensor"),
            P("tensor", "dp"),
            P(("dp", "tensor"), None),
        ),
        out_specs=(
            P(("dp", "tensor"), None),
            P(("dp", "tensor"), None),
            P(("dp", "tensor")),
            P(None, "dp", "tensor"),
            P("dp", "tensor"),
            P("dp", "tensor"),
            P(None, "tensor"),
            P(None, "tensor"),
            P("tensor"),
            P("tensor"),
            P("tensor"),
            P("tensor"),
            P("tensor", "dp"),
        ),
        check_vma=False,
    )
```

```python
import functools

import jax
import jax.numpy as jnp
from jax import lax
from jax.experimental import pallas as pl
from jax.experimental.pallas import tpu as pltpu
from jax.sharding import PartitionSpec as P

Q = 256
LEN = 1024
HEAD = 64
BW = 256
HB = BW // HEAD
LOG2E = 1.4426950408889634
FAR = -1e30
norm_eps = 1e-05
MESH = pl.DeviceIdType.MESH
f32 = jnp.float32
bf16 = jnp.bfloat16


def mm(a, b, ca=1, cb=0):
    return lax.dot_general(a, b, (((ca,), (cb,)), ((), ())), preferred_element_type=f32)


def sigmoid(v):
    return 1.0 / (1.0 + jnp.exp(-v))


def split3(a):
    hi = a.astype(bf16)
    rest = a - hi.astype(f32)
    mid = rest.astype(bf16)
    low = (rest - mid.astype(f32)).astype(bf16)
    return hi, mid, low


def split2(a):
    hi = a.astype(bf16)
    return hi, (a - hi.astype(f32)).astype(bf16)


def iota(shape, axis):
    return lax.broadcasted_iota(jnp.int32, shape, axis)


def expand(cols):
    rows = cols.shape[0]
    left = iota((rows, 128), 1) < HEAD
    return jnp.concatenate(
        [jnp.where(left, cols[:, 2 * q : 2 * q + 1], cols[:, 2 * q + 1 : 2 * q + 2]) for q in range(2)],
        axis=1,
    )


def conv_taps(window, kernel):
    out = kernel[4:5] + kernel[3:4] * window[8:]
    for k in range(3):
        out = out + kernel[k : k + 1] * pltpu.roll(window, 3 - k, 0)[8:]
    return out


def head_masks():
    lane = iota((1, BW), 1) // HEAD
    return [(lane == j).astype(f32).astype(bf16) for j in range(HB)]


def quads():
    for r in range(0, Q, 64):
        for half in range(2):
            if half * 128 <= r:
                yield r, half, r < half * 128 + 128


def decay_chunk(col, row, r, half, diag):
    gap = col[r : r + 64] - row[:, half * 128 : half * 128 + 128]
    if diag:
        keep = iota((64, 128), 0) + (r - half * 128) >= iota((64, 128), 1)
        gap = jnp.where(keep, gap, FAR)
    return jnp.exp2(gap)


def mixer_forward(links, normed, wi, wsx, kin, kst, hp, *refs):
    refs = list(refs)
    if links:
        cot, pack = refs[:2]
        cot_out, wb = refs[12:14]
        refs = refs[2:12] + refs[14:]
    inner_out, ssd_out, states_out, cst_out, bc_out, step_out, cum_out, stepT_out, cumT_out, preT_out = refs[:10]
    buf, gram, colc, cols, rowp, mst, xst, state = refs[10:18]
    i = pl.program_id(0)
    tokens = normed.shape[0]
    spans = tokens // Q
    work = BesideForward(cot, pack, cot_out, wb, *refs[18:]) if links else None

    if links:
        pl.when(i == 0)(work.start)

    @pl.when(i == 0)
    def _():
        proj = mm(normed[...], wsx[...])
        buf[0:8] = jnp.zeros((8, BW), f32)
        cst_out[...] = proj[:, :BW]
        buf[8 : 8 + tokens] = proj[:, :BW]
        tri = (iota((Q, Q), 0) >= iota((Q, Q), 1)).astype(f32).astype(bf16)
        pre = proj[:, BW:] + hp[0:1]
        step = jnp.maximum(pre, 0.0) + jnp.log1p(jnp.exp(-jnp.abs(pre)))
        step_out[...] = step
        scaled = step * (hp[1:2] * LOG2E)
        for s in range(spans):
            parts = split3(scaled[s * Q : s * Q + Q])
            cum_out[s * Q : s * Q + Q] = mm(tri, parts[0]) + mm(tri, parts[1]) + mm(tri, parts[2])
            conv = conv_taps(buf[s * Q : s * Q + Q + 8], kst[...])
            bc = (conv * sigmoid(conv)).astype(bf16)
            bc_out[s * Q : s * Q + Q] = bc
            gram[s] = mm(bc[:, 128:], bc[:, :128], 1, 1)
        preT_out[...] = jnp.transpose(pre)[:48]
        stepT_out[...] = jnp.transpose(step)[:48]
        cumT_out[...] = jnp.transpose(cum_out[...])[:48]
        mst[...] = jnp.zeros(mst.shape, bf16)

    inner = mm(normed[...], wi[...])
    inner_out[...] = inner
    buf[8 : 8 + tokens] = inner
    turn = lax.rem(128 - 8 * i, 128)
    colc[...] = pltpu.roll(cum_out[...], turn, 1)
    cols[...] = pltpu.roll(step_out[...], turn, 1)
    rows8 = pl.ds(pl.multiple_of(8 * i, 8), 8)
    rowp[...] = cumT_out[rows8] - jnp.log2(stepT_out[rows8])
    state[...] = jnp.zeros(state.shape, f32)
    masks = head_masks()

    def span(s, carry):
        at = pl.multiple_of(s * Q, Q)
        rows = pl.ds(at, Q)
        conv = conv_taps(buf[pl.ds(at, Q + 8)], kin[...])
        xs = conv * sigmoid(conv)
        x_low = xs.astype(bf16)
        col = colc[rows]
        total = col[Q - 1 : Q]
        growth = expand(jnp.exp2(col[:, :8]))
        weight = expand(jnp.exp2(total[:, :8] - col[:, :8]) * cols[rows][:, :8])
        xw_low = (xs * weight).astype(bf16)
        for j in range(HB):
            xst[j * Q : j * Q + Q] = x_low * masks[j]
            row = rowp[j : j + 1, rows]
            for r, half, diag in quads():
                part = gram[s, r : r + 64, half * 128 : half * 128 + 128]
                dec = decay_chunk(col[:, j : j + 1], row, r, half, diag)
                mst[r : r + 64, j * Q + half * 128 : j * Q + half * 128 + 128] = (part * dec).astype(bf16)
        intra = mm(mst[...], xst[...])
        state_in = state[...]
        states_out[s] = state_in
        bc = bc_out[rows]
        readout = mm(bc[:, 128:], state_in.astype(bf16), 1, 1)
        ssd_out[rows] = intra + growth * readout + kin[5:6] * xs
        local = mm(xw_low, bc[:, :128], 0, 0)
        fade = jnp.exp2(total)
        for j in range(HB):
            at_j = slice(j * HEAD, j * HEAD + HEAD)
            state[at_j] = fade[:, j : j + 1] * state_in[at_j] + local[at_j]
        if links:
            work.step(i * spans + s)
        return carry

    lax.fori_loop(0, spans, span, 0)
    if links:
        pl.when(i == pl.num_programs(0) - 1)(work.finish)


class BesideForward:
    def __init__(self, cot, pack, cot_out, wb, ss, rs, xs, xr, ls):
        self.here = Place()
        self.moves = gathers(self.here, pack, wb, ss, rs)
        self.own = own_rows(self.here, pack, wb, ls.at[0])
        half = lax.axis_index("tensor")
        rows = cot.shape[0]
        slot = cot_out.at[pl.ds(pl.multiple_of(half * rows, rows), rows)]
        self.across = remote(cot, slot, xs, xr, tensor=1 - half)
        self.local = pltpu.make_async_copy(cot, slot, ls.at[1])

    def start(self):
        greet(self.here, True)
        for move in self.moves:
            move.start()
        self.across.start()
        self.own.start()
        self.local.start()

    def step(self, at):
        for when, chunk, hops in ((7, 0, 1), (11, 1, 1), (15, 0, 2), (19, 1, 2)):

            def go(move=self.moves[chunk], hops=hops):
                move.hop(hops)
                move.sides(hops - 1)

            pl.when(at == when)(go)

    def finish(self):
        for hops in (3, 4):
            for move in self.moves:
                if hops < 4:
                    move.hop(hops)
                move.sides(hops - 1)
        self.own.wait()
        self.local.wait()
        self.across.wait()
        for move in self.moves:
            move.finish()


def gate_forward(links, normed, cot, wg, wo, ssd, gain, gate_out, ggo_out, stats_out, sq, gi, *refs):
    i = pl.program_id(0)

    @pl.when(i == 0)
    def _():
        if links:
            barrier = pltpu.get_barrier_semaphore()
            other = {"tensor": 1 - lax.axis_index("tensor")}
            pl.semaphore_signal(barrier, 1, device_id=other, device_id_type=MESH)
            pl.semaphore_wait(barrier, 1)
        sq[...] = jnp.zeros(sq.shape, f32)
        gi[...] = jnp.zeros(gi.shape, f32)

    gate = mm(normed[...], wg[...])
    gate_out[...] = gate
    ggo = mm(cot[...], wo[...])
    ggo_out[...] = ggo
    gated = ssd[...] * (gate * sigmoid(gate))
    squares = gated * gated
    sq[...] += squares[:, :128] + squares[:, 128:]
    inner = ggo * gain[0:1] * gated
    gi[...] += inner[:, :128] + inner[:, 128:]

    @pl.when(i == pl.num_programs(0) - 1)
    def _():
        lane = iota(sq.shape, 1)
        both = jnp.where(
            lane == 0,
            jnp.sum(sq[...], axis=1, keepdims=True),
            jnp.where(lane == 1, jnp.sum(gi[...], axis=1, keepdims=True), 0.0),
        )
        if not links:
            stats_out[...] = jnp.transpose(both)[:8]
            return
        mine, landed, send, recv = refs
        mine[...] = jnp.transpose(both)[:8]
        swap = remote(mine, landed, send, recv, tensor=1 - lax.axis_index("tensor"))
        swap.start()
        swap.wait()
        stats_out[...] = mine[...] + landed[...]


def gate_backward(
    unit_total, stats, gate, ssd, ggo, gain, normed, cot, dy_out, dgate_out, ng_out, gg_out, grads_out, normed_t, cols, cot_t
):
    @pl.when(pl.program_id(0) == 0)
    def _():
        full = jnp.concatenate([stats[...], jnp.zeros((120, stats.shape[1]), f32)], axis=0)
        cols[...] = jnp.transpose(full)

        def turn(n, carry):
            here = pl.ds(pl.multiple_of(n * 128, 128), 128)
            normed_t[here] = jnp.transpose(normed[:, here])
            cot_t[here] = jnp.transpose(cot[:, here])
            return carry

        lax.fori_loop(0, normed.shape[1] // 128, turn, 0)

    rstd = lax.rsqrt(cols[:, 0:1] / unit_total + norm_eps)
    pull = rstd * rstd * rstd * (cols[:, 1:2] / unit_total)
    v = gate[...]
    sig = sigmoid(v)
    act = v * sig
    y = ssd[...]
    gated = y * act
    scaled = gated * rstd
    ng = (scaled * gain[0:1]).astype(bf16)
    ng_out[...] = ng
    grads_out[1] = mm(cot_t[...], ng).astype(bf16)
    gg = ggo[...]
    gg_out[...] = jnp.broadcast_to(jnp.sum(gg * scaled, axis=0, keepdims=True), gg_out.shape)
    grad = rstd * (gg * gain[0:1]) - gated * pull
    dy_out[...] = (grad * act).astype(bf16)
    dgate = (grad * y * (sig * (1.0 + v * (1.0 - sig)))).astype(bf16)
    dgate_out[...] = dgate
    grads_out[0] = mm(normed_t[...], dgate).astype(bf16)


class BesideBackward:
    def __init__(self, mixed, grads, far_out, shard_out, scratch):
        self.here = Place()
        half = lax.axis_index("tensor")
        rows = far_out.shape[0]
        other = mixed.at[pl.ds(pl.multiple_of((1 - half) * rows, rows), rows)]
        self.across = remote(other, far_out, scratch[0], scratch[1], tensor=1 - half)
        self.sum = Reduce(self.here, grads, shard_out, scratch[2:7], scratch[7:15])

    def start(self):
        greet(self.here, True)
        self.sum.start()
        self.across.start()

    def step(self, at):
        total = self.sum
        z = self.here.z
        ends = (z == 0) | (z == 3)
        for n, block in enumerate(total.order):
            pl.when(at == n)(lambda z=block: total.cores(z))
            pl.when(at == (4, 6, 7, 8)[n])(lambda z=block: total.stay(z))
            pl.when(at == (5, 10, 15, 19)[n])(lambda z=block: total.sides(z))
        for n, block in enumerate(total.order[:3]):
            when = jnp.where(ends, (5, 10, 15)[n], (11, 16, 17)[n])
            pl.when(at == when)(lambda z=block: total.pass_on(z))

    def finish(self):
        self.sum.finish()
        self.across.wait()


def mixer_backward(links, inner, dy, states, kin, kst, hp, cst, bc_in, step_in, cum_in, stepT, cumT, preT, rateT, *refs):
    refs = list(refs)
    if links:
        beside = refs[:2] + refs[7:9]
        refs = refs[2:7] + refs[9:]
        work = BesideBackward(*beside, refs[24:])
    dinner_out, gk_out, dsd_out, gks_out, hs_out = refs[:5]
    buf, dbuf, gram, gg, gb, gc, colc, cols, rowp, mst, dyst, gmix, sgrad = refs[5:18]
    rs_t, cs_t, dr_t, wg_t, gt_t, gtaps = refs[18:24]
    i = pl.program_id(0)
    if links:
        pl.when(i == 0)(work.start)
    tokens = inner.shape[0]
    spans = tokens // Q
    masks = head_masks()

    @pl.when(i == 0)
    def _():
        buf[0:8] = jnp.zeros((8, BW), f32)
        dbuf[tokens : tokens + 8] = jnp.zeros((8, BW), f32)
        for s in range(spans):
            bc = bc_in[s * Q : s * Q + Q]
            gram[s] = mm(bc[:, 128:], bc[:, :128], 1, 1)
        for ref in (gg, gb, gc, rs_t, cs_t, dr_t, wg_t, gt_t):
            ref[...] = jnp.zeros(ref.shape, f32)
        mst[...] = jnp.zeros(mst.shape, bf16)

    buf[8 : 8 + tokens] = inner[...]
    turn = lax.rem(128 - 8 * i, 128)
    colc[...] = pltpu.roll(cum_in[...], turn, 1)
    cols[...] = pltpu.roll(step_in[...], turn, 1)
    rows8 = pl.ds(pl.multiple_of(8 * i, 8), 8)
    rowp[...] = cumT[rows8] - jnp.log2(stepT[rows8])
    sgrad[...] = jnp.zeros(sgrad.shape, f32)
    gtaps[...] = jnp.zeros(gtaps.shape, f32)
    pick = (iota((8, BW), 1) // HEAD == iota((8, BW), 0)).astype(f32).astype(bf16)

    def conv_rows(at, kernel, grad_act):
        window = buf[pl.ds(at, Q + 8)]
        conv = conv_taps(window, kernel)
        sig = sigmoid(conv)
        gco = grad_act * (sig * (1.0 + conv * (1.0 - sig)))
        dbuf[pl.ds(at, Q)] = gco
        for k in range(4):
            prod = gco * (window[8:] if k == 3 else pltpu.roll(window, 3 - k, 0)[8:])
            gtaps[k : k + 1] += jnp.sum(prod, axis=0, keepdims=True)
        gtaps[4:5] += jnp.sum(gco, axis=0, keepdims=True)
        after = dbuf[pl.ds(at, Q + 8)]
        grad_in = kernel[3:4] * gco
        for k in range(3):
            grad_in = grad_in + kernel[k : k + 1] * pltpu.roll(after, Q + 8 - (3 - k), 0)[:Q]
        return grad_in

    def span(back, carry):
        s = spans - 1 - back
        at = pl.multiple_of(s * Q, Q)
        rows = pl.ds(at, Q)
        conv = conv_taps(buf[pl.ds(at, Q + 8)], kin[...])
        xs = conv * sigmoid(conv)
        x_low = xs.astype(bf16)
        dy_s = dy[rows]
        dy_f = dy_s.astype(f32)
        bc = bc_in[rows]
        b_low, c_low = bc[:, :128], bc[:, 128:]
        col = colc[rows]
        total = col[Q - 1 : Q]
        for j in range(HB):
            dyst[j * Q : j * Q + Q] = dy_s * masks[j]
        gmix[...] = mm(dyst[...], x_low, 1, 1)
        lane = iota((Q, 128), 1)
        row_sums = jnp.zeros((Q, 128), f32)
        for j in range(HB):
            row = rowp[j : j + 1, rows]
            col_sum = [jnp.zeros((1, 128), f32), jnp.zeros((1, 128), f32)]
            row_parts = []
            for r, half, diag in quads():
                here = slice(half * 128, half * 128 + 128)
                dec = decay_chunk(col[:, j : j + 1], row, r, half, diag)
                part = gram[s, r : r + 64, here]
                p = gmix[j * Q + r : j * Q + r + 64, here] * dec
                gg[s, r : r + 64, here] += p
                q = p * part
                mst[j * Q + r : j * Q + r + 64, here] = (part * dec).astype(bf16)
                col_sum[half] = col_sum[half] + jnp.sum(q, axis=0, keepdims=True)
                if half == 0:
                    row_parts.append(q)
                else:
                    row_parts[-1] = row_parts[-1] + q
            sums = jnp.concatenate([jnp.sum(q, axis=1, keepdims=True) for q in row_parts], axis=0)
            row_sums = jnp.where(lane == j, sums, row_sums)
            cs_t[pl.ds(8 * i + j, 1), rows] = jnp.concatenate(col_sum, axis=1)
        rs_t[rows8, rows] = jnp.transpose(row_sums)[:8]
        grad_xs = mm(mst[...], dyst[...], 0, 0) + kin[5:6] * dy_f

        growth = expand(jnp.exp2(col[:, :8]))
        weight = expand(jnp.exp2(total[:, :8] - col[:, :8]) * cols[rows][:, :8])
        state_in = states[s]
        state_low = state_in.astype(bf16)
        state_grad = sgrad[...]
        carry_low = state_grad.astype(bf16)
        readout = mm(c_low, state_low, 1, 1)
        read_low = (dy_f * growth).astype(bf16)
        hi, low = split2(dy_f * readout)
        dr_t[rows8, rows] = mm(pick, hi, 1, 1) + mm(pick, low, 1, 1)
        gc[rows] += mm(read_low, state_low)
        grad_xw = mm(b_low, carry_low, 1, 1)
        xw_low = (xs * weight).astype(bf16)
        gb[rows] += mm(xw_low, carry_low)
        hi, low = split2(grad_xw * xs)
        wg_t[rows8, rows] = mm(pick, hi, 1, 1) + mm(pick, low, 1, 1)
        hi, low = split2(state_grad * state_in)
        sums = jnp.sum(mm(pick, hi) + mm(pick, low), axis=1, keepdims=True)
        gt_t[rows8] = jnp.where(iota((8, 128), 1) == s, sums, gt_t[rows8])
        grad_xs = grad_xs + grad_xw * weight
        local = mm(read_low, c_low, 0, 0)
        fade = jnp.exp2(total)
        for j in range(HB):
            at_j = slice(j * HEAD, j * HEAD + HEAD)
            sgrad[at_j] = fade[:, j : j + 1] * state_grad[at_j] + local[at_j]
        gtaps[5:6] += jnp.sum(dy_f * xs, axis=0, keepdims=True)
        dinner_out[rows] = conv_rows(at, kin[...], grad_xs).astype(bf16)
        if links:
            work.step(i * spans + back)
        return carry

    lax.fori_loop(0, spans, span, 0)
    gk_out[...] = gtaps[...]

    @pl.when(i == pl.num_programs(0) - 1)
    def _():
        buf[8 : 8 + tokens] = cst[...]
        gtaps[...] = jnp.zeros(gtaps.shape, f32)
        rate = rateT[:, 0:1]
        later = (iota((Q, Q), 0) >= iota((Q, Q), 1)).astype(f32).astype(bf16)
        last = iota((48, Q), 1) == Q - 1
        bias_sum = jnp.zeros((48, 1), f32)
        decay_sum = jnp.zeros((48, 1), f32)
        for back in range(spans):
            s = spans - 1 - back
            rows = slice(s * Q, s * Q + Q)
            bc = bc_in[rows]
            gl = gg[s].astype(bf16)
            grad_c = gc[rows] + mm(gl, bc[:, :128])
            grad_b = gb[rows] + mm(gl, bc[:, 128:], 0, 0)
            both = jnp.concatenate([grad_b, grad_c], axis=1)
            dsd_out[rows, :BW] = conv_rows(s * Q, kst[...], both).astype(bf16)

            cum, step, pre = cumT[:, rows], stepT[:, rows], preT[:, rows]
            total = cum[:, Q - 1 : Q]
            rate_w = jnp.exp2(total - cum)
            wg = wg_t[:, rows]
            cs = cs_t[:, rows]
            moved = wg * (rate_w * step)
            grad_cum = rs_t[:, rows] - cs + jnp.exp2(cum) * dr_t[:, rows] - moved
            grad_total = jnp.exp2(total) * gt_t[:, s : s + 1] + jnp.sum(moved, axis=1, keepdims=True)
            grad_cum = grad_cum + jnp.where(last, grad_total, 0.0)
            parts = split3(grad_cum)
            grad_rate = mm(parts[0], later) + mm(parts[1], later) + mm(parts[2], later)
            sig = sigmoid(pre)
            ratio = jnp.where(pre < -15.0, 1.0, sig / step)
            grad_pre = (wg * rate_w + grad_rate * rate) * sig + cs * ratio
            bias_sum = bias_sum + jnp.sum(grad_pre, axis=1, keepdims=True)
            decay_sum = decay_sum + jnp.sum(grad_rate * step, axis=1, keepdims=True)
            full = jnp.concatenate([grad_pre, jnp.zeros((80, Q), f32)], axis=0)
            dsd_out[rows, BW:] = jnp.transpose(full).astype(bf16)
        gks_out[...] = gtaps[...]
        lane = iota((48, 128), 1)
        hs_out[...] = jnp.where(lane == 0, bias_sum, jnp.where(lane == 1, decay_sum * rate, 0.0))
        if links:
            work.finish()


class Place:
    def __init__(self):
        me = lax.axis_index("dp")
        self.me = me
        self.c, self.y, self.z = me % 2, (me // 2) % 2, me // 4

    def at(self, z, y, c):
        return (z * 2 + y) * 2 + c

    def core(self):
        return self.at(self.z, self.y, 1 - self.c)

    def side(self):
        return self.at(self.z, 1 - self.y, self.c)

    def up(self):
        return self.me + 4

    def down(self):
        return self.me - 4


def greet(here, across):
    barrier = pltpu.get_barrier_semaphore()

    def signal(**device):
        pl.semaphore_signal(barrier, 1, device_id=device, device_id_type=MESH)

    signal(dp=here.core())
    signal(dp=here.side())
    pl.when(here.z < 3)(lambda: signal(dp=here.up()))
    pl.when(here.z > 0)(lambda: signal(dp=here.down()))
    if across:
        signal(tensor=1 - lax.axis_index("tensor"))
    ends = (here.z == 0).astype(jnp.int32) + (here.z == 3).astype(jnp.int32)
    pl.semaphore_wait(barrier, 4 + int(across) - ends)


def remote(src, dst, send_sem, recv_sem, **device):
    return pltpu.make_async_remote_copy(
        src_ref=src, dst_ref=dst, send_sem=send_sem, recv_sem=recv_sem, device_id=device, device_id_type=MESH
    )


class Gather:
    def __init__(self, here, pack, full, ss, rs, chunk, cols):
        self.here, self.full, self.ss, self.rs, self.chunk, self.cols = here, full, ss, rs, chunk, cols
        self.rows = pack.shape[0]
        self.own = pack.at[:, cols]

    def slot(self, origin):
        return self.full.at[pl.ds(pl.multiple_of(origin * self.rows, self.rows), self.rows), self.cols]

    def copy(self, origin, way, src=None):
        here = self.here
        target = (here.up, here.down, here.side, here.core)[way]()
        slot = self.slot(origin)
        sems = self.ss.at[self.chunk, origin, way], self.rs.at[self.chunk, origin]
        return remote(slot if src is None else src, slot, *sems, dp=target)

    def arrived(self, origin):
        self.copy(origin, 3).wait_recv()

    def each_send(self, act):
        here = self.here
        for hops in range(4):
            for way, origin_z in ((0, here.z - hops), (1, here.z + hops)):
                if hops == 0:
                    if way == 1:
                        continue
                    origin = here.me
                    pl.when(here.z < 3)(lambda o=origin: act(o, 0))
                    pl.when(here.z > 0)(lambda o=origin: act(o, 1))
                    act(origin, 2)
                    act(origin, 3)
                    continue
                origin = here.at(origin_z, here.y, here.c)

                def go(o=origin, way=way):
                    pl.when((here.z < 3) if way == 0 else (here.z > 0))(lambda: act(o, way))
                    act(o, 2)
                    act(o, 3)

                pl.when((origin_z >= 0) & (origin_z <= 3))(go)

    def start(self):
        here = self.here
        pl.when(here.z < 3)(lambda: self.copy(here.me, 0, self.own).start())
        pl.when(here.z > 0)(lambda: self.copy(here.me, 1, self.own).start())
        self.copy(here.me, 2, self.own).start()
        self.copy(here.me, 3, self.own).start()

    def hop(self, hops):
        here = self.here
        for way, origin_z in ((0, here.z - hops), (1, here.z + hops)):

            def go(way=way, origin_z=origin_z):
                origin = here.at(origin_z, here.y, here.c)
                self.arrived(origin)
                pl.when((here.z < 3) if way == 0 else (here.z > 0))(lambda: self.copy(origin, way).start())
                self.copy(origin, 2).start()
                self.copy(origin, 3).start()

            pl.when((origin_z >= 0) & (origin_z <= 3))(go)

    def sides(self, hops):
        here = self.here
        for way, origin_z in ((0, here.z - hops), (1, here.z + hops)):
            if hops == 0 and way == 1:
                continue

            def go(origin_z=origin_z):
                origin = here.at(origin_z, 1 - here.y, here.c)
                self.arrived(origin)
                self.copy(origin, 3).start()

            pl.when((origin_z >= 0) & (origin_z <= 3))(go)

    def finish(self):
        here = self.here
        for z in range(4):
            for y in range(2):
                self.arrived(here.at(z, y, 1 - here.c))
        self.each_send(lambda origin, way: self.copy(origin, way).wait_send())
        for z in range(4):
            self.copy(here.at(z, 1 - here.y, here.c), 3).wait_send()


def gathers(here, pack, full, ss, rs):
    cols = pack.shape[1]
    cut = cols // 256 * 128
    return [Gather(here, pack, full, ss, rs, n, c) for n, c in enumerate((slice(0, cut), slice(cut, cols)))]


def own_rows(here, pack, full, sem):
    rows = pack.shape[0]
    return pltpu.make_async_copy(pack, full.at[pl.ds(pl.multiple_of(here.me * rows, rows), rows)], sem)


def gather_scratch():
    sem = pltpu.SemaphoreType.DMA
    return [sem((2, 16, 4)), sem((2, 16))]


def gather_kernel(tokens_in, gain, pack, tokens_out, full, low, ss, rs, xs, xr, ls):
    here = Place()
    half = lax.axis_index("tensor")
    rows = tokens_in.shape[0]
    greet(here, True)
    moves = gathers(here, pack, full, ss, rs)
    for move in moves:
        move.start()
    own = own_rows(here, pack, full, ls.at[0])
    own.start()
    part = rows // 4
    across, local = [], []
    for n in range(4):
        piece = slice(n * part, n * part + part)
        v = tokens_in[piece].astype(f32)
        scale = lax.rsqrt(jnp.mean(v * v, axis=1, keepdims=True) + norm_eps)
        low[piece] = (v * scale * gain[...]).astype(bf16)
        slot = tokens_out.at[pl.ds(pl.multiple_of(half * rows + n * part, part), part)]
        across.append(remote(low.at[piece], slot, xs.at[n], xr.at[n], tensor=1 - half))
        across[-1].start()
        local.append(pltpu.make_async_copy(low.at[piece], slot, ls.at[n + 1]))
        local[-1].start()
    for hops in range(1, 5):
        for move in moves:
            if hops < 4:
                move.hop(hops)
            move.sides(hops - 1)
    own.wait()
    for n in range(4):
        local[n].wait()
        across[n].wait()
    for move in moves:
        move.finish()


def gather_rows(tokens_in, gain, pack, ways, collective_id):
    rows, width = tokens_in.shape
    vmem = pl.BlockSpec(memory_space=pltpu.VMEM)
    hbm = pl.BlockSpec(memory_space=pl.ANY)
    return pl.pallas_call(
        gather_kernel,
        name="gather_rows",
        in_specs=[vmem, vmem, vmem],
        out_specs=[hbm, hbm],
        out_shape=[sds((2 * rows, width), bf16), sds((ways * pack.shape[0], pack.shape[1]), bf16)],
        scratch_shapes=[
            pltpu.VMEM((rows, width), bf16), *gather_scratch(),
            pltpu.SemaphoreType.DMA((4,)), pltpu.SemaphoreType.DMA((4,)), pltpu.SemaphoreType.DMA((5,)),
        ],
        compiler_params=pltpu.CompilerParams(
            collective_id=collective_id, has_side_effects=True, vmem_limit_bytes=60 * 1024 * 1024
        ),
    )(tokens_in, gain, pack)


class Reduce:
    def __init__(self, here, grads, out, bufs, sems):
        self.here, self.grads, self.out = here, grads, out
        self.held, self.buf_a, self.buf_b, self.buf_up, self.buf_dn = bufs
        self.local, self.send_a, self.recv_a, self.send_b, self.recv_b, self.send_c, self.recv_up, self.recv_dn = sems
        self.parts, self.rows = out.shape[:2]
        z = here.z
        self.order = (3 * (1 - z // 2), (3 * z + 2) % 5, 1 + z % 2, z)

    def spot(self, z, y, c):
        if self.grads is None:
            return z, (y * 2 + c) * self.rows
        return z * 2 + y, 0

    def own(self, z, y, c=None):
        at, base = self.spot(z, y, self.here.c if c is None else c)
        return self.held.at[at, :, pl.ds(pl.multiple_of(base, 16), self.rows)]

    def block(self, z, y, c):
        if self.grads is None:
            return self.own(z, y, c)
        at = pl.multiple_of(self.here.at(z, y, c) * self.rows, self.rows)
        return self.grads.at[:, pl.ds(at, self.rows)]

    def copy_a(self, z, y):
        here, at = self.here, z * 2 + y
        return remote(self.block(z, y, 1 - here.c), self.buf_a.at[at], self.send_a.at[at], self.recv_a.at[at], dp=here.core())

    def take(self, z, y):
        return pltpu.make_async_copy(self.block(z, y, self.here.c), self.own(z, y), self.local.at[z * 2 + y])

    def copy_b(self, z):
        here = self.here
        return remote(self.own(z, 1 - here.y), self.buf_b.at[z], self.send_b.at[z], self.recv_b.at[z], dp=here.side())

    def copy_up(self, z):
        return remote(self.own(z, self.here.y), self.buf_up.at[z], self.send_c.at[z], self.recv_up.at[z], dp=self.here.up())

    def copy_dn(self, z):
        return remote(self.own(z, self.here.y), self.buf_dn.at[z], self.send_c.at[z], self.recv_dn.at[z], dp=self.here.down())

    def add(self, z, y, buf, slot):
        at, base = self.spot(z, y, self.here.c)

        def rows(n, carry):
            piece = pl.ds(pl.multiple_of(n * 16, 16), 16)
            held = pl.ds(pl.multiple_of(base + n * 16, 16), 16)
            for part in range(self.parts):
                total = self.held[at, part, held].astype(f32) + buf[slot, part, piece].astype(f32)
                self.held[at, part, held] = total.astype(bf16)
            return carry

        lax.fori_loop(0, self.rows // 16, rows, 0)

    def start(self):
        here = self.here
        for side in (1 - here.y, here.y):
            for z in self.order:
                self.copy_a(z, side).start()
                self.take(z, side).start()

    def join(self, z, y):
        if self.grads is not None:
            self.take(z, y).wait()
        self.copy_a(z, y).wait_recv()
        self.add(z, y, self.buf_a, z * 2 + y)

    def cores(self, z):
        self.join(z, 1 - self.here.y)
        self.copy_b(z).start()

    def stay(self, z):
        self.join(z, self.here.y)

    def sides(self, z):
        self.copy_b(z).wait_recv()
        self.add(z, self.here.y, self.buf_b, z)

    def pass_on(self, z):
        here = self.here

        def up():
            def below():
                self.copy_up(z).wait_recv()
                self.add(z, here.y, self.buf_up, z)

            pl.when(here.z > 0)(below)
            self.copy_up(z).start()

        def down():
            def above():
                self.copy_dn(z).wait_recv()
                self.add(z, here.y, self.buf_dn, z)

            pl.when(here.z < 3)(above)
            self.copy_dn(z).start()

        pl.when(z > here.z)(up)
        pl.when(z < here.z)(down)

    def finish(self):
        here = self.here
        z = here.z
        at, base = self.spot(z, here.y, here.c)
        pl.when(z > 0)(lambda: self.copy_up(z).wait_recv())
        pl.when(z < 3)(lambda: self.copy_dn(z).wait_recv())

        def rows(n, carry):
            piece = pl.ds(pl.multiple_of(n * 16, 16), 16)
            held = pl.ds(pl.multiple_of(base + n * 16, 16), 16)
            for part in range(self.parts):
                below = jnp.where(z > 0, self.buf_up[z, part, piece].astype(f32), 0.0)
                above = jnp.where(z < 3, self.buf_dn[z, part, piece].astype(f32), 0.0)
                self.out[part, piece] = self.held[at, part, held].astype(f32) + below + above
            return carry

        lax.fori_loop(0, self.rows // 16, rows, 0)
        for zn in self.order:
            self.copy_a(zn, 0).wait_send()
            self.copy_a(zn, 1).wait_send()
            self.copy_b(zn).wait_send()
            pl.when(zn > z)(lambda zn=zn: self.copy_up(zn).wait_send())
            pl.when(zn < z)(lambda zn=zn: self.copy_dn(zn).wait_send())


def reduce_scratch(parts, rows, cols, by_z=False):
    sem = pltpu.SemaphoreType.DMA
    block = (parts, rows, cols)
    held = (4, parts, 4 * rows, cols) if by_z else (8,) + block
    return [
        pltpu.VMEM(held, bf16), pltpu.VMEM((8,) + block, bf16), pltpu.VMEM((4,) + block, bf16),
        pltpu.VMEM((4,) + block, bf16), pltpu.VMEM((4,) + block, bf16),
        sem((8,)), sem((8,)), sem((8,)), sem((4,)), sem((4,)), sem((4,)), sem((4,)), sem((4,)),
    ]


def tail_kernel(
    normed_t, dinner, dsd, dgate, wb, wa, small, gn_out, shard_out, small_out,
    nt_v, dinner_v, dsd_v, dgate_v, wg_v, wa_v, away, came, total, landed, loads, send_x, recv_x, send, recv, *scratch,
):
    here = Place()
    half = lax.axis_index("tensor")
    units = dgate.shape[1]
    sources = (normed_t, dinner, dsd, dgate, wb.at[:, :units], wa)
    pending = [
        pltpu.make_async_copy(src, dst, loads.at[n])
        for n, (src, dst) in enumerate(zip(sources, (nt_v, dinner_v, dsd_v, dgate_v, wg_v, wa_v)))
    ]
    for copy in pending:
        copy.start()
    far = pltpu.get_barrier_semaphore()
    partners = [here.me + bit - 2 * bit * ((here.me // bit) % 2) for bit in (1, 2, 4, 8)]
    for partner in partners:
        pl.semaphore_signal(far, 1, device_id={"dp": partner}, device_id_type=MESH)
    pl.semaphore_signal(far, 1, device_id={"tensor": 1 - half}, device_id_type=MESH)
    middle = (here.z == 1) | (here.z == 2)
    pl.when(here.z == 1)(lambda: pl.semaphore_signal(far, 1, device_id={"dp": here.up()}, device_id_type=MESH))
    pl.when(here.z == 2)(lambda: pl.semaphore_signal(far, 1, device_id={"dp": here.down()}, device_id_type=MESH))
    pl.semaphore_wait(far, 5 + middle.astype(jnp.int32))
    work = Reduce(here, None, shard_out, scratch[:5], scratch[5:])
    order = work.order
    rows = gn_out.shape[0]
    chunks, _, wide = away.shape

    def swap(k):
        return remote(total.at[k], landed.at[k], send.at[k], recv.at[k], dp=partners[k])

    def swapped(k):
        swap(k).wait()
        total[k + 1] = total[k] + landed[k]
        if k < 3:
            swap(k + 1).start()

    def across(n):
        return remote(away.at[n], came.at[n], send_x.at[n], recv_x.at[n], tensor=1 - half)

    def pulled(which, n):
        mine = pl.ds(pl.multiple_of(which * rows, rows), rows)
        at = pl.ds(pl.multiple_of(n * wide, wide), wide)
        return (
            mm(dgate_v[mine], wg_v[at], 1, 1)
            + mm(dinner_v[mine], wa_v[at, :units], 1, 1)
            + mm(dsd_v[mine], wa_v[at, units:], 1, 1)
        )

    def far_chunk(n, carry):
        away[n] = pulled(1 - half, n).astype(bf16)
        across(n).start()
        return carry

    def near_chunk(n, carry):
        gn_out[:, pl.ds(pl.multiple_of(n * wide, wide), wide)] = pulled(half, n)
        return carry

    def grads(n, carry):
        z = jnp.where(n == 0, order[0], jnp.where(n == 1, order[1], jnp.where(n == 2, order[2], order[3])))
        count = 4 * work.rows
        left = nt_v[pl.ds(pl.multiple_of(z * count, count), count)]
        work.held[z, 0, :, :units] = mm(left, dinner_v[...]).astype(bf16)
        work.held[z, 0, :, units:] = mm(left, dsd_v[...]).astype(bf16)
        work.copy_a(z, 1 - here.y).start()
        work.copy_a(z, here.y).start()

        @pl.when(n == 0)
        def _():
            for copy in pending[3:]:
                copy.wait()

        far_chunk(n, carry)
        work.cores(z)
        return carry

    total[0] = small[...]
    swap(0).start()
    for copy in pending[:3]:
        copy.wait()
    lax.fori_loop(0, 4, grads, 0)
    swapped(0)
    work.stay(order[0])
    work.sides(order[0])
    pl.when(~middle)(lambda: work.pass_on(order[0]))
    lax.fori_loop(4, chunks, far_chunk, 0)
    swapped(1)
    for n in range(1, 4):
        work.stay(order[n])
    work.sides(order[1])
    pl.when(~middle)(lambda: work.pass_on(order[1]))
    lax.fori_loop(0, 3, near_chunk, 0)
    swapped(2)
    pl.when(middle)(lambda: work.pass_on(order[0]))
    work.sides(order[2])
    pl.when(~middle)(lambda: work.pass_on(order[2]))
    lax.fori_loop(3, chunks, near_chunk, 0)
    swapped(3)
    small_out[...] = total[4]
    pl.when(middle)(lambda: work.pass_on(order[1]))
    work.sides(order[3])
    pl.when(middle)(lambda: work.pass_on(order[2]))
    work.finish()

    def arrive(n, carry):
        across(n).wait()
        at = pl.ds(pl.multiple_of(n * wide, wide), wide)
        gn_out[:, at] = gn_out[:, at] + came[n].astype(f32)
        return carry

    lax.fori_loop(0, chunks, arrive, 0)


def reduce_tail(normed_t, dinner, dsd, dgate, wb, wa, small, ways, collective_id):
    width, tokens = normed_t.shape
    units, cols, rows = dgate.shape[1], wa.shape[1], width // ways
    chunks = width // BW
    vmem = pl.BlockSpec(memory_space=pltpu.VMEM)
    hbm = pl.BlockSpec(memory_space=pl.ANY)
    sem = pltpu.SemaphoreType.DMA
    return pl.pallas_call(
        tail_kernel, name="tail", in_specs=[hbm] * 6 + [vmem], out_specs=[vmem] * 3,
        out_shape=[sds((tokens // 2, width)), sds((1, rows, cols)), sds(small.shape)],
        scratch_shapes=[
            pltpu.VMEM(normed_t.shape, bf16), pltpu.VMEM(dinner.shape, bf16), pltpu.VMEM(dsd.shape, bf16),
            pltpu.VMEM(dgate.shape, bf16), pltpu.VMEM((width, units), bf16), pltpu.VMEM(wa.shape, bf16),
            pltpu.VMEM((chunks, tokens // 2, BW), bf16), pltpu.VMEM((chunks, tokens // 2, BW), bf16),
            pltpu.VMEM((5,) + small.shape, f32), pltpu.VMEM((4,) + small.shape, f32),
            sem((6,)), sem((chunks,)), sem((chunks,)), sem((4,)), sem((4,)),
        ] + reduce_scratch(1, rows, cols, True),
        compiler_params=pltpu.CompilerParams(
            collective_id=collective_id, has_side_effects=True, vmem_limit_bytes=62 * 1024 * 1024
        ),
    )(normed_t, dinner, dsd, dgate, wb, wa, small)


def swap(v):
    return lax.ppermute(v, "tensor", [(0, 1), (1, 0)])


def halves(v, axis):
    size = v.shape[axis] // 2
    me = lax.axis_index("tensor")
    return (
        lax.dynamic_slice_in_dim(v, me * size, size, axis),
        lax.dynamic_slice_in_dim(v, (1 - me) * size, size, axis),
    )


def once(shape, at=None):
    where = at or (0,) * len(shape)
    return pl.BlockSpec(shape, lambda i: where, pipeline_mode=pl.Buffered(1))


def by_cols(rows, offset=0):
    return pl.BlockSpec((rows, BW), lambda i: (0, i + offset))


def params(collective_id=None):
    return pltpu.CompilerParams(
        dimension_semantics=("arbitrary",), vmem_limit_bytes=60 * 1024 * 1024,
        collective_id=collective_id, has_side_effects=collective_id is not None,
    )


def spread(v):
    lead = v.shape[:-1]
    v = v.reshape(lead + (v.shape[-1] // HB, HB))
    v = jnp.pad(v, [(0, 0)] * len(lead) + [(0, 0), (0, 8 - HB)]).reshape(lead + (-1,))
    return jnp.pad(v, [(0, 0)] * len(lead) + [(0, 128 - v.shape[-1])])


def gathered_heads(v, heads):
    return v[..., : heads * 2].reshape(v.shape[:-1] + (heads // HB, 8))[..., :HB].reshape(v.shape[:-1] + (heads,))


def sds(shape, dtype=f32):
    return jax.ShapeDtypeStruct(shape, dtype)


def on_device(
    residual, norm_gain, w_gate_inner, w_state_io, w_step, conv_inner, conv_state,
    step_bias, decay_log, skip_gain, gate_gain, w_output, cotangent,
):
    width = residual.shape[1]
    units = w_gate_inner.shape[2]
    heads = w_step.shape[1]
    blocks = units // BW
    unit_total = units * lax.axis_size("tensor")
    ways = lax.axis_size("dp")
    own_links = ways == 16
    rows_in = residual.astype(f32)
    rstd_in = lax.rsqrt(jnp.mean(rows_in * rows_in, axis=1, keepdims=True) + norm_eps)
    scaled = rows_in * rstd_in
    pack_a = jnp.concatenate([w_gate_inner[1], w_state_io, spread(w_step)], axis=1)
    pack_b = jnp.concatenate([w_gate_inner[0], w_output.T], axis=1)
    if own_links:
        normed, wa = gather_rows(residual, norm_gain[None], pack_a, ways, 1)
    else:
        wa = lax.all_gather(pack_a, "dp", axis=0, tiled=True)
        normed = lax.all_gather((scaled * norm_gain).astype(bf16), "tensor", axis=0, tiled=True)
    tokens = normed.shape[0]
    spans = tokens // Q
    rate = -jnp.exp(decay_log)
    kin = jnp.concatenate([conv_inner, jnp.repeat(skip_gain, HEAD)[None], jnp.zeros((2, units), f32)], axis=0)
    kst = jnp.concatenate([conv_state, jnp.zeros((3, BW), f32)], axis=0)
    hp = jnp.concatenate([spread(step_bias)[None], spread(rate)[None], jnp.zeros((6, 128), f32)], axis=0)
    rate_t = jnp.broadcast_to(spread(rate)[:48, None], (48, 128))
    gain8 = jnp.broadcast_to(gate_gain[None], (8, units))

    hbm = pl.BlockSpec(memory_space=pl.ANY)
    sem = pltpu.SemaphoreType.DMA
    inner, ssd, states, cst, bc, step, cum, step_t, cum_t, pre_t, *sent = pl.pallas_call(
        functools.partial(mixer_forward, own_links),
        name="mixer_forward",
        grid=(blocks,),
        in_specs=[
            once((tokens, width)), by_cols(width), once((width, 384), (0, units // 384)),
            by_cols(8), once((8, BW)), once((8, 128)),
        ] + [once(cotangent.shape), once(pack_b.shape)] * own_links,
        out_specs=[
            by_cols(tokens), by_cols(tokens), pl.BlockSpec((spans, BW, 128), lambda i: (0, i, 0)),
            once((tokens, BW)), once((tokens, BW)), once((tokens, 128)), once((tokens, 128)),
            once((48, tokens)), once((48, tokens)), once((48, tokens)),
        ] + [hbm, hbm] * own_links,
        out_shape=[
            sds((tokens, units)), sds((tokens, units)), sds((spans, units, 128)),
            sds((tokens, BW)), sds((tokens, BW), bf16), sds((tokens, 128)), sds((tokens, 128)),
            sds((48, tokens)), sds((48, tokens)), sds((48, tokens)),
        ] + [sds((tokens, width), bf16), sds((width, 2 * units), bf16)] * own_links,
        scratch_shapes=[
            pltpu.VMEM((tokens + 8, BW), f32), pltpu.VMEM((spans, Q, Q), f32),
            pltpu.VMEM((tokens, 128), f32), pltpu.VMEM((tokens, 128), f32), pltpu.VMEM((8, tokens), f32),
            pltpu.VMEM((Q, HB * Q), bf16), pltpu.VMEM((HB * Q, BW), bf16), pltpu.VMEM((BW, 128), f32),
        ] + (gather_scratch() + [sem, sem, sem((2,))]) * own_links,
        compiler_params=params(2 if own_links else None),
        cost_estimate=pl.CostEstimate(flops=2 * tokens * width * (units + 384) + 4 * tokens * 256 * units, bytes_accessed=30_000_000, transcendentals=heads * spans * Q * Q),
    )(normed, wa, wa, kin, kst, hp, *[cotangent, pack_b] * own_links)

    if own_links:
        cot, wb = sent
    else:
        wb = lax.all_gather(pack_b, "dp", axis=0, tiled=True)
        cot = lax.all_gather(cotangent, "tensor", axis=0, tiled=True)

    gate, ggo, stats = pl.pallas_call(
        functools.partial(gate_forward, own_links),
        name="gate_forward",
        grid=(blocks,),
        in_specs=[
            once((tokens, width)), once((tokens, width)), by_cols(width), by_cols(width, blocks),
            by_cols(tokens), by_cols(8),
        ],
        out_specs=[by_cols(tokens), by_cols(tokens), once((8, tokens))],
        out_shape=[sds((tokens, units)), sds((tokens, units)), sds((8, tokens))],
        scratch_shapes=[pltpu.VMEM((tokens, 128), f32), pltpu.VMEM((tokens, 128), f32)]
        + [pltpu.VMEM((8, tokens), f32), pltpu.VMEM((8, tokens), f32), sem, sem] * own_links,
        compiler_params=params(3 if own_links else None),
        cost_estimate=pl.CostEstimate(flops=4 * tokens * width * units, bytes_accessed=35_000_000, transcendentals=tokens * units),
    )(normed, cot, wb, wb, ssd, gain8)
    if not own_links:
        stats = stats + swap(stats)

    dy, dgate, ng, ggg, grad_b, normed_t = pl.pallas_call(
        functools.partial(gate_backward, float(unit_total)),
        name="gate_backward",
        grid=(blocks,),
        in_specs=[
            once((8, tokens)), by_cols(tokens), by_cols(tokens), by_cols(tokens), by_cols(8),
            once((tokens, width)), once((tokens, width)),
        ],
        out_specs=[
            by_cols(tokens), by_cols(tokens), by_cols(tokens), by_cols(8),
            pl.BlockSpec((2, width, BW), lambda i: (0, 0, i)), once((width, tokens)),
        ],
        out_shape=[
            sds((tokens, units), bf16), sds((tokens, units), bf16), sds((tokens, units), bf16), sds((8, units)),
            sds((2, width, units), bf16), sds((width, tokens), bf16),
        ],
        scratch_shapes=[pltpu.VMEM((tokens, 128), f32), pltpu.VMEM((width, tokens), bf16)],
        compiler_params=params(),
        cost_estimate=pl.CostEstimate(flops=4 * tokens * units * width, bytes_accessed=45_000_000, transcendentals=tokens * units),
    )(stats, gate, ssd, ggo, gain8, normed, cot)

    mixed = mm(ng, wb[:, units:], 1, 1).astype(bf16)
    mixed_near, mixed_far = halves(mixed, 0)

    dinner, gk, dsd, gks, hs, *sent = pl.pallas_call(
        functools.partial(mixer_backward, own_links),
        name="mixer_backward",
        grid=(blocks,),
        in_specs=[
            by_cols(tokens), by_cols(tokens), pl.BlockSpec((spans, BW, 128), lambda i: (0, i, 0)),
            by_cols(8), once((8, BW)), once((8, 128)),
            once((tokens, BW)), once((tokens, BW)), once((tokens, 128)), once((tokens, 128)),
            once((48, tokens)), once((48, tokens)), once((48, tokens)), once((48, 128)),
        ] + [hbm, hbm] * own_links,
        out_specs=[by_cols(tokens), by_cols(8), once((tokens, 384)), once((8, BW)), once((48, 128))]
        + [hbm, once((2, width // ways, units))] * own_links,
        out_shape=[sds((tokens, units), bf16), sds((8, units)), sds((tokens, 384), bf16), sds((8, BW)), sds((48, 128))]
        + [sds((tokens // 2, width), bf16), sds((2, width // ways, units))] * own_links,
        scratch_shapes=[
            pltpu.VMEM((tokens + 8, BW), f32), pltpu.VMEM((tokens + 8, BW), f32),
            pltpu.VMEM((spans, Q, Q), f32), pltpu.VMEM((spans, Q, Q), f32),
            pltpu.VMEM((tokens, 128), f32), pltpu.VMEM((tokens, 128), f32),
            pltpu.VMEM((tokens, 128), f32), pltpu.VMEM((tokens, 128), f32), pltpu.VMEM((8, tokens), f32),
            pltpu.VMEM((HB * Q, Q), bf16), pltpu.VMEM((HB * Q, BW), bf16), pltpu.VMEM((HB * Q, Q), f32),
            pltpu.VMEM((BW, 128), f32),
            pltpu.VMEM((48, tokens), f32), pltpu.VMEM((48, tokens), f32), pltpu.VMEM((48, tokens), f32),
            pltpu.VMEM((48, tokens), f32), pltpu.VMEM((48, 128), f32), pltpu.VMEM((8, BW), f32),
        ] + ([sem, sem] + reduce_scratch(2, width // ways, units)) * own_links,
        compiler_params=params(4 if own_links else None),
        cost_estimate=pl.CostEstimate(flops=40_000_000_000, bytes_accessed=30_000_000, transcendentals=heads * spans * Q * Q),
    )(inner, dy, states, kin, kst, hp, cst, bc, step, cum, step_t, cum_t, pre_t, rate_t, *[mixed, grad_b] * own_links)
    if own_links:
        mixed_got, wb_shard = sent
    else:
        mixed_got = swap(mixed_far)
        wb_shard = lax.psum_scatter(grad_b, "dp", scatter_dimension=1, tiled=True).astype(f32)
    output = (rows_in + mixed_near.astype(f32) + mixed_got.astype(f32)).astype(bf16)

    last = jnp.concatenate([gks[:5].reshape(-1), hs[:, 0], hs[:, 1], jnp.zeros((units - 5 * BW - 96,), f32)])
    small = jnp.concatenate([gk[:6], ggg[:1], last[None]], axis=0)
    if own_links:
        grad_normed, wa_shard, small = reduce_tail(normed_t, dinner, dsd, dgate, wb, wa, small, ways, 5)
        wa_shard = wa_shard[0]
    else:
        grad_a = jnp.concatenate([mm(normed_t, dinner).astype(bf16), mm(normed_t, dsd).astype(bf16)], axis=1)
        pulled = mm(dgate, wb[:, :units], 1, 1) + mm(dinner, wa[:, :units], 1, 1) + mm(dsd, wa[:, units:], 1, 1)
        near, far = halves(pulled.astype(bf16), 0)
        wa_shard = lax.psum_scatter(grad_a, "dp", scatter_dimension=0, tiled=True).astype(f32)
        small = lax.psum(small, "dp")
        grad_normed = near.astype(f32) + swap(far).astype(f32)
    grad_v = grad_normed * norm_gain
    grad_residual = cotangent.astype(f32) + rstd_in * (
        grad_v - scaled * jnp.mean(grad_v * scaled, axis=1, keepdims=True)
    )

    conv_state_sum = small[7, : 5 * BW].reshape(5, BW)
    bias_sum = gathered_heads(small[7, 5 * BW : 5 * BW + 48], heads)
    decay_sum = gathered_heads(small[7, 5 * BW + 48 : 5 * BW + 96], heads)
    skip_sum = jnp.sum(small[5].reshape(heads, HEAD), axis=1)

    gain_rows = jnp.sum(wb_shard[0] * w_gate_inner[0].astype(f32), axis=1) + jnp.sum(
        wa_shard * pack_a.astype(f32), axis=1
    )
    count = gain_rows.shape[0]
    gain_own = gain_rows / lax.dynamic_slice_in_dim(norm_gain, lax.axis_index("dp") * count, count)
    near_s, far_s = halves(jnp.concatenate([wa_shard[:, units : units + BW], conv_state_sum], axis=0), 1)
    near_g, far_g = halves(gain_own, 0)
    far_all = jnp.concatenate([far_s.reshape(-1), far_g])
    got = swap(far_all)
    both = near_s + got[: far_s.size].reshape(far_s.shape)
    gain_part = near_g + got[far_s.size :]
    return (
        output,
        grad_residual,
        gain_part,
        jnp.stack([wb_shard[0], wa_shard[:, :units]]),
        both[:count],
        gathered_heads(wa_shard[:, units + BW :], heads),
        small[0:5],
        both[count:],
        bias_sum,
        decay_sum,
        skip_sum,
        small[6],
        wb_shard[1].T,
    )


def solution(mesh):
    return jax.shard_map(
        on_device,
        mesh=mesh,
        in_specs=(
            P(("dp", "tensor"), None),
            P(),
            P(None, "dp", "tensor"),
            P("dp", None),
            P("dp", "tensor"),
            P(None, "tensor"),
            P(),
            P("tensor"),
            P("tensor"),
            P("tensor"),
            P("tensor"),
            P("tensor", "dp"),
            P(("dp", "tensor"), None),
        ),
        out_specs=(
            P(("dp", "tensor"), None),
            P(("dp", "tensor"), None),
            P(("dp", "tensor")),
            P(None, "dp", "tensor"),
            P("dp", "tensor"),
            P("dp", "tensor"),
            P(None, "tensor"),
            P(None, "tensor"),
            P("tensor"),
            P("tensor"),
            P("tensor"),
            P("tensor"),
            P("tensor", "dp"),
        ),
        check_vma=False,
    )
```

```python
import functools

import jax
import jax.numpy as jnp
from jax import lax
from jax.experimental import pallas as pl
from jax.experimental.pallas import tpu as pltpu
from jax.sharding import PartitionSpec as P

Q = 256
LEN = 1024
HEAD = 64
BW = 256
HB = BW // HEAD
LOG2E = 1.4426950408889634
FAR = -1e30
norm_eps = 1e-05
MESH = pl.DeviceIdType.MESH
f32 = jnp.float32
bf16 = jnp.bfloat16


def mm(a, b, ca=1, cb=0):
    return lax.dot_general(a, b, (((ca,), (cb,)), ((), ())), preferred_element_type=f32)


def sigmoid(v):
    return 1.0 / (1.0 + jnp.exp(-v))


def split3(a):
    hi = a.astype(bf16)
    rest = a - hi.astype(f32)
    mid = rest.astype(bf16)
    low = (rest - mid.astype(f32)).astype(bf16)
    return hi, mid, low


def split2(a):
    hi = a.astype(bf16)
    return hi, (a - hi.astype(f32)).astype(bf16)


def iota(shape, axis):
    return lax.broadcasted_iota(jnp.int32, shape, axis)


def expand(cols):
    rows = cols.shape[0]
    left = iota((rows, 128), 1) < HEAD
    return jnp.concatenate(
        [jnp.where(left, cols[:, 2 * q : 2 * q + 1], cols[:, 2 * q + 1 : 2 * q + 2]) for q in range(2)],
        axis=1,
    )


def conv_taps(window, kernel):
    out = kernel[4:5] + kernel[3:4] * window[8:]
    for k in range(3):
        out = out + kernel[k : k + 1] * pltpu.roll(window, 3 - k, 0)[8:]
    return out


def head_row(ref):
    return jnp.broadcast_to(ref[...][None, :], (8, ref.shape[0]))


def lay(rows, pick):
    parts = split3(rows)
    return mm(parts[0], pick) + mm(parts[1], pick) + mm(parts[2], pick)


def as_places(heads):
    lane = iota((heads, 128), 1)
    place = lane % 8
    return ((lane // 8 * HB + place == iota((heads, 128), 0)) & (place < HB)).astype(f32).astype(bf16)


def as_units(heads, block):
    return (iota((heads, BW), 1) // HEAD + HB * block == iota((heads, BW), 0)).astype(f32).astype(bf16)


def head_masks():
    lane = iota((1, BW), 1) // HEAD
    return [(lane == j).astype(f32).astype(bf16) for j in range(HB)]


def quads():
    for r in range(0, Q, 64):
        for half in range(2):
            if half * 128 <= r:
                yield r, half, r < half * 128 + 128


def decay_chunk(col, row, r, half, diag):
    gap = col[r : r + 64] - row[:, half * 128 : half * 128 + 128]
    if diag:
        keep = iota((64, 128), 0) + (r - half * 128) >= iota((64, 128), 1)
        gap = jnp.where(keep, gap, FAR)
    return jnp.exp2(gap)


def mixer_forward(links, normed, wi, wsx, kin, kst, bias, log_rate, skip_in, *refs):
    refs = list(refs)
    if links:
        sent = refs[:3] + refs[13:15]
        refs = refs[3:13] + refs[15:]
    inner_out, ssd_out, states_out, cst_out, bc_out, step_out, cum_out, stepT_out, cumT_out, preT_out = refs[:10]
    buf, gram, colc, cols, rowp, mst, xst, state = refs[10:18]
    i = pl.program_id(0)
    tokens = normed.shape[0]
    spans = tokens // Q
    work = BesideForward(*sent, *refs[18:]) if links else None
    heads = bias.shape[0]
    skip = lay(head_row(skip_in), as_units(heads, i))[0:1]

    if links:
        pl.when(i == 0)(work.start)

    @pl.when(i == 0)
    def _():
        proj = mm(normed[...], wsx[...])
        buf[0:8] = jnp.zeros((8, BW), f32)
        cst_out[...] = proj[:, :BW]
        buf[8 : 8 + tokens] = proj[:, :BW]
        tri = (iota((Q, Q), 0) >= iota((Q, Q), 1)).astype(f32).astype(bf16)
        places = as_places(heads)
        pre = proj[:, BW:] + lay(head_row(bias), places)[0:1]
        step = jnp.maximum(pre, 0.0) + jnp.log1p(jnp.exp(-jnp.abs(pre)))
        step_out[...] = step
        scaled = step * (lay(-jnp.exp(head_row(log_rate)), places)[0:1] * LOG2E)
        for s in range(spans):
            parts = split3(scaled[s * Q : s * Q + Q])
            cum_out[s * Q : s * Q + Q] = mm(tri, parts[0]) + mm(tri, parts[1]) + mm(tri, parts[2])
            conv = conv_taps(buf[s * Q : s * Q + Q + 8], kst[...])
            bc = (conv * sigmoid(conv)).astype(bf16)
            bc_out[s * Q : s * Q + Q] = bc
            gram[s] = mm(bc[:, 128:], bc[:, :128], 1, 1)
        preT_out[...] = jnp.transpose(pre)[:48]
        stepT_out[...] = jnp.transpose(step)[:48]
        cumT_out[...] = jnp.transpose(cum_out[...])[:48]
        mst[...] = jnp.zeros(mst.shape, bf16)

    inner = mm(normed[...], wi[...])
    inner_out[...] = inner
    buf[8 : 8 + tokens] = inner
    turn = lax.rem(128 - 8 * i, 128)
    colc[...] = pltpu.roll(cum_out[...], turn, 1)
    cols[...] = pltpu.roll(step_out[...], turn, 1)
    rows8 = pl.ds(pl.multiple_of(8 * i, 8), 8)
    rowp[...] = cumT_out[rows8] - jnp.log2(stepT_out[rows8])
    state[...] = jnp.zeros(state.shape, f32)
    masks = head_masks()

    def span(s, carry):
        at = pl.multiple_of(s * Q, Q)
        rows = pl.ds(at, Q)
        conv = conv_taps(buf[pl.ds(at, Q + 8)], kin[...])
        xs = conv * sigmoid(conv)
        x_low = xs.astype(bf16)
        col = colc[rows]
        total = col[Q - 1 : Q]
        growth = expand(jnp.exp2(col[:, :8]))
        weight = expand(jnp.exp2(total[:, :8] - col[:, :8]) * cols[rows][:, :8])
        xw_low = (xs * weight).astype(bf16)
        for j in range(HB):
            xst[j * Q : j * Q + Q] = x_low * masks[j]
            row = rowp[j : j + 1, rows]
            for r, half, diag in quads():
                part = gram[s, r : r + 64, half * 128 : half * 128 + 128]
                dec = decay_chunk(col[:, j : j + 1], row, r, half, diag)
                mst[r : r + 64, j * Q + half * 128 : j * Q + half * 128 + 128] = (part * dec).astype(bf16)
        intra = mm(mst[...], xst[...])
        state_in = state[...]
        states_out[s] = state_in
        bc = bc_out[rows]
        readout = mm(bc[:, 128:], state_in.astype(bf16), 1, 1)
        ssd_out[rows] = intra + growth * readout + skip * xs
        local = mm(xw_low, bc[:, :128], 0, 0)
        fade = jnp.exp2(total)
        for j in range(HB):
            at_j = slice(j * HEAD, j * HEAD + HEAD)
            state[at_j] = fade[:, j : j + 1] * state_in[at_j] + local[at_j]
        if links:
            work.step(i * spans + s)
        return carry

    lax.fori_loop(0, spans, span, 0)
    if links:
        pl.when(i == pl.num_programs(0) - 1)(work.finish)


class BesideForward:
    def __init__(self, cot, w_gate_inner, w_output_t, cot_out, wb, ss, rs, ls, xs, xr, xl):
        self.here = Place()
        units = w_output_t.shape[1]
        self.moves = [
            Gather(self.here, own, wb, ss, rs, ls, n, slice(n * units, n * units + units))
            for n, own in enumerate((w_gate_inner.at[0], w_output_t))
        ]
        half = lax.axis_index("tensor")
        rows = cot.shape[0]
        slot = cot_out.at[pl.ds(pl.multiple_of(half * rows, rows), rows)]
        self.across = remote(cot, slot, xs, xr, tensor=1 - half)
        self.local = pltpu.make_async_copy(cot, slot, xl)

    def start(self):
        greet(self.here, True)
        for move in self.moves:
            move.start()
        self.across.start()
        self.local.start()

    def step(self, at):
        for when, chunk, hops in ((7, 0, 1), (11, 1, 1), (15, 0, 2), (19, 1, 2)):

            def go(move=self.moves[chunk], hops=hops):
                move.hop(hops)
                move.sides(hops - 1)

            pl.when(at == when)(go)

    def finish(self):
        for hops in (3, 4):
            for move in self.moves:
                if hops < 4:
                    move.hop(hops)
                move.sides(hops - 1)
        self.local.wait()
        self.across.wait()
        for move in self.moves:
            move.finish()


def gate_forward(links, normed, cot, wg, wo, ssd, gain, gate_out, ggo_out, stats_out, sq, gi, *refs):
    i = pl.program_id(0)

    @pl.when(i == 0)
    def _():
        if links:
            barrier = pltpu.get_barrier_semaphore()
            other = {"tensor": 1 - lax.axis_index("tensor")}
            pl.semaphore_signal(barrier, 1, device_id=other, device_id_type=MESH)
            pl.semaphore_wait(barrier, 1)
        sq[...] = jnp.zeros(sq.shape, f32)
        gi[...] = jnp.zeros(gi.shape, f32)

    gate = mm(normed[...], wg[...])
    gate_out[...] = gate
    ggo = mm(cot[...], wo[...])
    ggo_out[...] = ggo
    gated = ssd[...] * (gate * sigmoid(gate))
    squares = gated * gated
    sq[...] += squares[:, :128] + squares[:, 128:]
    inner = ggo * gain[0:1] * gated
    gi[...] += inner[:, :128] + inner[:, 128:]

    @pl.when(i == pl.num_programs(0) - 1)
    def _():
        lane = iota(sq.shape, 1)
        both = jnp.where(
            lane == 0,
            jnp.sum(sq[...], axis=1, keepdims=True),
            jnp.where(lane == 1, jnp.sum(gi[...], axis=1, keepdims=True), 0.0),
        )
        if not links:
            stats_out[...] = jnp.transpose(both)[:8]
            return
        mine, landed, send, recv = refs
        mine[...] = jnp.transpose(both)[:8]
        swap = remote(mine, landed, send, recv, tensor=1 - lax.axis_index("tensor"))
        swap.start()
        swap.wait()
        stats_out[...] = mine[...] + landed[...]


def gate_backward(
    unit_total, stats, gate, ssd, ggo, gain, normed, cot, dy_out, dgate_out, ng_out, gg_out, grads_out, normed_t, cols, cot_t
):
    @pl.when(pl.program_id(0) == 0)
    def _():
        full = jnp.concatenate([stats[...], jnp.zeros((120, stats.shape[1]), f32)], axis=0)
        cols[...] = jnp.transpose(full)

        def turn(n, carry):
            here = pl.ds(pl.multiple_of(n * 128, 128), 128)
            normed_t[here] = jnp.transpose(normed[:, here])
            cot_t[here] = jnp.transpose(cot[:, here])
            return carry

        lax.fori_loop(0, normed.shape[1] // 128, turn, 0)

    rstd = lax.rsqrt(cols[:, 0:1] / unit_total + norm_eps)
    pull = rstd * rstd * rstd * (cols[:, 1:2] / unit_total)
    v = gate[...]
    sig = sigmoid(v)
    act = v * sig
    y = ssd[...]
    gated = y * act
    scaled = gated * rstd
    ng = (scaled * gain[0:1]).astype(bf16)
    ng_out[...] = ng
    grads_out[1] = mm(cot_t[...], ng).astype(bf16)
    gg = ggo[...]
    gg_out[...] = jnp.broadcast_to(jnp.sum(gg * scaled, axis=0, keepdims=True), gg_out.shape)
    grad = rstd * (gg * gain[0:1]) - gated * pull
    dy_out[...] = (grad * act).astype(bf16)
    dgate = (grad * y * (sig * (1.0 + v * (1.0 - sig)))).astype(bf16)
    dgate_out[...] = dgate
    grads_out[0] = mm(normed_t[...], dgate).astype(bf16)


class BesideBackward:
    def __init__(self, mixed, grads, far_out, shard_out, scratch):
        self.here = Place()
        half = lax.axis_index("tensor")
        rows = far_out.shape[0]
        other = mixed.at[pl.ds(pl.multiple_of((1 - half) * rows, rows), rows)]
        self.across = remote(other, far_out, scratch[0], scratch[1], tensor=1 - half)
        self.sum = Reduce(self.here, grads, shard_out, scratch[2:7], scratch[7:15])

    def start(self):
        greet(self.here, True)
        self.sum.start()
        self.across.start()

    def step(self, at):
        total = self.sum
        z = self.here.z
        ends = (z == 0) | (z == 3)
        for n, block in enumerate(total.order):
            pl.when(at == n)(lambda z=block: total.cores(z))
            pl.when(at == (4, 6, 7, 8)[n])(lambda z=block: total.stay(z))
            pl.when(at == (5, 10, 15, 19)[n])(lambda z=block: total.sides(z))
        for n, block in enumerate(total.order[:3]):
            when = jnp.where(ends, (5, 10, 15)[n], (11, 16, 17)[n])
            pl.when(at == when)(lambda z=block: total.pass_on(z))

    def finish(self):
        self.sum.finish()
        self.across.wait()


def mixer_backward(links, inner, dy, states, kin, kst, log_rate, skip_in, cst, bc_in, step_in, cum_in, stepT, cumT, preT, *refs):
    refs = list(refs)
    if links:
        beside = refs[:2] + refs[7:9]
        refs = refs[2:7] + refs[9:]
        work = BesideBackward(*beside, refs[24:])
    dinner_out, gk_out, dsd_out, gks_out, hs_out = refs[:5]
    buf, dbuf, gram, gg, gb, gc, colc, cols, rowp, mst, dyst, gmix, sgrad = refs[5:18]
    rs_t, cs_t, dr_t, wg_t, gt_t, gtaps = refs[18:24]
    i = pl.program_id(0)
    if links:
        pl.when(i == 0)(work.start)
    heads = log_rate.shape[0]
    skip = lay(head_row(skip_in), as_units(heads, i))[0:1]
    tokens = inner.shape[0]
    spans = tokens // Q
    masks = head_masks()

    @pl.when(i == 0)
    def _():
        buf[0:8] = jnp.zeros((8, BW), f32)
        dbuf[tokens : tokens + 8] = jnp.zeros((8, BW), f32)
        for s in range(spans):
            bc = bc_in[s * Q : s * Q + Q]
            gram[s] = mm(bc[:, 128:], bc[:, :128], 1, 1)
        for ref in (gg, gb, gc, rs_t, cs_t, dr_t, wg_t, gt_t):
            ref[...] = jnp.zeros(ref.shape, f32)
        mst[...] = jnp.zeros(mst.shape, bf16)

    buf[8 : 8 + tokens] = inner[...]
    turn = lax.rem(128 - 8 * i, 128)
    colc[...] = pltpu.roll(cum_in[...], turn, 1)
    cols[...] = pltpu.roll(step_in[...], turn, 1)
    rows8 = pl.ds(pl.multiple_of(8 * i, 8), 8)
    rowp[...] = cumT[rows8] - jnp.log2(stepT[rows8])
    sgrad[...] = jnp.zeros(sgrad.shape, f32)
    gtaps[...] = jnp.zeros(gtaps.shape, f32)
    pick = (iota((8, BW), 1) // HEAD == iota((8, BW), 0)).astype(f32).astype(bf16)

    def conv_rows(at, kernel, grad_act, conv, sig):
        gco = grad_act * (sig * (1.0 + conv * (1.0 - sig)))
        dbuf[pl.ds(at, Q)] = gco
        into = buf[pl.ds(pl.multiple_of(at + 8, 8), Q)]
        gtaps[4:5] += jnp.sum(gco, axis=0, keepdims=True)
        after = dbuf[pl.ds(at, Q + 8)]
        grad_in = kernel[3:4] * gco
        gtaps[3:4] += jnp.sum(gco * into, axis=0, keepdims=True)
        for k in range(3):
            later = pltpu.roll(after, Q + 8 - (3 - k), 0)[:Q]
            gtaps[k : k + 1] += jnp.sum(later * into, axis=0, keepdims=True)
            grad_in = grad_in + kernel[k : k + 1] * later
        return grad_in

    def span(back, carry):
        s = spans - 1 - back
        at = pl.multiple_of(s * Q, Q)
        rows = pl.ds(at, Q)
        conv = conv_taps(buf[pl.ds(at, Q + 8)], kin[...])
        sig = sigmoid(conv)
        xs = conv * sig
        x_low = xs.astype(bf16)
        dy_s = dy[rows]
        dy_f = dy_s.astype(f32)
        bc = bc_in[rows]
        b_low, c_low = bc[:, :128], bc[:, 128:]
        col = colc[rows]
        total = col[Q - 1 : Q]
        for j in range(HB):
            dyst[j * Q : j * Q + Q] = dy_s * masks[j]
        gmix[...] = mm(dyst[...], x_low, 1, 1)
        lane = iota((Q, 128), 1)
        row_sums = jnp.zeros((Q, 128), f32)
        for j in range(HB):
            row = rowp[j : j + 1, rows]
            col_sum = [jnp.zeros((1, 128), f32), jnp.zeros((1, 128), f32)]
            row_parts = []
            for r, half, diag in quads():
                here = slice(half * 128, half * 128 + 128)
                dec = decay_chunk(col[:, j : j + 1], row, r, half, diag)
                part = gram[s, r : r + 64, here]
                p = gmix[j * Q + r : j * Q + r + 64, here] * dec
                gg[s, r : r + 64, here] += p
                q = p * part
                mst[j * Q + r : j * Q + r + 64, here] = (part * dec).astype(bf16)
                col_sum[half] = col_sum[half] + jnp.sum(q, axis=0, keepdims=True)
                if half == 0:
                    row_parts.append(q)
                else:
                    row_parts[-1] = row_parts[-1] + q
            sums = jnp.concatenate([jnp.sum(q, axis=1, keepdims=True) for q in row_parts], axis=0)
            row_sums = jnp.where(lane == j, sums, row_sums)
            cs_t[pl.ds(8 * i + j, 1), rows] = jnp.concatenate(col_sum, axis=1)
        rs_t[rows8, rows] = jnp.transpose(row_sums)[:8]
        grad_xs = mm(mst[...], dyst[...], 0, 0) + skip * dy_f

        growth = expand(jnp.exp2(col[:, :8]))
        weight = expand(jnp.exp2(total[:, :8] - col[:, :8]) * cols[rows][:, :8])
        state_in = states[s]
        state_low = state_in.astype(bf16)
        state_grad = sgrad[...]
        carry_low = state_grad.astype(bf16)
        readout = mm(c_low, state_low, 1, 1)
        read_low = (dy_f * growth).astype(bf16)
        hi, low = split2(dy_f * readout)
        dr_t[rows8, rows] = mm(pick, hi, 1, 1) + mm(pick, low, 1, 1)
        gc[rows] += mm(read_low, state_low)
        grad_xw = mm(b_low, carry_low, 1, 1)
        xw_low = (xs * weight).astype(bf16)
        gb[rows] += mm(xw_low, carry_low)
        hi, low = split2(grad_xw * xs)
        wg_t[rows8, rows] = mm(pick, hi, 1, 1) + mm(pick, low, 1, 1)
        hi, low = split2(state_grad * state_in)
        sums = jnp.sum(mm(pick, hi) + mm(pick, low), axis=1, keepdims=True)
        gt_t[rows8] = jnp.where(iota((8, 128), 1) == s, sums, gt_t[rows8])
        grad_xs = grad_xs + grad_xw * weight
        local = mm(read_low, c_low, 0, 0)
        fade = jnp.exp2(total)
        for j in range(HB):
            at_j = slice(j * HEAD, j * HEAD + HEAD)
            sgrad[at_j] = fade[:, j : j + 1] * state_grad[at_j] + local[at_j]
        gtaps[5:6] += jnp.sum(dy_f * xs, axis=0, keepdims=True)
        dinner_out[rows] = conv_rows(at, kin[...], grad_xs, conv, sig).astype(bf16)
        if links:
            work.step(i * spans + back)
        return carry

    lax.fori_loop(0, spans, span, 0)
    gk_out[...] = gtaps[...]

    @pl.when(i == pl.num_programs(0) - 1)
    def _():
        buf[8 : 8 + tokens] = cst[...]
        gtaps[...] = jnp.zeros(gtaps.shape, f32)
        rates = lay(-jnp.exp(head_row(log_rate)), as_places(heads))[0:1]
        rate = jnp.transpose(jnp.broadcast_to(rates, (128, 128)))[:48, 0:1]
        later = (iota((Q, Q), 0) >= iota((Q, Q), 1)).astype(f32).astype(bf16)
        last = iota((48, Q), 1) == Q - 1
        bias_sum = jnp.zeros((48, 1), f32)
        decay_sum = jnp.zeros((48, 1), f32)
        for back in range(spans):
            s = spans - 1 - back
            rows = slice(s * Q, s * Q + Q)
            bc = bc_in[rows]
            gl = gg[s].astype(bf16)
            grad_c = gc[rows] + mm(gl, bc[:, :128])
            grad_b = gb[rows] + mm(gl, bc[:, 128:], 0, 0)
            both = jnp.concatenate([grad_b, grad_c], axis=1)
            conv = conv_taps(buf[s * Q : s * Q + Q + 8], kst[...])
            dsd_out[rows, :BW] = conv_rows(s * Q, kst[...], both, conv, sigmoid(conv)).astype(bf16)

            cum, step, pre = cumT[:, rows], stepT[:, rows], preT[:, rows]
            total = cum[:, Q - 1 : Q]
            rate_w = jnp.exp2(total - cum)
            wg = wg_t[:, rows]
            cs = cs_t[:, rows]
            moved = wg * (rate_w * step)
            grad_cum = rs_t[:, rows] - cs + jnp.exp2(cum) * dr_t[:, rows] - moved
            grad_total = jnp.exp2(total) * gt_t[:, s : s + 1] + jnp.sum(moved, axis=1, keepdims=True)
            grad_cum = grad_cum + jnp.where(last, grad_total, 0.0)
            parts = split3(grad_cum)
            grad_rate = mm(parts[0], later) + mm(parts[1], later) + mm(parts[2], later)
            sig = sigmoid(pre)
            ratio = jnp.where(pre < -15.0, 1.0, sig / step)
            grad_pre = (wg * rate_w + grad_rate * rate) * sig + cs * ratio
            bias_sum = bias_sum + jnp.sum(grad_pre, axis=1, keepdims=True)
            decay_sum = decay_sum + jnp.sum(grad_rate * step, axis=1, keepdims=True)
            full = jnp.concatenate([grad_pre, jnp.zeros((80, Q), f32)], axis=0)
            dsd_out[rows, BW:] = jnp.transpose(full).astype(bf16)
        gks_out[...] = gtaps[...]
        lane = iota((48, 128), 1)
        both = jnp.where(lane == 0, bias_sum, jnp.where(lane == 1, decay_sum * rate, 0.0))
        hs_out[...] = jnp.transpose(jnp.concatenate([both, jnp.zeros((80, 128), f32)], axis=0))[:8]
        if links:
            work.finish()


class Place:
    def __init__(self):
        me = lax.axis_index("dp")
        self.me = me
        self.c, self.y, self.z = me % 2, (me // 2) % 2, me // 4

    def at(self, z, y, c):
        return (z * 2 + y) * 2 + c

    def core(self):
        return self.at(self.z, self.y, 1 - self.c)

    def side(self):
        return self.at(self.z, 1 - self.y, self.c)

    def up(self):
        return self.me + 4

    def down(self):
        return self.me - 4


def greet(here, across):
    barrier = pltpu.get_barrier_semaphore()

    def signal(**device):
        pl.semaphore_signal(barrier, 1, device_id=device, device_id_type=MESH)

    signal(dp=here.core())
    signal(dp=here.side())
    pl.when(here.z < 3)(lambda: signal(dp=here.up()))
    pl.when(here.z > 0)(lambda: signal(dp=here.down()))
    if across:
        signal(tensor=1 - lax.axis_index("tensor"))
    ends = (here.z == 0).astype(jnp.int32) + (here.z == 3).astype(jnp.int32)
    pl.semaphore_wait(barrier, 4 + int(across) - ends)


def remote(src, dst, send_sem, recv_sem, **device):
    return pltpu.make_async_remote_copy(
        src_ref=src, dst_ref=dst, send_sem=send_sem, recv_sem=recv_sem, device_id=device, device_id_type=MESH
    )


class Gather:
    def __init__(self, here, own, full, ss, rs, ls, chunk, cols):
        self.here, self.full, self.ss, self.rs, self.chunk, self.cols = here, full, ss, rs, chunk, cols
        self.rows = own.shape[0]
        self.own = own
        self.local = pltpu.make_async_copy(own, self.slot(here.me), ls.at[chunk])

    def slot(self, origin):
        return self.full.at[pl.ds(pl.multiple_of(origin * self.rows, self.rows), self.rows), self.cols]

    def copy(self, origin, way, src=None):
        here = self.here
        target = (here.up, here.down, here.side, here.core)[way]()
        slot = self.slot(origin)
        sems = self.ss.at[self.chunk, origin, way], self.rs.at[self.chunk, origin]
        return remote(slot if src is None else src, slot, *sems, dp=target)

    def arrived(self, origin):
        self.copy(origin, 3).wait_recv()

    def each_send(self, act):
        here = self.here
        for hops in range(4):
            for way, origin_z in ((0, here.z - hops), (1, here.z + hops)):
                if hops == 0:
                    if way == 1:
                        continue
                    origin = here.me
                    pl.when(here.z < 3)(lambda o=origin: act(o, 0))
                    pl.when(here.z > 0)(lambda o=origin: act(o, 1))
                    act(origin, 2)
                    act(origin, 3)
                    continue
                origin = here.at(origin_z, here.y, here.c)

                def go(o=origin, way=way):
                    pl.when((here.z < 3) if way == 0 else (here.z > 0))(lambda: act(o, way))
                    act(o, 2)
                    act(o, 3)

                pl.when((origin_z >= 0) & (origin_z <= 3))(go)

    def start(self):
        here = self.here
        pl.when(here.z < 3)(lambda: self.copy(here.me, 0, self.own).start())
        pl.when(here.z > 0)(lambda: self.copy(here.me, 1, self.own).start())
        self.copy(here.me, 2, self.own).start()
        self.copy(here.me, 3, self.own).start()
        self.local.start()

    def hop(self, hops):
        here = self.here
        for way, origin_z in ((0, here.z - hops), (1, here.z + hops)):

            def go(way=way, origin_z=origin_z):
                origin = here.at(origin_z, here.y, here.c)
                self.arrived(origin)
                pl.when((here.z < 3) if way == 0 else (here.z > 0))(lambda: self.copy(origin, way).start())
                self.copy(origin, 2).start()
                self.copy(origin, 3).start()

            pl.when((origin_z >= 0) & (origin_z <= 3))(go)

    def sides(self, hops):
        here = self.here
        for way, origin_z in ((0, here.z - hops), (1, here.z + hops)):
            if hops == 0 and way == 1:
                continue

            def go(origin_z=origin_z):
                origin = here.at(origin_z, 1 - here.y, here.c)
                self.arrived(origin)
                self.copy(origin, 3).start()

            pl.when((origin_z >= 0) & (origin_z <= 3))(go)

    def finish(self):
        here = self.here
        self.local.wait()
        for z in range(4):
            for y in range(2):
                self.arrived(here.at(z, y, 1 - here.c))
        self.each_send(lambda origin, way: self.copy(origin, way).wait_send())
        for z in range(4):
            self.copy(here.at(z, 1 - here.y, here.c), 3).wait_send()


def gather_scratch():
    sem = pltpu.SemaphoreType.DMA
    return [sem((2, 16, 4)), sem((2, 16)), sem((2,))]


def gather_kernel(tokens_in, gain, w_gate_inner, w_state_io, w_step, tokens_out, full, pack, low, ss, rs, ls, xs, xr, xl):
    here = Place()
    half = lax.axis_index("tensor")
    rows = tokens_in.shape[0]
    units, cols = w_gate_inner.shape[2], full.shape[1]
    pack[:, :units] = w_gate_inner[1]
    pack[:, units : units + BW] = w_state_io[...]
    pack[:, units + BW :] = mm(w_step[...], as_places(w_step.shape[1])).astype(bf16)
    greet(here, True)
    cut = cols // 256 * 128
    moves = [
        Gather(here, pack.at[:, c], full, ss, rs, ls, n, c) for n, c in enumerate((slice(0, cut), slice(cut, cols)))
    ]
    for move in moves:
        move.start()
    part = rows // 4
    across, local = [], []
    for n in range(4):
        piece = slice(n * part, n * part + part)
        v = tokens_in[piece].astype(f32)
        scale = lax.rsqrt(jnp.mean(v * v, axis=1, keepdims=True) + norm_eps)
        low[piece] = (v * scale * gain[0:1]).astype(bf16)
        slot = tokens_out.at[pl.ds(pl.multiple_of(half * rows + n * part, part), part)]
        across.append(remote(low.at[piece], slot, xs.at[n], xr.at[n], tensor=1 - half))
        across[-1].start()
        local.append(pltpu.make_async_copy(low.at[piece], slot, xl.at[n]))
        local[-1].start()
    for hops in range(1, 5):
        for move in moves:
            if hops < 4:
                move.hop(hops)
            move.sides(hops - 1)
    for n in range(4):
        local[n].wait()
        across[n].wait()
    for move in moves:
        move.finish()


def gather_rows(tokens_in, gain, w_gate_inner, w_state_io, w_step, ways, collective_id):
    rows, width = tokens_in.shape
    _, own, units = w_gate_inner.shape
    cols = units + BW + 128
    vmem = pl.BlockSpec(memory_space=pltpu.VMEM)
    hbm = pl.BlockSpec(memory_space=pl.ANY)
    sem = pltpu.SemaphoreType.DMA
    return pl.pallas_call(
        gather_kernel,
        name="gather_rows",
        in_specs=[vmem] * 5,
        out_specs=[hbm, hbm],
        out_shape=[sds((2 * rows, width), bf16), sds((ways * own, cols), bf16)],
        scratch_shapes=[
            pltpu.VMEM((own, cols), bf16), pltpu.VMEM((rows, width), bf16), *gather_scratch(),
            sem((4,)), sem((4,)), sem((4,)),
        ],
        compiler_params=pltpu.CompilerParams(
            collective_id=collective_id, has_side_effects=True, vmem_limit_bytes=60 * 1024 * 1024
        ),
    )(tokens_in, gain, w_gate_inner, w_state_io, w_step)


class Reduce:
    def __init__(self, here, grads, out, bufs, sems):
        self.here, self.grads, self.out = here, grads, out
        self.held, self.buf_a, self.buf_b, self.buf_up, self.buf_dn = bufs
        self.local, self.send_a, self.recv_a, self.send_b, self.recv_b, self.send_c, self.recv_up, self.recv_dn = sems
        self.parts, self.rows = out.shape[:2]
        z = here.z
        self.order = (3 * (1 - z // 2), (3 * z + 2) % 5, 1 + z % 2, z)

    def spot(self, z, y, c):
        if self.grads is None:
            return z, (y * 2 + c) * self.rows
        return z * 2 + y, 0

    def own(self, z, y, c=None):
        at, base = self.spot(z, y, self.here.c if c is None else c)
        return self.held.at[at, :, pl.ds(pl.multiple_of(base, 16), self.rows)]

    def block(self, z, y, c):
        if self.grads is None:
            return self.own(z, y, c)
        at = pl.multiple_of(self.here.at(z, y, c) * self.rows, self.rows)
        return self.grads.at[:, pl.ds(at, self.rows)]

    def copy_a(self, z, y):
        here, at = self.here, z * 2 + y
        return remote(self.block(z, y, 1 - here.c), self.buf_a.at[at], self.send_a.at[at], self.recv_a.at[at], dp=here.core())

    def take(self, z, y):
        return pltpu.make_async_copy(self.block(z, y, self.here.c), self.own(z, y), self.local.at[z * 2 + y])

    def copy_b(self, z):
        here = self.here
        return remote(self.own(z, 1 - here.y), self.buf_b.at[z], self.send_b.at[z], self.recv_b.at[z], dp=here.side())

    def copy_up(self, z):
        return remote(self.own(z, self.here.y), self.buf_up.at[z], self.send_c.at[z], self.recv_up.at[z], dp=self.here.up())

    def copy_dn(self, z):
        return remote(self.own(z, self.here.y), self.buf_dn.at[z], self.send_c.at[z], self.recv_dn.at[z], dp=self.here.down())

    def add(self, z, y, buf, slot):
        at, base = self.spot(z, y, self.here.c)

        def rows(n, carry):
            piece = pl.ds(pl.multiple_of(n * 16, 16), 16)
            held = pl.ds(pl.multiple_of(base + n * 16, 16), 16)
            for part in range(self.parts):
                total = self.held[at, part, held].astype(f32) + buf[slot, part, piece].astype(f32)
                self.held[at, part, held] = total.astype(bf16)
            return carry

        lax.fori_loop(0, self.rows // 16, rows, 0)

    def start(self):
        here = self.here
        for side in (1 - here.y, here.y):
            for z in self.order:
                self.copy_a(z, side).start()
                self.take(z, side).start()

    def join(self, z, y):
        if self.grads is not None:
            self.take(z, y).wait()
        self.copy_a(z, y).wait_recv()
        self.add(z, y, self.buf_a, z * 2 + y)

    def cores(self, z):
        self.join(z, 1 - self.here.y)
        self.copy_b(z).start()

    def stay(self, z):
        self.join(z, self.here.y)

    def sides(self, z):
        self.copy_b(z).wait_recv()
        self.add(z, self.here.y, self.buf_b, z)

    def pass_on(self, z):
        here = self.here

        def up():
            def below():
                self.copy_up(z).wait_recv()
                self.add(z, here.y, self.buf_up, z)

            pl.when(here.z > 0)(below)
            self.copy_up(z).start()

        def down():
            def above():
                self.copy_dn(z).wait_recv()
                self.add(z, here.y, self.buf_dn, z)

            pl.when(here.z < 3)(above)
            self.copy_dn(z).start()

        pl.when(z > here.z)(up)
        pl.when(z < here.z)(down)

    def finish(self):
        here = self.here
        z = here.z
        at, base = self.spot(z, here.y, here.c)
        pl.when(z > 0)(lambda: self.copy_up(z).wait_recv())
        pl.when(z < 3)(lambda: self.copy_dn(z).wait_recv())

        def rows(n, carry):
            piece = pl.ds(pl.multiple_of(n * 16, 16), 16)
            held = pl.ds(pl.multiple_of(base + n * 16, 16), 16)
            for part in range(self.parts):
                below = jnp.where(z > 0, self.buf_up[z, part, piece].astype(f32), 0.0)
                above = jnp.where(z < 3, self.buf_dn[z, part, piece].astype(f32), 0.0)
                self.out[part, piece] = self.held[at, part, held].astype(f32) + below + above
            return carry

        lax.fori_loop(0, self.rows // 16, rows, 0)
        for zn in self.order:
            self.copy_a(zn, 0).wait_send()
            self.copy_a(zn, 1).wait_send()
            self.copy_b(zn).wait_send()
            pl.when(zn > z)(lambda zn=zn: self.copy_up(zn).wait_send())
            pl.when(zn < z)(lambda zn=zn: self.copy_dn(zn).wait_send())


def reduce_scratch(parts, rows, cols, by_z=False):
    sem = pltpu.SemaphoreType.DMA
    block = (parts, rows, cols)
    held = (4, parts, 4 * rows, cols) if by_z else (8,) + block
    return [
        pltpu.VMEM(held, bf16), pltpu.VMEM((8,) + block, bf16), pltpu.VMEM((4,) + block, bf16),
        pltpu.VMEM((4,) + block, bf16), pltpu.VMEM((4,) + block, bf16),
        sem((8,)), sem((8,)), sem((8,)), sem((4,)), sem((4,)), sem((4,)), sem((4,)), sem((4,)),
    ]


def tail_kernel(
    normed_t, dinner, dsd, dgate, wb, wa, gk, ggg, gks, hs, gn_out, shard_out, small_out,
    nt_v, dinner_v, dsd_v, dgate_v, wg_v, wa_v, away, came, total, landed, loads, send_x, recv_x, send, recv, *scratch,
):
    here = Place()
    half = lax.axis_index("tensor")
    units = dgate.shape[1]
    sources = (normed_t, dinner, dsd, dgate, wb.at[:, :units], wa)
    pending = [
        pltpu.make_async_copy(src, dst, loads.at[n])
        for n, (src, dst) in enumerate(zip(sources, (nt_v, dinner_v, dsd_v, dgate_v, wg_v, wa_v)))
    ]
    for copy in pending:
        copy.start()
    far = pltpu.get_barrier_semaphore()
    partners = [here.me + bit - 2 * bit * ((here.me // bit) % 2) for bit in (2, 4, 8, 1)]
    for partner in partners:
        pl.semaphore_signal(far, 1, device_id={"dp": partner}, device_id_type=MESH)
    pl.semaphore_signal(far, 1, device_id={"tensor": 1 - half}, device_id_type=MESH)
    middle = (here.z == 1) | (here.z == 2)
    pl.when(here.z == 1)(lambda: pl.semaphore_signal(far, 1, device_id={"dp": here.up()}, device_id_type=MESH))
    pl.when(here.z == 2)(lambda: pl.semaphore_signal(far, 1, device_id={"dp": here.down()}, device_id_type=MESH))
    pl.semaphore_wait(far, 5 + middle.astype(jnp.int32))
    work = Reduce(here, None, shard_out, scratch[:5], scratch[5:])
    order = work.order
    rows = gn_out.shape[0]
    chunks, _, wide = away.shape

    def swap(k):
        return remote(total.at[k], landed.at[k], send.at[k], recv.at[k], dp=partners[k])

    def swapped(k):
        swap(k).wait()
        total[k + 1] = total[k] + landed[k]
        if k < 3:
            swap(k + 1).start()

    def across(n):
        return remote(away.at[n], came.at[n], send_x.at[n], recv_x.at[n], tensor=1 - half)

    def pulled(which, n):
        mine = pl.ds(pl.multiple_of(which * rows, rows), rows)
        at = pl.ds(pl.multiple_of(n * wide, wide), wide)
        return (
            mm(dgate_v[mine], wg_v[at], 1, 1)
            + mm(dinner_v[mine], wa_v[at, :units], 1, 1)
            + mm(dsd_v[mine], wa_v[at, units:], 1, 1)
        )

    def far_chunk(n, carry):
        away[n] = pulled(1 - half, n).astype(bf16)
        across(n).start()
        return carry

    def near_chunk(n, carry):
        gn_out[:, pl.ds(pl.multiple_of(n * wide, wide), wide)] = pulled(half, n)
        return carry

    def grads(n, carry):
        z = jnp.where(n == 0, order[0], jnp.where(n == 1, order[1], jnp.where(n == 2, order[2], order[3])))
        count = 4 * work.rows
        left = nt_v[pl.ds(pl.multiple_of(z * count, count), count)]
        work.held[z, 0, :, :units] = mm(left, dinner_v[...]).astype(bf16)
        work.held[z, 0, :, units:] = mm(left, dsd_v[...]).astype(bf16)
        work.copy_a(z, 1 - here.y).start()
        work.copy_a(z, here.y).start()

        @pl.when(n == 0)
        def _():
            for copy in pending[3:]:
                copy.wait()

        far_chunk(n, carry)
        work.cores(z)
        return carry

    total[0, 0:6] = gk[0:6]
    total[0, 6:7] = ggg[0:1]
    for k in range(5):
        total[0, 7:8, k * BW : k * BW + BW] = gks[k : k + 1]
    for k in range(2):
        total[0, 7:8, 5 * BW + k * 128 : 5 * BW + k * 128 + 128] = hs[k : k + 1]
    swap(0).start()
    for copy in pending[:3]:
        copy.wait()
    swapped(0)
    lax.fori_loop(0, 4, grads, 0)
    swapped(1)
    work.stay(order[0])
    work.sides(order[0])
    pl.when(~middle)(lambda: work.pass_on(order[0]))
    lax.fori_loop(4, chunks, far_chunk, 0)
    swapped(2)
    for n in range(1, 4):
        work.stay(order[n])
    work.sides(order[1])
    pl.when(~middle)(lambda: work.pass_on(order[1]))
    lax.fori_loop(0, 3, near_chunk, 0)
    pl.when(middle)(lambda: work.pass_on(order[0]))
    work.sides(order[2])
    pl.when(~middle)(lambda: work.pass_on(order[2]))
    lax.fori_loop(3, chunks, near_chunk, 0)
    swapped(3)
    small_out[...] = total[4]
    pl.when(middle)(lambda: work.pass_on(order[1]))
    work.sides(order[3])
    pl.when(middle)(lambda: work.pass_on(order[2]))
    work.finish()

    def arrive(n, carry):
        across(n).wait()
        at = pl.ds(pl.multiple_of(n * wide, wide), wide)
        gn_out[:, at] = gn_out[:, at] + came[n].astype(f32)
        return carry

    lax.fori_loop(0, chunks, arrive, 0)


def reduce_tail(normed_t, dinner, dsd, dgate, wb, wa, sums, ways, collective_id):
    width, tokens = normed_t.shape
    small = sums[0]
    units, cols, rows = dgate.shape[1], wa.shape[1], width // ways
    chunks = width // BW
    vmem = pl.BlockSpec(memory_space=pltpu.VMEM)
    hbm = pl.BlockSpec(memory_space=pl.ANY)
    sem = pltpu.SemaphoreType.DMA
    return pl.pallas_call(
        tail_kernel, name="tail", in_specs=[hbm] * 6 + [vmem] * 4, out_specs=[vmem] * 3,
        out_shape=[sds((tokens // 2, width)), sds((1, rows, cols)), sds(small.shape)],
        scratch_shapes=[
            pltpu.VMEM(normed_t.shape, bf16), pltpu.VMEM(dinner.shape, bf16), pltpu.VMEM(dsd.shape, bf16),
            pltpu.VMEM(dgate.shape, bf16), pltpu.VMEM((width, units), bf16), pltpu.VMEM(wa.shape, bf16),
            pltpu.VMEM((chunks, tokens // 2, BW), bf16), pltpu.VMEM((chunks, tokens // 2, BW), bf16),
            pltpu.VMEM((5,) + small.shape, f32), pltpu.VMEM((4,) + small.shape, f32),
            sem((6,)), sem((chunks,)), sem((chunks,)), sem((4,)), sem((4,)),
        ] + reduce_scratch(1, rows, cols, True),
        compiler_params=pltpu.CompilerParams(
            collective_id=collective_id, has_side_effects=True, vmem_limit_bytes=62 * 1024 * 1024
        ),
    )(normed_t, dinner, dsd, dgate, wb, wa, *sums)


def swap(v):
    return lax.ppermute(v, "tensor", [(0, 1), (1, 0)])


def halves(v, axis):
    size = v.shape[axis] // 2
    me = lax.axis_index("tensor")
    return (
        lax.dynamic_slice_in_dim(v, me * size, size, axis),
        lax.dynamic_slice_in_dim(v, (1 - me) * size, size, axis),
    )


def once(shape, at=None):
    where = at or (0,) * len(shape)
    return pl.BlockSpec(shape, lambda i: where, pipeline_mode=pl.Buffered(1))


def by_cols(rows, offset=0):
    return pl.BlockSpec((rows, BW), lambda i: (0, i + offset))


def params(collective_id=None):
    return pltpu.CompilerParams(
        dimension_semantics=("arbitrary",), vmem_limit_bytes=60 * 1024 * 1024,
        collective_id=collective_id, has_side_effects=collective_id is not None,
    )


def spread(v):
    lead = v.shape[:-1]
    v = v.reshape(lead + (v.shape[-1] // HB, HB))
    v = jnp.pad(v, [(0, 0)] * len(lead) + [(0, 0), (0, 8 - HB)]).reshape(lead + (-1,))
    return jnp.pad(v, [(0, 0)] * len(lead) + [(0, 128 - v.shape[-1])])


def gathered_heads(v, heads):
    return v[..., : heads * 2].reshape(v.shape[:-1] + (heads // HB, 8))[..., :HB].reshape(v.shape[:-1] + (heads,))


def sds(shape, dtype=f32):
    return jax.ShapeDtypeStruct(shape, dtype)


def on_device(
    residual, norm_gain, w_gate_inner, w_state_io, w_step, conv_inner, conv_state,
    step_bias, decay_log, skip_gain, gate_gain, w_output, cotangent,
):
    width = residual.shape[1]
    units = w_gate_inner.shape[2]
    heads = w_step.shape[1]
    blocks = units // BW
    unit_total = units * lax.axis_size("tensor")
    ways = lax.axis_size("dp")
    own_links = ways == 16
    rows_in = residual.astype(f32)
    rstd_in = lax.rsqrt(jnp.mean(rows_in * rows_in, axis=1, keepdims=True) + norm_eps)
    scaled = rows_in * rstd_in
    pack_a = jnp.concatenate([w_gate_inner[1], w_state_io, spread(w_step)], axis=1)
    w_output_t = w_output.T
    if own_links:
        normed, wa = gather_rows(
            residual, jnp.broadcast_to(norm_gain[None], (8, width)), w_gate_inner, w_state_io, w_step, ways, 1
        )
    else:
        wa = lax.all_gather(pack_a, "dp", axis=0, tiled=True)
        normed = lax.all_gather((scaled * norm_gain).astype(bf16), "tensor", axis=0, tiled=True)
    tokens = normed.shape[0]
    spans = tokens // Q
    gain8 = jnp.broadcast_to(gate_gain[None], (8, units))

    hbm = pl.BlockSpec(memory_space=pl.ANY)
    sem = pltpu.SemaphoreType.DMA
    inner, ssd, states, cst, bc, step, cum, step_t, cum_t, pre_t, *sent = pl.pallas_call(
        functools.partial(mixer_forward, own_links),
        name="mixer_forward",
        grid=(blocks,),
        in_specs=[
            once((tokens, width)), by_cols(width), once((width, 384), (0, units // 384)),
            by_cols(5), once((5, BW)), once((heads,)), once((heads,)), once((heads,)),
        ] + [once(v.shape) for v in (cotangent, w_gate_inner, w_output_t)] * own_links,
        out_specs=[
            by_cols(tokens), by_cols(tokens), pl.BlockSpec((spans, BW, 128), lambda i: (0, i, 0)),
            once((tokens, BW)), once((tokens, BW)), once((tokens, 128)), once((tokens, 128)),
            once((48, tokens)), once((48, tokens)), once((48, tokens)),
        ] + [hbm, hbm] * own_links,
        out_shape=[
            sds((tokens, units)), sds((tokens, units)), sds((spans, units, 128)),
            sds((tokens, BW)), sds((tokens, BW), bf16), sds((tokens, 128)), sds((tokens, 128)),
            sds((48, tokens)), sds((48, tokens)), sds((48, tokens)),
        ] + [sds((tokens, width), bf16), sds((width, 2 * units), bf16)] * own_links,
        scratch_shapes=[
            pltpu.VMEM((tokens + 8, BW), f32), pltpu.VMEM((spans, Q, Q), f32),
            pltpu.VMEM((tokens, 128), f32), pltpu.VMEM((tokens, 128), f32), pltpu.VMEM((8, tokens), f32),
            pltpu.VMEM((Q, HB * Q), bf16), pltpu.VMEM((HB * Q, BW), bf16), pltpu.VMEM((BW, 128), f32),
        ] + (gather_scratch() + [sem, sem, sem]) * own_links,
        compiler_params=params(2 if own_links else None),
        cost_estimate=pl.CostEstimate(flops=2 * tokens * width * (units + 384) + 4 * tokens * 256 * units, bytes_accessed=30_000_000, transcendentals=heads * spans * Q * Q),
    )(
        normed, wa, wa, conv_inner, conv_state, step_bias, decay_log, skip_gain,
        *[cotangent, w_gate_inner, w_output_t] * own_links,
    )

    if own_links:
        cot, wb = sent
    else:
        wb = lax.all_gather(jnp.concatenate([w_gate_inner[0], w_output_t], axis=1), "dp", axis=0, tiled=True)
        cot = lax.all_gather(cotangent, "tensor", axis=0, tiled=True)

    gate, ggo, stats = pl.pallas_call(
        functools.partial(gate_forward, own_links),
        name="gate_forward",
        grid=(blocks,),
        in_specs=[
            once((tokens, width)), once((tokens, width)), by_cols(width), by_cols(width, blocks),
            by_cols(tokens), by_cols(8),
        ],
        out_specs=[by_cols(tokens), by_cols(tokens), once((8, tokens))],
        out_shape=[sds((tokens, units)), sds((tokens, units)), sds((8, tokens))],
        scratch_shapes=[pltpu.VMEM((tokens, 128), f32), pltpu.VMEM((tokens, 128), f32)]
        + [pltpu.VMEM((8, tokens), f32), pltpu.VMEM((8, tokens), f32), sem, sem] * own_links,
        compiler_params=params(3 if own_links else None),
        cost_estimate=pl.CostEstimate(flops=4 * tokens * width * units, bytes_accessed=35_000_000, transcendentals=tokens * units),
    )(normed, cot, wb, wb, ssd, gain8)
    if not own_links:
        stats = stats + swap(stats)

    dy, dgate, ng, ggg, grad_b, normed_t = pl.pallas_call(
        functools.partial(gate_backward, float(unit_total)),
        name="gate_backward",
        grid=(blocks,),
        in_specs=[
            once((8, tokens)), by_cols(tokens), by_cols(tokens), by_cols(tokens), by_cols(8),
            once((tokens, width)), once((tokens, width)),
        ],
        out_specs=[
            by_cols(tokens), by_cols(tokens), by_cols(tokens), by_cols(8),
            pl.BlockSpec((2, width, BW), lambda i: (0, 0, i)), once((width, tokens)),
        ],
        out_shape=[
            sds((tokens, units), bf16), sds((tokens, units), bf16), sds((tokens, units), bf16), sds((8, units)),
            sds((2, width, units), bf16), sds((width, tokens), bf16),
        ],
        scratch_shapes=[pltpu.VMEM((tokens, 128), f32), pltpu.VMEM((width, tokens), bf16)],
        compiler_params=params(),
        cost_estimate=pl.CostEstimate(flops=4 * tokens * units * width, bytes_accessed=45_000_000, transcendentals=tokens * units),
    )(stats, gate, ssd, ggo, gain8, normed, cot)

    mixed = mm(ng, wb[:, units:], 1, 1).astype(bf16)
    mixed_near, mixed_far = halves(mixed, 0)

    dinner, gk, dsd, gks, hs, *sent = pl.pallas_call(
        functools.partial(mixer_backward, own_links),
        name="mixer_backward",
        grid=(blocks,),
        in_specs=[
            by_cols(tokens), by_cols(tokens), pl.BlockSpec((spans, BW, 128), lambda i: (0, i, 0)),
            by_cols(5), once((5, BW)), once((heads,)), once((heads,)),
            once((tokens, BW)), once((tokens, BW)), once((tokens, 128)), once((tokens, 128)),
            once((48, tokens)), once((48, tokens)), once((48, tokens)),
        ] + [hbm, hbm] * own_links,
        out_specs=[by_cols(tokens), by_cols(8), once((tokens, 384)), once((8, BW)), once((8, 128))]
        + [hbm, once((2, width // ways, units))] * own_links,
        out_shape=[sds((tokens, units), bf16), sds((8, units)), sds((tokens, 384), bf16), sds((8, BW)), sds((8, 128))]
        + [sds((tokens // 2, width), bf16), sds((2, width // ways, units))] * own_links,
        scratch_shapes=[
            pltpu.VMEM((tokens + 8, BW), f32), pltpu.VMEM((tokens + 8, BW), f32),
            pltpu.VMEM((spans, Q, Q), f32), pltpu.VMEM((spans, Q, Q), f32),
            pltpu.VMEM((tokens, 128), f32), pltpu.VMEM((tokens, 128), f32),
            pltpu.VMEM((tokens, 128), f32), pltpu.VMEM((tokens, 128), f32), pltpu.VMEM((8, tokens), f32),
            pltpu.VMEM((HB * Q, Q), bf16), pltpu.VMEM((HB * Q, BW), bf16), pltpu.VMEM((HB * Q, Q), f32),
            pltpu.VMEM((BW, 128), f32),
            pltpu.VMEM((48, tokens), f32), pltpu.VMEM((48, tokens), f32), pltpu.VMEM((48, tokens), f32),
            pltpu.VMEM((48, tokens), f32), pltpu.VMEM((48, 128), f32), pltpu.VMEM((8, BW), f32),
        ] + ([sem, sem] + reduce_scratch(2, width // ways, units)) * own_links,
        compiler_params=params(4 if own_links else None),
        cost_estimate=pl.CostEstimate(flops=40_000_000_000, bytes_accessed=30_000_000, transcendentals=heads * spans * Q * Q),
    )(
        inner, dy, states, conv_inner, conv_state, decay_log, skip_gain, cst, bc, step, cum, step_t, cum_t, pre_t,
        *[mixed, grad_b] * own_links,
    )
    if own_links:
        mixed_got, wb_shard = sent
    else:
        mixed_got = swap(mixed_far)
        wb_shard = lax.psum_scatter(grad_b, "dp", scatter_dimension=1, tiled=True).astype(f32)
    output = (rows_in + mixed_near.astype(f32) + mixed_got.astype(f32)).astype(bf16)

    if own_links:
        grad_normed, wa_shard, small = reduce_tail(normed_t, dinner, dsd, dgate, wb, wa, (gk, ggg, gks, hs), ways, 5)
        wa_shard = wa_shard[0]
    else:
        last = jnp.concatenate([gks[:5].reshape(-1), hs[0], hs[1]])
        small = jnp.concatenate([gk[:6], ggg[:1], last[None]], axis=0)
        grad_a = jnp.concatenate([mm(normed_t, dinner).astype(bf16), mm(normed_t, dsd).astype(bf16)], axis=1)
        pulled = mm(dgate, wb[:, :units], 1, 1) + mm(dinner, wa[:, :units], 1, 1) + mm(dsd, wa[:, units:], 1, 1)
        near, far = halves(pulled.astype(bf16), 0)
        wa_shard = lax.psum_scatter(grad_a, "dp", scatter_dimension=0, tiled=True).astype(f32)
        small = lax.psum(small, "dp")
        grad_normed = near.astype(f32) + swap(far).astype(f32)
    grad_v = grad_normed * norm_gain
    grad_residual = cotangent.astype(f32) + rstd_in * (
        grad_v - scaled * jnp.mean(grad_v * scaled, axis=1, keepdims=True)
    )

    conv_state_sum = small[7, : 5 * BW].reshape(5, BW)
    bias_sum = gathered_heads(small[7, 5 * BW : 5 * BW + 128], heads)
    decay_sum = gathered_heads(small[7, 5 * BW + 128 : 5 * BW + 256], heads)
    skip_sum = jnp.sum(small[5].reshape(heads, HEAD), axis=1)

    gain_rows = jnp.sum(wb_shard[0] * w_gate_inner[0].astype(f32), axis=1) + jnp.sum(
        wa_shard * pack_a.astype(f32), axis=1
    )
    count = gain_rows.shape[0]
    gain_own = gain_rows / lax.dynamic_slice_in_dim(norm_gain, lax.axis_index("dp") * count, count)
    near_s, far_s = halves(jnp.concatenate([wa_shard[:, units : units + BW], conv_state_sum], axis=0), 1)
    near_g, far_g = halves(gain_own, 0)
    far_all = jnp.concatenate([far_s.reshape(-1), far_g])
    got = swap(far_all)
    both = near_s + got[: far_s.size].reshape(far_s.shape)
    gain_part = near_g + got[far_s.size :]
    return (
        output,
        grad_residual,
        gain_part,
        jnp.stack([wb_shard[0], wa_shard[:, :units]]),
        both[:count],
        gathered_heads(wa_shard[:, units + BW :], heads),
        small[0:5],
        both[count:],
        bias_sum,
        decay_sum,
        skip_sum,
        small[6],
        wb_shard[1].T,
    )


def solution(mesh):
    return jax.shard_map(
        on_device,
        mesh=mesh,
        in_specs=(
            P(("dp", "tensor"), None),
            P(),
            P(None, "dp", "tensor"),
            P("dp", None),
            P("dp", "tensor"),
            P(None, "tensor"),
            P(),
            P("tensor"),
            P("tensor"),
            P("tensor"),
            P("tensor"),
            P("tensor", "dp"),
            P(("dp", "tensor"), None),
        ),
        out_specs=(
            P(("dp", "tensor"), None),
            P(("dp", "tensor"), None),
            P(("dp", "tensor")),
            P(None, "dp", "tensor"),
            P("dp", "tensor"),
            P("dp", "tensor"),
            P(None, "tensor"),
            P(None, "tensor"),
            P("tensor"),
            P("tensor"),
            P("tensor"),
            P("tensor"),
            P("tensor", "dp"),
        ),
        check_vma=False,
    )
```

```python
import functools

import jax
import jax.numpy as jnp
from jax import lax
from jax.experimental import pallas as pl
from jax.experimental.pallas import tpu as pltpu
from jax.sharding import PartitionSpec as P

Q = 256
LEN = 1024
HEAD = 64
BW = 256
HB = BW // HEAD
LOG2E = 1.4426950408889634
FAR = -1e30
norm_eps = 1e-05
MESH = pl.DeviceIdType.MESH
f32 = jnp.float32
bf16 = jnp.bfloat16


def mm(a, b, ca=1, cb=0):
    return lax.dot_general(a, b, (((ca,), (cb,)), ((), ())), preferred_element_type=f32)


def sigmoid(v):
    return 1.0 / (1.0 + jnp.exp(-v))


def split3(a):
    hi = a.astype(bf16)
    rest = a - hi.astype(f32)
    mid = rest.astype(bf16)
    low = (rest - mid.astype(f32)).astype(bf16)
    return hi, mid, low


def split2(a):
    hi = a.astype(bf16)
    return hi, (a - hi.astype(f32)).astype(bf16)


def iota(shape, axis):
    return lax.broadcasted_iota(jnp.int32, shape, axis)


def expand(cols):
    rows = cols.shape[0]
    left = iota((rows, 128), 1) < HEAD
    return jnp.concatenate(
        [jnp.where(left, cols[:, 2 * q : 2 * q + 1], cols[:, 2 * q + 1 : 2 * q + 2]) for q in range(2)],
        axis=1,
    )


def conv_taps(window, kernel):
    out = kernel[4:5] + kernel[3:4] * window[8:]
    for k in range(3):
        out = out + kernel[k : k + 1] * pltpu.roll(window, 3 - k, 0)[8:]
    return out


def head_row(ref):
    return jnp.broadcast_to(ref[...][None, :], (8, ref.shape[0]))


def lay(rows, pick):
    parts = split3(rows)
    return mm(parts[0], pick) + mm(parts[1], pick) + mm(parts[2], pick)


def as_places(heads):
    lane = iota((heads, 128), 1)
    place = lane % 8
    return ((lane // 8 * HB + place == iota((heads, 128), 0)) & (place < HB)).astype(f32).astype(bf16)


def as_units(heads, block):
    return (iota((heads, BW), 1) // HEAD + HB * block == iota((heads, BW), 0)).astype(f32).astype(bf16)


def head_masks():
    lane = iota((1, BW), 1) // HEAD
    return [(lane == j).astype(f32).astype(bf16) for j in range(HB)]


def quads():
    for r in range(0, Q, 64):
        for half in range(2):
            if half * 128 <= r:
                yield r, half, r < half * 128 + 128


def decay_chunk(col, row, r, half, diag):
    gap = col[r : r + 64] - row[:, half * 128 : half * 128 + 128]
    if diag:
        keep = iota((64, 128), 0) + (r - half * 128) >= iota((64, 128), 1)
        gap = jnp.where(keep, gap, FAR)
    return jnp.exp2(gap)


def mixer_forward(links, normed, wi, wsx, kin, kst, bias, log_rate, skip_in, *refs):
    refs = list(refs)
    if links:
        sent = refs[:3] + refs[14:16]
        gain, gate_refs = refs[3], refs[16:19]
        refs = refs[4:14] + refs[19:]
    inner_out, ssd_out, states_out, cst_out, bc_out, step_out, cum_out, stepT_out, cumT_out, preT_out = refs[:10]
    buf, gram, colc, cols, rowp, mst, xst, state = refs[10:18]
    i = pl.program_id(0)
    tokens = normed.shape[0]
    spans = tokens // Q
    blocks = inner_out.shape[1] // BW
    if links:
        work = BesideForward(*sent, *refs[27:])
        ssd_v, *gate_scratch = refs[18:27]
        blocks = ssd_v.shape[0] - 1
    heads = bias.shape[0]
    skip = lay(head_row(skip_in), as_units(heads, i))[0:1]

    if links:
        pl.when(i == 0)(work.start)

    @pl.when(i == 0)
    def _():
        proj = mm(normed[...], wsx[...])
        buf[0:8] = jnp.zeros((8, BW), f32)
        cst_out[...] = proj[:, :BW]
        buf[8 : 8 + tokens] = proj[:, :BW]
        tri = (iota((Q, Q), 0) >= iota((Q, Q), 1)).astype(f32).astype(bf16)
        places = as_places(heads)
        pre = proj[:, BW:] + lay(head_row(bias), places)[0:1]
        step = jnp.maximum(pre, 0.0) + jnp.log1p(jnp.exp(-jnp.abs(pre)))
        step_out[...] = step
        scaled = step * (lay(-jnp.exp(head_row(log_rate)), places)[0:1] * LOG2E)
        for s in range(spans):
            parts = split3(scaled[s * Q : s * Q + Q])
            cum_out[s * Q : s * Q + Q] = mm(tri, parts[0]) + mm(tri, parts[1]) + mm(tri, parts[2])
            conv = conv_taps(buf[s * Q : s * Q + Q + 8], kst[...])
            bc = (conv * sigmoid(conv)).astype(bf16)
            bc_out[s * Q : s * Q + Q] = bc
            gram[s] = mm(bc[:, 128:], bc[:, :128], 1, 1)
        preT_out[...] = jnp.transpose(pre)[:48]
        stepT_out[...] = jnp.transpose(step)[:48]
        cumT_out[...] = jnp.transpose(cum_out[...])[:48]
        mst[...] = jnp.zeros(mst.shape, bf16)

    def mix():
        inner = mm(normed[...], wi[...])
        inner_out[...] = inner
        buf[8 : 8 + tokens] = inner
        turn = lax.rem(128 - 8 * i, 128)
        colc[...] = pltpu.roll(cum_out[...], turn, 1)
        cols[...] = pltpu.roll(step_out[...], turn, 1)
        rows8 = pl.ds(pl.multiple_of(8 * i, 8), 8)
        rowp[...] = cumT_out[rows8] - jnp.log2(stepT_out[rows8])
        state[...] = jnp.zeros(state.shape, f32)
        masks = head_masks()

        def span(s, carry):
            at = pl.multiple_of(s * Q, Q)
            rows = pl.ds(at, Q)
            conv = conv_taps(buf[pl.ds(at, Q + 8)], kin[...])
            xs = conv * sigmoid(conv)
            x_low = xs.astype(bf16)
            col = colc[rows]
            total = col[Q - 1 : Q]
            growth = expand(jnp.exp2(col[:, :8]))
            weight = expand(jnp.exp2(total[:, :8] - col[:, :8]) * cols[rows][:, :8])
            xw_low = (xs * weight).astype(bf16)
            for j in range(HB):
                xst[j * Q : j * Q + Q] = x_low * masks[j]
                row = rowp[j : j + 1, rows]
                for r, half, diag in quads():
                    part = gram[s, r : r + 64, half * 128 : half * 128 + 128]
                    dec = decay_chunk(col[:, j : j + 1], row, r, half, diag)
                    mst[r : r + 64, j * Q + half * 128 : j * Q + half * 128 + 128] = (part * dec).astype(bf16)
            intra = mm(mst[...], xst[...])
            state_in = state[...]
            states_out[s] = state_in
            bc = bc_out[rows]
            readout = mm(bc[:, 128:], state_in.astype(bf16), 1, 1)
            ssd = intra + growth * readout + skip * xs
            ssd_out[rows] = ssd
            if links:
                ssd_v[blocks, rows] = ssd
            local = mm(xw_low, bc[:, :128], 0, 0)
            fade = jnp.exp2(total)
            for j in range(HB):
                at_j = slice(j * HEAD, j * HEAD + HEAD)
                state[at_j] = fade[:, j : j + 1] * state_in[at_j] + local[at_j]
            if links:
                work.step(i * spans + s)
            return carry

        lax.fori_loop(0, spans, span, 0)

    if not links:
        mix()
        return
    pl.when(i < blocks)(mix)

    @pl.when(i < blocks)
    def _():
        ssd_v[i] = ssd_v[blocks]

    gates = GateForward(i - blocks, blocks, normed, sent[3], sent[4], gain, ssd_v, *gate_refs, *gate_scratch)

    @pl.when(i == blocks)
    def _():
        work.first()
        gates.start(0)

    pl.when((i >= blocks) & (i < 2 * blocks))(gates.gate)

    @pl.when(i == 2 * blocks)
    def _():
        work.finish()
        gates.start(1)

    pl.when(i >= 2 * blocks)(gates.pull)


class GateForward:
    def __init__(
        self, at, blocks, normed, cot, wb, gain, ssd_v, gate_out, ggo_out, stats_out, w_v, cot_v, sq, gi, mine, landed, wl, cl
    ):
        self.at, self.blocks, self.normed, self.cot, self.wb, self.gain, self.ssd_v = at, blocks, normed, cot, wb, gain, ssd_v
        self.gate_out, self.ggo_out, self.stats_out = gate_out, ggo_out, stats_out
        self.w_v, self.cot_v, self.sq, self.gi, self.mine, self.landed, self.wl, self.cl = w_v, cot_v, sq, gi, mine, landed, wl, cl

    def load(self, which, n):
        cols = slice((which * self.blocks + n) * BW, (which * self.blocks + n + 1) * BW)
        return pltpu.make_async_copy(self.wb.at[:, cols], self.w_v.at[n], self.wl.at[n])

    def tokens(self):
        return pltpu.make_async_copy(self.cot, self.cot_v, self.cl.at[0])

    def start(self, which):
        if which:
            self.tokens().start()
        for n in range(self.blocks):
            self.load(which, n).start()
        if which:
            self.tokens().wait()
        total = self.gi if which else self.sq
        total[...] = jnp.zeros(total.shape, f32)

    def gate(self):
        b = self.at
        pltpu.make_async_copy(self.wb.at[:, :BW], self.w_v.at[b], self.wl.at[b]).wait()
        gate = mm(self.normed[...], self.w_v[b])
        self.gate_out[...] = gate
        gated = self.ssd_v[b] * (gate * sigmoid(gate))
        self.ssd_v[b] = gated
        squares = gated * gated
        self.sq[...] += squares[:, :128] + squares[:, 128:]

    def pull(self):
        b = self.at - self.blocks
        pltpu.make_async_copy(self.wb.at[:, :BW], self.w_v.at[b], self.wl.at[b]).wait()
        ggo = mm(self.cot_v[...], self.w_v[b])
        self.ggo_out[...] = ggo
        inner = ggo * self.gain[0:1] * self.ssd_v[b]
        self.gi[...] += inner[:, :128] + inner[:, 128:]
        pl.when(b == self.blocks - 1)(self.last)

    def last(self):
        self.mine[...] = token_sums(self.sq[...], self.gi[...])
        swap = remote(self.mine, self.landed, self.cl.at[1], self.cl.at[2], tensor=1 - lax.axis_index("tensor"))
        swap.start()
        swap.wait()
        self.stats_out[...] = self.mine[...] + self.landed[...]


def token_sums(sq, gi):
    lane = iota(sq.shape, 1)
    both = jnp.where(
        lane == 0,
        jnp.sum(sq, axis=1, keepdims=True),
        jnp.where(lane == 1, jnp.sum(gi, axis=1, keepdims=True), 0.0),
    )
    return jnp.transpose(both)[:8]


class BesideForward:
    def __init__(self, cot, w_gate_inner, w_output_t, cot_out, wb, ss, rs, ls, xs, xr, xl):
        self.here = Place()
        units = w_output_t.shape[1]
        self.moves = [
            Gather(self.here, own, wb, ss, rs, ls, n, slice(n * units, n * units + units))
            for n, own in enumerate((w_gate_inner.at[0], w_output_t))
        ]
        half = lax.axis_index("tensor")
        rows = cot.shape[0]
        slot = cot_out.at[pl.ds(pl.multiple_of(half * rows, rows), rows)]
        self.across = remote(cot, slot, xs, xr, tensor=1 - half)
        self.local = pltpu.make_async_copy(cot, slot, xl)

    def start(self):
        greet(self.here, True)
        for move in self.moves:
            move.start()
        self.across.start()
        self.local.start()

    def step(self, at):
        for when, chunk, hops in ((7, 0, 1), (11, 1, 1), (15, 0, 2), (19, 1, 2)):

            def go(move=self.moves[chunk], hops=hops):
                move.hop(hops)
                move.sides(hops - 1)

            pl.when(at == when)(go)

    def first(self):
        for move in self.moves:
            move.hop(3)
            move.sides(2)
        self.moves[0].sides(3)
        self.moves[0].finish()

    def finish(self):
        self.moves[1].sides(3)
        self.moves[1].finish()
        self.local.wait()
        self.across.wait()


def gate_forward(normed, cot, wg, wo, ssd, gain, gate_out, ggo_out, stats_out, sq, gi):
    i = pl.program_id(0)

    @pl.when(i == 0)
    def _():
        sq[...] = jnp.zeros(sq.shape, f32)
        gi[...] = jnp.zeros(gi.shape, f32)

    gate = mm(normed[...], wg[...])
    gate_out[...] = gate
    ggo = mm(cot[...], wo[...])
    ggo_out[...] = ggo
    gated = ssd[...] * (gate * sigmoid(gate))
    squares = gated * gated
    sq[...] += squares[:, :128] + squares[:, 128:]
    inner = ggo * gain[0:1] * gated
    gi[...] += inner[:, :128] + inner[:, 128:]

    @pl.when(i == pl.num_programs(0) - 1)
    def _():
        stats_out[...] = token_sums(sq[...], gi[...])


def gate_backward(
    unit_total, stats, gate, ssd, ggo, gain, normed, cot, dy_out, dgate_out, ng_out, gg_out, grads_out, normed_t, cols, cot_t
):
    @pl.when(pl.program_id(0) == 0)
    def _():
        full = jnp.concatenate([stats[...], jnp.zeros((120, stats.shape[1]), f32)], axis=0)
        cols[...] = jnp.transpose(full)

        def turn(n, carry):
            here = pl.ds(pl.multiple_of(n * 128, 128), 128)
            normed_t[here] = jnp.transpose(normed[:, here])
            cot_t[here] = jnp.transpose(cot[:, here])
            return carry

        lax.fori_loop(0, normed.shape[1] // 128, turn, 0)

    rstd = lax.rsqrt(cols[:, 0:1] / unit_total + norm_eps)
    pull = rstd * rstd * rstd * (cols[:, 1:2] / unit_total)
    v = gate[...]
    sig = sigmoid(v)
    act = v * sig
    y = ssd[...]
    gated = y * act
    scaled = gated * rstd
    ng = (scaled * gain[0:1]).astype(bf16)
    ng_out[...] = ng
    grads_out[1] = mm(cot_t[...], ng).astype(bf16)
    gg = ggo[...]
    gg_out[...] = jnp.broadcast_to(jnp.sum(gg * scaled, axis=0, keepdims=True), gg_out.shape)
    grad = rstd * (gg * gain[0:1]) - gated * pull
    dy_out[...] = (grad * act).astype(bf16)
    dgate = (grad * y * (sig * (1.0 + v * (1.0 - sig)))).astype(bf16)
    dgate_out[...] = dgate
    grads_out[0] = mm(normed_t[...], dgate).astype(bf16)


class BesideBackward:
    def __init__(self, mixed, grads, far_out, shard_out, scratch):
        self.here = Place()
        half = lax.axis_index("tensor")
        rows = far_out.shape[0]
        other = mixed.at[pl.ds(pl.multiple_of((1 - half) * rows, rows), rows)]
        self.across = remote(other, far_out, scratch[0], scratch[1], tensor=1 - half)
        self.sum = Reduce(self.here, grads, shard_out, scratch[2:7], scratch[7:15])

    def start(self):
        greet(self.here, True)
        self.sum.start()
        self.across.start()

    def step(self, at):
        total = self.sum
        z = self.here.z
        ends = (z == 0) | (z == 3)
        for n, block in enumerate(total.order):
            pl.when(at == n)(lambda z=block: total.cores(z))
            pl.when(at == (4, 6, 7, 8)[n])(lambda z=block: total.stay(z))
            pl.when(at == (5, 10, 15, 19)[n])(lambda z=block: total.sides(z))
        for n, block in enumerate(total.order[:3]):
            when = jnp.where(ends, (5, 10, 15)[n], (11, 16, 17)[n])
            pl.when(at == when)(lambda z=block: total.pass_on(z))

    def finish(self):
        self.sum.finish()
        self.across.wait()


def mixer_backward(links, inner, dy, states, kin, kst, log_rate, skip_in, cst, bc_in, step_in, cum_in, stepT, cumT, preT, *refs):
    refs = list(refs)
    if links:
        beside = refs[:2] + refs[7:9]
        refs = refs[2:7] + refs[9:]
        work = BesideBackward(*beside, refs[24:])
    dinner_out, gk_out, dsd_out, gks_out, hs_out = refs[:5]
    buf, dbuf, gram, gg, gb, gc, colc, cols, rowp, mst, dyst, gmix, sgrad = refs[5:18]
    rs_t, cs_t, dr_t, wg_t, gt_t, gtaps = refs[18:24]
    i = pl.program_id(0)
    if links:
        pl.when(i == 0)(work.start)
    heads = log_rate.shape[0]
    skip = lay(head_row(skip_in), as_units(heads, i))[0:1]
    tokens = inner.shape[0]
    spans = tokens // Q
    masks = head_masks()

    @pl.when(i == 0)
    def _():
        buf[0:8] = jnp.zeros((8, BW), f32)
        dbuf[tokens : tokens + 8] = jnp.zeros((8, BW), f32)
        for s in range(spans):
            bc = bc_in[s * Q : s * Q + Q]
            gram[s] = mm(bc[:, 128:], bc[:, :128], 1, 1)
        for ref in (gg, gb, gc, rs_t, cs_t, dr_t, wg_t, gt_t):
            ref[...] = jnp.zeros(ref.shape, f32)
        mst[...] = jnp.zeros(mst.shape, bf16)

    buf[8 : 8 + tokens] = inner[...]
    turn = lax.rem(128 - 8 * i, 128)
    colc[...] = pltpu.roll(cum_in[...], turn, 1)
    cols[...] = pltpu.roll(step_in[...], turn, 1)
    rows8 = pl.ds(pl.multiple_of(8 * i, 8), 8)
    rowp[...] = cumT[rows8] - jnp.log2(stepT[rows8])
    sgrad[...] = jnp.zeros(sgrad.shape, f32)
    gtaps[...] = jnp.zeros(gtaps.shape, f32)
    pick = (iota((8, BW), 1) // HEAD == iota((8, BW), 0)).astype(f32).astype(bf16)

    def conv_rows(at, kernel, grad_act, conv, sig):
        gco = grad_act * (sig * (1.0 + conv * (1.0 - sig)))
        dbuf[pl.ds(at, Q)] = gco
        into = buf[pl.ds(pl.multiple_of(at + 8, 8), Q)]
        gtaps[4:5] += jnp.sum(gco, axis=0, keepdims=True)
        after = dbuf[pl.ds(at, Q + 8)]
        grad_in = kernel[3:4] * gco
        gtaps[3:4] += jnp.sum(gco * into, axis=0, keepdims=True)
        for k in range(3):
            later = pltpu.roll(after, Q + 8 - (3 - k), 0)[:Q]
            gtaps[k : k + 1] += jnp.sum(later * into, axis=0, keepdims=True)
            grad_in = grad_in + kernel[k : k + 1] * later
        return grad_in

    def span(back, carry):
        s = spans - 1 - back
        at = pl.multiple_of(s * Q, Q)
        rows = pl.ds(at, Q)
        conv = conv_taps(buf[pl.ds(at, Q + 8)], kin[...])
        sig = sigmoid(conv)
        xs = conv * sig
        x_low = xs.astype(bf16)
        dy_s = dy[rows]
        dy_f = dy_s.astype(f32)
        bc = bc_in[rows]
        b_low, c_low = bc[:, :128], bc[:, 128:]
        col = colc[rows]
        total = col[Q - 1 : Q]
        for j in range(HB):
            dyst[j * Q : j * Q + Q] = dy_s * masks[j]
        gmix[...] = mm(dyst[...], x_low, 1, 1)
        lane = iota((Q, 128), 1)
        row_sums = jnp.zeros((Q, 128), f32)
        for j in range(HB):
            row = rowp[j : j + 1, rows]
            col_sum = [jnp.zeros((1, 128), f32), jnp.zeros((1, 128), f32)]
            row_parts = []
            for r, half, diag in quads():
                here = slice(half * 128, half * 128 + 128)
                dec = decay_chunk(col[:, j : j + 1], row, r, half, diag)
                part = gram[s, r : r + 64, here]
                p = gmix[j * Q + r : j * Q + r + 64, here] * dec
                gg[s, r : r + 64, here] += p
                q = p * part
                mst[j * Q + r : j * Q + r + 64, here] = (part * dec).astype(bf16)
                col_sum[half] = col_sum[half] + jnp.sum(q, axis=0, keepdims=True)
                if half == 0:
                    row_parts.append(q)
                else:
                    row_parts[-1] = row_parts[-1] + q
            sums = jnp.concatenate([jnp.sum(q, axis=1, keepdims=True) for q in row_parts], axis=0)
            row_sums = jnp.where(lane == j, sums, row_sums)
            cs_t[pl.ds(8 * i + j, 1), rows] = jnp.concatenate(col_sum, axis=1)
        rs_t[rows8, rows] = jnp.transpose(row_sums)[:8]
        grad_xs = mm(mst[...], dyst[...], 0, 0) + skip * dy_f

        growth = expand(jnp.exp2(col[:, :8]))
        weight = expand(jnp.exp2(total[:, :8] - col[:, :8]) * cols[rows][:, :8])
        state_in = states[s]
        state_low = state_in.astype(bf16)
        state_grad = sgrad[...]
        carry_low = state_grad.astype(bf16)
        readout = mm(c_low, state_low, 1, 1)
        read_low = (dy_f * growth).astype(bf16)
        hi, low = split2(dy_f * readout)
        dr_t[rows8, rows] = mm(pick, hi, 1, 1) + mm(pick, low, 1, 1)
        gc[rows] += mm(read_low, state_low)
        grad_xw = mm(b_low, carry_low, 1, 1)
        xw_low = (xs * weight).astype(bf16)
        gb[rows] += mm(xw_low, carry_low)
        hi, low = split2(grad_xw * xs)
        wg_t[rows8, rows] = mm(pick, hi, 1, 1) + mm(pick, low, 1, 1)
        hi, low = split2(state_grad * state_in)
        sums = jnp.sum(mm(pick, hi) + mm(pick, low), axis=1, keepdims=True)
        gt_t[rows8] = jnp.where(iota((8, 128), 1) == s, sums, gt_t[rows8])
        grad_xs = grad_xs + grad_xw * weight
        local = mm(read_low, c_low, 0, 0)
        fade = jnp.exp2(total)
        for j in range(HB):
            at_j = slice(j * HEAD, j * HEAD + HEAD)
            sgrad[at_j] = fade[:, j : j + 1] * state_grad[at_j] + local[at_j]
        gtaps[5:6] += jnp.sum(dy_f * xs, axis=0, keepdims=True)
        dinner_out[rows] = conv_rows(at, kin[...], grad_xs, conv, sig).astype(bf16)
        if links:
            work.step(i * spans + back)
        return carry

    lax.fori_loop(0, spans, span, 0)
    gk_out[...] = gtaps[...]

    @pl.when(i == pl.num_programs(0) - 1)
    def _():
        buf[8 : 8 + tokens] = cst[...]
        gtaps[...] = jnp.zeros(gtaps.shape, f32)
        rates = lay(-jnp.exp(head_row(log_rate)), as_places(heads))[0:1]
        rate = jnp.transpose(jnp.broadcast_to(rates, (128, 128)))[:48, 0:1]
        later = (iota((Q, Q), 0) >= iota((Q, Q), 1)).astype(f32).astype(bf16)
        last = iota((48, Q), 1) == Q - 1
        bias_sum = jnp.zeros((48, 1), f32)
        decay_sum = jnp.zeros((48, 1), f32)
        for back in range(spans):
            s = spans - 1 - back
            rows = slice(s * Q, s * Q + Q)
            bc = bc_in[rows]
            gl = gg[s].astype(bf16)
            grad_c = gc[rows] + mm(gl, bc[:, :128])
            grad_b = gb[rows] + mm(gl, bc[:, 128:], 0, 0)
            both = jnp.concatenate([grad_b, grad_c], axis=1)
            conv = conv_taps(buf[s * Q : s * Q + Q + 8], kst[...])
            dsd_out[rows, :BW] = conv_rows(s * Q, kst[...], both, conv, sigmoid(conv)).astype(bf16)

            cum, step, pre = cumT[:, rows], stepT[:, rows], preT[:, rows]
            total = cum[:, Q - 1 : Q]
            rate_w = jnp.exp2(total - cum)
            wg = wg_t[:, rows]
            cs = cs_t[:, rows]
            moved = wg * (rate_w * step)
            grad_cum = rs_t[:, rows] - cs + jnp.exp2(cum) * dr_t[:, rows] - moved
            grad_total = jnp.exp2(total) * gt_t[:, s : s + 1] + jnp.sum(moved, axis=1, keepdims=True)
            grad_cum = grad_cum + jnp.where(last, grad_total, 0.0)
            parts = split3(grad_cum)
            grad_rate = mm(parts[0], later) + mm(parts[1], later) + mm(parts[2], later)
            sig = sigmoid(pre)
            ratio = jnp.where(pre < -15.0, 1.0, sig / step)
            grad_pre = (wg * rate_w + grad_rate * rate) * sig + cs * ratio
            bias_sum = bias_sum + jnp.sum(grad_pre, axis=1, keepdims=True)
            decay_sum = decay_sum + jnp.sum(grad_rate * step, axis=1, keepdims=True)
            full = jnp.concatenate([grad_pre, jnp.zeros((80, Q), f32)], axis=0)
            dsd_out[rows, BW:] = jnp.transpose(full).astype(bf16)
        gks_out[...] = gtaps[...]
        lane = iota((48, 128), 1)
        both = jnp.where(lane == 0, bias_sum, jnp.where(lane == 1, decay_sum * rate, 0.0))
        hs_out[...] = jnp.transpose(jnp.concatenate([both, jnp.zeros((80, 128), f32)], axis=0))[:8]
        if links:
            work.finish()


class Place:
    def __init__(self):
        me = lax.axis_index("dp")
        self.me = me
        self.c, self.y, self.z = me % 2, (me // 2) % 2, me // 4

    def at(self, z, y, c):
        return (z * 2 + y) * 2 + c

    def core(self):
        return self.at(self.z, self.y, 1 - self.c)

    def side(self):
        return self.at(self.z, 1 - self.y, self.c)

    def up(self):
        return self.me + 4

    def down(self):
        return self.me - 4


def greet(here, across):
    barrier = pltpu.get_barrier_semaphore()

    def signal(**device):
        pl.semaphore_signal(barrier, 1, device_id=device, device_id_type=MESH)

    signal(dp=here.core())
    signal(dp=here.side())
    pl.when(here.z < 3)(lambda: signal(dp=here.up()))
    pl.when(here.z > 0)(lambda: signal(dp=here.down()))
    if across:
        signal(tensor=1 - lax.axis_index("tensor"))
    ends = (here.z == 0).astype(jnp.int32) + (here.z == 3).astype(jnp.int32)
    pl.semaphore_wait(barrier, 4 + int(across) - ends)


def remote(src, dst, send_sem, recv_sem, **device):
    return pltpu.make_async_remote_copy(
        src_ref=src, dst_ref=dst, send_sem=send_sem, recv_sem=recv_sem, device_id=device, device_id_type=MESH
    )


class Gather:
    def __init__(self, here, own, full, ss, rs, ls, chunk, cols):
        self.here, self.full, self.ss, self.rs, self.chunk, self.cols = here, full, ss, rs, chunk, cols
        self.rows = own.shape[0]
        self.own = own
        self.local = pltpu.make_async_copy(own, self.slot(here.me), ls.at[chunk])

    def slot(self, origin):
        return self.full.at[pl.ds(pl.multiple_of(origin * self.rows, self.rows), self.rows), self.cols]

    def copy(self, origin, way, src=None):
        here = self.here
        target = (here.up, here.down, here.side, here.core)[way]()
        slot = self.slot(origin)
        sems = self.ss.at[self.chunk, origin, way], self.rs.at[self.chunk, origin]
        return remote(slot if src is None else src, slot, *sems, dp=target)

    def arrived(self, origin):
        self.copy(origin, 3).wait_recv()

    def each_send(self, act):
        here = self.here
        for hops in range(4):
            for way, origin_z in ((0, here.z - hops), (1, here.z + hops)):
                if hops == 0:
                    if way == 1:
                        continue
                    origin = here.me
                    pl.when(here.z < 3)(lambda o=origin: act(o, 0))
                    pl.when(here.z > 0)(lambda o=origin: act(o, 1))
                    act(origin, 2)
                    act(origin, 3)
                    continue
                origin = here.at(origin_z, here.y, here.c)

                def go(o=origin, way=way):
                    pl.when((here.z < 3) if way == 0 else (here.z > 0))(lambda: act(o, way))
                    act(o, 2)
                    act(o, 3)

                pl.when((origin_z >= 0) & (origin_z <= 3))(go)

    def start(self):
        here = self.here
        pl.when(here.z < 3)(lambda: self.copy(here.me, 0, self.own).start())
        pl.when(here.z > 0)(lambda: self.copy(here.me, 1, self.own).start())
        self.copy(here.me, 2, self.own).start()
        self.copy(here.me, 3, self.own).start()
        self.local.start()

    def hop(self, hops):
        here = self.here
        for way, origin_z in ((0, here.z - hops), (1, here.z + hops)):

            def go(way=way, origin_z=origin_z):
                origin = here.at(origin_z, here.y, here.c)
                self.arrived(origin)
                pl.when((here.z < 3) if way == 0 else (here.z > 0))(lambda: self.copy(origin, way).start())
                self.copy(origin, 2).start()
                self.copy(origin, 3).start()

            pl.when((origin_z >= 0) & (origin_z <= 3))(go)

    def sides(self, hops):
        here = self.here
        for way, origin_z in ((0, here.z - hops), (1, here.z + hops)):
            if hops == 0 and way == 1:
                continue

            def go(origin_z=origin_z):
                origin = here.at(origin_z, 1 - here.y, here.c)
                self.arrived(origin)
                self.copy(origin, 3).start()

            pl.when((origin_z >= 0) & (origin_z <= 3))(go)

    def finish(self):
        here = self.here
        self.local.wait()
        for z in range(4):
            for y in range(2):
                self.arrived(here.at(z, y, 1 - here.c))
        self.each_send(lambda origin, way: self.copy(origin, way).wait_send())
        for z in range(4):
            self.copy(here.at(z, 1 - here.y, here.c), 3).wait_send()


def gather_scratch():
    sem = pltpu.SemaphoreType.DMA
    return [sem((2, 16, 4)), sem((2, 16)), sem((2,))]


def gather_kernel(tokens_in, gain, w_gate_inner, w_state_io, w_step, tokens_out, full, pack, low, ss, rs, ls, xs, xr, xl):
    here = Place()
    half = lax.axis_index("tensor")
    rows = tokens_in.shape[0]
    units, cols = w_gate_inner.shape[2], full.shape[1]
    pack[:, :units] = w_gate_inner[1]
    pack[:, units : units + BW] = w_state_io[...]
    pack[:, units + BW :] = mm(w_step[...], as_places(w_step.shape[1])).astype(bf16)
    greet(here, True)
    cut = cols // 256 * 128
    moves = [
        Gather(here, pack.at[:, c], full, ss, rs, ls, n, c) for n, c in enumerate((slice(0, cut), slice(cut, cols)))
    ]
    for move in moves:
        move.start()
    part = rows // 4
    across, local = [], []
    for n in range(4):
        piece = slice(n * part, n * part + part)
        v = tokens_in[piece].astype(f32)
        scale = lax.rsqrt(jnp.mean(v * v, axis=1, keepdims=True) + norm_eps)
        low[piece] = (v * scale * gain[0:1]).astype(bf16)
        slot = tokens_out.at[pl.ds(pl.multiple_of(half * rows + n * part, part), part)]
        across.append(remote(low.at[piece], slot, xs.at[n], xr.at[n], tensor=1 - half))
        across[-1].start()
        local.append(pltpu.make_async_copy(low.at[piece], slot, xl.at[n]))
        local[-1].start()
    for hops in range(1, 5):
        for move in moves:
            if hops < 4:
                move.hop(hops)
            move.sides(hops - 1)
    for n in range(4):
        local[n].wait()
        across[n].wait()
    for move in moves:
        move.finish()


def gather_rows(tokens_in, gain, w_gate_inner, w_state_io, w_step, ways, collective_id):
    rows, width = tokens_in.shape
    _, own, units = w_gate_inner.shape
    cols = units + BW + 128
    vmem = pl.BlockSpec(memory_space=pltpu.VMEM)
    hbm = pl.BlockSpec(memory_space=pl.ANY)
    sem = pltpu.SemaphoreType.DMA
    return pl.pallas_call(
        gather_kernel,
        name="gather_rows",
        in_specs=[vmem] * 5,
        out_specs=[hbm, hbm],
        out_shape=[sds((2 * rows, width), bf16), sds((ways * own, cols), bf16)],
        scratch_shapes=[
            pltpu.VMEM((own, cols), bf16), pltpu.VMEM((rows, width), bf16), *gather_scratch(),
            sem((4,)), sem((4,)), sem((4,)),
        ],
        compiler_params=pltpu.CompilerParams(
            collective_id=collective_id, has_side_effects=True, vmem_limit_bytes=60 * 1024 * 1024
        ),
    )(tokens_in, gain, w_gate_inner, w_state_io, w_step)


class Reduce:
    def __init__(self, here, grads, out, bufs, sems):
        self.here, self.grads, self.out = here, grads, out
        self.held, self.buf_a, self.buf_b, self.buf_up, self.buf_dn = bufs
        self.local, self.send_a, self.recv_a, self.send_b, self.recv_b, self.send_c, self.recv_up, self.recv_dn = sems
        self.parts, self.rows = out.shape[:2]
        z = here.z
        self.order = (3 * (1 - z // 2), (3 * z + 2) % 5, 1 + z % 2, z)

    def spot(self, z, y, c):
        if self.grads is None:
            return z, (y * 2 + c) * self.rows
        return z * 2 + y, 0

    def own(self, z, y, c=None):
        at, base = self.spot(z, y, self.here.c if c is None else c)
        return self.held.at[at, :, pl.ds(pl.multiple_of(base, 16), self.rows)]

    def block(self, z, y, c):
        if self.grads is None:
            return self.own(z, y, c)
        at = pl.multiple_of(self.here.at(z, y, c) * self.rows, self.rows)
        return self.grads.at[:, pl.ds(at, self.rows)]

    def copy_a(self, z, y):
        here, at = self.here, z * 2 + y
        return remote(self.block(z, y, 1 - here.c), self.buf_a.at[at], self.send_a.at[at], self.recv_a.at[at], dp=here.core())

    def take(self, z, y):
        return pltpu.make_async_copy(self.block(z, y, self.here.c), self.own(z, y), self.local.at[z * 2 + y])

    def copy_b(self, z):
        here = self.here
        return remote(self.own(z, 1 - here.y), self.buf_b.at[z], self.send_b.at[z], self.recv_b.at[z], dp=here.side())

    def copy_up(self, z):
        return remote(self.own(z, self.here.y), self.buf_up.at[z], self.send_c.at[z], self.recv_up.at[z], dp=self.here.up())

    def copy_dn(self, z):
        return remote(self.own(z, self.here.y), self.buf_dn.at[z], self.send_c.at[z], self.recv_dn.at[z], dp=self.here.down())

    def add(self, z, y, buf, slot):
        at, base = self.spot(z, y, self.here.c)

        def rows(n, carry):
            piece = pl.ds(pl.multiple_of(n * 16, 16), 16)
            held = pl.ds(pl.multiple_of(base + n * 16, 16), 16)
            for part in range(self.parts):
                total = self.held[at, part, held].astype(f32) + buf[slot, part, piece].astype(f32)
                self.held[at, part, held] = total.astype(bf16)
            return carry

        lax.fori_loop(0, self.rows // 16, rows, 0)

    def start(self):
        here = self.here
        for side in (1 - here.y, here.y):
            for z in self.order:
                self.copy_a(z, side).start()
                self.take(z, side).start()

    def join(self, z, y):
        if self.grads is not None:
            self.take(z, y).wait()
        self.copy_a(z, y).wait_recv()
        self.add(z, y, self.buf_a, z * 2 + y)

    def cores(self, z):
        self.join(z, 1 - self.here.y)
        self.copy_b(z).start()

    def stay(self, z):
        self.join(z, self.here.y)

    def sides(self, z):
        self.copy_b(z).wait_recv()
        self.add(z, self.here.y, self.buf_b, z)

    def pass_on(self, z):
        here = self.here

        def up():
            def below():
                self.copy_up(z).wait_recv()
                self.add(z, here.y, self.buf_up, z)

            pl.when(here.z > 0)(below)
            self.copy_up(z).start()

        def down():
            def above():
                self.copy_dn(z).wait_recv()
                self.add(z, here.y, self.buf_dn, z)

            pl.when(here.z < 3)(above)
            self.copy_dn(z).start()

        pl.when(z > here.z)(up)
        pl.when(z < here.z)(down)

    def finish(self):
        here = self.here
        z = here.z
        at, base = self.spot(z, here.y, here.c)
        pl.when(z > 0)(lambda: self.copy_up(z).wait_recv())
        pl.when(z < 3)(lambda: self.copy_dn(z).wait_recv())

        def rows(n, carry):
            piece = pl.ds(pl.multiple_of(n * 16, 16), 16)
            held = pl.ds(pl.multiple_of(base + n * 16, 16), 16)
            for part in range(self.parts):
                below = jnp.where(z > 0, self.buf_up[z, part, piece].astype(f32), 0.0)
                above = jnp.where(z < 3, self.buf_dn[z, part, piece].astype(f32), 0.0)
                self.out[part, piece] = self.held[at, part, held].astype(f32) + below + above
            return carry

        lax.fori_loop(0, self.rows // 16, rows, 0)
        for zn in self.order:
            self.copy_a(zn, 0).wait_send()
            self.copy_a(zn, 1).wait_send()
            self.copy_b(zn).wait_send()
            pl.when(zn > z)(lambda zn=zn: self.copy_up(zn).wait_send())
            pl.when(zn < z)(lambda zn=zn: self.copy_dn(zn).wait_send())


def reduce_scratch(parts, rows, cols, by_z=False):
    sem = pltpu.SemaphoreType.DMA
    block = (parts, rows, cols)
    held = (4, parts, 4 * rows, cols) if by_z else (8,) + block
    return [
        pltpu.VMEM(held, bf16), pltpu.VMEM((8,) + block, bf16), pltpu.VMEM((4,) + block, bf16),
        pltpu.VMEM((4,) + block, bf16), pltpu.VMEM((4,) + block, bf16),
        sem((8,)), sem((8,)), sem((8,)), sem((4,)), sem((4,)), sem((4,)), sem((4,)), sem((4,)),
    ]


def tail_kernel(
    normed_t, dinner, dsd, dgate, wb, wa, gk, ggg, gks, hs, gn_out, shard_out, small_out,
    nt_v, dinner_v, dsd_v, dgate_v, wg_v, wa_v, away, came, total, landed, loads, send_x, recv_x, send, recv, *scratch,
):
    here = Place()
    half = lax.axis_index("tensor")
    units = dgate.shape[1]
    sources = (normed_t, dinner, dsd, dgate, wb.at[:, :units], wa)
    pending = [
        pltpu.make_async_copy(src, dst, loads.at[n])
        for n, (src, dst) in enumerate(zip(sources, (nt_v, dinner_v, dsd_v, dgate_v, wg_v, wa_v)))
    ]
    for copy in pending:
        copy.start()
    far = pltpu.get_barrier_semaphore()
    partners = [here.me + bit - 2 * bit * ((here.me // bit) % 2) for bit in (2, 4, 8, 1)]
    for partner in partners:
        pl.semaphore_signal(far, 1, device_id={"dp": partner}, device_id_type=MESH)
    pl.semaphore_signal(far, 1, device_id={"tensor": 1 - half}, device_id_type=MESH)
    middle = (here.z == 1) | (here.z == 2)
    pl.when(here.z == 1)(lambda: pl.semaphore_signal(far, 1, device_id={"dp": here.up()}, device_id_type=MESH))
    pl.when(here.z == 2)(lambda: pl.semaphore_signal(far, 1, device_id={"dp": here.down()}, device_id_type=MESH))
    pl.semaphore_wait(far, 5 + middle.astype(jnp.int32))
    work = Reduce(here, None, shard_out, scratch[:5], scratch[5:])
    order = work.order
    rows = gn_out.shape[0]
    chunks, _, wide = away.shape

    def swap(k):
        return remote(total.at[k], landed.at[k], send.at[k], recv.at[k], dp=partners[k])

    def swapped(k):
        swap(k).wait()
        total[k + 1] = total[k] + landed[k]
        if k < 3:
            swap(k + 1).start()

    def across(n):
        return remote(away.at[n], came.at[n], send_x.at[n], recv_x.at[n], tensor=1 - half)

    def pulled(which, n):
        mine = pl.ds(pl.multiple_of(which * rows, rows), rows)
        at = pl.ds(pl.multiple_of(n * wide, wide), wide)
        return (
            mm(dgate_v[mine], wg_v[at], 1, 1)
            + mm(dinner_v[mine], wa_v[at, :units], 1, 1)
            + mm(dsd_v[mine], wa_v[at, units:], 1, 1)
        )

    def far_chunk(n, carry):
        away[n] = pulled(1 - half, n).astype(bf16)
        across(n).start()
        return carry

    def near_chunk(n, carry):
        gn_out[:, pl.ds(pl.multiple_of(n * wide, wide), wide)] = pulled(half, n)
        return carry

    def grads(n, carry):
        z = jnp.where(n == 0, order[0], jnp.where(n == 1, order[1], jnp.where(n == 2, order[2], order[3])))
        count = 4 * work.rows
        left = nt_v[pl.ds(pl.multiple_of(z * count, count), count)]
        work.held[z, 0, :, :units] = mm(left, dinner_v[...]).astype(bf16)
        work.held[z, 0, :, units:] = mm(left, dsd_v[...]).astype(bf16)
        work.copy_a(z, 1 - here.y).start()
        work.copy_a(z, here.y).start()

        @pl.when(n == 0)
        def _():
            for copy in pending[3:]:
                copy.wait()

        far_chunk(n, carry)
        work.cores(z)
        return carry

    total[0, 0:6] = gk[0:6]
    total[0, 6:7] = ggg[0:1]
    for k in range(5):
        total[0, 7:8, k * BW : k * BW + BW] = gks[k : k + 1]
    for k in range(2):
        total[0, 7:8, 5 * BW + k * 128 : 5 * BW + k * 128 + 128] = hs[k : k + 1]
    swap(0).start()
    for copy in pending[:3]:
        copy.wait()
    swapped(0)
    lax.fori_loop(0, 4, grads, 0)
    swapped(1)
    work.stay(order[0])
    work.sides(order[0])
    pl.when(~middle)(lambda: work.pass_on(order[0]))
    lax.fori_loop(4, chunks, far_chunk, 0)
    swapped(2)
    for n in range(1, 4):
        work.stay(order[n])
    work.sides(order[1])
    pl.when(~middle)(lambda: work.pass_on(order[1]))
    lax.fori_loop(0, 3, near_chunk, 0)
    pl.when(middle)(lambda: work.pass_on(order[0]))
    work.sides(order[2])
    pl.when(~middle)(lambda: work.pass_on(order[2]))
    lax.fori_loop(3, chunks, near_chunk, 0)
    swapped(3)
    small_out[...] = total[4]
    pl.when(middle)(lambda: work.pass_on(order[1]))
    work.sides(order[3])
    pl.when(middle)(lambda: work.pass_on(order[2]))
    work.finish()

    def arrive(n, carry):
        across(n).wait()
        at = pl.ds(pl.multiple_of(n * wide, wide), wide)
        gn_out[:, at] = gn_out[:, at] + came[n].astype(f32)
        return carry

    lax.fori_loop(0, chunks, arrive, 0)


def reduce_tail(normed_t, dinner, dsd, dgate, wb, wa, sums, ways, collective_id):
    width, tokens = normed_t.shape
    small = sums[0]
    units, cols, rows = dgate.shape[1], wa.shape[1], width // ways
    chunks = width // BW
    vmem = pl.BlockSpec(memory_space=pltpu.VMEM)
    hbm = pl.BlockSpec(memory_space=pl.ANY)
    sem = pltpu.SemaphoreType.DMA
    return pl.pallas_call(
        tail_kernel, name="tail", in_specs=[hbm] * 6 + [vmem] * 4, out_specs=[vmem] * 3,
        out_shape=[sds((tokens // 2, width)), sds((1, rows, cols)), sds(small.shape)],
        scratch_shapes=[
            pltpu.VMEM(normed_t.shape, bf16), pltpu.VMEM(dinner.shape, bf16), pltpu.VMEM(dsd.shape, bf16),
            pltpu.VMEM(dgate.shape, bf16), pltpu.VMEM((width, units), bf16), pltpu.VMEM(wa.shape, bf16),
            pltpu.VMEM((chunks, tokens // 2, BW), bf16), pltpu.VMEM((chunks, tokens // 2, BW), bf16),
            pltpu.VMEM((5,) + small.shape, f32), pltpu.VMEM((4,) + small.shape, f32),
            sem((6,)), sem((chunks,)), sem((chunks,)), sem((4,)), sem((4,)),
        ] + reduce_scratch(1, rows, cols, True),
        compiler_params=pltpu.CompilerParams(
            collective_id=collective_id, has_side_effects=True, vmem_limit_bytes=62 * 1024 * 1024
        ),
    )(normed_t, dinner, dsd, dgate, wb, wa, *sums)


def swap(v):
    return lax.ppermute(v, "tensor", [(0, 1), (1, 0)])


def halves(v, axis):
    size = v.shape[axis] // 2
    me = lax.axis_index("tensor")
    return (
        lax.dynamic_slice_in_dim(v, me * size, size, axis),
        lax.dynamic_slice_in_dim(v, (1 - me) * size, size, axis),
    )


def once(shape, at=None):
    where = at or (0,) * len(shape)
    return pl.BlockSpec(shape, lambda i: where, pipeline_mode=pl.Buffered(1))


def by_cols(rows, offset=0):
    return pl.BlockSpec((rows, BW), lambda i: (0, i + offset))


def params(collective_id=None):
    return pltpu.CompilerParams(
        dimension_semantics=("arbitrary",), vmem_limit_bytes=60 * 1024 * 1024,
        collective_id=collective_id, has_side_effects=collective_id is not None,
    )


def spread(v):
    lead = v.shape[:-1]
    v = v.reshape(lead + (v.shape[-1] // HB, HB))
    v = jnp.pad(v, [(0, 0)] * len(lead) + [(0, 0), (0, 8 - HB)]).reshape(lead + (-1,))
    return jnp.pad(v, [(0, 0)] * len(lead) + [(0, 128 - v.shape[-1])])


def gathered_heads(v, heads):
    return v[..., : heads * 2].reshape(v.shape[:-1] + (heads // HB, 8))[..., :HB].reshape(v.shape[:-1] + (heads,))


def sds(shape, dtype=f32):
    return jax.ShapeDtypeStruct(shape, dtype)


def on_device(
    residual, norm_gain, w_gate_inner, w_state_io, w_step, conv_inner, conv_state,
    step_bias, decay_log, skip_gain, gate_gain, w_output, cotangent,
):
    width = residual.shape[1]
    units = w_gate_inner.shape[2]
    heads = w_step.shape[1]
    blocks = units // BW
    unit_total = units * lax.axis_size("tensor")
    ways = lax.axis_size("dp")
    own_links = ways == 16
    rows_in = residual.astype(f32)
    rstd_in = lax.rsqrt(jnp.mean(rows_in * rows_in, axis=1, keepdims=True) + norm_eps)
    scaled = rows_in * rstd_in
    pack_a = jnp.concatenate([w_gate_inner[1], w_state_io, spread(w_step)], axis=1)
    w_output_t = w_output.T
    if own_links:
        normed, wa = gather_rows(
            residual, jnp.broadcast_to(norm_gain[None], (8, width)), w_gate_inner, w_state_io, w_step, ways, 1
        )
    else:
        wa = lax.all_gather(pack_a, "dp", axis=0, tiled=True)
        normed = lax.all_gather((scaled * norm_gain).astype(bf16), "tensor", axis=0, tiled=True)
    tokens = normed.shape[0]
    spans = tokens // Q
    gain8 = jnp.broadcast_to(gate_gain[None], (8, units))

    hbm = pl.BlockSpec(memory_space=pl.ANY)
    sem = pltpu.SemaphoreType.DMA
    def stage(rows, first):
        return pl.BlockSpec((rows, BW), lambda i: (0, jnp.clip(i - first, 0, blocks - 1)))

    inner, ssd, states, cst, bc, step, cum, step_t, cum_t, pre_t, *sent = pl.pallas_call(
        functools.partial(mixer_forward, own_links),
        name="mixer_forward",
        grid=(blocks * (3 if own_links else 1),),
        in_specs=[
            once((tokens, width)), stage(width, 0), once((width, 384), (0, units // 384)),
            stage(5, 0), once((5, BW)), once((heads,)), once((heads,)), once((heads,)),
        ] + ([once(v.shape) for v in (cotangent, w_gate_inner, w_output_t)] + [stage(8, 2 * blocks)]) * own_links,
        out_specs=[
            stage(tokens, 0), stage(tokens, 0), pl.BlockSpec((spans, BW, 128), lambda i: (0, jnp.clip(i, 0, blocks - 1), 0)),
            once((tokens, BW)), once((tokens, BW)), once((tokens, 128)), once((tokens, 128)),
            once((48, tokens)), once((48, tokens)), once((48, tokens)),
        ] + [hbm, hbm, stage(tokens, blocks), stage(tokens, 2 * blocks), once((8, tokens))] * own_links,
        out_shape=[
            sds((tokens, units)), sds((tokens, units)), sds((spans, units, 128)),
            sds((tokens, BW)), sds((tokens, BW), bf16), sds((tokens, 128)), sds((tokens, 128)),
            sds((48, tokens)), sds((48, tokens)), sds((48, tokens)),
        ] + [
            sds((tokens, width), bf16), sds((width, 2 * units), bf16), sds((tokens, units)), sds((tokens, units)),
            sds((8, tokens)),
        ] * own_links,
        scratch_shapes=[
            pltpu.VMEM((tokens + 8, BW), f32), pltpu.VMEM((spans, Q, Q), f32),
            pltpu.VMEM((tokens, 128), f32), pltpu.VMEM((tokens, 128), f32), pltpu.VMEM((8, tokens), f32),
            pltpu.VMEM((Q, HB * Q), bf16), pltpu.VMEM((HB * Q, BW), bf16), pltpu.VMEM((BW, 128), f32),
        ] + ([
            pltpu.VMEM((blocks + 1, tokens, BW), f32), pltpu.VMEM((blocks, width, BW), bf16), pltpu.VMEM((tokens, width), bf16),
            pltpu.VMEM((tokens, 128), f32), pltpu.VMEM((tokens, 128), f32), pltpu.VMEM((8, tokens), f32),
            pltpu.VMEM((8, tokens), f32), sem((blocks,)), sem((3,)),
        ] + gather_scratch() + [sem, sem, sem]) * own_links,
        compiler_params=params(2 if own_links else None),
        cost_estimate=pl.CostEstimate(flops=2 * tokens * width * (units + 384) + 4 * tokens * 256 * units, bytes_accessed=30_000_000, transcendentals=heads * spans * Q * Q),
    )(
        normed, wa, wa, conv_inner, conv_state, step_bias, decay_log, skip_gain,
        *[cotangent, w_gate_inner, w_output_t, gain8] * own_links,
    )

    if own_links:
        cot, wb, gate, ggo, stats = sent
    else:
        wb = lax.all_gather(jnp.concatenate([w_gate_inner[0], w_output_t], axis=1), "dp", axis=0, tiled=True)
        cot = lax.all_gather(cotangent, "tensor", axis=0, tiled=True)
        gate, ggo, stats = pl.pallas_call(
            gate_forward,
            name="gate_forward",
            grid=(blocks,),
            in_specs=[
                once((tokens, width)), once((tokens, width)), by_cols(width), by_cols(width, blocks),
                by_cols(tokens), by_cols(8),
            ],
            out_specs=[by_cols(tokens), by_cols(tokens), once((8, tokens))],
            out_shape=[sds((tokens, units)), sds((tokens, units)), sds((8, tokens))],
            scratch_shapes=[pltpu.VMEM((tokens, 128), f32), pltpu.VMEM((tokens, 128), f32)],
            compiler_params=params(),
            cost_estimate=pl.CostEstimate(flops=4 * tokens * width * units, bytes_accessed=35_000_000, transcendentals=tokens * units),
        )(normed, cot, wb, wb, ssd, gain8)
        stats = stats + swap(stats)

    dy, dgate, ng, ggg, grad_b, normed_t = pl.pallas_call(
        functools.partial(gate_backward, float(unit_total)),
        name="gate_backward",
        grid=(blocks,),
        in_specs=[
            once((8, tokens)), by_cols(tokens), by_cols(tokens), by_cols(tokens), by_cols(8),
            once((tokens, width)), once((tokens, width)),
        ],
        out_specs=[
            by_cols(tokens), by_cols(tokens), by_cols(tokens), by_cols(8),
            pl.BlockSpec((2, width, BW), lambda i: (0, 0, i)), once((width, tokens)),
        ],
        out_shape=[
            sds((tokens, units), bf16), sds((tokens, units), bf16), sds((tokens, units), bf16), sds((8, units)),
            sds((2, width, units), bf16), sds((width, tokens), bf16),
        ],
        scratch_shapes=[pltpu.VMEM((tokens, 128), f32), pltpu.VMEM((width, tokens), bf16)],
        compiler_params=params(),
        cost_estimate=pl.CostEstimate(flops=4 * tokens * units * width, bytes_accessed=45_000_000, transcendentals=tokens * units),
    )(stats, gate, ssd, ggo, gain8, normed, cot)

    mixed = mm(ng, wb[:, units:], 1, 1).astype(bf16)
    mixed_near, mixed_far = halves(mixed, 0)

    dinner, gk, dsd, gks, hs, *sent = pl.pallas_call(
        functools.partial(mixer_backward, own_links),
        name="mixer_backward",
        grid=(blocks,),
        in_specs=[
            by_cols(tokens), by_cols(tokens), pl.BlockSpec((spans, BW, 128), lambda i: (0, i, 0)),
            by_cols(5), once((5, BW)), once((heads,)), once((heads,)),
            once((tokens, BW)), once((tokens, BW)), once((tokens, 128)), once((tokens, 128)),
            once((48, tokens)), once((48, tokens)), once((48, tokens)),
        ] + [hbm, hbm] * own_links,
        out_specs=[by_cols(tokens), by_cols(8), once((tokens, 384)), once((8, BW)), once((8, 128))]
        + [hbm, once((2, width // ways, units))] * own_links,
        out_shape=[sds((tokens, units), bf16), sds((8, units)), sds((tokens, 384), bf16), sds((8, BW)), sds((8, 128))]
        + [sds((tokens // 2, width), bf16), sds((2, width // ways, units))] * own_links,
        scratch_shapes=[
            pltpu.VMEM((tokens + 8, BW), f32), pltpu.VMEM((tokens + 8, BW), f32),
            pltpu.VMEM((spans, Q, Q), f32), pltpu.VMEM((spans, Q, Q), f32),
            pltpu.VMEM((tokens, 128), f32), pltpu.VMEM((tokens, 128), f32),
            pltpu.VMEM((tokens, 128), f32), pltpu.VMEM((tokens, 128), f32), pltpu.VMEM((8, tokens), f32),
            pltpu.VMEM((HB * Q, Q), bf16), pltpu.VMEM((HB * Q, BW), bf16), pltpu.VMEM((HB * Q, Q), f32),
            pltpu.VMEM((BW, 128), f32),
            pltpu.VMEM((48, tokens), f32), pltpu.VMEM((48, tokens), f32), pltpu.VMEM((48, tokens), f32),
            pltpu.VMEM((48, tokens), f32), pltpu.VMEM((48, 128), f32), pltpu.VMEM((8, BW), f32),
        ] + ([sem, sem] + reduce_scratch(2, width // ways, units)) * own_links,
        compiler_params=params(4 if own_links else None),
        cost_estimate=pl.CostEstimate(flops=40_000_000_000, bytes_accessed=30_000_000, transcendentals=heads * spans * Q * Q),
    )(
        inner, dy, states, conv_inner, conv_state, decay_log, skip_gain, cst, bc, step, cum, step_t, cum_t, pre_t,
        *[mixed, grad_b] * own_links,
    )
    if own_links:
        mixed_got, wb_shard = sent
    else:
        mixed_got = swap(mixed_far)
        wb_shard = lax.psum_scatter(grad_b, "dp", scatter_dimension=1, tiled=True).astype(f32)
    output = (rows_in + mixed_near.astype(f32) + mixed_got.astype(f32)).astype(bf16)

    if own_links:
        grad_normed, wa_shard, small = reduce_tail(normed_t, dinner, dsd, dgate, wb, wa, (gk, ggg, gks, hs), ways, 5)
        wa_shard = wa_shard[0]
    else:
        last = jnp.concatenate([gks[:5].reshape(-1), hs[0], hs[1]])
        small = jnp.concatenate([gk[:6], ggg[:1], last[None]], axis=0)
        grad_a = jnp.concatenate([mm(normed_t, dinner).astype(bf16), mm(normed_t, dsd).astype(bf16)], axis=1)
        pulled = mm(dgate, wb[:, :units], 1, 1) + mm(dinner, wa[:, :units], 1, 1) + mm(dsd, wa[:, units:], 1, 1)
        near, far = halves(pulled.astype(bf16), 0)
        wa_shard = lax.psum_scatter(grad_a, "dp", scatter_dimension=0, tiled=True).astype(f32)
        small = lax.psum(small, "dp")
        grad_normed = near.astype(f32) + swap(far).astype(f32)
    grad_v = grad_normed * norm_gain
    grad_residual = cotangent.astype(f32) + rstd_in * (
        grad_v - scaled * jnp.mean(grad_v * scaled, axis=1, keepdims=True)
    )

    conv_state_sum = small[7, : 5 * BW].reshape(5, BW)
    bias_sum = gathered_heads(small[7, 5 * BW : 5 * BW + 128], heads)
    decay_sum = gathered_heads(small[7, 5 * BW + 128 : 5 * BW + 256], heads)
    skip_sum = jnp.sum(small[5].reshape(heads, HEAD), axis=1)

    gain_rows = jnp.sum(wb_shard[0] * w_gate_inner[0].astype(f32), axis=1) + jnp.sum(
        wa_shard * pack_a.astype(f32), axis=1
    )
    count = gain_rows.shape[0]
    gain_own = gain_rows / lax.dynamic_slice_in_dim(norm_gain, lax.axis_index("dp") * count, count)
    near_s, far_s = halves(jnp.concatenate([wa_shard[:, units : units + BW], conv_state_sum], axis=0), 1)
    near_g, far_g = halves(gain_own, 0)
    far_all = jnp.concatenate([far_s.reshape(-1), far_g])
    got = swap(far_all)
    both = near_s + got[: far_s.size].reshape(far_s.shape)
    gain_part = near_g + got[far_s.size :]
    return (
        output,
        grad_residual,
        gain_part,
        jnp.stack([wb_shard[0], wa_shard[:, :units]]),
        both[:count],
        gathered_heads(wa_shard[:, units + BW :], heads),
        small[0:5],
        both[count:],
        bias_sum,
        decay_sum,
        skip_sum,
        small[6],
        wb_shard[1].T,
    )


def solution(mesh):
    return jax.shard_map(
        on_device,
        mesh=mesh,
        in_specs=(
            P(("dp", "tensor"), None),
            P(),
            P(None, "dp", "tensor"),
            P("dp", None),
            P("dp", "tensor"),
            P(None, "tensor"),
            P(),
            P("tensor"),
            P("tensor"),
            P("tensor"),
            P("tensor"),
            P("tensor", "dp"),
            P(("dp", "tensor"), None),
        ),
        out_specs=(
            P(("dp", "tensor"), None),
            P(("dp", "tensor"), None),
            P(("dp", "tensor")),
            P(None, "dp", "tensor"),
            P("dp", "tensor"),
            P("dp", "tensor"),
            P(None, "tensor"),
            P(None, "tensor"),
            P("tensor"),
            P("tensor"),
            P("tensor"),
            P("tensor"),
            P("tensor", "dp"),
        ),
        check_vma=False,
    )
```

```python
import functools

import jax
import jax.numpy as jnp
from jax import lax
from jax.experimental import pallas as pl
from jax.experimental.pallas import tpu as pltpu
from jax.sharding import PartitionSpec as P

Q = 256
LEN = 1024
HEAD = 64
BW = 256
HB = BW // HEAD
LOG2E = 1.4426950408889634
FAR = -1e30
norm_eps = 1e-05
MESH = pl.DeviceIdType.MESH
f32 = jnp.float32
bf16 = jnp.bfloat16


def mm(a, b, ca=1, cb=0):
    return lax.dot_general(a, b, (((ca,), (cb,)), ((), ())), preferred_element_type=f32)


def sigmoid(v):
    return 1.0 / (1.0 + jnp.exp(-v))


def split3(a):
    hi = a.astype(bf16)
    rest = a - hi.astype(f32)
    mid = rest.astype(bf16)
    low = (rest - mid.astype(f32)).astype(bf16)
    return hi, mid, low


def split2(a):
    hi = a.astype(bf16)
    return hi, (a - hi.astype(f32)).astype(bf16)


def iota(shape, axis):
    return lax.broadcasted_iota(jnp.int32, shape, axis)


def expand(cols):
    rows = cols.shape[0]
    left = iota((rows, 128), 1) < HEAD
    return jnp.concatenate(
        [jnp.where(left, cols[:, 2 * q : 2 * q + 1], cols[:, 2 * q + 1 : 2 * q + 2]) for q in range(2)],
        axis=1,
    )


def conv_taps(window, kernel):
    out = kernel[4:5] + kernel[3:4] * window[8:]
    for k in range(3):
        out = out + kernel[k : k + 1] * pltpu.roll(window, 3 - k, 0)[8:]
    return out


def head_row(ref):
    return jnp.broadcast_to(ref[...][None, :], (8, ref.shape[0]))


def lay(rows, pick):
    parts = split3(rows)
    return mm(parts[0], pick) + mm(parts[1], pick) + mm(parts[2], pick)


def as_places(heads):
    lane = iota((heads, 128), 1)
    place = lane % 8
    return ((lane // 8 * HB + place == iota((heads, 128), 0)) & (place < HB)).astype(f32).astype(bf16)


def as_units(heads, block):
    return (iota((heads, BW), 1) // HEAD + HB * block == iota((heads, BW), 0)).astype(f32).astype(bf16)


def head_masks():
    lane = iota((1, BW), 1) // HEAD
    return [(lane == j).astype(f32).astype(bf16) for j in range(HB)]


def quads():
    for r in range(0, Q, 64):
        for half in range(2):
            if half * 128 <= r:
                yield r, half, r < half * 128 + 128


def decay_chunk(col, row, r, half, diag):
    gap = col[r : r + 64] - row[:, half * 128 : half * 128 + 128]
    if diag:
        keep = iota((64, 128), 0) + (r - half * 128) >= iota((64, 128), 1)
        gap = jnp.where(keep, gap, FAR)
    return jnp.exp2(gap)


def mixer_forward(links, normed, wi, wsx, kin, kst, bias, log_rate, skip_in, *refs):
    refs = list(refs)
    if links:
        sent = refs[:3] + refs[14:16]
        gain, gate_refs = refs[3], refs[16:19]
        refs = refs[4:14] + refs[19:]
    inner_out, ssd_out, states_out, cst_out, bc_out, step_out, cum_out, stepT_out, cumT_out, preT_out = refs[:10]
    buf, gram, colc, cols, rowp, mst, xst, state = refs[10:18]
    i = pl.program_id(0)
    tokens = normed.shape[0]
    spans = tokens // Q
    blocks = inner_out.shape[1] // BW
    if links:
        work = BesideForward(*sent, *refs[27:])
        ssd_v, *gate_scratch = refs[18:27]
        blocks = ssd_v.shape[0] - 1
    heads = bias.shape[0]
    skip = lay(head_row(skip_in), as_units(heads, i))[0:1]

    if links:
        pl.when(i == 0)(work.start)

    @pl.when(i == 0)
    def _():
        proj = mm(normed[...], wsx[...])
        buf[0:8] = jnp.zeros((8, BW), f32)
        cst_out[...] = proj[:, :BW]
        buf[8 : 8 + tokens] = proj[:, :BW]
        tri = (iota((Q, Q), 0) >= iota((Q, Q), 1)).astype(f32).astype(bf16)
        places = as_places(heads)
        pre = proj[:, BW:] + lay(head_row(bias), places)[0:1]
        step = jnp.maximum(pre, 0.0) + jnp.log1p(jnp.exp(-jnp.abs(pre)))
        step_out[...] = step
        scaled = step * (lay(-jnp.exp(head_row(log_rate)), places)[0:1] * LOG2E)
        for s in range(spans):
            parts = split3(scaled[s * Q : s * Q + Q])
            cum_out[s * Q : s * Q + Q] = mm(tri, parts[0]) + mm(tri, parts[1]) + mm(tri, parts[2])
            conv = conv_taps(buf[s * Q : s * Q + Q + 8], kst[...])
            bc = (conv * sigmoid(conv)).astype(bf16)
            bc_out[s * Q : s * Q + Q] = bc
            gram[s] = mm(bc[:, 128:], bc[:, :128], 1, 1)
        preT_out[...] = jnp.transpose(pre)[:48]
        stepT_out[...] = jnp.transpose(step)[:48]
        cumT_out[...] = jnp.transpose(cum_out[...])[:48]
        mst[...] = jnp.zeros(mst.shape, bf16)

    def mix():
        inner = mm(normed[...], wi[...])
        inner_out[...] = inner
        buf[8 : 8 + tokens] = inner
        turn = lax.rem(128 - 8 * i, 128)
        colc[...] = pltpu.roll(cum_out[...], turn, 1)
        cols[...] = pltpu.roll(step_out[...], turn, 1)
        rows8 = pl.ds(pl.multiple_of(8 * i, 8), 8)
        rowp[...] = cumT_out[rows8] - jnp.log2(stepT_out[rows8])
        state[...] = jnp.zeros(state.shape, f32)
        masks = head_masks()

        def span(s, carry):
            at = pl.multiple_of(s * Q, Q)
            rows = pl.ds(at, Q)
            conv = conv_taps(buf[pl.ds(at, Q + 8)], kin[...])
            xs = conv * sigmoid(conv)
            x_low = xs.astype(bf16)
            col = colc[rows]
            total = col[Q - 1 : Q]
            growth = expand(jnp.exp2(col[:, :8]))
            weight = expand(jnp.exp2(total[:, :8] - col[:, :8]) * cols[rows][:, :8])
            xw_low = (xs * weight).astype(bf16)
            for j in range(HB):
                xst[j * Q : j * Q + Q] = x_low * masks[j]
                row = rowp[j : j + 1, rows]
                for r, half, diag in quads():
                    part = gram[s, r : r + 64, half * 128 : half * 128 + 128]
                    dec = decay_chunk(col[:, j : j + 1], row, r, half, diag)
                    mst[r : r + 64, j * Q + half * 128 : j * Q + half * 128 + 128] = (part * dec).astype(bf16)
            intra = mm(mst[...], xst[...])
            state_in = state[...]
            states_out[s] = state_in
            bc = bc_out[rows]
            readout = mm(bc[:, 128:], state_in.astype(bf16), 1, 1)
            ssd = intra + growth * readout + skip * xs
            ssd_out[rows] = ssd
            if links:
                ssd_v[blocks, rows] = ssd
            local = mm(xw_low, bc[:, :128], 0, 0)
            fade = jnp.exp2(total)
            for j in range(HB):
                at_j = slice(j * HEAD, j * HEAD + HEAD)
                state[at_j] = fade[:, j : j + 1] * state_in[at_j] + local[at_j]
            if links:
                work.step(i * spans + s)
            return carry

        lax.fori_loop(0, spans, span, 0)

    if not links:
        mix()
        return
    pl.when(i < blocks)(mix)

    @pl.when(i < blocks)
    def _():
        ssd_v[i] = ssd_v[blocks]

    gates = GateForward(i - blocks, blocks, normed, sent[3], sent[4], gain, ssd_v, *gate_refs, *gate_scratch)

    @pl.when(i == blocks)
    def _():
        work.first()
        gates.start(0)

    pl.when((i >= blocks) & (i < 2 * blocks))(gates.gate)

    @pl.when(i == 2 * blocks)
    def _():
        work.finish()
        gates.start(1)

    pl.when(i >= 2 * blocks)(gates.pull)


class GateForward:
    def __init__(
        self, at, blocks, normed, cot, wb, gain, ssd_v, gate_out, ggo_out, stats_out, w_v, cot_v, sq, gi, mine, landed, wl, cl
    ):
        self.at, self.blocks, self.normed, self.cot, self.wb, self.gain, self.ssd_v = at, blocks, normed, cot, wb, gain, ssd_v
        self.gate_out, self.ggo_out, self.stats_out = gate_out, ggo_out, stats_out
        self.w_v, self.cot_v, self.sq, self.gi, self.mine, self.landed, self.wl, self.cl = w_v, cot_v, sq, gi, mine, landed, wl, cl

    def load(self, which, n):
        cols = slice((which * self.blocks + n) * BW, (which * self.blocks + n + 1) * BW)
        return pltpu.make_async_copy(self.wb.at[:, cols], self.w_v.at[n], self.wl.at[n])

    def tokens(self):
        return pltpu.make_async_copy(self.cot, self.cot_v, self.cl.at[0])

    def start(self, which):
        if which:
            self.tokens().start()
        for n in range(self.blocks):
            self.load(which, n).start()
        if which:
            self.tokens().wait()
        total = self.gi if which else self.sq
        total[...] = jnp.zeros(total.shape, f32)

    def gate(self):
        b = self.at
        pltpu.make_async_copy(self.wb.at[:, :BW], self.w_v.at[b], self.wl.at[b]).wait()
        gate = mm(self.normed[...], self.w_v[b])
        self.gate_out[...] = gate
        gated = self.ssd_v[b] * (gate * sigmoid(gate))
        self.ssd_v[b] = gated
        squares = gated * gated
        self.sq[...] += squares[:, :128] + squares[:, 128:]

    def pull(self):
        b = self.at - self.blocks
        pltpu.make_async_copy(self.wb.at[:, :BW], self.w_v.at[b], self.wl.at[b]).wait()
        ggo = mm(self.cot_v[...], self.w_v[b])
        self.ggo_out[...] = ggo
        inner = ggo * self.gain[0:1] * self.ssd_v[b]
        self.gi[...] += inner[:, :128] + inner[:, 128:]
        pl.when(b == self.blocks - 1)(self.last)

    def last(self):
        self.mine[...] = token_sums(self.sq[...], self.gi[...])
        swap = remote(self.mine, self.landed, self.cl.at[1], self.cl.at[2], tensor=1 - lax.axis_index("tensor"))
        swap.start()
        swap.wait()
        self.stats_out[...] = self.mine[...] + self.landed[...]


def token_sums(sq, gi):
    lane = iota(sq.shape, 1)
    both = jnp.where(
        lane == 0,
        jnp.sum(sq, axis=1, keepdims=True),
        jnp.where(lane == 1, jnp.sum(gi, axis=1, keepdims=True), 0.0),
    )
    return jnp.transpose(both)[:8]


class BesideForward:
    def __init__(self, cot, w_gate_inner, w_output_t, cot_out, wb, ss, rs, ls, xs, xr, xl):
        self.here = Place()
        units = w_output_t.shape[1]
        self.moves = [
            Gather(self.here, own, wb, ss, rs, ls, n, slice(n * units, n * units + units))
            for n, own in enumerate((w_gate_inner.at[0], w_output_t))
        ]
        half = lax.axis_index("tensor")
        rows = cot.shape[0]
        slot = cot_out.at[pl.ds(pl.multiple_of(half * rows, rows), rows)]
        self.across = remote(cot, slot, xs, xr, tensor=1 - half)
        self.local = pltpu.make_async_copy(cot, slot, xl)

    def start(self):
        greet(self.here, True)
        self.moves[0].start()
        self.across.start()
        self.local.start()

    def step(self, at):
        for when, chunk, hops in ((4, 0, 1), (9, 0, 2), (15, 0, 3), (19, 1, 1)):

            def go(move=self.moves[chunk], chunk=chunk, hops=hops):
                move.hop(hops)
                move.sides(hops - 1)
                if chunk == 0 and hops == 2:
                    self.moves[1].start()

            pl.when(at == when)(go)

    def first(self):
        self.moves[0].sides(3)
        self.moves[1].hop(2)
        self.moves[0].finish()

    def finish(self):
        move = self.moves[1]
        move.sides(1)
        move.hop(3)
        move.sides(2)
        move.sides(3)
        move.finish()
        self.local.wait()
        self.across.wait()


def gate_forward(normed, cot, wg, wo, ssd, gain, gate_out, ggo_out, stats_out, sq, gi):
    i = pl.program_id(0)

    @pl.when(i == 0)
    def _():
        sq[...] = jnp.zeros(sq.shape, f32)
        gi[...] = jnp.zeros(gi.shape, f32)

    gate = mm(normed[...], wg[...])
    gate_out[...] = gate
    ggo = mm(cot[...], wo[...])
    ggo_out[...] = ggo
    gated = ssd[...] * (gate * sigmoid(gate))
    squares = gated * gated
    sq[...] += squares[:, :128] + squares[:, 128:]
    inner = ggo * gain[0:1] * gated
    gi[...] += inner[:, :128] + inner[:, 128:]

    @pl.when(i == pl.num_programs(0) - 1)
    def _():
        stats_out[...] = token_sums(sq[...], gi[...])


def gate_backward(
    unit_total, stats, gate, ssd, ggo, gain, normed, cot, dy_out, dgate_out, ng_out, gg_out, grads_out, normed_t, cols, cot_t
):
    @pl.when(pl.program_id(0) == 0)
    def _():
        full = jnp.concatenate([stats[...], jnp.zeros((120, stats.shape[1]), f32)], axis=0)
        cols[...] = jnp.transpose(full)

        def turn(n, carry):
            here = pl.ds(pl.multiple_of(n * 128, 128), 128)
            normed_t[here] = jnp.transpose(normed[:, here])
            cot_t[here] = jnp.transpose(cot[:, here])
            return carry

        lax.fori_loop(0, normed.shape[1] // 128, turn, 0)

    rstd = lax.rsqrt(cols[:, 0:1] / unit_total + norm_eps)
    pull = rstd * rstd * rstd * (cols[:, 1:2] / unit_total)
    v = gate[...]
    sig = sigmoid(v)
    act = v * sig
    y = ssd[...]
    gated = y * act
    scaled = gated * rstd
    ng = (scaled * gain[0:1]).astype(bf16)
    ng_out[...] = ng
    grads_out[1] = mm(cot_t[...], ng).astype(bf16)
    gg = ggo[...]
    gg_out[...] = jnp.broadcast_to(jnp.sum(gg * scaled, axis=0, keepdims=True), gg_out.shape)
    grad = rstd * (gg * gain[0:1]) - gated * pull
    dy_out[...] = (grad * act).astype(bf16)
    dgate = (grad * y * (sig * (1.0 + v * (1.0 - sig)))).astype(bf16)
    dgate_out[...] = dgate
    grads_out[0] = mm(normed_t[...], dgate).astype(bf16)


class BesideBackward:
    def __init__(self, mixed, grads, far_out, shard_out, scratch):
        self.here = Place()
        half = lax.axis_index("tensor")
        rows = far_out.shape[0]
        other = mixed.at[pl.ds(pl.multiple_of((1 - half) * rows, rows), rows)]
        self.across = remote(other, far_out, scratch[0], scratch[1], tensor=1 - half)
        self.sum = Reduce(self.here, grads, shard_out, scratch[2:7], scratch[7:15])

    def start(self):
        greet(self.here, True)
        self.sum.start()
        self.across.start()

    def step(self, at):
        total = self.sum
        z = self.here.z
        ends = (z == 0) | (z == 3)
        for n, block in enumerate(total.order):
            pl.when(at == n)(lambda z=block: total.cores(z))
            pl.when(at == (4, 5, 7, 8)[n])(lambda z=block: total.stay(z))
            pl.when(at == (6, 11, 17, 22)[n])(lambda z=block: total.sides(z))
        for n, block in enumerate(total.order[:3]):
            when = jnp.where(ends, (6, 11, 17)[n], (12, 18, 19)[n])
            pl.when(at == when)(lambda z=block: total.pass_on(z))

    def finish(self):
        self.sum.finish()
        self.across.wait()


def mixer_backward(links, inner, dy, states, kin, kst, log_rate, skip_in, cst, bc_in, step_in, cum_in, stepT, cumT, preT, *refs):
    refs = list(refs)
    if links:
        beside = refs[:2] + refs[7:9]
        refs = refs[2:7] + refs[9:]
        work = BesideBackward(*beside, refs[24:])
    dinner_out, gk_out, dsd_out, gks_out, hs_out = refs[:5]
    buf, dbuf, gram, gg, gb, gc, colc, cols, rowp, mst, dyst, gmix, sgrad = refs[5:18]
    rs_t, cs_t, dr_t, wg_t, gt_t, gtaps = refs[18:24]
    i = pl.program_id(0)
    if links:
        pl.when(i == 0)(work.start)
    heads = log_rate.shape[0]
    skip = lay(head_row(skip_in), as_units(heads, i))[0:1]
    tokens = inner.shape[0]
    spans = tokens // Q
    masks = head_masks()

    @pl.when(i == 0)
    def _():
        buf[0:8] = jnp.zeros((8, BW), f32)
        dbuf[tokens : tokens + 8] = jnp.zeros((8, BW), f32)
        for s in range(spans):
            bc = bc_in[s * Q : s * Q + Q]
            gram[s] = mm(bc[:, 128:], bc[:, :128], 1, 1)
        for ref in (gg, gb, gc, rs_t, cs_t, dr_t, wg_t, gt_t):
            ref[...] = jnp.zeros(ref.shape, f32)
        mst[...] = jnp.zeros(mst.shape, bf16)

    buf[8 : 8 + tokens] = inner[...]
    turn = lax.rem(128 - 8 * i, 128)
    colc[...] = pltpu.roll(cum_in[...], turn, 1)
    cols[...] = pltpu.roll(step_in[...], turn, 1)
    rows8 = pl.ds(pl.multiple_of(8 * i, 8), 8)
    rowp[...] = cumT[rows8] - jnp.log2(stepT[rows8])
    sgrad[...] = jnp.zeros(sgrad.shape, f32)
    gtaps[...] = jnp.zeros(gtaps.shape, f32)
    pick = (iota((8, BW), 1) // HEAD == iota((8, BW), 0)).astype(f32).astype(bf16)

    def conv_rows(at, kernel, grad_act, conv, sig):
        gco = grad_act * (sig * (1.0 + conv * (1.0 - sig)))
        dbuf[pl.ds(at, Q)] = gco
        into = buf[pl.ds(pl.multiple_of(at + 8, 8), Q)]
        gtaps[4:5] += jnp.sum(gco, axis=0, keepdims=True)
        after = dbuf[pl.ds(at, Q + 8)]
        grad_in = kernel[3:4] * gco
        gtaps[3:4] += jnp.sum(gco * into, axis=0, keepdims=True)
        for k in range(3):
            later = pltpu.roll(after, Q + 8 - (3 - k), 0)[:Q]
            gtaps[k : k + 1] += jnp.sum(later * into, axis=0, keepdims=True)
            grad_in = grad_in + kernel[k : k + 1] * later
        return grad_in

    def span(back, carry):
        s = spans - 1 - back
        at = pl.multiple_of(s * Q, Q)
        rows = pl.ds(at, Q)
        conv = conv_taps(buf[pl.ds(at, Q + 8)], kin[...])
        sig = sigmoid(conv)
        xs = conv * sig
        x_low = xs.astype(bf16)
        dy_s = dy[rows]
        dy_f = dy_s.astype(f32)
        bc = bc_in[rows]
        b_low, c_low = bc[:, :128], bc[:, 128:]
        col = colc[rows]
        total = col[Q - 1 : Q]
        for j in range(HB):
            dyst[j * Q : j * Q + Q] = dy_s * masks[j]
        gmix[...] = mm(dyst[...], x_low, 1, 1)
        lane = iota((Q, 128), 1)
        row_sums = jnp.zeros((Q, 128), f32)
        for j in range(HB):
            row = rowp[j : j + 1, rows]
            col_sum = [jnp.zeros((1, 128), f32), jnp.zeros((1, 128), f32)]
            row_parts = []
            for r, half, diag in quads():
                here = slice(half * 128, half * 128 + 128)
                dec = decay_chunk(col[:, j : j + 1], row, r, half, diag)
                part = gram[s, r : r + 64, here]
                p = gmix[j * Q + r : j * Q + r + 64, here] * dec
                gg[s, r : r + 64, here] += p
                q = p * part
                mst[j * Q + r : j * Q + r + 64, here] = (part * dec).astype(bf16)
                col_sum[half] = col_sum[half] + jnp.sum(q, axis=0, keepdims=True)
                if half == 0:
                    row_parts.append(q)
                else:
                    row_parts[-1] = row_parts[-1] + q
            sums = jnp.concatenate([jnp.sum(q, axis=1, keepdims=True) for q in row_parts], axis=0)
            row_sums = jnp.where(lane == j, sums, row_sums)
            cs_t[pl.ds(8 * i + j, 1), rows] = jnp.concatenate(col_sum, axis=1)
        rs_t[rows8, rows] = jnp.transpose(row_sums)[:8]
        grad_xs = mm(mst[...], dyst[...], 0, 0) + skip * dy_f

        growth = expand(jnp.exp2(col[:, :8]))
        weight = expand(jnp.exp2(total[:, :8] - col[:, :8]) * cols[rows][:, :8])
        state_in = states[s]
        state_low = state_in.astype(bf16)
        state_grad = sgrad[...]
        carry_low = state_grad.astype(bf16)
        readout = mm(c_low, state_low, 1, 1)
        read_low = (dy_f * growth).astype(bf16)
        hi, low = split2(dy_f * readout)
        dr_t[rows8, rows] = mm(pick, hi, 1, 1) + mm(pick, low, 1, 1)
        gc[rows] += mm(read_low, state_low)
        grad_xw = mm(b_low, carry_low, 1, 1)
        xw_low = (xs * weight).astype(bf16)
        gb[rows] += mm(xw_low, carry_low)
        hi, low = split2(grad_xw * xs)
        wg_t[rows8, rows] = mm(pick, hi, 1, 1) + mm(pick, low, 1, 1)
        hi, low = split2(state_grad * state_in)
        sums = jnp.sum(mm(pick, hi) + mm(pick, low), axis=1, keepdims=True)
        gt_t[rows8] = jnp.where(iota((8, 128), 1) == s, sums, gt_t[rows8])
        grad_xs = grad_xs + grad_xw * weight
        local = mm(read_low, c_low, 0, 0)
        fade = jnp.exp2(total)
        for j in range(HB):
            at_j = slice(j * HEAD, j * HEAD + HEAD)
            sgrad[at_j] = fade[:, j : j + 1] * state_grad[at_j] + local[at_j]
        gtaps[5:6] += jnp.sum(dy_f * xs, axis=0, keepdims=True)
        dinner_out[rows] = conv_rows(at, kin[...], grad_xs, conv, sig).astype(bf16)
        if links:
            work.step(i * spans + back)
        return carry

    lax.fori_loop(0, spans, span, 0)
    gk_out[...] = gtaps[...]

    @pl.when(i == pl.num_programs(0) - 1)
    def _():
        buf[8 : 8 + tokens] = cst[...]
        gtaps[...] = jnp.zeros(gtaps.shape, f32)
        rates = lay(-jnp.exp(head_row(log_rate)), as_places(heads))[0:1]
        rate = jnp.transpose(jnp.broadcast_to(rates, (128, 128)))[:48, 0:1]
        later = (iota((Q, Q), 0) >= iota((Q, Q), 1)).astype(f32).astype(bf16)
        last = iota((48, Q), 1) == Q - 1
        bias_sum = jnp.zeros((48, 1), f32)
        decay_sum = jnp.zeros((48, 1), f32)
        for back in range(spans):
            s = spans - 1 - back
            rows = slice(s * Q, s * Q + Q)
            bc = bc_in[rows]
            gl = gg[s].astype(bf16)
            grad_c = gc[rows] + mm(gl, bc[:, :128])
            grad_b = gb[rows] + mm(gl, bc[:, 128:], 0, 0)
            both = jnp.concatenate([grad_b, grad_c], axis=1)
            conv = conv_taps(buf[s * Q : s * Q + Q + 8], kst[...])
            dsd_out[rows, :BW] = conv_rows(s * Q, kst[...], both, conv, sigmoid(conv)).astype(bf16)

            cum, step, pre = cumT[:, rows], stepT[:, rows], preT[:, rows]
            total = cum[:, Q - 1 : Q]
            rate_w = jnp.exp2(total - cum)
            wg = wg_t[:, rows]
            cs = cs_t[:, rows]
            moved = wg * (rate_w * step)
            grad_cum = rs_t[:, rows] - cs + jnp.exp2(cum) * dr_t[:, rows] - moved
            grad_total = jnp.exp2(total) * gt_t[:, s : s + 1] + jnp.sum(moved, axis=1, keepdims=True)
            grad_cum = grad_cum + jnp.where(last, grad_total, 0.0)
            parts = split3(grad_cum)
            grad_rate = mm(parts[0], later) + mm(parts[1], later) + mm(parts[2], later)
            sig = sigmoid(pre)
            ratio = jnp.where(pre < -15.0, 1.0, sig / step)
            grad_pre = (wg * rate_w + grad_rate * rate) * sig + cs * ratio
            bias_sum = bias_sum + jnp.sum(grad_pre, axis=1, keepdims=True)
            decay_sum = decay_sum + jnp.sum(grad_rate * step, axis=1, keepdims=True)
            full = jnp.concatenate([grad_pre, jnp.zeros((80, Q), f32)], axis=0)
            dsd_out[rows, BW:] = jnp.transpose(full).astype(bf16)
        gks_out[...] = gtaps[...]
        lane = iota((48, 128), 1)
        both = jnp.where(lane == 0, bias_sum, jnp.where(lane == 1, decay_sum * rate, 0.0))
        hs_out[...] = jnp.transpose(jnp.concatenate([both, jnp.zeros((80, 128), f32)], axis=0))[:8]
        if links:
            work.finish()


class Place:
    def __init__(self):
        me = lax.axis_index("dp")
        self.me = me
        self.c, self.y, self.z = me % 2, (me // 2) % 2, me // 4

    def at(self, z, y, c):
        return (z * 2 + y) * 2 + c

    def core(self):
        return self.at(self.z, self.y, 1 - self.c)

    def side(self):
        return self.at(self.z, 1 - self.y, self.c)

    def up(self):
        return self.me + 4

    def down(self):
        return self.me - 4


def greet(here, across):
    barrier = pltpu.get_barrier_semaphore()

    def signal(**device):
        pl.semaphore_signal(barrier, 1, device_id=device, device_id_type=MESH)

    signal(dp=here.core())
    signal(dp=here.side())
    pl.when(here.z < 3)(lambda: signal(dp=here.up()))
    pl.when(here.z > 0)(lambda: signal(dp=here.down()))
    if across:
        signal(tensor=1 - lax.axis_index("tensor"))
    ends = (here.z == 0).astype(jnp.int32) + (here.z == 3).astype(jnp.int32)
    pl.semaphore_wait(barrier, 4 + int(across) - ends)


def remote(src, dst, send_sem, recv_sem, **device):
    return pltpu.make_async_remote_copy(
        src_ref=src, dst_ref=dst, send_sem=send_sem, recv_sem=recv_sem, device_id=device, device_id_type=MESH
    )


class Gather:
    def __init__(self, here, own, full, ss, rs, ls, chunk, cols):
        self.here, self.full, self.ss, self.rs, self.chunk, self.cols = here, full, ss, rs, chunk, cols
        self.rows = own.shape[0]
        self.own = own
        self.local = pltpu.make_async_copy(own, self.slot(here.me), ls.at[chunk])

    def slot(self, origin):
        return self.full.at[pl.ds(pl.multiple_of(origin * self.rows, self.rows), self.rows), self.cols]

    def copy(self, origin, way, src=None):
        here = self.here
        target = (here.up, here.down, here.side, here.core)[way]()
        slot = self.slot(origin)
        sems = self.ss.at[self.chunk, origin, way], self.rs.at[self.chunk, origin]
        return remote(slot if src is None else src, slot, *sems, dp=target)

    def arrived(self, origin):
        self.copy(origin, 3).wait_recv()

    def each_send(self, act):
        here = self.here
        for hops in range(4):
            for way, origin_z in ((0, here.z - hops), (1, here.z + hops)):
                if hops == 0:
                    if way == 1:
                        continue
                    origin = here.me
                    pl.when(here.z < 3)(lambda o=origin: act(o, 0))
                    pl.when(here.z > 0)(lambda o=origin: act(o, 1))
                    act(origin, 2)
                    act(origin, 3)
                    continue
                origin = here.at(origin_z, here.y, here.c)

                def go(o=origin, way=way):
                    pl.when((here.z < 3) if way == 0 else (here.z > 0))(lambda: act(o, way))
                    act(o, 2)
                    act(o, 3)

                pl.when((origin_z >= 0) & (origin_z <= 3))(go)

    def start(self):
        here = self.here
        pl.when(here.z < 3)(lambda: self.copy(here.me, 0, self.own).start())
        pl.when(here.z > 0)(lambda: self.copy(here.me, 1, self.own).start())
        self.copy(here.me, 2, self.own).start()
        self.copy(here.me, 3, self.own).start()
        self.local.start()

    def hop(self, hops):
        here = self.here
        for way, origin_z in ((0, here.z - hops), (1, here.z + hops)):

            def go(way=way, origin_z=origin_z):
                origin = here.at(origin_z, here.y, here.c)
                self.arrived(origin)
                pl.when((here.z < 3) if way == 0 else (here.z > 0))(lambda: self.copy(origin, way).start())
                self.copy(origin, 2).start()
                self.copy(origin, 3).start()

            pl.when((origin_z >= 0) & (origin_z <= 3))(go)

    def sides(self, hops):
        here = self.here
        for way, origin_z in ((0, here.z - hops), (1, here.z + hops)):
            if hops == 0 and way == 1:
                continue

            def go(origin_z=origin_z):
                origin = here.at(origin_z, 1 - here.y, here.c)
                self.arrived(origin)
                self.copy(origin, 3).start()

            pl.when((origin_z >= 0) & (origin_z <= 3))(go)

    def finish(self):
        here = self.here
        self.local.wait()
        for z in range(4):
            for y in range(2):
                self.arrived(here.at(z, y, 1 - here.c))
        self.each_send(lambda origin, way: self.copy(origin, way).wait_send())
        for z in range(4):
            self.copy(here.at(z, 1 - here.y, here.c), 3).wait_send()


def gather_scratch():
    sem = pltpu.SemaphoreType.DMA
    return [sem((2, 16, 4)), sem((2, 16)), sem((2,))]


def gather_kernel(tokens_in, gain, w_gate_inner, w_state_io, w_step, tokens_out, full, pack, low, ss, rs, ls, xs, xr, xl):
    here = Place()
    half = lax.axis_index("tensor")
    rows = tokens_in.shape[0]
    units, cols = w_gate_inner.shape[2], full.shape[1]
    pack[:, :units] = w_gate_inner[1]
    pack[:, units : units + BW] = w_state_io[...]
    pack[:, units + BW :] = mm(w_step[...], as_places(w_step.shape[1])).astype(bf16)
    greet(here, True)
    cut = cols // 256 * 128
    moves = [
        Gather(here, pack.at[:, c], full, ss, rs, ls, n, c) for n, c in enumerate((slice(0, cut), slice(cut, cols)))
    ]
    for move in moves:
        move.start()
    part = rows // 4
    across, local = [], []
    for n in range(4):
        piece = slice(n * part, n * part + part)
        v = tokens_in[piece].astype(f32)
        scale = lax.rsqrt(jnp.mean(v * v, axis=1, keepdims=True) + norm_eps)
        low[piece] = (v * scale * gain[0:1]).astype(bf16)
        slot = tokens_out.at[pl.ds(pl.multiple_of(half * rows + n * part, part), part)]
        across.append(remote(low.at[piece], slot, xs.at[n], xr.at[n], tensor=1 - half))
        across[-1].start()
        local.append(pltpu.make_async_copy(low.at[piece], slot, xl.at[n]))
        local[-1].start()
    for hops in range(1, 5):
        for move in moves:
            if hops < 4:
                move.hop(hops)
            move.sides(hops - 1)
    for n in range(4):
        local[n].wait()
        across[n].wait()
    for move in moves:
        move.finish()


def gather_rows(tokens_in, gain, w_gate_inner, w_state_io, w_step, ways, collective_id):
    rows, width = tokens_in.shape
    _, own, units = w_gate_inner.shape
    cols = units + BW + 128
    vmem = pl.BlockSpec(memory_space=pltpu.VMEM)
    hbm = pl.BlockSpec(memory_space=pl.ANY)
    sem = pltpu.SemaphoreType.DMA
    return pl.pallas_call(
        gather_kernel,
        name="gather_rows",
        in_specs=[vmem] * 5,
        out_specs=[hbm, hbm],
        out_shape=[sds((2 * rows, width), bf16), sds((ways * own, cols), bf16)],
        scratch_shapes=[
            pltpu.VMEM((own, cols), bf16), pltpu.VMEM((rows, width), bf16), *gather_scratch(),
            sem((4,)), sem((4,)), sem((4,)),
        ],
        compiler_params=pltpu.CompilerParams(
            collective_id=collective_id, has_side_effects=True, vmem_limit_bytes=60 * 1024 * 1024
        ),
    )(tokens_in, gain, w_gate_inner, w_state_io, w_step)


class Reduce:
    def __init__(self, here, grads, out, bufs, sems):
        self.here, self.grads, self.out = here, grads, out
        self.held, self.buf_a, self.buf_b, self.buf_up, self.buf_dn = bufs
        self.local, self.send_a, self.recv_a, self.send_b, self.recv_b, self.send_c, self.recv_up, self.recv_dn = sems
        self.parts, self.rows = out.shape[:2]
        z = here.z
        self.order = (3 * (1 - z // 2), (3 * z + 2) % 5, 1 + z % 2, z)

    def spot(self, z, y, c):
        if self.grads is None:
            return z, (y * 2 + c) * self.rows
        return z * 2 + y, 0

    def own(self, z, y, c=None):
        at, base = self.spot(z, y, self.here.c if c is None else c)
        return self.held.at[at, :, pl.ds(pl.multiple_of(base, 16), self.rows)]

    def block(self, z, y, c):
        if self.grads is None:
            return self.own(z, y, c)
        at = pl.multiple_of(self.here.at(z, y, c) * self.rows, self.rows)
        return self.grads.at[:, pl.ds(at, self.rows)]

    def copy_a(self, z, y):
        here, at = self.here, z * 2 + y
        return remote(self.block(z, y, 1 - here.c), self.buf_a.at[at], self.send_a.at[at], self.recv_a.at[at], dp=here.core())

    def take(self, z, y):
        return pltpu.make_async_copy(self.block(z, y, self.here.c), self.own(z, y), self.local.at[z * 2 + y])

    def copy_b(self, z):
        here = self.here
        return remote(self.own(z, 1 - here.y), self.buf_b.at[z], self.send_b.at[z], self.recv_b.at[z], dp=here.side())

    def copy_up(self, z):
        return remote(self.own(z, self.here.y), self.buf_up.at[z], self.send_c.at[z], self.recv_up.at[z], dp=self.here.up())

    def copy_dn(self, z):
        return remote(self.own(z, self.here.y), self.buf_dn.at[z], self.send_c.at[z], self.recv_dn.at[z], dp=self.here.down())

    def add(self, z, y, buf, slot):
        at, base = self.spot(z, y, self.here.c)

        def rows(n, carry):
            piece = pl.ds(pl.multiple_of(n * 16, 16), 16)
            held = pl.ds(pl.multiple_of(base + n * 16, 16), 16)
            for part in range(self.parts):
                total = self.held[at, part, held].astype(f32) + buf[slot, part, piece].astype(f32)
                self.held[at, part, held] = total.astype(bf16)
            return carry

        lax.fori_loop(0, self.rows // 16, rows, 0)

    def start(self):
        here = self.here
        for side in (1 - here.y, here.y):
            for z in self.order:
                self.copy_a(z, side).start()
                self.take(z, side).start()

    def join(self, z, y):
        if self.grads is not None:
            self.take(z, y).wait()
        self.copy_a(z, y).wait_recv()
        self.add(z, y, self.buf_a, z * 2 + y)

    def cores(self, z):
        self.join(z, 1 - self.here.y)
        self.copy_b(z).start()

    def stay(self, z):
        self.join(z, self.here.y)

    def sides(self, z):
        self.copy_b(z).wait_recv()
        self.add(z, self.here.y, self.buf_b, z)

    def pass_on(self, z):
        here = self.here

        def up():
            def below():
                self.copy_up(z).wait_recv()
                self.add(z, here.y, self.buf_up, z)

            pl.when(here.z > 0)(below)
            self.copy_up(z).start()

        def down():
            def above():
                self.copy_dn(z).wait_recv()
                self.add(z, here.y, self.buf_dn, z)

            pl.when(here.z < 3)(above)
            self.copy_dn(z).start()

        pl.when(z > here.z)(up)
        pl.when(z < here.z)(down)

    def finish(self):
        here = self.here
        z = here.z
        at, base = self.spot(z, here.y, here.c)
        pl.when(z > 0)(lambda: self.copy_up(z).wait_recv())
        pl.when(z < 3)(lambda: self.copy_dn(z).wait_recv())

        def rows(n, carry):
            piece = pl.ds(pl.multiple_of(n * 16, 16), 16)
            held = pl.ds(pl.multiple_of(base + n * 16, 16), 16)
            for part in range(self.parts):
                below = jnp.where(z > 0, self.buf_up[z, part, piece].astype(f32), 0.0)
                above = jnp.where(z < 3, self.buf_dn[z, part, piece].astype(f32), 0.0)
                self.out[part, piece] = self.held[at, part, held].astype(f32) + below + above
            return carry

        lax.fori_loop(0, self.rows // 16, rows, 0)
        for zn in self.order:
            self.copy_a(zn, 0).wait_send()
            self.copy_a(zn, 1).wait_send()
            self.copy_b(zn).wait_send()
            pl.when(zn > z)(lambda zn=zn: self.copy_up(zn).wait_send())
            pl.when(zn < z)(lambda zn=zn: self.copy_dn(zn).wait_send())


def reduce_scratch(parts, rows, cols, by_z=False):
    sem = pltpu.SemaphoreType.DMA
    block = (parts, rows, cols)
    held = (4, parts, 4 * rows, cols) if by_z else (8,) + block
    return [
        pltpu.VMEM(held, bf16), pltpu.VMEM((8,) + block, bf16), pltpu.VMEM((4,) + block, bf16),
        pltpu.VMEM((4,) + block, bf16), pltpu.VMEM((4,) + block, bf16),
        sem((8,)), sem((8,)), sem((8,)), sem((4,)), sem((4,)), sem((4,)), sem((4,)), sem((4,)),
    ]


def tail_kernel(
    normed_t, dinner, dsd, dgate, wb, wa, gk, ggg, gks, hs, gn_out, shard_out, small_out,
    nt_v, dinner_v, dsd_v, dgate_v, wg_v, wa_v, away, came, total, landed, loads, send_x, recv_x, send, recv, *scratch,
):
    here = Place()
    half = lax.axis_index("tensor")
    units = dgate.shape[1]
    sources = (normed_t, dinner, dsd, dgate, wb.at[:, :units], wa)
    pending = [
        pltpu.make_async_copy(src, dst, loads.at[n])
        for n, (src, dst) in enumerate(zip(sources, (nt_v, dinner_v, dsd_v, dgate_v, wg_v, wa_v)))
    ]
    for copy in pending:
        copy.start()
    far = pltpu.get_barrier_semaphore()
    partners = [here.me + bit - 2 * bit * ((here.me // bit) % 2) for bit in (2, 4, 8, 1)]
    for partner in partners:
        pl.semaphore_signal(far, 1, device_id={"dp": partner}, device_id_type=MESH)
    pl.semaphore_signal(far, 1, device_id={"tensor": 1 - half}, device_id_type=MESH)
    middle = (here.z == 1) | (here.z == 2)
    pl.when(here.z == 1)(lambda: pl.semaphore_signal(far, 1, device_id={"dp": here.up()}, device_id_type=MESH))
    pl.when(here.z == 2)(lambda: pl.semaphore_signal(far, 1, device_id={"dp": here.down()}, device_id_type=MESH))
    pl.semaphore_wait(far, 5 + middle.astype(jnp.int32))
    work = Reduce(here, None, shard_out, scratch[:5], scratch[5:])
    order = work.order
    rows = gn_out.shape[0]
    chunks, _, wide = away.shape

    def swap(k):
        return remote(total.at[k], landed.at[k], send.at[k], recv.at[k], dp=partners[k])

    def swapped(k):
        swap(k).wait()
        total[k + 1] = total[k] + landed[k]
        if k < 3:
            swap(k + 1).start()

    def across(n):
        return remote(away.at[n], came.at[n], send_x.at[n], recv_x.at[n], tensor=1 - half)

    def pulled(which, n):
        mine = pl.ds(pl.multiple_of(which * rows, rows), rows)
        at = pl.ds(pl.multiple_of(n * wide, wide), wide)
        return (
            mm(dgate_v[mine], wg_v[at], 1, 1)
            + mm(dinner_v[mine], wa_v[at, :units], 1, 1)
            + mm(dsd_v[mine], wa_v[at, units:], 1, 1)
        )

    def far_chunk(n, carry):
        away[n] = pulled(1 - half, n).astype(bf16)
        across(n).start()
        return carry

    def near_chunk(n, carry):
        gn_out[:, pl.ds(pl.multiple_of(n * wide, wide), wide)] = pulled(half, n)
        return carry

    def grads(n, carry):
        z = jnp.where(n == 0, order[0], jnp.where(n == 1, order[1], jnp.where(n == 2, order[2], order[3])))
        count = 4 * work.rows
        left = nt_v[pl.ds(pl.multiple_of(z * count, count), count)]
        work.held[z, 0, :, :units] = mm(left, dinner_v[...]).astype(bf16)
        work.held[z, 0, :, units:] = mm(left, dsd_v[...]).astype(bf16)
        work.copy_a(z, 1 - here.y).start()
        work.copy_a(z, here.y).start()

        @pl.when(n == 0)
        def _():
            for copy in pending[3:]:
                copy.wait()

        far_chunk(n, carry)
        work.cores(z)
        return carry

    total[0, 0:6] = gk[0:6]
    total[0, 6:7] = ggg[0:1]
    for k in range(5):
        total[0, 7:8, k * BW : k * BW + BW] = gks[k : k + 1]
    for k in range(2):
        total[0, 7:8, 5 * BW + k * 128 : 5 * BW + k * 128 + 128] = hs[k : k + 1]
    swap(0).start()
    for copy in pending[:3]:
        copy.wait()
    swapped(0)
    lax.fori_loop(0, 4, grads, 0)
    swapped(1)
    work.stay(order[0])
    work.sides(order[0])
    pl.when(~middle)(lambda: work.pass_on(order[0]))
    lax.fori_loop(4, chunks, far_chunk, 0)
    swapped(2)
    for n in range(1, 4):
        work.stay(order[n])
    work.sides(order[1])
    pl.when(~middle)(lambda: work.pass_on(order[1]))
    lax.fori_loop(0, 3, near_chunk, 0)
    pl.when(middle)(lambda: work.pass_on(order[0]))
    work.sides(order[2])
    pl.when(~middle)(lambda: work.pass_on(order[2]))
    lax.fori_loop(3, chunks, near_chunk, 0)
    swapped(3)
    small_out[...] = total[4]
    pl.when(middle)(lambda: work.pass_on(order[1]))
    work.sides(order[3])
    pl.when(middle)(lambda: work.pass_on(order[2]))
    work.finish()

    def arrive(n, carry):
        across(n).wait()
        at = pl.ds(pl.multiple_of(n * wide, wide), wide)
        gn_out[:, at] = gn_out[:, at] + came[n].astype(f32)
        return carry

    lax.fori_loop(0, chunks, arrive, 0)


def reduce_tail(normed_t, dinner, dsd, dgate, wb, wa, sums, ways, collective_id):
    width, tokens = normed_t.shape
    small = sums[0]
    units, cols, rows = dgate.shape[1], wa.shape[1], width // ways
    chunks = width // BW
    vmem = pl.BlockSpec(memory_space=pltpu.VMEM)
    hbm = pl.BlockSpec(memory_space=pl.ANY)
    sem = pltpu.SemaphoreType.DMA
    return pl.pallas_call(
        tail_kernel, name="tail", in_specs=[hbm] * 6 + [vmem] * 4, out_specs=[vmem] * 3,
        out_shape=[sds((tokens // 2, width)), sds((1, rows, cols)), sds(small.shape)],
        scratch_shapes=[
            pltpu.VMEM(normed_t.shape, bf16), pltpu.VMEM(dinner.shape, bf16), pltpu.VMEM(dsd.shape, bf16),
            pltpu.VMEM(dgate.shape, bf16), pltpu.VMEM((width, units), bf16), pltpu.VMEM(wa.shape, bf16),
            pltpu.VMEM((chunks, tokens // 2, BW), bf16), pltpu.VMEM((chunks, tokens // 2, BW), bf16),
            pltpu.VMEM((5,) + small.shape, f32), pltpu.VMEM((4,) + small.shape, f32),
            sem((6,)), sem((chunks,)), sem((chunks,)), sem((4,)), sem((4,)),
        ] + reduce_scratch(1, rows, cols, True),
        compiler_params=pltpu.CompilerParams(
            collective_id=collective_id, has_side_effects=True, vmem_limit_bytes=62 * 1024 * 1024
        ),
    )(normed_t, dinner, dsd, dgate, wb, wa, *sums)


def swap(v):
    return lax.ppermute(v, "tensor", [(0, 1), (1, 0)])


def halves(v, axis):
    size = v.shape[axis] // 2
    me = lax.axis_index("tensor")
    return (
        lax.dynamic_slice_in_dim(v, me * size, size, axis),
        lax.dynamic_slice_in_dim(v, (1 - me) * size, size, axis),
    )


def once(shape, at=None):
    where = at or (0,) * len(shape)
    return pl.BlockSpec(shape, lambda i: where, pipeline_mode=pl.Buffered(1))


def by_cols(rows, offset=0):
    return pl.BlockSpec((rows, BW), lambda i: (0, i + offset))


def params(collective_id=None):
    return pltpu.CompilerParams(
        dimension_semantics=("arbitrary",), vmem_limit_bytes=60 * 1024 * 1024,
        collective_id=collective_id, has_side_effects=collective_id is not None,
    )


def spread(v):
    lead = v.shape[:-1]
    v = v.reshape(lead + (v.shape[-1] // HB, HB))
    v = jnp.pad(v, [(0, 0)] * len(lead) + [(0, 0), (0, 8 - HB)]).reshape(lead + (-1,))
    return jnp.pad(v, [(0, 0)] * len(lead) + [(0, 128 - v.shape[-1])])


def gathered_heads(v, heads):
    return v[..., : heads * 2].reshape(v.shape[:-1] + (heads // HB, 8))[..., :HB].reshape(v.shape[:-1] + (heads,))


def sds(shape, dtype=f32):
    return jax.ShapeDtypeStruct(shape, dtype)


def on_device(
    residual, norm_gain, w_gate_inner, w_state_io, w_step, conv_inner, conv_state,
    step_bias, decay_log, skip_gain, gate_gain, w_output, cotangent,
):
    width = residual.shape[1]
    units = w_gate_inner.shape[2]
    heads = w_step.shape[1]
    blocks = units // BW
    unit_total = units * lax.axis_size("tensor")
    ways = lax.axis_size("dp")
    own_links = ways == 16
    rows_in = residual.astype(f32)
    rstd_in = lax.rsqrt(jnp.mean(rows_in * rows_in, axis=1, keepdims=True) + norm_eps)
    scaled = rows_in * rstd_in
    pack_a = jnp.concatenate([w_gate_inner[1], w_state_io, spread(w_step)], axis=1)
    w_output_t = w_output.T
    if own_links:
        normed, wa = gather_rows(
            residual, jnp.broadcast_to(norm_gain[None], (8, width)), w_gate_inner, w_state_io, w_step, ways, 1
        )
    else:
        wa = lax.all_gather(pack_a, "dp", axis=0, tiled=True)
        normed = lax.all_gather((scaled * norm_gain).astype(bf16), "tensor", axis=0, tiled=True)
    tokens = normed.shape[0]
    spans = tokens // Q
    gain8 = jnp.broadcast_to(gate_gain[None], (8, units))

    hbm = pl.BlockSpec(memory_space=pl.ANY)
    sem = pltpu.SemaphoreType.DMA
    def stage(rows, first):
        return pl.BlockSpec((rows, BW), lambda i: (0, jnp.clip(i - first, 0, blocks - 1)))

    inner, ssd, states, cst, bc, step, cum, step_t, cum_t, pre_t, *sent = pl.pallas_call(
        functools.partial(mixer_forward, own_links),
        name="mixer_forward",
        grid=(blocks * (3 if own_links else 1),),
        in_specs=[
            once((tokens, width)), stage(width, 0), once((width, 384), (0, units // 384)),
            stage(5, 0), once((5, BW)), once((heads,)), once((heads,)), once((heads,)),
        ] + ([once(v.shape) for v in (cotangent, w_gate_inner, w_output_t)] + [stage(8, 2 * blocks)]) * own_links,
        out_specs=[
            stage(tokens, 0), stage(tokens, 0), pl.BlockSpec((spans, BW, 128), lambda i: (0, jnp.clip(i, 0, blocks - 1), 0)),
            once((tokens, BW)), once((tokens, BW)), once((tokens, 128)), once((tokens, 128)),
            once((48, tokens)), once((48, tokens)), once((48, tokens)),
        ] + [hbm, hbm, stage(tokens, blocks), stage(tokens, 2 * blocks), once((8, tokens))] * own_links,
        out_shape=[
            sds((tokens, units)), sds((tokens, units)), sds((spans, units, 128)),
            sds((tokens, BW)), sds((tokens, BW), bf16), sds((tokens, 128)), sds((tokens, 128)),
            sds((48, tokens)), sds((48, tokens)), sds((48, tokens)),
        ] + [
            sds((tokens, width), bf16), sds((width, 2 * units), bf16), sds((tokens, units)), sds((tokens, units)),
            sds((8, tokens)),
        ] * own_links,
        scratch_shapes=[
            pltpu.VMEM((tokens + 8, BW), f32), pltpu.VMEM((spans, Q, Q), f32),
            pltpu.VMEM((tokens, 128), f32), pltpu.VMEM((tokens, 128), f32), pltpu.VMEM((8, tokens), f32),
            pltpu.VMEM((Q, HB * Q), bf16), pltpu.VMEM((HB * Q, BW), bf16), pltpu.VMEM((BW, 128), f32),
        ] + ([
            pltpu.VMEM((blocks + 1, tokens, BW), f32), pltpu.VMEM((blocks, width, BW), bf16), pltpu.VMEM((tokens, width), bf16),
            pltpu.VMEM((tokens, 128), f32), pltpu.VMEM((tokens, 128), f32), pltpu.VMEM((8, tokens), f32),
            pltpu.VMEM((8, tokens), f32), sem((blocks,)), sem((3,)),
        ] + gather_scratch() + [sem, sem, sem]) * own_links,
        compiler_params=params(2 if own_links else None),
        cost_estimate=pl.CostEstimate(flops=2 * tokens * width * (units + 384) + 4 * tokens * 256 * units, bytes_accessed=30_000_000, transcendentals=heads * spans * Q * Q),
    )(
        normed, wa, wa, conv_inner, conv_state, step_bias, decay_log, skip_gain,
        *[cotangent, w_gate_inner, w_output_t, gain8] * own_links,
    )

    if own_links:
        cot, wb, gate, ggo, stats = sent
    else:
        wb = lax.all_gather(jnp.concatenate([w_gate_inner[0], w_output_t], axis=1), "dp", axis=0, tiled=True)
        cot = lax.all_gather(cotangent, "tensor", axis=0, tiled=True)
        gate, ggo, stats = pl.pallas_call(
            gate_forward,
            name="gate_forward",
            grid=(blocks,),
            in_specs=[
                once((tokens, width)), once((tokens, width)), by_cols(width), by_cols(width, blocks),
                by_cols(tokens), by_cols(8),
            ],
            out_specs=[by_cols(tokens), by_cols(tokens), once((8, tokens))],
            out_shape=[sds((tokens, units)), sds((tokens, units)), sds((8, tokens))],
            scratch_shapes=[pltpu.VMEM((tokens, 128), f32), pltpu.VMEM((tokens, 128), f32)],
            compiler_params=params(),
            cost_estimate=pl.CostEstimate(flops=4 * tokens * width * units, bytes_accessed=35_000_000, transcendentals=tokens * units),
        )(normed, cot, wb, wb, ssd, gain8)
        stats = stats + swap(stats)

    dy, dgate, ng, ggg, grad_b, normed_t = pl.pallas_call(
        functools.partial(gate_backward, float(unit_total)),
        name="gate_backward",
        grid=(blocks,),
        in_specs=[
            once((8, tokens)), by_cols(tokens), by_cols(tokens), by_cols(tokens), by_cols(8),
            once((tokens, width)), once((tokens, width)),
        ],
        out_specs=[
            by_cols(tokens), by_cols(tokens), by_cols(tokens), by_cols(8),
            pl.BlockSpec((2, width, BW), lambda i: (0, 0, i)), once((width, tokens)),
        ],
        out_shape=[
            sds((tokens, units), bf16), sds((tokens, units), bf16), sds((tokens, units), bf16), sds((8, units)),
            sds((2, width, units), bf16), sds((width, tokens), bf16),
        ],
        scratch_shapes=[pltpu.VMEM((tokens, 128), f32), pltpu.VMEM((width, tokens), bf16)],
        compiler_params=params(),
        cost_estimate=pl.CostEstimate(flops=4 * tokens * units * width, bytes_accessed=45_000_000, transcendentals=tokens * units),
    )(stats, gate, ssd, ggo, gain8, normed, cot)

    mixed = mm(ng, wb[:, units:], 1, 1).astype(bf16)
    mixed_near, mixed_far = halves(mixed, 0)

    dinner, gk, dsd, gks, hs, *sent = pl.pallas_call(
        functools.partial(mixer_backward, own_links),
        name="mixer_backward",
        grid=(blocks,),
        in_specs=[
            by_cols(tokens), by_cols(tokens), pl.BlockSpec((spans, BW, 128), lambda i: (0, i, 0)),
            by_cols(5), once((5, BW)), once((heads,)), once((heads,)),
            once((tokens, BW)), once((tokens, BW)), once((tokens, 128)), once((tokens, 128)),
            once((48, tokens)), once((48, tokens)), once((48, tokens)),
        ] + [hbm, hbm] * own_links,
        out_specs=[by_cols(tokens), by_cols(8), once((tokens, 384)), once((8, BW)), once((8, 128))]
        + [hbm, once((2, width // ways, units))] * own_links,
        out_shape=[sds((tokens, units), bf16), sds((8, units)), sds((tokens, 384), bf16), sds((8, BW)), sds((8, 128))]
        + [sds((tokens // 2, width), bf16), sds((2, width // ways, units))] * own_links,
        scratch_shapes=[
            pltpu.VMEM((tokens + 8, BW), f32), pltpu.VMEM((tokens + 8, BW), f32),
            pltpu.VMEM((spans, Q, Q), f32), pltpu.VMEM((spans, Q, Q), f32),
            pltpu.VMEM((tokens, 128), f32), pltpu.VMEM((tokens, 128), f32),
            pltpu.VMEM((tokens, 128), f32), pltpu.VMEM((tokens, 128), f32), pltpu.VMEM((8, tokens), f32),
            pltpu.VMEM((HB * Q, Q), bf16), pltpu.VMEM((HB * Q, BW), bf16), pltpu.VMEM((HB * Q, Q), f32),
            pltpu.VMEM((BW, 128), f32),
            pltpu.VMEM((48, tokens), f32), pltpu.VMEM((48, tokens), f32), pltpu.VMEM((48, tokens), f32),
            pltpu.VMEM((48, tokens), f32), pltpu.VMEM((48, 128), f32), pltpu.VMEM((8, BW), f32),
        ] + ([sem, sem] + reduce_scratch(2, width // ways, units)) * own_links,
        compiler_params=params(4 if own_links else None),
        cost_estimate=pl.CostEstimate(flops=40_000_000_000, bytes_accessed=30_000_000, transcendentals=heads * spans * Q * Q),
    )(
        inner, dy, states, conv_inner, conv_state, decay_log, skip_gain, cst, bc, step, cum, step_t, cum_t, pre_t,
        *[mixed, grad_b] * own_links,
    )
    if own_links:
        mixed_got, wb_shard = sent
    else:
        mixed_got = swap(mixed_far)
        wb_shard = lax.psum_scatter(grad_b, "dp", scatter_dimension=1, tiled=True).astype(f32)
    output = (rows_in + mixed_near.astype(f32) + mixed_got.astype(f32)).astype(bf16)

    if own_links:
        grad_normed, wa_shard, small = reduce_tail(normed_t, dinner, dsd, dgate, wb, wa, (gk, ggg, gks, hs), ways, 5)
        wa_shard = wa_shard[0]
    else:
        last = jnp.concatenate([gks[:5].reshape(-1), hs[0], hs[1]])
        small = jnp.concatenate([gk[:6], ggg[:1], last[None]], axis=0)
        grad_a = jnp.concatenate([mm(normed_t, dinner).astype(bf16), mm(normed_t, dsd).astype(bf16)], axis=1)
        pulled = mm(dgate, wb[:, :units], 1, 1) + mm(dinner, wa[:, :units], 1, 1) + mm(dsd, wa[:, units:], 1, 1)
        near, far = halves(pulled.astype(bf16), 0)
        wa_shard = lax.psum_scatter(grad_a, "dp", scatter_dimension=0, tiled=True).astype(f32)
        small = lax.psum(small, "dp")
        grad_normed = near.astype(f32) + swap(far).astype(f32)
    grad_v = grad_normed * norm_gain
    grad_residual = cotangent.astype(f32) + rstd_in * (
        grad_v - scaled * jnp.mean(grad_v * scaled, axis=1, keepdims=True)
    )

    conv_state_sum = small[7, : 5 * BW].reshape(5, BW)
    bias_sum = gathered_heads(small[7, 5 * BW : 5 * BW + 128], heads)
    decay_sum = gathered_heads(small[7, 5 * BW + 128 : 5 * BW + 256], heads)
    skip_sum = jnp.sum(small[5].reshape(heads, HEAD), axis=1)

    gain_rows = jnp.sum(wb_shard[0] * w_gate_inner[0].astype(f32), axis=1) + jnp.sum(
        wa_shard * pack_a.astype(f32), axis=1
    )
    count = gain_rows.shape[0]
    gain_own = gain_rows / lax.dynamic_slice_in_dim(norm_gain, lax.axis_index("dp") * count, count)
    near_s, far_s = halves(jnp.concatenate([wa_shard[:, units : units + BW], conv_state_sum], axis=0), 1)
    near_g, far_g = halves(gain_own, 0)
    far_all = jnp.concatenate([far_s.reshape(-1), far_g])
    got = swap(far_all)
    both = near_s + got[: far_s.size].reshape(far_s.shape)
    gain_part = near_g + got[far_s.size :]
    return (
        output,
        grad_residual,
        gain_part,
        jnp.stack([wb_shard[0], wa_shard[:, :units]]),
        both[:count],
        gathered_heads(wa_shard[:, units + BW :], heads),
        small[0:5],
        both[count:],
        bias_sum,
        decay_sum,
        skip_sum,
        small[6],
        wb_shard[1].T,
    )


def solution(mesh):
    return jax.shard_map(
        on_device,
        mesh=mesh,
        in_specs=(
            P(("dp", "tensor"), None),
            P(),
            P(None, "dp", "tensor"),
            P("dp", None),
            P("dp", "tensor"),
            P(None, "tensor"),
            P(),
            P("tensor"),
            P("tensor"),
            P("tensor"),
            P("tensor"),
            P("tensor", "dp"),
            P(("dp", "tensor"), None),
        ),
        out_specs=(
            P(("dp", "tensor"), None),
            P(("dp", "tensor"), None),
            P(("dp", "tensor")),
            P(None, "dp", "tensor"),
            P("dp", "tensor"),
            P("dp", "tensor"),
            P(None, "tensor"),
            P(None, "tensor"),
            P("tensor"),
            P("tensor"),
            P("tensor"),
            P("tensor"),
            P("tensor", "dp"),
        ),
        check_vma=False,
    )
```

```python
import functools

import jax
import jax.numpy as jnp
from jax import lax
from jax.experimental import pallas as pl
from jax.experimental.pallas import tpu as pltpu
from jax.sharding import PartitionSpec as P

Q = 256
LEN = 1024
HEAD = 64
BW = 256
HB = BW // HEAD
LOG2E = 1.4426950408889634
FAR = -1e30
norm_eps = 1e-05
MESH = pl.DeviceIdType.MESH
f32 = jnp.float32
bf16 = jnp.bfloat16


def mm(a, b, ca=1, cb=0):
    return lax.dot_general(a, b, (((ca,), (cb,)), ((), ())), preferred_element_type=f32)


def sigmoid(v):
    return 1.0 / (1.0 + jnp.exp(-v))


def split3(a):
    hi = a.astype(bf16)
    rest = a - hi.astype(f32)
    mid = rest.astype(bf16)
    low = (rest - mid.astype(f32)).astype(bf16)
    return hi, mid, low


def split2(a):
    hi = a.astype(bf16)
    return hi, (a - hi.astype(f32)).astype(bf16)


def iota(shape, axis):
    return lax.broadcasted_iota(jnp.int32, shape, axis)


def expand(cols):
    rows = cols.shape[0]
    left = iota((rows, 128), 1) < HEAD
    return jnp.concatenate(
        [jnp.where(left, cols[:, 2 * q : 2 * q + 1], cols[:, 2 * q + 1 : 2 * q + 2]) for q in range(2)],
        axis=1,
    )


def conv_taps(window, kernel):
    out = kernel[4:5] + kernel[3:4] * window[8:]
    for k in range(3):
        out = out + kernel[k : k + 1] * pltpu.roll(window, 3 - k, 0)[8:]
    return out


def head_row(ref):
    return jnp.broadcast_to(ref[...][None, :], (8, ref.shape[0]))


def lay(rows, pick):
    parts = split3(rows)
    return mm(parts[0], pick) + mm(parts[1], pick) + mm(parts[2], pick)


def as_places(heads):
    lane = iota((heads, 128), 1)
    place = lane % 8
    return ((lane // 8 * HB + place == iota((heads, 128), 0)) & (place < HB)).astype(f32).astype(bf16)


def as_units(heads, block):
    return (iota((heads, BW), 1) // HEAD + HB * block == iota((heads, BW), 0)).astype(f32).astype(bf16)


def head_masks():
    lane = iota((1, BW), 1) // HEAD
    return [(lane == j).astype(f32).astype(bf16) for j in range(HB)]


def quads():
    for r in range(0, Q, 64):
        for half in range(2):
            if half * 128 <= r:
                yield r, half, r < half * 128 + 128


def decay_chunk(col, row, r, half, diag):
    gap = col[r : r + 64] - row[:, half * 128 : half * 128 + 128]
    if diag:
        keep = iota((64, 128), 0) + (r - half * 128) >= iota((64, 128), 1)
        gap = jnp.where(keep, gap, FAR)
    return jnp.exp2(gap)


def mixer_forward(links, normed, wi, wsx, kin, kst, bias, log_rate, skip_in, *refs):
    refs = list(refs)
    if links:
        sent = refs[:3] + refs[14:16]
        gain, gate_refs = refs[3], refs[16:19]
        refs = refs[4:14] + refs[19:]
    inner_out, ssd_out, states_out, cst_out, bc_out, step_out, cum_out, stepT_out, cumT_out, preT_out = refs[:10]
    buf, gram, colc, cols, rowp, mst, xst, state = refs[10:18]
    i = pl.program_id(0)
    tokens = normed.shape[0]
    spans = tokens // Q
    blocks = inner_out.shape[1] // BW
    if links:
        work = BesideForward(*sent, *refs[27:])
        ssd_v, *gate_scratch = refs[18:27]
        blocks = ssd_v.shape[0] - 1
    heads = bias.shape[0]
    skip = lay(head_row(skip_in), as_units(heads, i))[0:1]

    if links:
        pl.when(i == 0)(work.start)

    @pl.when(i == 0)
    def _():
        proj = mm(normed[...], wsx[...])
        buf[0:8] = jnp.zeros((8, BW), f32)
        cst_out[...] = proj[:, :BW]
        buf[8 : 8 + tokens] = proj[:, :BW]
        tri = (iota((Q, Q), 0) >= iota((Q, Q), 1)).astype(f32).astype(bf16)
        places = as_places(heads)
        pre = proj[:, BW:] + lay(head_row(bias), places)[0:1]
        step = jnp.maximum(pre, 0.0) + jnp.log1p(jnp.exp(-jnp.abs(pre)))
        step_out[...] = step
        scaled = step * (lay(-jnp.exp(head_row(log_rate)), places)[0:1] * LOG2E)
        for s in range(spans):
            parts = split3(scaled[s * Q : s * Q + Q])
            cum_out[s * Q : s * Q + Q] = mm(tri, parts[0]) + mm(tri, parts[1]) + mm(tri, parts[2])
            conv = conv_taps(buf[s * Q : s * Q + Q + 8], kst[...])
            bc = (conv * sigmoid(conv)).astype(bf16)
            bc_out[s * Q : s * Q + Q] = bc
            gram[s] = mm(bc[:, 128:], bc[:, :128], 1, 1)
        preT_out[...] = jnp.transpose(pre)[:48]
        stepT_out[...] = jnp.transpose(step)[:48]
        cumT_out[...] = jnp.transpose(cum_out[...])[:48]
        mst[...] = jnp.zeros(mst.shape, bf16)

    def mix():
        inner = mm(normed[...], wi[...])
        inner_out[...] = inner
        buf[8 : 8 + tokens] = inner
        turn = lax.rem(128 - 8 * i, 128)
        colc[...] = pltpu.roll(cum_out[...], turn, 1)
        cols[...] = pltpu.roll(step_out[...], turn, 1)
        rows8 = pl.ds(pl.multiple_of(8 * i, 8), 8)
        rowp[...] = cumT_out[rows8] - jnp.log2(stepT_out[rows8])
        state[...] = jnp.zeros(state.shape, f32)
        masks = head_masks()

        def span(s, carry):
            at = pl.multiple_of(s * Q, Q)
            rows = pl.ds(at, Q)
            conv = conv_taps(buf[pl.ds(at, Q + 8)], kin[...])
            xs = conv * sigmoid(conv)
            x_low = xs.astype(bf16)
            col = colc[rows]
            total = col[Q - 1 : Q]
            growth = expand(jnp.exp2(col[:, :8]))
            weight = expand(jnp.exp2(total[:, :8] - col[:, :8]) * cols[rows][:, :8])
            xw_low = (xs * weight).astype(bf16)
            for j in range(HB):
                xst[j * Q : j * Q + Q] = x_low * masks[j]
                row = rowp[j : j + 1, rows]
                for r, half, diag in quads():
                    part = gram[s, r : r + 64, half * 128 : half * 128 + 128]
                    dec = decay_chunk(col[:, j : j + 1], row, r, half, diag)
                    mst[r : r + 64, j * Q + half * 128 : j * Q + half * 128 + 128] = (part * dec).astype(bf16)
            intra = mm(mst[...], xst[...])
            state_in = state[...]
            states_out[s] = state_in
            bc = bc_out[rows]
            readout = mm(bc[:, 128:], state_in.astype(bf16), 1, 1)
            ssd = intra + growth * readout + skip * xs
            ssd_out[rows] = ssd
            if links:
                ssd_v[blocks, rows] = ssd
            local = mm(xw_low, bc[:, :128], 0, 0)
            fade = jnp.exp2(total)
            for j in range(HB):
                at_j = slice(j * HEAD, j * HEAD + HEAD)
                state[at_j] = fade[:, j : j + 1] * state_in[at_j] + local[at_j]
            if links:
                work.step(i * spans + s)
            return carry

        lax.fori_loop(0, spans, span, 0)

    if not links:
        mix()
        return
    pl.when(i < blocks)(mix)

    @pl.when(i < blocks)
    def _():
        ssd_v[i] = ssd_v[blocks]

    gates = GateForward(i - blocks, blocks, normed, sent[3], sent[4], gain, ssd_v, *gate_refs, *gate_scratch)

    @pl.when(i == blocks)
    def _():
        work.first()
        gates.start(0)


    @pl.when((i >= blocks) & (i < 2 * blocks))
    def _():
        gates.gate()
        work.between(i - blocks)


    @pl.when(i == 2 * blocks)
    def _():
        work.finish()
        gates.start(1)

    pl.when(i >= 2 * blocks)(gates.pull)


class GateForward:
    def __init__(
        self, at, blocks, normed, cot, wb, gain, ssd_v, gate_out, ggo_out, stats_out, w_v, cot_v, sq, gi, mine, landed, wl, cl
    ):
        self.at, self.blocks, self.normed, self.cot, self.wb, self.gain, self.ssd_v = at, blocks, normed, cot, wb, gain, ssd_v
        self.gate_out, self.ggo_out, self.stats_out = gate_out, ggo_out, stats_out
        self.w_v, self.cot_v, self.sq, self.gi, self.mine, self.landed, self.wl, self.cl = w_v, cot_v, sq, gi, mine, landed, wl, cl

    def load(self, which, n):
        cols = slice((which * self.blocks + n) * BW, (which * self.blocks + n + 1) * BW)
        return pltpu.make_async_copy(self.wb.at[:, cols], self.w_v.at[n], self.wl.at[n])

    def tokens(self):
        return pltpu.make_async_copy(self.cot, self.cot_v, self.cl.at[0])

    def start(self, which):
        if which:
            self.tokens().start()
        for n in range(self.blocks):
            self.load(which, n).start()
        if which:
            self.tokens().wait()
        total = self.gi if which else self.sq
        total[...] = jnp.zeros(total.shape, f32)

    def gate(self):
        b = self.at
        pltpu.make_async_copy(self.wb.at[:, :BW], self.w_v.at[b], self.wl.at[b]).wait()
        gate = mm(self.normed[...], self.w_v[b])
        self.gate_out[...] = gate
        gated = self.ssd_v[b] * (gate * sigmoid(gate))
        self.ssd_v[b] = gated
        squares = gated * gated
        self.sq[...] += squares[:, :128] + squares[:, 128:]

    def pull(self):
        b = self.at - self.blocks
        pltpu.make_async_copy(self.wb.at[:, :BW], self.w_v.at[b], self.wl.at[b]).wait()
        ggo = mm(self.cot_v[...], self.w_v[b])
        self.ggo_out[...] = ggo
        inner = ggo * self.gain[0:1] * self.ssd_v[b]
        self.gi[...] += inner[:, :128] + inner[:, 128:]
        pl.when(b == self.blocks - 1)(self.last)

    def last(self):
        self.mine[...] = token_sums(self.sq[...], self.gi[...])
        swap = remote(self.mine, self.landed, self.cl.at[1], self.cl.at[2], tensor=1 - lax.axis_index("tensor"))
        swap.start()
        swap.wait()
        self.stats_out[...] = self.mine[...] + self.landed[...]


def token_sums(sq, gi):
    lane = iota(sq.shape, 1)
    both = jnp.where(
        lane == 0,
        jnp.sum(sq, axis=1, keepdims=True),
        jnp.where(lane == 1, jnp.sum(gi, axis=1, keepdims=True), 0.0),
    )
    return jnp.transpose(both)[:8]


class BesideForward:
    def __init__(self, cot, w_gate_inner, w_output_t, cot_out, wb, ss, rs, ls, xs, xr, xl):
        self.here = Place()
        units = w_output_t.shape[1]
        self.moves = [
            Gather(self.here, own, wb, ss, rs, ls, n, slice(n * units, n * units + units))
            for n, own in enumerate((w_gate_inner.at[0], w_output_t))
        ]
        half = lax.axis_index("tensor")
        rows = cot.shape[0]
        slot = cot_out.at[pl.ds(pl.multiple_of(half * rows, rows), rows)]
        self.across = remote(cot, slot, xs, xr, tensor=1 - half)
        self.local = pltpu.make_async_copy(cot, slot, xl)

    def start(self):
        greet(self.here, True)
        self.moves[0].start()
        self.across.start()
        self.local.start()

    def step(self, at):
        for when, chunk, hops in ((4, 0, 1), (9, 0, 2), (15, 0, 3), (19, 1, 1)):

            def go(move=self.moves[chunk], chunk=chunk, hops=hops):
                move.hop(hops)
                move.sides(hops - 1)
                if chunk == 0 and hops == 2:
                    self.moves[1].start()

            pl.when(at == when)(go)

    def first(self):
        self.moves[0].sides(3)
        self.moves[0].finish()

    def between(self, at):
        move = self.moves[1]
        pl.when(at == 1)(lambda: move.hop(2))
        pl.when(at == 3)(lambda: move.sides(1))
        pl.when(at == 5)(lambda: move.hop(3))

    def finish(self):
        move = self.moves[1]
        move.sides(2)
        move.sides(3)
        move.finish()
        self.local.wait()
        self.across.wait()


def gate_forward(normed, cot, wg, wo, ssd, gain, gate_out, ggo_out, stats_out, sq, gi):
    i = pl.program_id(0)

    @pl.when(i == 0)
    def _():
        sq[...] = jnp.zeros(sq.shape, f32)
        gi[...] = jnp.zeros(gi.shape, f32)

    gate = mm(normed[...], wg[...])
    gate_out[...] = gate
    ggo = mm(cot[...], wo[...])
    ggo_out[...] = ggo
    gated = ssd[...] * (gate * sigmoid(gate))
    squares = gated * gated
    sq[...] += squares[:, :128] + squares[:, 128:]
    inner = ggo * gain[0:1] * gated
    gi[...] += inner[:, :128] + inner[:, 128:]

    @pl.when(i == pl.num_programs(0) - 1)
    def _():
        stats_out[...] = token_sums(sq[...], gi[...])


def gate_backward(
    unit_total, stats, gate, ssd, ggo, gain, normed, cot, dy_out, dgate_out, ng_out, gg_out, grads_out, normed_t, cols, cot_t
):
    @pl.when(pl.program_id(0) == 0)
    def _():
        full = jnp.concatenate([stats[...], jnp.zeros((120, stats.shape[1]), f32)], axis=0)
        cols[...] = jnp.transpose(full)

        def turn(n, carry):
            here = pl.ds(pl.multiple_of(n * 128, 128), 128)
            normed_t[here] = jnp.transpose(normed[:, here])
            cot_t[here] = jnp.transpose(cot[:, here])
            return carry

        lax.fori_loop(0, normed.shape[1] // 128, turn, 0)

    rstd = lax.rsqrt(cols[:, 0:1] / unit_total + norm_eps)
    pull = rstd * rstd * rstd * (cols[:, 1:2] / unit_total)
    v = gate[...]
    sig = sigmoid(v)
    act = v * sig
    y = ssd[...]
    gated = y * act
    scaled = gated * rstd
    ng = (scaled * gain[0:1]).astype(bf16)
    ng_out[...] = ng
    grads_out[1] = mm(cot_t[...], ng).astype(bf16)
    gg = ggo[...]
    gg_out[...] = jnp.broadcast_to(jnp.sum(gg * scaled, axis=0, keepdims=True), gg_out.shape)
    grad = rstd * (gg * gain[0:1]) - gated * pull
    dy_out[...] = (grad * act).astype(bf16)
    dgate = (grad * y * (sig * (1.0 + v * (1.0 - sig)))).astype(bf16)
    dgate_out[...] = dgate
    grads_out[0] = mm(normed_t[...], dgate).astype(bf16)


class BesideBackward:
    def __init__(self, mixed, grads, far_out, shard_out, scratch):
        self.here = Place()
        half = lax.axis_index("tensor")
        rows = far_out.shape[0]
        other = mixed.at[pl.ds(pl.multiple_of((1 - half) * rows, rows), rows)]
        self.across = remote(other, far_out, scratch[0], scratch[1], tensor=1 - half)
        self.sum = Reduce(self.here, grads, shard_out, scratch[2:7], scratch[7:15])

    def start(self):
        greet(self.here, True)
        self.sum.start()
        self.across.start()

    def step(self, at):
        total = self.sum
        z = self.here.z
        ends = (z == 0) | (z == 3)
        for n, block in enumerate(total.order):
            pl.when(at == n)(lambda z=block: total.cores(z))
            pl.when(at == (4, 5, 7, 8)[n])(lambda z=block: total.stay(z))
            pl.when(at == (6, 11, 17, 22)[n])(lambda z=block: total.sides(z))
        for n, block in enumerate(total.order[:3]):
            when = jnp.where(ends, (6, 11, 17)[n], (12, 18, 19)[n])
            pl.when(at == when)(lambda z=block: total.pass_on(z))

    def finish(self):
        self.sum.finish()
        self.across.wait()


def mixer_backward(links, inner, dy, states, kin, kst, log_rate, skip_in, cst, bc_in, step_in, cum_in, stepT, cumT, preT, *refs):
    refs = list(refs)
    if links:
        beside = refs[:2] + refs[7:9]
        refs = refs[2:7] + refs[9:]
        work = BesideBackward(*beside, refs[24:])
    dinner_out, gk_out, dsd_out, gks_out, hs_out = refs[:5]
    buf, dbuf, gram, gg, gb, gc, colc, cols, rowp, mst, dyst, gmix, sgrad = refs[5:18]
    rs_t, cs_t, dr_t, wg_t, gt_t, gtaps = refs[18:24]
    i = pl.program_id(0)
    if links:
        pl.when(i == 0)(work.start)
    heads = log_rate.shape[0]
    skip = lay(head_row(skip_in), as_units(heads, i))[0:1]
    tokens = inner.shape[0]
    spans = tokens // Q
    masks = head_masks()

    @pl.when(i == 0)
    def _():
        buf[0:8] = jnp.zeros((8, BW), f32)
        dbuf[tokens : tokens + 8] = jnp.zeros((8, BW), f32)
        for s in range(spans):
            bc = bc_in[s * Q : s * Q + Q]
            gram[s] = mm(bc[:, 128:], bc[:, :128], 1, 1)
        for ref in (gg, gb, gc, rs_t, cs_t, dr_t, wg_t, gt_t):
            ref[...] = jnp.zeros(ref.shape, f32)
        mst[...] = jnp.zeros(mst.shape, bf16)

    buf[8 : 8 + tokens] = inner[...]
    turn = lax.rem(128 - 8 * i, 128)
    colc[...] = pltpu.roll(cum_in[...], turn, 1)
    cols[...] = pltpu.roll(step_in[...], turn, 1)
    rows8 = pl.ds(pl.multiple_of(8 * i, 8), 8)
    rowp[...] = cumT[rows8] - jnp.log2(stepT[rows8])
    sgrad[...] = jnp.zeros(sgrad.shape, f32)
    gtaps[...] = jnp.zeros(gtaps.shape, f32)
    pick = (iota((8, BW), 1) // HEAD == iota((8, BW), 0)).astype(f32).astype(bf16)

    def conv_rows(at, kernel, grad_act, conv, sig):
        gco = grad_act * (sig * (1.0 + conv * (1.0 - sig)))
        dbuf[pl.ds(at, Q)] = gco
        into = buf[pl.ds(pl.multiple_of(at + 8, 8), Q)]
        gtaps[4:5] += jnp.sum(gco, axis=0, keepdims=True)
        after = dbuf[pl.ds(at, Q + 8)]
        grad_in = kernel[3:4] * gco
        gtaps[3:4] += jnp.sum(gco * into, axis=0, keepdims=True)
        for k in range(3):
            later = pltpu.roll(after, Q + 8 - (3 - k), 0)[:Q]
            gtaps[k : k + 1] += jnp.sum(later * into, axis=0, keepdims=True)
            grad_in = grad_in + kernel[k : k + 1] * later
        return grad_in

    def span(back, carry):
        s = spans - 1 - back
        at = pl.multiple_of(s * Q, Q)
        rows = pl.ds(at, Q)
        conv = conv_taps(buf[pl.ds(at, Q + 8)], kin[...])
        sig = sigmoid(conv)
        xs = conv * sig
        x_low = xs.astype(bf16)
        dy_s = dy[rows]
        dy_f = dy_s.astype(f32)
        bc = bc_in[rows]
        b_low, c_low = bc[:, :128], bc[:, 128:]
        col = colc[rows]
        total = col[Q - 1 : Q]
        for j in range(HB):
            dyst[j * Q : j * Q + Q] = dy_s * masks[j]
        gmix[...] = mm(dyst[...], x_low, 1, 1)
        lane = iota((Q, 128), 1)
        row_sums = jnp.zeros((Q, 128), f32)
        for j in range(HB):
            row = rowp[j : j + 1, rows]
            col_sum = [jnp.zeros((1, 128), f32), jnp.zeros((1, 128), f32)]
            row_parts = []
            for r, half, diag in quads():
                here = slice(half * 128, half * 128 + 128)
                dec = decay_chunk(col[:, j : j + 1], row, r, half, diag)
                part = gram[s, r : r + 64, here]
                p = gmix[j * Q + r : j * Q + r + 64, here] * dec
                gg[s, r : r + 64, here] += p
                q = p * part
                mst[j * Q + r : j * Q + r + 64, here] = (part * dec).astype(bf16)
                col_sum[half] = col_sum[half] + jnp.sum(q, axis=0, keepdims=True)
                if half == 0:
                    row_parts.append(q)
                else:
                    row_parts[-1] = row_parts[-1] + q
            sums = jnp.concatenate([jnp.sum(q, axis=1, keepdims=True) for q in row_parts], axis=0)
            row_sums = jnp.where(lane == j, sums, row_sums)
            cs_t[pl.ds(8 * i + j, 1), rows] = jnp.concatenate(col_sum, axis=1)
        rs_t[rows8, rows] = jnp.transpose(row_sums)[:8]
        grad_xs = mm(mst[...], dyst[...], 0, 0) + skip * dy_f

        growth = expand(jnp.exp2(col[:, :8]))
        weight = expand(jnp.exp2(total[:, :8] - col[:, :8]) * cols[rows][:, :8])
        state_in = states[s]
        state_low = state_in.astype(bf16)
        state_grad = sgrad[...]
        carry_low = state_grad.astype(bf16)
        readout = mm(c_low, state_low, 1, 1)
        read_low = (dy_f * growth).astype(bf16)
        hi, low = split2(dy_f * readout)
        dr_t[rows8, rows] = mm(pick, hi, 1, 1) + mm(pick, low, 1, 1)
        gc[rows] += mm(read_low, state_low)
        grad_xw = mm(b_low, carry_low, 1, 1)
        xw_low = (xs * weight).astype(bf16)
        gb[rows] += mm(xw_low, carry_low)
        hi, low = split2(grad_xw * xs)
        wg_t[rows8, rows] = mm(pick, hi, 1, 1) + mm(pick, low, 1, 1)
        hi, low = split2(state_grad * state_in)
        sums = jnp.sum(mm(pick, hi) + mm(pick, low), axis=1, keepdims=True)
        gt_t[rows8] = jnp.where(iota((8, 128), 1) == s, sums, gt_t[rows8])
        grad_xs = grad_xs + grad_xw * weight
        local = mm(read_low, c_low, 0, 0)
        fade = jnp.exp2(total)
        for j in range(HB):
            at_j = slice(j * HEAD, j * HEAD + HEAD)
            sgrad[at_j] = fade[:, j : j + 1] * state_grad[at_j] + local[at_j]
        gtaps[5:6] += jnp.sum(dy_f * xs, axis=0, keepdims=True)
        dinner_out[rows] = conv_rows(at, kin[...], grad_xs, conv, sig).astype(bf16)
        if links:
            work.step(i * spans + back)
        return carry

    lax.fori_loop(0, spans, span, 0)
    gk_out[...] = gtaps[...]

    @pl.when(i == pl.num_programs(0) - 1)
    def _():
        buf[8 : 8 + tokens] = cst[...]
        gtaps[...] = jnp.zeros(gtaps.shape, f32)
        rates = lay(-jnp.exp(head_row(log_rate)), as_places(heads))[0:1]
        rate = jnp.transpose(jnp.broadcast_to(rates, (128, 128)))[:48, 0:1]
        later = (iota((Q, Q), 0) >= iota((Q, Q), 1)).astype(f32).astype(bf16)
        last = iota((48, Q), 1) == Q - 1
        bias_sum = jnp.zeros((48, 1), f32)
        decay_sum = jnp.zeros((48, 1), f32)
        for back in range(spans):
            s = spans - 1 - back
            rows = slice(s * Q, s * Q + Q)
            bc = bc_in[rows]
            gl = gg[s].astype(bf16)
            grad_c = gc[rows] + mm(gl, bc[:, :128])
            grad_b = gb[rows] + mm(gl, bc[:, 128:], 0, 0)
            both = jnp.concatenate([grad_b, grad_c], axis=1)
            conv = conv_taps(buf[s * Q : s * Q + Q + 8], kst[...])
            dsd_out[rows, :BW] = conv_rows(s * Q, kst[...], both, conv, sigmoid(conv)).astype(bf16)

            cum, step, pre = cumT[:, rows], stepT[:, rows], preT[:, rows]
            total = cum[:, Q - 1 : Q]
            rate_w = jnp.exp2(total - cum)
            wg = wg_t[:, rows]
            cs = cs_t[:, rows]
            moved = wg * (rate_w * step)
            grad_cum = rs_t[:, rows] - cs + jnp.exp2(cum) * dr_t[:, rows] - moved
            grad_total = jnp.exp2(total) * gt_t[:, s : s + 1] + jnp.sum(moved, axis=1, keepdims=True)
            grad_cum = grad_cum + jnp.where(last, grad_total, 0.0)
            parts = split3(grad_cum)
            grad_rate = mm(parts[0], later) + mm(parts[1], later) + mm(parts[2], later)
            sig = sigmoid(pre)
            ratio = jnp.where(pre < -15.0, 1.0, sig / step)
            grad_pre = (wg * rate_w + grad_rate * rate) * sig + cs * ratio
            bias_sum = bias_sum + jnp.sum(grad_pre, axis=1, keepdims=True)
            decay_sum = decay_sum + jnp.sum(grad_rate * step, axis=1, keepdims=True)
            full = jnp.concatenate([grad_pre, jnp.zeros((80, Q), f32)], axis=0)
            dsd_out[rows, BW:] = jnp.transpose(full).astype(bf16)
        gks_out[...] = gtaps[...]
        lane = iota((48, 128), 1)
        both = jnp.where(lane == 0, bias_sum, jnp.where(lane == 1, decay_sum * rate, 0.0))
        hs_out[...] = jnp.transpose(jnp.concatenate([both, jnp.zeros((80, 128), f32)], axis=0))[:8]
        if links:
            work.finish()


class Place:
    def __init__(self):
        me = lax.axis_index("dp")
        self.me = me
        self.c, self.y, self.z = me % 2, (me // 2) % 2, me // 4

    def at(self, z, y, c):
        return (z * 2 + y) * 2 + c

    def core(self):
        return self.at(self.z, self.y, 1 - self.c)

    def side(self):
        return self.at(self.z, 1 - self.y, self.c)

    def up(self):
        return self.me + 4

    def down(self):
        return self.me - 4


def greet(here, across):
    barrier = pltpu.get_barrier_semaphore()

    def signal(**device):
        pl.semaphore_signal(barrier, 1, device_id=device, device_id_type=MESH)

    signal(dp=here.core())
    signal(dp=here.side())
    pl.when(here.z < 3)(lambda: signal(dp=here.up()))
    pl.when(here.z > 0)(lambda: signal(dp=here.down()))
    if across:
        signal(tensor=1 - lax.axis_index("tensor"))
    ends = (here.z == 0).astype(jnp.int32) + (here.z == 3).astype(jnp.int32)
    pl.semaphore_wait(barrier, 4 + int(across) - ends)


def remote(src, dst, send_sem, recv_sem, **device):
    return pltpu.make_async_remote_copy(
        src_ref=src, dst_ref=dst, send_sem=send_sem, recv_sem=recv_sem, device_id=device, device_id_type=MESH
    )


class Gather:
    def __init__(self, here, own, full, ss, rs, ls, chunk, cols):
        self.here, self.full, self.ss, self.rs, self.chunk, self.cols = here, full, ss, rs, chunk, cols
        self.rows = own.shape[0]
        self.own = own
        self.local = pltpu.make_async_copy(own, self.slot(here.me), ls.at[chunk])

    def slot(self, origin):
        return self.full.at[pl.ds(pl.multiple_of(origin * self.rows, self.rows), self.rows), self.cols]

    def copy(self, origin, way, src=None):
        here = self.here
        target = (here.up, here.down, here.side, here.core)[way]()
        slot = self.slot(origin)
        sems = self.ss.at[self.chunk, origin, way], self.rs.at[self.chunk, origin]
        return remote(slot if src is None else src, slot, *sems, dp=target)

    def arrived(self, origin):
        self.copy(origin, 3).wait_recv()

    def each_send(self, act):
        here = self.here
        for hops in range(4):
            for way, origin_z in ((0, here.z - hops), (1, here.z + hops)):
                if hops == 0:
                    if way == 1:
                        continue
                    origin = here.me
                    pl.when(here.z < 3)(lambda o=origin: act(o, 0))
                    pl.when(here.z > 0)(lambda o=origin: act(o, 1))
                    act(origin, 2)
                    act(origin, 3)
                    continue
                origin = here.at(origin_z, here.y, here.c)

                def go(o=origin, way=way):
                    pl.when((here.z < 3) if way == 0 else (here.z > 0))(lambda: act(o, way))
                    act(o, 2)
                    act(o, 3)

                pl.when((origin_z >= 0) & (origin_z <= 3))(go)

    def start(self):
        here = self.here
        pl.when(here.z < 3)(lambda: self.copy(here.me, 0, self.own).start())
        pl.when(here.z > 0)(lambda: self.copy(here.me, 1, self.own).start())
        self.copy(here.me, 2, self.own).start()
        self.copy(here.me, 3, self.own).start()
        self.local.start()

    def hop(self, hops):
        here = self.here
        for way, origin_z in ((0, here.z - hops), (1, here.z + hops)):

            def go(way=way, origin_z=origin_z):
                origin = here.at(origin_z, here.y, here.c)
                self.arrived(origin)
                pl.when((here.z < 3) if way == 0 else (here.z > 0))(lambda: self.copy(origin, way).start())
                self.copy(origin, 2).start()
                self.copy(origin, 3).start()

            pl.when((origin_z >= 0) & (origin_z <= 3))(go)

    def sides(self, hops):
        here = self.here
        for way, origin_z in ((0, here.z - hops), (1, here.z + hops)):
            if hops == 0 and way == 1:
                continue

            def go(origin_z=origin_z):
                origin = here.at(origin_z, 1 - here.y, here.c)
                self.arrived(origin)
                self.copy(origin, 3).start()

            pl.when((origin_z >= 0) & (origin_z <= 3))(go)

    def finish(self):
        here = self.here
        self.local.wait()
        for z in range(4):
            for y in range(2):
                self.arrived(here.at(z, y, 1 - here.c))
        self.each_send(lambda origin, way: self.copy(origin, way).wait_send())
        for z in range(4):
            self.copy(here.at(z, 1 - here.y, here.c), 3).wait_send()


def gather_scratch():
    sem = pltpu.SemaphoreType.DMA
    return [sem((2, 16, 4)), sem((2, 16)), sem((2,))]


def gather_kernel(tokens_in, gain, w_gate_inner, w_state_io, w_step, tokens_out, full, pack, low, ss, rs, ls, xs, xr, xl):
    here = Place()
    half = lax.axis_index("tensor")
    rows = tokens_in.shape[0]
    units, cols = w_gate_inner.shape[2], full.shape[1]
    pack[:, :units] = w_gate_inner[1]
    pack[:, units : units + BW] = w_state_io[...]
    pack[:, units + BW :] = mm(w_step[...], as_places(w_step.shape[1])).astype(bf16)
    greet(here, True)
    cut = cols // 256 * 128
    moves = [
        Gather(here, pack.at[:, c], full, ss, rs, ls, n, c) for n, c in enumerate((slice(0, cut), slice(cut, cols)))
    ]
    for move in moves:
        move.start()
    part = rows // 4
    across, local = [], []
    for n in range(4):
        piece = slice(n * part, n * part + part)
        v = tokens_in[piece].astype(f32)
        scale = lax.rsqrt(jnp.mean(v * v, axis=1, keepdims=True) + norm_eps)
        low[piece] = (v * scale * gain[0:1]).astype(bf16)
        slot = tokens_out.at[pl.ds(pl.multiple_of(half * rows + n * part, part), part)]
        across.append(remote(low.at[piece], slot, xs.at[n], xr.at[n], tensor=1 - half))
        across[-1].start()
        local.append(pltpu.make_async_copy(low.at[piece], slot, xl.at[n]))
        local[-1].start()
    for hops in range(1, 5):
        for move in moves:
            if hops < 4:
                move.hop(hops)
            move.sides(hops - 1)
    for n in range(4):
        local[n].wait()
        across[n].wait()
    for move in moves:
        move.finish()


def gather_rows(tokens_in, gain, w_gate_inner, w_state_io, w_step, ways, collective_id):
    rows, width = tokens_in.shape
    _, own, units = w_gate_inner.shape
    cols = units + BW + 128
    vmem = pl.BlockSpec(memory_space=pltpu.VMEM)
    hbm = pl.BlockSpec(memory_space=pl.ANY)
    sem = pltpu.SemaphoreType.DMA
    return pl.pallas_call(
        gather_kernel,
        name="gather_rows",
        in_specs=[vmem] * 5,
        out_specs=[hbm, hbm],
        out_shape=[sds((2 * rows, width), bf16), sds((ways * own, cols), bf16)],
        scratch_shapes=[
            pltpu.VMEM((own, cols), bf16), pltpu.VMEM((rows, width), bf16), *gather_scratch(),
            sem((4,)), sem((4,)), sem((4,)),
        ],
        compiler_params=pltpu.CompilerParams(
            collective_id=collective_id, has_side_effects=True, vmem_limit_bytes=60 * 1024 * 1024
        ),
    )(tokens_in, gain, w_gate_inner, w_state_io, w_step)


class Reduce:
    def __init__(self, here, grads, out, bufs, sems):
        self.here, self.grads, self.out = here, grads, out
        self.held, self.buf_a, self.buf_b, self.buf_up, self.buf_dn = bufs
        self.local, self.send_a, self.recv_a, self.send_b, self.recv_b, self.send_c, self.recv_up, self.recv_dn = sems
        self.parts, self.rows = out.shape[:2]
        z = here.z
        self.order = (3 * (1 - z // 2), (3 * z + 2) % 5, 1 + z % 2, z)

    def spot(self, z, y, c):
        if self.grads is None:
            return z, (y * 2 + c) * self.rows
        return z * 2 + y, 0

    def own(self, z, y, c=None):
        at, base = self.spot(z, y, self.here.c if c is None else c)
        return self.held.at[at, :, pl.ds(pl.multiple_of(base, 16), self.rows)]

    def block(self, z, y, c):
        if self.grads is None:
            return self.own(z, y, c)
        at = pl.multiple_of(self.here.at(z, y, c) * self.rows, self.rows)
        return self.grads.at[:, pl.ds(at, self.rows)]

    def copy_a(self, z, y):
        here, at = self.here, z * 2 + y
        return remote(self.block(z, y, 1 - here.c), self.buf_a.at[at], self.send_a.at[at], self.recv_a.at[at], dp=here.core())

    def take(self, z, y):
        return pltpu.make_async_copy(self.block(z, y, self.here.c), self.own(z, y), self.local.at[z * 2 + y])

    def copy_b(self, z):
        here = self.here
        return remote(self.own(z, 1 - here.y), self.buf_b.at[z], self.send_b.at[z], self.recv_b.at[z], dp=here.side())

    def copy_up(self, z):
        return remote(self.own(z, self.here.y), self.buf_up.at[z], self.send_c.at[z], self.recv_up.at[z], dp=self.here.up())

    def copy_dn(self, z):
        return remote(self.own(z, self.here.y), self.buf_dn.at[z], self.send_c.at[z], self.recv_dn.at[z], dp=self.here.down())

    def add(self, z, y, buf, slot):
        at, base = self.spot(z, y, self.here.c)

        def rows(n, carry):
            piece = pl.ds(pl.multiple_of(n * 16, 16), 16)
            held = pl.ds(pl.multiple_of(base + n * 16, 16), 16)
            for part in range(self.parts):
                total = self.held[at, part, held].astype(f32) + buf[slot, part, piece].astype(f32)
                self.held[at, part, held] = total.astype(bf16)
            return carry

        lax.fori_loop(0, self.rows // 16, rows, 0)

    def start(self):
        here = self.here
        for side in (1 - here.y, here.y):
            for z in self.order:
                self.copy_a(z, side).start()
                self.take(z, side).start()

    def join(self, z, y):
        if self.grads is not None:
            self.take(z, y).wait()
        self.copy_a(z, y).wait_recv()
        self.add(z, y, self.buf_a, z * 2 + y)

    def cores(self, z):
        self.join(z, 1 - self.here.y)
        self.copy_b(z).start()

    def stay(self, z):
        self.join(z, self.here.y)

    def sides(self, z):
        self.copy_b(z).wait_recv()
        self.add(z, self.here.y, self.buf_b, z)

    def pass_on(self, z):
        here = self.here

        def up():
            def below():
                self.copy_up(z).wait_recv()
                self.add(z, here.y, self.buf_up, z)

            pl.when(here.z > 0)(below)
            self.copy_up(z).start()

        def down():
            def above():
                self.copy_dn(z).wait_recv()
                self.add(z, here.y, self.buf_dn, z)

            pl.when(here.z < 3)(above)
            self.copy_dn(z).start()

        pl.when(z > here.z)(up)
        pl.when(z < here.z)(down)

    def finish(self):
        here = self.here
        z = here.z
        at, base = self.spot(z, here.y, here.c)
        pl.when(z > 0)(lambda: self.copy_up(z).wait_recv())
        pl.when(z < 3)(lambda: self.copy_dn(z).wait_recv())

        def rows(n, carry):
            piece = pl.ds(pl.multiple_of(n * 16, 16), 16)
            held = pl.ds(pl.multiple_of(base + n * 16, 16), 16)
            for part in range(self.parts):
                below = jnp.where(z > 0, self.buf_up[z, part, piece].astype(f32), 0.0)
                above = jnp.where(z < 3, self.buf_dn[z, part, piece].astype(f32), 0.0)
                self.out[part, piece] = self.held[at, part, held].astype(f32) + below + above
            return carry

        lax.fori_loop(0, self.rows // 16, rows, 0)
        for zn in self.order:
            self.copy_a(zn, 0).wait_send()
            self.copy_a(zn, 1).wait_send()
            self.copy_b(zn).wait_send()
            pl.when(zn > z)(lambda zn=zn: self.copy_up(zn).wait_send())
            pl.when(zn < z)(lambda zn=zn: self.copy_dn(zn).wait_send())


def reduce_scratch(parts, rows, cols, by_z=False):
    sem = pltpu.SemaphoreType.DMA
    block = (parts, rows, cols)
    held = (4, parts, 4 * rows, cols) if by_z else (8,) + block
    return [
        pltpu.VMEM(held, bf16), pltpu.VMEM((8,) + block, bf16), pltpu.VMEM((4,) + block, bf16),
        pltpu.VMEM((4,) + block, bf16), pltpu.VMEM((4,) + block, bf16),
        sem((8,)), sem((8,)), sem((8,)), sem((4,)), sem((4,)), sem((4,)), sem((4,)), sem((4,)),
    ]


def tail_kernel(
    normed_t, dinner, dsd, dgate, wb, wa, gk, ggg, gks, hs, norm_gain, w_gate_inner, w_state_io, w_step, gate_grads,
    gn_out, inner_out, step_out, both_out, small_out, shard_out, give, got, send_g, recv_g, nt_v, dinner_v, dsd_v, dgate_v, wg_v, wa_v, away, came, total, landed, loads, send_x, recv_x, send, recv, *scratch,
):
    here = Place()
    half = lax.axis_index("tensor")
    units = dgate.shape[1]
    sources = (normed_t, dinner, dsd, dgate, wb.at[:, :units], wa)
    pending = [
        pltpu.make_async_copy(src, dst, loads.at[n])
        for n, (src, dst) in enumerate(zip(sources, (nt_v, dinner_v, dsd_v, dgate_v, wg_v, wa_v)))
    ]
    for copy in pending:
        copy.start()
    far = pltpu.get_barrier_semaphore()
    partners = [here.me + bit - 2 * bit * ((here.me // bit) % 2) for bit in (2, 4, 8, 1)]
    for partner in partners:
        pl.semaphore_signal(far, 1, device_id={"dp": partner}, device_id_type=MESH)
    pl.semaphore_signal(far, 1, device_id={"tensor": 1 - half}, device_id_type=MESH)
    middle = (here.z == 1) | (here.z == 2)
    pl.when(here.z == 1)(lambda: pl.semaphore_signal(far, 1, device_id={"dp": here.up()}, device_id_type=MESH))
    pl.when(here.z == 2)(lambda: pl.semaphore_signal(far, 1, device_id={"dp": here.down()}, device_id_type=MESH))
    pl.semaphore_wait(far, 5 + middle.astype(jnp.int32))
    work = Reduce(here, None, shard_out, scratch[:5], scratch[5:])
    order = work.order
    rows = gn_out.shape[0]
    chunks, _, wide = away.shape

    def swap(k):
        return remote(total.at[k], landed.at[k], send.at[k], recv.at[k], dp=partners[k])

    def swapped(k):
        swap(k).wait()
        total[k + 1] = total[k] + landed[k]
        if k < 3:
            swap(k + 1).start()

    def across(n):
        return remote(away.at[n], came.at[n], send_x.at[n], recv_x.at[n], tensor=1 - half)

    def pulled(which, n):
        mine = pl.ds(pl.multiple_of(which * rows, rows), rows)
        at = pl.ds(pl.multiple_of(n * wide, wide), wide)
        return (
            mm(dgate_v[mine], wg_v[at], 1, 1)
            + mm(dinner_v[mine], wa_v[at, :units], 1, 1)
            + mm(dsd_v[mine], wa_v[at, units:], 1, 1)
        )

    def far_chunk(n, carry):
        away[n] = pulled(1 - half, n).astype(bf16)
        across(n).start()
        return carry

    def near_chunk(n, carry):
        gn_out[:, pl.ds(pl.multiple_of(n * wide, wide), wide)] = pulled(half, n)
        return carry

    def grads(n, carry):
        z = jnp.where(n == 0, order[0], jnp.where(n == 1, order[1], jnp.where(n == 2, order[2], order[3])))
        count = 4 * work.rows
        left = nt_v[pl.ds(pl.multiple_of(z * count, count), count)]
        work.held[z, 0, :, :units] = mm(left, dinner_v[...]).astype(bf16)
        work.held[z, 0, :, units:] = mm(left, dsd_v[...]).astype(bf16)
        work.copy_a(z, 1 - here.y).start()
        work.copy_a(z, here.y).start()

        @pl.when(n == 0)
        def _():
            for copy in pending[3:]:
                copy.wait()

        far_chunk(n, carry)
        work.cores(z)
        return carry

    total[0, 0:6] = gk[0:6]
    total[0, 6:7] = ggg[0:1]
    for k in range(5):
        total[0, 7:8, k * BW : k * BW + BW] = gks[k : k + 1]
    for k in range(2):
        total[0, 7:8, 5 * BW + k * 128 : 5 * BW + k * 128 + 128] = hs[k : k + 1]
    swap(0).start()
    for copy in pending[:3]:
        copy.wait()
    swapped(0)
    lax.fori_loop(0, 4, grads, 0)
    swapped(1)
    work.stay(order[0])
    work.sides(order[0])
    pl.when(~middle)(lambda: work.pass_on(order[0]))
    lax.fori_loop(4, chunks, far_chunk, 0)
    swapped(2)
    for n in range(1, 4):
        work.stay(order[n])
    work.sides(order[1])
    pl.when(~middle)(lambda: work.pass_on(order[1]))
    lax.fori_loop(0, 3, near_chunk, 0)
    pl.when(middle)(lambda: work.pass_on(order[0]))
    work.sides(order[2])
    pl.when(~middle)(lambda: work.pass_on(order[2]))
    lax.fori_loop(3, chunks, near_chunk, 0)
    swapped(3)
    small_out[...] = total[4]
    pl.when(middle)(lambda: work.pass_on(order[1]))
    work.sides(order[3])
    pl.when(middle)(lambda: work.pass_on(order[2]))
    work.finish()

    def arrive(n, carry):
        across(n).wait()
        at = pl.ds(pl.multiple_of(n * wide, wide), wide)
        gn_out[:, at] = gn_out[:, at] + came[n].astype(f32)
        return carry

    inner_out[0] = gate_grads[0]
    inner_out[1] = shard_out[0, :, :units]
    step_out[...] = shard_out[0, :, units + BW :]
    count = work.rows
    part = shard_out[0, :, units + BW :] * mm(w_step[...], as_places(w_step.shape[1]))
    for c in range(2):
        at = slice(units + c * 128, units + c * 128 + 128)
        part = part + shard_out[0, :, at] * w_state_io[:, c * 128 : c * 128 + 128].astype(f32)
    for c in range(units // 128):
        at = slice(c * 128, c * 128 + 128)
        part = part + gate_grads[0, :, at] * w_gate_inner[0, :, at].astype(f32)
        part = part + shard_out[0, :, at] * w_gate_inner[1, :, at].astype(f32)
    part = jnp.concatenate([part, jnp.zeros((128 - count, 128), f32)], axis=0)
    row = jnp.sum(jnp.transpose(part), axis=0, keepdims=True)
    shape = (norm_gain.shape[1], 128)
    pick = (iota(shape, 0) == iota(shape, 1) + here.me * count) & (iota(shape, 1) < count)
    gain = lay(norm_gain[...], pick.astype(f32).astype(bf16))[0:1]
    row = row / jnp.where(iota((1, 128), 1) < count, gain, 1.0)
    low = pltpu.roll(row, 128 - count // 2, 1)
    first = half == 0

    def share(at, a, b):
        both_out[at] = jnp.where(first, a, b)
        give[at] = jnp.where(first, b, a)

    share(slice(0, count), shard_out[0, :, units : units + 128], shard_out[0, :, units + 128 : units + 256])
    for k in range(5):
        pair = [small_out[7:8, k * BW + c * 128 : k * BW + c * 128 + 128] for c in range(2)]
        share(slice(count + k, count + k + 1), *pair)
    share(slice(count + 5, count + 6), row, low)
    share(slice(count + 6, count + 8), jnp.zeros((2, 128), f32), jnp.zeros((2, 128), f32))
    last = remote(give, got, send_g, recv_g, tensor=1 - half)
    last.start()
    lax.fori_loop(0, chunks, arrive, 0)
    last.wait()
    both_out[...] = both_out[...] + got[...]


def reduce_tail(normed_t, dinner, dsd, dgate, wb, wa, sums, weights, ways, collective_id):
    width, tokens = normed_t.shape
    small = sums[0]
    units, cols, rows = dgate.shape[1], wa.shape[1], width // ways
    chunks = width // BW
    vmem = pl.BlockSpec(memory_space=pltpu.VMEM)
    hbm = pl.BlockSpec(memory_space=pl.ANY)
    sem = pltpu.SemaphoreType.DMA
    return pl.pallas_call(
        tail_kernel, name="tail", in_specs=[hbm] * 6 + [vmem] * 9, out_specs=[vmem] * 5,
        out_shape=[
            sds((tokens // 2, width)), sds((2, rows, units)), sds((rows, 128)), sds((rows + 8, 128)), sds(small.shape),
        ],
        scratch_shapes=[
            pltpu.VMEM((1, rows, cols), f32), pltpu.VMEM((rows + 8, 128), f32), pltpu.VMEM((rows + 8, 128), f32), sem, sem,
            pltpu.VMEM(normed_t.shape, bf16), pltpu.VMEM(dinner.shape, bf16), pltpu.VMEM(dsd.shape, bf16),
            pltpu.VMEM(dgate.shape, bf16), pltpu.VMEM((width, units), bf16), pltpu.VMEM(wa.shape, bf16),
            pltpu.VMEM((chunks, tokens // 2, BW), bf16), pltpu.VMEM((chunks, tokens // 2, BW), bf16),
            pltpu.VMEM((5,) + small.shape, f32), pltpu.VMEM((4,) + small.shape, f32),
            sem((6,)), sem((chunks,)), sem((chunks,)), sem((4,)), sem((4,)),
        ] + reduce_scratch(1, rows, cols, True),
        compiler_params=pltpu.CompilerParams(
            collective_id=collective_id, has_side_effects=True, vmem_limit_bytes=62 * 1024 * 1024
        ),
    )(normed_t, dinner, dsd, dgate, wb, wa, *sums, *weights)


def swap(v):
    return lax.ppermute(v, "tensor", [(0, 1), (1, 0)])


def halves(v, axis):
    size = v.shape[axis] // 2
    me = lax.axis_index("tensor")
    return (
        lax.dynamic_slice_in_dim(v, me * size, size, axis),
        lax.dynamic_slice_in_dim(v, (1 - me) * size, size, axis),
    )


def once(shape, at=None):
    where = at or (0,) * len(shape)
    return pl.BlockSpec(shape, lambda i: where, pipeline_mode=pl.Buffered(1))


def by_cols(rows, offset=0):
    return pl.BlockSpec((rows, BW), lambda i: (0, i + offset))


def params(collective_id=None):
    return pltpu.CompilerParams(
        dimension_semantics=("arbitrary",), vmem_limit_bytes=60 * 1024 * 1024,
        collective_id=collective_id, has_side_effects=collective_id is not None,
    )


def spread(v):
    lead = v.shape[:-1]
    v = v.reshape(lead + (v.shape[-1] // HB, HB))
    v = jnp.pad(v, [(0, 0)] * len(lead) + [(0, 0), (0, 8 - HB)]).reshape(lead + (-1,))
    return jnp.pad(v, [(0, 0)] * len(lead) + [(0, 128 - v.shape[-1])])


def gathered_heads(v, heads):
    return v[..., : heads * 2].reshape(v.shape[:-1] + (heads // HB, 8))[..., :HB].reshape(v.shape[:-1] + (heads,))


def sds(shape, dtype=f32):
    return jax.ShapeDtypeStruct(shape, dtype)


def on_device(
    residual, norm_gain, w_gate_inner, w_state_io, w_step, conv_inner, conv_state,
    step_bias, decay_log, skip_gain, gate_gain, w_output, cotangent,
):
    width = residual.shape[1]
    units = w_gate_inner.shape[2]
    heads = w_step.shape[1]
    blocks = units // BW
    unit_total = units * lax.axis_size("tensor")
    ways = lax.axis_size("dp")
    own_links = ways == 16
    rows_in = residual.astype(f32)
    rstd_in = lax.rsqrt(jnp.mean(rows_in * rows_in, axis=1, keepdims=True) + norm_eps)
    scaled = rows_in * rstd_in
    pack_a = jnp.concatenate([w_gate_inner[1], w_state_io, spread(w_step)], axis=1)
    w_output_t = w_output.T
    gain_in = jnp.broadcast_to(norm_gain[None], (8, width))
    if own_links:
        normed, wa = gather_rows(residual, gain_in, w_gate_inner, w_state_io, w_step, ways, 1)
    else:
        wa = lax.all_gather(pack_a, "dp", axis=0, tiled=True)
        normed = lax.all_gather((scaled * norm_gain).astype(bf16), "tensor", axis=0, tiled=True)
    tokens = normed.shape[0]
    spans = tokens // Q
    gain8 = jnp.broadcast_to(gate_gain[None], (8, units))

    hbm = pl.BlockSpec(memory_space=pl.ANY)
    sem = pltpu.SemaphoreType.DMA
    def stage(rows, first):
        return pl.BlockSpec((rows, BW), lambda i: (0, jnp.clip(i - first, 0, blocks - 1)))

    inner, ssd, states, cst, bc, step, cum, step_t, cum_t, pre_t, *sent = pl.pallas_call(
        functools.partial(mixer_forward, own_links),
        name="mixer_forward",
        grid=(blocks * (3 if own_links else 1),),
        in_specs=[
            once((tokens, width)), stage(width, 0), once((width, 384), (0, units // 384)),
            stage(5, 0), once((5, BW)), once((heads,)), once((heads,)), once((heads,)),
        ] + ([once(v.shape) for v in (cotangent, w_gate_inner, w_output_t)] + [stage(8, 2 * blocks)]) * own_links,
        out_specs=[
            stage(tokens, 0), stage(tokens, 0), pl.BlockSpec((spans, BW, 128), lambda i: (0, jnp.clip(i, 0, blocks - 1), 0)),
            once((tokens, BW)), once((tokens, BW)), once((tokens, 128)), once((tokens, 128)),
            once((48, tokens)), once((48, tokens)), once((48, tokens)),
        ] + [hbm, hbm, stage(tokens, blocks), stage(tokens, 2 * blocks), once((8, tokens))] * own_links,
        out_shape=[
            sds((tokens, units)), sds((tokens, units)), sds((spans, units, 128)),
            sds((tokens, BW)), sds((tokens, BW), bf16), sds((tokens, 128)), sds((tokens, 128)),
            sds((48, tokens)), sds((48, tokens)), sds((48, tokens)),
        ] + [
            sds((tokens, width), bf16), sds((width, 2 * units), bf16), sds((tokens, units)), sds((tokens, units)),
            sds((8, tokens)),
        ] * own_links,
        scratch_shapes=[
            pltpu.VMEM((tokens + 8, BW), f32), pltpu.VMEM((spans, Q, Q), f32),
            pltpu.VMEM((tokens, 128), f32), pltpu.VMEM((tokens, 128), f32), pltpu.VMEM((8, tokens), f32),
            pltpu.VMEM((Q, HB * Q), bf16), pltpu.VMEM((HB * Q, BW), bf16), pltpu.VMEM((BW, 128), f32),
        ] + ([
            pltpu.VMEM((blocks + 1, tokens, BW), f32), pltpu.VMEM((blocks, width, BW), bf16), pltpu.VMEM((tokens, width), bf16),
            pltpu.VMEM((tokens, 128), f32), pltpu.VMEM((tokens, 128), f32), pltpu.VMEM((8, tokens), f32),
            pltpu.VMEM((8, tokens), f32), sem((blocks,)), sem((3,)),
        ] + gather_scratch() + [sem, sem, sem]) * own_links,
        compiler_params=params(2 if own_links else None),
        cost_estimate=pl.CostEstimate(flops=2 * tokens * width * (units + 384) + 4 * tokens * 256 * units, bytes_accessed=30_000_000, transcendentals=heads * spans * Q * Q),
    )(
        normed, wa, wa, conv_inner, conv_state, step_bias, decay_log, skip_gain,
        *[cotangent, w_gate_inner, w_output_t, gain8] * own_links,
    )

    if own_links:
        cot, wb, gate, ggo, stats = sent
    else:
        wb = lax.all_gather(jnp.concatenate([w_gate_inner[0], w_output_t], axis=1), "dp", axis=0, tiled=True)
        cot = lax.all_gather(cotangent, "tensor", axis=0, tiled=True)
        gate, ggo, stats = pl.pallas_call(
            gate_forward,
            name="gate_forward",
            grid=(blocks,),
            in_specs=[
                once((tokens, width)), once((tokens, width)), by_cols(width), by_cols(width, blocks),
                by_cols(tokens), by_cols(8),
            ],
            out_specs=[by_cols(tokens), by_cols(tokens), once((8, tokens))],
            out_shape=[sds((tokens, units)), sds((tokens, units)), sds((8, tokens))],
            scratch_shapes=[pltpu.VMEM((tokens, 128), f32), pltpu.VMEM((tokens, 128), f32)],
            compiler_params=params(),
            cost_estimate=pl.CostEstimate(flops=4 * tokens * width * units, bytes_accessed=35_000_000, transcendentals=tokens * units),
        )(normed, cot, wb, wb, ssd, gain8)
        stats = stats + swap(stats)

    dy, dgate, ng, ggg, grad_b, normed_t = pl.pallas_call(
        functools.partial(gate_backward, float(unit_total)),
        name="gate_backward",
        grid=(blocks,),
        in_specs=[
            once((8, tokens)), by_cols(tokens), by_cols(tokens), by_cols(tokens), by_cols(8),
            once((tokens, width)), once((tokens, width)),
        ],
        out_specs=[
            by_cols(tokens), by_cols(tokens), by_cols(tokens), by_cols(8),
            pl.BlockSpec((2, width, BW), lambda i: (0, 0, i)), once((width, tokens)),
        ],
        out_shape=[
            sds((tokens, units), bf16), sds((tokens, units), bf16), sds((tokens, units), bf16), sds((8, units)),
            sds((2, width, units), bf16), sds((width, tokens), bf16),
        ],
        scratch_shapes=[pltpu.VMEM((tokens, 128), f32), pltpu.VMEM((width, tokens), bf16)],
        compiler_params=params(),
        cost_estimate=pl.CostEstimate(flops=4 * tokens * units * width, bytes_accessed=45_000_000, transcendentals=tokens * units),
    )(stats, gate, ssd, ggo, gain8, normed, cot)

    mixed = mm(ng, wb[:, units:], 1, 1).astype(bf16)
    mixed_near, mixed_far = halves(mixed, 0)

    dinner, gk, dsd, gks, hs, *sent = pl.pallas_call(
        functools.partial(mixer_backward, own_links),
        name="mixer_backward",
        grid=(blocks,),
        in_specs=[
            by_cols(tokens), by_cols(tokens), pl.BlockSpec((spans, BW, 128), lambda i: (0, i, 0)),
            by_cols(5), once((5, BW)), once((heads,)), once((heads,)),
            once((tokens, BW)), once((tokens, BW)), once((tokens, 128)), once((tokens, 128)),
            once((48, tokens)), once((48, tokens)), once((48, tokens)),
        ] + [hbm, hbm] * own_links,
        out_specs=[by_cols(tokens), by_cols(8), once((tokens, 384)), once((8, BW)), once((8, 128))]
        + [hbm, once((2, width // ways, units))] * own_links,
        out_shape=[sds((tokens, units), bf16), sds((8, units)), sds((tokens, 384), bf16), sds((8, BW)), sds((8, 128))]
        + [sds((tokens // 2, width), bf16), sds((2, width // ways, units))] * own_links,
        scratch_shapes=[
            pltpu.VMEM((tokens + 8, BW), f32), pltpu.VMEM((tokens + 8, BW), f32),
            pltpu.VMEM((spans, Q, Q), f32), pltpu.VMEM((spans, Q, Q), f32),
            pltpu.VMEM((tokens, 128), f32), pltpu.VMEM((tokens, 128), f32),
            pltpu.VMEM((tokens, 128), f32), pltpu.VMEM((tokens, 128), f32), pltpu.VMEM((8, tokens), f32),
            pltpu.VMEM((HB * Q, Q), bf16), pltpu.VMEM((HB * Q, BW), bf16), pltpu.VMEM((HB * Q, Q), f32),
            pltpu.VMEM((BW, 128), f32),
            pltpu.VMEM((48, tokens), f32), pltpu.VMEM((48, tokens), f32), pltpu.VMEM((48, tokens), f32),
            pltpu.VMEM((48, tokens), f32), pltpu.VMEM((48, 128), f32), pltpu.VMEM((8, BW), f32),
        ] + ([sem, sem] + reduce_scratch(2, width // ways, units)) * own_links,
        compiler_params=params(4 if own_links else None),
        cost_estimate=pl.CostEstimate(flops=40_000_000_000, bytes_accessed=30_000_000, transcendentals=heads * spans * Q * Q),
    )(
        inner, dy, states, conv_inner, conv_state, decay_log, skip_gain, cst, bc, step, cum, step_t, cum_t, pre_t,
        *[mixed, grad_b] * own_links,
    )
    if own_links:
        mixed_got, wb_shard = sent
    else:
        mixed_got = swap(mixed_far)
        wb_shard = lax.psum_scatter(grad_b, "dp", scatter_dimension=1, tiled=True).astype(f32)
    output = (rows_in + mixed_near.astype(f32) + mixed_got.astype(f32)).astype(bf16)

    if own_links:
        weights = (gain_in, w_gate_inner, w_state_io, w_step, wb_shard)
        sums = (gk, ggg, gks, hs)
        grad_normed, inner_grads, step_grads, both, small = reduce_tail(
            normed_t, dinner, dsd, dgate, wb, wa, sums, weights, ways, 5
        )
    else:
        last = jnp.concatenate([gks[:5].reshape(-1), hs[0], hs[1]])
        small = jnp.concatenate([gk[:6], ggg[:1], last[None]], axis=0)
        grad_a = jnp.concatenate([mm(normed_t, dinner).astype(bf16), mm(normed_t, dsd).astype(bf16)], axis=1)
        pulled = mm(dgate, wb[:, :units], 1, 1) + mm(dinner, wa[:, :units], 1, 1) + mm(dsd, wa[:, units:], 1, 1)
        near, far = halves(pulled.astype(bf16), 0)
        wa_shard = lax.psum_scatter(grad_a, "dp", scatter_dimension=0, tiled=True).astype(f32)
        small = lax.psum(small, "dp")
        grad_normed = near.astype(f32) + swap(far).astype(f32)
    grad_v = grad_normed * norm_gain
    grad_residual = cotangent.astype(f32) + rstd_in * (
        grad_v - scaled * jnp.mean(grad_v * scaled, axis=1, keepdims=True)
    )

    bias_sum = gathered_heads(small[7, 5 * BW : 5 * BW + 128], heads)
    decay_sum = gathered_heads(small[7, 5 * BW + 128 : 5 * BW + 256], heads)
    skip_sum = jnp.sum(small[5].reshape(heads, HEAD), axis=1)

    count = width // ways
    if own_links:
        gain_part = both[count + 5, : count // 2]
    else:
        conv_state_sum = small[7, : 5 * BW].reshape(5, BW)
        gain_rows = jnp.sum(wb_shard[0] * w_gate_inner[0].astype(f32), axis=1) + jnp.sum(
            wa_shard * pack_a.astype(f32), axis=1
        )
        gain_own = gain_rows / lax.dynamic_slice_in_dim(norm_gain, lax.axis_index("dp") * count, count)
        near_s, far_s = halves(jnp.concatenate([wa_shard[:, units : units + BW], conv_state_sum], axis=0), 1)
        near_g, far_g = halves(gain_own, 0)
        far_all = jnp.concatenate([far_s.reshape(-1), far_g])
        got = swap(far_all)
        both = near_s + got[: far_s.size].reshape(far_s.shape)
        gain_part = near_g + got[far_s.size :]
        inner_grads = jnp.stack([wb_shard[0], wa_shard[:, :units]])
        step_grads = wa_shard[:, units + BW :]
    return (
        output,
        grad_residual,
        gain_part,
        inner_grads,
        both[:count],
        gathered_heads(step_grads, heads),
        small[0:5],
        both[count : count + 5],
        bias_sum,
        decay_sum,
        skip_sum,
        small[6],
        wb_shard[1].T,
    )


def solution(mesh):
    return jax.shard_map(
        on_device,
        mesh=mesh,
        in_specs=(
            P(("dp", "tensor"), None),
            P(),
            P(None, "dp", "tensor"),
            P("dp", None),
            P("dp", "tensor"),
            P(None, "tensor"),
            P(),
            P("tensor"),
            P("tensor"),
            P("tensor"),
            P("tensor"),
            P("tensor", "dp"),
            P(("dp", "tensor"), None),
        ),
        out_specs=(
            P(("dp", "tensor"), None),
            P(("dp", "tensor"), None),
            P(("dp", "tensor")),
            P(None, "dp", "tensor"),
            P("dp", "tensor"),
            P("dp", "tensor"),
            P(None, "tensor"),
            P(None, "tensor"),
            P("tensor"),
            P("tensor"),
            P("tensor"),
            P("tensor"),
            P("tensor", "dp"),
        ),
        check_vma=False,
    )
```

```python
import functools

import jax
import jax.numpy as jnp
from jax import lax
from jax.experimental import pallas as pl
from jax.experimental.pallas import tpu as pltpu
from jax.sharding import PartitionSpec as P

Q = 256
LEN = 1024
HEAD = 64
BW = 256
HB = BW // HEAD
LOG2E = 1.4426950408889634
FAR = -1e30
norm_eps = 1e-05
MESH = pl.DeviceIdType.MESH
f32 = jnp.float32
bf16 = jnp.bfloat16


def mm(a, b, ca=1, cb=0):
    return lax.dot_general(a, b, (((ca,), (cb,)), ((), ())), preferred_element_type=f32)


def sigmoid(v):
    return 1.0 / (1.0 + jnp.exp(-v))


def split3(a):
    hi = a.astype(bf16)
    rest = a - hi.astype(f32)
    mid = rest.astype(bf16)
    low = (rest - mid.astype(f32)).astype(bf16)
    return hi, mid, low


def split2(a):
    hi = a.astype(bf16)
    return hi, (a - hi.astype(f32)).astype(bf16)


def iota(shape, axis):
    return lax.broadcasted_iota(jnp.int32, shape, axis)


def expand(cols):
    rows = cols.shape[0]
    left = iota((rows, 128), 1) < HEAD
    return jnp.concatenate(
        [jnp.where(left, cols[:, 2 * q : 2 * q + 1], cols[:, 2 * q + 1 : 2 * q + 2]) for q in range(2)],
        axis=1,
    )


def conv_taps(window, kernel):
    out = kernel[4:5] + kernel[3:4] * window[8:]
    for k in range(3):
        out = out + kernel[k : k + 1] * pltpu.roll(window, 3 - k, 0)[8:]
    return out


def head_row(ref):
    return jnp.broadcast_to(ref[...][None, :], (8, ref.shape[0]))


def lay(rows, pick):
    parts = split3(rows)
    return mm(parts[0], pick) + mm(parts[1], pick) + mm(parts[2], pick)


def as_places(heads):
    lane = iota((heads, 128), 1)
    place = lane % 8
    return ((lane // 8 * HB + place == iota((heads, 128), 0)) & (place < HB)).astype(f32).astype(bf16)


def as_units(heads, block):
    return (iota((heads, BW), 1) // HEAD + HB * block == iota((heads, BW), 0)).astype(f32).astype(bf16)


def head_masks():
    lane = iota((1, BW), 1) // HEAD
    return [(lane == j).astype(f32).astype(bf16) for j in range(HB)]


def quads():
    for r in range(0, Q, 64):
        for half in range(2):
            if half * 128 <= r:
                yield r, half, r < half * 128 + 128


def decay_chunk(col, row, r, half, diag):
    gap = col[r : r + 64] - row[:, half * 128 : half * 128 + 128]
    if diag:
        keep = iota((64, 128), 0) + (r - half * 128) >= iota((64, 128), 1)
        gap = jnp.where(keep, gap, FAR)
    return jnp.exp2(gap)


def mixer_forward(links, normed, wi, wsx, kin, kst, bias, log_rate, skip_in, *refs):
    refs = list(refs)
    if links:
        sent = refs[:3] + refs[14:16]
        gain, gate_refs = refs[3], refs[16:19]
        refs = refs[4:14] + refs[19:]
    inner_out, ssd_out, states_out, cst_out, bc_out, step_out, cum_out, stepT_out, cumT_out, preT_out = refs[:10]
    buf, gram, colc, cols, rowp, mst, xst, state = refs[10:18]
    i = pl.program_id(0)
    tokens = normed.shape[0]
    spans = tokens // Q
    blocks = inner_out.shape[1] // BW
    if links:
        work = BesideForward(*sent, *refs[27:])
        ssd_v, *gate_scratch = refs[18:27]
        blocks = ssd_v.shape[0] - 1
    heads = bias.shape[0]
    skip = lay(head_row(skip_in), as_units(heads, i))[0:1]

    if links:
        pl.when(i == 0)(work.start)

    @pl.when(i == 0)
    def _():
        proj = mm(normed[...], wsx[...])
        buf[0:8] = jnp.zeros((8, BW), f32)
        cst_out[...] = proj[:, :BW]
        buf[8 : 8 + tokens] = proj[:, :BW]
        tri = (iota((Q, Q), 0) >= iota((Q, Q), 1)).astype(f32).astype(bf16)
        places = as_places(heads)
        pre = proj[:, BW:] + lay(head_row(bias), places)[0:1]
        step = jnp.maximum(pre, 0.0) + jnp.log1p(jnp.exp(-jnp.abs(pre)))
        step_out[...] = step
        scaled = step * (lay(-jnp.exp(head_row(log_rate)), places)[0:1] * LOG2E)
        for s in range(spans):
            parts = split3(scaled[s * Q : s * Q + Q])
            cum_out[s * Q : s * Q + Q] = mm(tri, parts[0]) + mm(tri, parts[1]) + mm(tri, parts[2])
            conv = conv_taps(buf[s * Q : s * Q + Q + 8], kst[...])
            bc = (conv * sigmoid(conv)).astype(bf16)
            bc_out[s * Q : s * Q + Q] = bc
            gram[s] = mm(bc[:, 128:], bc[:, :128], 1, 1)
        preT_out[...] = jnp.transpose(pre)[:48]
        stepT_out[...] = jnp.transpose(step)[:48]
        cumT_out[...] = jnp.transpose(cum_out[...])[:48]
        mst[...] = jnp.zeros(mst.shape, bf16)

    def mix():
        inner = mm(normed[...], wi[...])
        inner_out[...] = inner
        buf[8 : 8 + tokens] = inner
        turn = lax.rem(128 - 8 * i, 128)
        colc[...] = pltpu.roll(cum_out[...], turn, 1)
        cols[...] = pltpu.roll(step_out[...], turn, 1)
        rows8 = pl.ds(pl.multiple_of(8 * i, 8), 8)
        rowp[...] = cumT_out[rows8] - jnp.log2(stepT_out[rows8])
        state[...] = jnp.zeros(state.shape, f32)
        masks = head_masks()

        def span(s, carry):
            at = pl.multiple_of(s * Q, Q)
            rows = pl.ds(at, Q)
            conv = conv_taps(buf[pl.ds(at, Q + 8)], kin[...])
            xs = conv * sigmoid(conv)
            x_low = xs.astype(bf16)
            col = colc[rows]
            total = col[Q - 1 : Q]
            growth = expand(jnp.exp2(col[:, :8]))
            weight = expand(jnp.exp2(total[:, :8] - col[:, :8]) * cols[rows][:, :8])
            xw_low = (xs * weight).astype(bf16)
            for j in range(HB):
                xst[j * Q : j * Q + Q] = x_low * masks[j]
                row = rowp[j : j + 1, rows]
                for r, half, diag in quads():
                    part = gram[s, r : r + 64, half * 128 : half * 128 + 128]
                    dec = decay_chunk(col[:, j : j + 1], row, r, half, diag)
                    mst[r : r + 64, j * Q + half * 128 : j * Q + half * 128 + 128] = (part * dec).astype(bf16)
            intra = mm(mst[...], xst[...])
            state_in = state[...]
            states_out[s] = state_in
            bc = bc_out[rows]
            readout = mm(bc[:, 128:], state_in.astype(bf16), 1, 1)
            ssd = intra + growth * readout + skip * xs
            ssd_out[rows] = ssd
            if links:
                ssd_v[blocks, rows] = ssd
            local = mm(xw_low, bc[:, :128], 0, 0)
            fade = jnp.exp2(total)
            for j in range(HB):
                at_j = slice(j * HEAD, j * HEAD + HEAD)
                state[at_j] = fade[:, j : j + 1] * state_in[at_j] + local[at_j]
            if links:
                work.step(i * spans + s)
            return carry

        lax.fori_loop(0, spans, span, 0)

    if not links:
        mix()
        return
    pl.when(i < blocks)(mix)

    @pl.when(i < blocks)
    def _():
        ssd_v[i] = ssd_v[blocks]

    gates = GateForward(i - blocks, blocks, normed, sent[3], sent[4], gain, ssd_v, *gate_refs, *gate_scratch)

    @pl.when(i == blocks)
    def _():
        work.first()
        gates.start(0)


    @pl.when((i >= blocks) & (i < 2 * blocks))
    def _():
        gates.gate()
        work.between(i - blocks)


    @pl.when(i == 2 * blocks)
    def _():
        work.finish()
        gates.start(1)

    pl.when(i >= 2 * blocks)(gates.pull)


class GateForward:
    def __init__(
        self, at, blocks, normed, cot, wb, gain, ssd_v, gate_out, ggo_out, stats_out, w_v, cot_v, sq, gi, mine, landed, wl, cl
    ):
        self.at, self.blocks, self.normed, self.cot, self.wb, self.gain, self.ssd_v = at, blocks, normed, cot, wb, gain, ssd_v
        self.gate_out, self.ggo_out, self.stats_out = gate_out, ggo_out, stats_out
        self.w_v, self.cot_v, self.sq, self.gi, self.mine, self.landed, self.wl, self.cl = w_v, cot_v, sq, gi, mine, landed, wl, cl

    def load(self, which, n):
        cols = slice((which * self.blocks + n) * BW, (which * self.blocks + n + 1) * BW)
        return pltpu.make_async_copy(self.wb.at[:, cols], self.w_v.at[n], self.wl.at[n])

    def tokens(self):
        return pltpu.make_async_copy(self.cot, self.cot_v, self.cl.at[0])

    def start(self, which):
        if not which:
            self.tokens().start()
        for n in range(self.blocks):
            self.load(which, n).start()
        if which:
            self.tokens().wait()
        total = self.gi if which else self.sq
        total[...] = jnp.zeros(total.shape, f32)

    def gate(self):
        b = self.at
        pltpu.make_async_copy(self.wb.at[:, :BW], self.w_v.at[b], self.wl.at[b]).wait()
        gate = mm(self.normed[...], self.w_v[b])
        self.gate_out[...] = gate
        gated = self.ssd_v[b] * (gate * sigmoid(gate))
        self.ssd_v[b] = gated
        squares = gated * gated
        self.sq[...] += squares[:, :128] + squares[:, 128:]

    def pull(self):
        b = self.at - self.blocks
        pltpu.make_async_copy(self.wb.at[:, :BW], self.w_v.at[b], self.wl.at[b]).wait()
        ggo = mm(self.cot_v[...], self.w_v[b])
        self.ggo_out[...] = ggo
        inner = ggo * self.gain[0:1] * self.ssd_v[b]
        self.gi[...] += inner[:, :128] + inner[:, 128:]
        pl.when(b == self.blocks - 1)(self.last)

    def last(self):
        self.mine[...] = token_sums(self.sq[...], self.gi[...])
        swap = remote(self.mine, self.landed, self.cl.at[1], self.cl.at[2], tensor=1 - lax.axis_index("tensor"))
        swap.start()
        swap.wait()
        self.stats_out[...] = self.mine[...] + self.landed[...]


def token_sums(sq, gi):
    lane = iota(sq.shape, 1)
    both = jnp.where(
        lane == 0,
        jnp.sum(sq, axis=1, keepdims=True),
        jnp.where(lane == 1, jnp.sum(gi, axis=1, keepdims=True), 0.0),
    )
    return jnp.transpose(both)[:8]


class BesideForward:
    def __init__(self, cot, w_gate_inner, w_output_t, cot_out, wb, ss, rs, ls, xs, xr, xl):
        self.here = Place()
        units = w_output_t.shape[1]
        self.moves = [
            Gather(self.here, own, wb, ss, rs, ls, n, slice(n * units, n * units + units))
            for n, own in enumerate((w_gate_inner.at[0], w_output_t))
        ]
        half = lax.axis_index("tensor")
        rows = cot.shape[0]
        slot = cot_out.at[pl.ds(pl.multiple_of(half * rows, rows), rows)]
        self.across = remote(cot, slot, xs, xr, tensor=1 - half)
        self.local = pltpu.make_async_copy(cot, slot, xl)

    def start(self):
        greet(self.here, True)
        for move in self.moves:
            move.start()
        self.across.start()
        self.local.start()

    def step(self, at):
        for when, chunk, hops in ((6, 0, 1), (10, 1, 1), (14, 0, 2), (18, 1, 2), (22, 0, 3)):

            def go(move=self.moves[chunk], hops=hops):
                move.hop(hops)
                move.sides(hops - 1)

            pl.when(at == when)(go)

    def first(self):
        self.moves[0].sides(3)
        self.moves[1].hop(3)
        self.moves[0].finish()
        self.local.wait()
        self.across.wait()

    def between(self, at):
        pl.when(at == 1)(lambda: self.moves[1].sides(2))

    def finish(self):
        move = self.moves[1]
        move.sides(3)
        move.finish()


def gate_forward(normed, cot, wg, wo, ssd, gain, gate_out, ggo_out, stats_out, sq, gi):
    i = pl.program_id(0)

    @pl.when(i == 0)
    def _():
        sq[...] = jnp.zeros(sq.shape, f32)
        gi[...] = jnp.zeros(gi.shape, f32)

    gate = mm(normed[...], wg[...])
    gate_out[...] = gate
    ggo = mm(cot[...], wo[...])
    ggo_out[...] = ggo
    gated = ssd[...] * (gate * sigmoid(gate))
    squares = gated * gated
    sq[...] += squares[:, :128] + squares[:, 128:]
    inner = ggo * gain[0:1] * gated
    gi[...] += inner[:, :128] + inner[:, 128:]

    @pl.when(i == pl.num_programs(0) - 1)
    def _():
        stats_out[...] = token_sums(sq[...], gi[...])


def gate_backward(
    unit_total, stats, gate, ssd, ggo, gain, normed, cot, dy_out, dgate_out, ng_out, gg_out, grads_out, normed_t, cols, cot_t
):
    @pl.when(pl.program_id(0) == 0)
    def _():
        full = jnp.concatenate([stats[...], jnp.zeros((120, stats.shape[1]), f32)], axis=0)
        cols[...] = jnp.transpose(full)

        def turn(n, carry):
            here = pl.ds(pl.multiple_of(n * 128, 128), 128)
            normed_t[here] = jnp.transpose(normed[:, here])
            cot_t[here] = jnp.transpose(cot[:, here])
            return carry

        lax.fori_loop(0, normed.shape[1] // 128, turn, 0)

    rstd = lax.rsqrt(cols[:, 0:1] / unit_total + norm_eps)
    pull = rstd * rstd * rstd * (cols[:, 1:2] / unit_total)
    v = gate[...]
    sig = sigmoid(v)
    act = v * sig
    y = ssd[...]
    gated = y * act
    scaled = gated * rstd
    ng = (scaled * gain[0:1]).astype(bf16)
    ng_out[...] = ng
    grads_out[1] = mm(cot_t[...], ng).astype(bf16)
    gg = ggo[...]
    gg_out[...] = jnp.broadcast_to(jnp.sum(gg * scaled, axis=0, keepdims=True), gg_out.shape)
    grad = rstd * (gg * gain[0:1]) - gated * pull
    dy_out[...] = (grad * act).astype(bf16)
    dgate = (grad * y * (sig * (1.0 + v * (1.0 - sig)))).astype(bf16)
    dgate_out[...] = dgate
    grads_out[0] = mm(normed_t[...], dgate).astype(bf16)


class BesideBackward:
    def __init__(self, mixed, grads, far_out, shard_out, scratch):
        self.here = Place()
        half = lax.axis_index("tensor")
        rows = far_out.shape[0]
        other = mixed.at[pl.ds(pl.multiple_of((1 - half) * rows, rows), rows)]
        self.across = remote(other, far_out, scratch[0], scratch[1], tensor=1 - half)
        self.sum = Reduce(self.here, grads, shard_out, scratch[2:7], scratch[7:15])

    def start(self):
        greet(self.here, True)
        self.sum.start()
        self.across.start()

    def step(self, at):
        total = self.sum
        z = self.here.z
        ends = (z == 0) | (z == 3)
        for n, block in enumerate(total.order):
            pl.when(at == n)(lambda z=block: total.cores(z))
            pl.when(at == (4, 5, 7, 8)[n])(lambda z=block: total.stay(z))
            pl.when(at == (6, 11, 17, 22)[n])(lambda z=block: total.sides(z))
        for n, block in enumerate(total.order[:3]):
            when = jnp.where(ends, (6, 11, 17)[n], (12, 18, 19)[n])
            pl.when(at == when)(lambda z=block: total.pass_on(z))

    def finish(self):
        self.sum.finish()
        self.across.wait()


def mixer_backward(links, inner, dy, states, kin, kst, log_rate, skip_in, cst, bc_in, step_in, cum_in, stepT, cumT, preT, *refs):
    refs = list(refs)
    if links:
        beside = refs[:2] + refs[7:9]
        refs = refs[2:7] + refs[9:]
        work = BesideBackward(*beside, refs[24:])
    dinner_out, gk_out, dsd_out, gks_out, hs_out = refs[:5]
    buf, dbuf, gram, gg, gb, gc, colc, cols, rowp, mst, dyst, gmix, sgrad = refs[5:18]
    rs_t, cs_t, dr_t, wg_t, gt_t, gtaps = refs[18:24]
    i = pl.program_id(0)
    if links:
        pl.when(i == 0)(work.start)
    heads = log_rate.shape[0]
    skip = lay(head_row(skip_in), as_units(heads, i))[0:1]
    tokens = inner.shape[0]
    spans = tokens // Q
    masks = head_masks()

    @pl.when(i == 0)
    def _():
        buf[0:8] = jnp.zeros((8, BW), f32)
        dbuf[tokens : tokens + 8] = jnp.zeros((8, BW), f32)
        for s in range(spans):
            bc = bc_in[s * Q : s * Q + Q]
            gram[s] = mm(bc[:, 128:], bc[:, :128], 1, 1)
        for ref in (gg, gb, gc, rs_t, cs_t, dr_t, wg_t, gt_t):
            ref[...] = jnp.zeros(ref.shape, f32)
        mst[...] = jnp.zeros(mst.shape, bf16)

    buf[8 : 8 + tokens] = inner[...]
    turn = lax.rem(128 - 8 * i, 128)
    colc[...] = pltpu.roll(cum_in[...], turn, 1)
    cols[...] = pltpu.roll(step_in[...], turn, 1)
    rows8 = pl.ds(pl.multiple_of(8 * i, 8), 8)
    rowp[...] = cumT[rows8] - jnp.log2(stepT[rows8])
    sgrad[...] = jnp.zeros(sgrad.shape, f32)
    gtaps[...] = jnp.zeros(gtaps.shape, f32)
    pick = (iota((8, BW), 1) // HEAD == iota((8, BW), 0)).astype(f32).astype(bf16)

    def conv_rows(at, kernel, grad_act, conv, sig):
        gco = grad_act * (sig * (1.0 + conv * (1.0 - sig)))
        dbuf[pl.ds(at, Q)] = gco
        into = buf[pl.ds(pl.multiple_of(at + 8, 8), Q)]
        gtaps[4:5] += jnp.sum(gco, axis=0, keepdims=True)
        after = dbuf[pl.ds(at, Q + 8)]
        grad_in = kernel[3:4] * gco
        gtaps[3:4] += jnp.sum(gco * into, axis=0, keepdims=True)
        for k in range(3):
            later = pltpu.roll(after, Q + 8 - (3 - k), 0)[:Q]
            gtaps[k : k + 1] += jnp.sum(later * into, axis=0, keepdims=True)
            grad_in = grad_in + kernel[k : k + 1] * later
        return grad_in

    def span(back, carry):
        s = spans - 1 - back
        at = pl.multiple_of(s * Q, Q)
        rows = pl.ds(at, Q)
        conv = conv_taps(buf[pl.ds(at, Q + 8)], kin[...])
        sig = sigmoid(conv)
        xs = conv * sig
        x_low = xs.astype(bf16)
        dy_s = dy[rows]
        dy_f = dy_s.astype(f32)
        bc = bc_in[rows]
        b_low, c_low = bc[:, :128], bc[:, 128:]
        col = colc[rows]
        total = col[Q - 1 : Q]
        for j in range(HB):
            dyst[j * Q : j * Q + Q] = dy_s * masks[j]
        gmix[...] = mm(dyst[...], x_low, 1, 1)
        lane = iota((Q, 128), 1)
        row_sums = jnp.zeros((Q, 128), f32)
        for j in range(HB):
            row = rowp[j : j + 1, rows]
            col_sum = [jnp.zeros((1, 128), f32), jnp.zeros((1, 128), f32)]
            row_parts = []
            for r, half, diag in quads():
                here = slice(half * 128, half * 128 + 128)
                dec = decay_chunk(col[:, j : j + 1], row, r, half, diag)
                part = gram[s, r : r + 64, here]
                p = gmix[j * Q + r : j * Q + r + 64, here] * dec
                gg[s, r : r + 64, here] += p
                q = p * part
                mst[j * Q + r : j * Q + r + 64, here] = (part * dec).astype(bf16)
                col_sum[half] = col_sum[half] + jnp.sum(q, axis=0, keepdims=True)
                if half == 0:
                    row_parts.append(q)
                else:
                    row_parts[-1] = row_parts[-1] + q
            sums = jnp.concatenate([jnp.sum(q, axis=1, keepdims=True) for q in row_parts], axis=0)
            row_sums = jnp.where(lane == j, sums, row_sums)
            cs_t[pl.ds(8 * i + j, 1), rows] = jnp.concatenate(col_sum, axis=1)
        rs_t[rows8, rows] = jnp.transpose(row_sums)[:8]
        grad_xs = mm(mst[...], dyst[...], 0, 0) + skip * dy_f

        growth = expand(jnp.exp2(col[:, :8]))
        weight = expand(jnp.exp2(total[:, :8] - col[:, :8]) * cols[rows][:, :8])
        state_in = states[s]
        state_low = state_in.astype(bf16)
        state_grad = sgrad[...]
        carry_low = state_grad.astype(bf16)
        readout = mm(c_low, state_low, 1, 1)
        read_low = (dy_f * growth).astype(bf16)
        hi, low = split2(dy_f * readout)
        dr_t[rows8, rows] = mm(pick, hi, 1, 1) + mm(pick, low, 1, 1)
        gc[rows] += mm(read_low, state_low)
        grad_xw = mm(b_low, carry_low, 1, 1)
        xw_low = (xs * weight).astype(bf16)
        gb[rows] += mm(xw_low, carry_low)
        hi, low = split2(grad_xw * xs)
        wg_t[rows8, rows] = mm(pick, hi, 1, 1) + mm(pick, low, 1, 1)
        hi, low = split2(state_grad * state_in)
        sums = jnp.sum(mm(pick, hi) + mm(pick, low), axis=1, keepdims=True)
        gt_t[rows8] = jnp.where(iota((8, 128), 1) == s, sums, gt_t[rows8])
        grad_xs = grad_xs + grad_xw * weight
        local = mm(read_low, c_low, 0, 0)
        fade = jnp.exp2(total)
        for j in range(HB):
            at_j = slice(j * HEAD, j * HEAD + HEAD)
            sgrad[at_j] = fade[:, j : j + 1] * state_grad[at_j] + local[at_j]
        gtaps[5:6] += jnp.sum(dy_f * xs, axis=0, keepdims=True)
        dinner_out[rows] = conv_rows(at, kin[...], grad_xs, conv, sig).astype(bf16)
        if links:
            work.step(i * spans + back)
        return carry

    lax.fori_loop(0, spans, span, 0)
    gk_out[...] = gtaps[...]

    @pl.when(i == pl.num_programs(0) - 1)
    def _():
        buf[8 : 8 + tokens] = cst[...]
        gtaps[...] = jnp.zeros(gtaps.shape, f32)
        rates = lay(-jnp.exp(head_row(log_rate)), as_places(heads))[0:1]
        rate = jnp.transpose(jnp.broadcast_to(rates, (128, 128)))[:48, 0:1]
        later = (iota((Q, Q), 0) >= iota((Q, Q), 1)).astype(f32).astype(bf16)
        last = iota((48, Q), 1) == Q - 1
        bias_sum = jnp.zeros((48, 1), f32)
        decay_sum = jnp.zeros((48, 1), f32)
        for back in range(spans):
            s = spans - 1 - back
            rows = slice(s * Q, s * Q + Q)
            bc = bc_in[rows]
            gl = gg[s].astype(bf16)
            grad_c = gc[rows] + mm(gl, bc[:, :128])
            grad_b = gb[rows] + mm(gl, bc[:, 128:], 0, 0)
            both = jnp.concatenate([grad_b, grad_c], axis=1)
            conv = conv_taps(buf[s * Q : s * Q + Q + 8], kst[...])
            dsd_out[rows, :BW] = conv_rows(s * Q, kst[...], both, conv, sigmoid(conv)).astype(bf16)

            cum, step, pre = cumT[:, rows], stepT[:, rows], preT[:, rows]
            total = cum[:, Q - 1 : Q]
            rate_w = jnp.exp2(total - cum)
            wg = wg_t[:, rows]
            cs = cs_t[:, rows]
            moved = wg * (rate_w * step)
            grad_cum = rs_t[:, rows] - cs + jnp.exp2(cum) * dr_t[:, rows] - moved
            grad_total = jnp.exp2(total) * gt_t[:, s : s + 1] + jnp.sum(moved, axis=1, keepdims=True)
            grad_cum = grad_cum + jnp.where(last, grad_total, 0.0)
            parts = split3(grad_cum)
            grad_rate = mm(parts[0], later) + mm(parts[1], later) + mm(parts[2], later)
            sig = sigmoid(pre)
            ratio = jnp.where(pre < -15.0, 1.0, sig / step)
            grad_pre = (wg * rate_w + grad_rate * rate) * sig + cs * ratio
            bias_sum = bias_sum + jnp.sum(grad_pre, axis=1, keepdims=True)
            decay_sum = decay_sum + jnp.sum(grad_rate * step, axis=1, keepdims=True)
            full = jnp.concatenate([grad_pre, jnp.zeros((80, Q), f32)], axis=0)
            dsd_out[rows, BW:] = jnp.transpose(full).astype(bf16)
        gks_out[...] = gtaps[...]
        lane = iota((48, 128), 1)
        both = jnp.where(lane == 0, bias_sum, jnp.where(lane == 1, decay_sum * rate, 0.0))
        hs_out[...] = jnp.transpose(jnp.concatenate([both, jnp.zeros((80, 128), f32)], axis=0))[:8]
        if links:
            work.finish()


class Place:
    def __init__(self):
        me = lax.axis_index("dp")
        self.me = me
        self.c, self.y, self.z = me % 2, (me // 2) % 2, me // 4

    def at(self, z, y, c):
        return (z * 2 + y) * 2 + c

    def core(self):
        return self.at(self.z, self.y, 1 - self.c)

    def side(self):
        return self.at(self.z, 1 - self.y, self.c)

    def up(self):
        return self.me + 4

    def down(self):
        return self.me - 4


def greet(here, across):
    barrier = pltpu.get_barrier_semaphore()

    def signal(**device):
        pl.semaphore_signal(barrier, 1, device_id=device, device_id_type=MESH)

    signal(dp=here.core())
    signal(dp=here.side())
    pl.when(here.z < 3)(lambda: signal(dp=here.up()))
    pl.when(here.z > 0)(lambda: signal(dp=here.down()))
    if across:
        signal(tensor=1 - lax.axis_index("tensor"))
    ends = (here.z == 0).astype(jnp.int32) + (here.z == 3).astype(jnp.int32)
    pl.semaphore_wait(barrier, 4 + int(across) - ends)


def remote(src, dst, send_sem, recv_sem, **device):
    return pltpu.make_async_remote_copy(
        src_ref=src, dst_ref=dst, send_sem=send_sem, recv_sem=recv_sem, device_id=device, device_id_type=MESH
    )


class Gather:
    def __init__(self, here, own, full, ss, rs, ls, chunk, cols):
        self.here, self.full, self.ss, self.rs, self.chunk, self.cols = here, full, ss, rs, chunk, cols
        self.rows = own.shape[0]
        self.own = own
        self.lift = chunk == 0
        self.local = pltpu.make_async_copy(own, self.slot(here.me), ls.at[chunk])

    def slot(self, origin):
        return self.full.at[pl.ds(pl.multiple_of(origin * self.rows, self.rows), self.rows), self.cols]

    def copy(self, origin, way, src=None):
        here = self.here
        target = (here.up, here.down, here.side, here.core)[way]()
        slot = self.slot(origin)
        sems = self.ss.at[self.chunk, origin, way], self.rs.at[self.chunk, origin]
        return remote(slot if src is None else src, slot, *sems, dp=target)

    def arrived(self, origin):
        self.copy(origin, 3).wait_recv()

    def ways(self, hops):
        z = self.here.z
        return ((0, z),) if hops == 0 else ((0, z - hops), (1, z + hops))

    def onward(self, way):
        return (self.here.z < 3) if way == 0 else (self.here.z > 0)

    def own_sends(self, hops, way, origin_z, act):
        here = self.here
        origin = here.at(origin_z, here.y, here.c)
        for along in (0, 1) if hops == 0 else (way,):
            pl.when(self.onward(along))(lambda along=along: act(origin, along))
        if hops and self.lift:
            pl.when((origin_z != 0) & (origin_z != 3))(lambda: act(origin, 2))
        else:
            act(origin, 2)
        act(origin, 3)

    def side_sends(self, hops, way, origin_z, act):
        here = self.here
        origin = here.at(origin_z, 1 - here.y, here.c)
        act(origin, 3)
        if self.lift and hops == 0:
            pl.when(here.z == 0)(lambda: act(origin, 0))
            pl.when(here.z == 3)(lambda: act(origin, 1))
        elif self.lift:
            pl.when((origin_z == 3 * way) & self.onward(way))(lambda: act(origin, way))

    def each(self, hops, act):
        for way, origin_z in self.ways(hops):
            if hops == 0:
                act(way, origin_z)
            else:
                pl.when((origin_z >= 0) & (origin_z <= 3))(lambda way=way, origin_z=origin_z: act(way, origin_z))

    def send(self, origin, way):
        self.copy(origin, way).start()

    def start(self):
        self.own_sends(0, 0, self.here.z, lambda origin, way: self.copy(origin, way, self.own).start())
        self.local.start()

    def hop(self, hops):
        def go(way, origin_z):
            self.arrived(self.here.at(origin_z, self.here.y, self.here.c))
            self.own_sends(hops, way, origin_z, self.send)

        self.each(hops, go)

    def sides(self, hops):
        def go(way, origin_z):
            self.arrived(self.here.at(origin_z, 1 - self.here.y, self.here.c))
            self.side_sends(hops, way, origin_z, self.send)

        self.each(hops, go)

    def finish(self):
        here = self.here
        self.local.wait()
        for z in range(4):
            for y in range(2):
                self.arrived(here.at(z, y, 1 - here.c))

        def sent(origin, way):
            self.copy(origin, way).wait_send()

        for hops in range(4):

            def go(way, origin_z, hops=hops):
                self.own_sends(hops, way, origin_z, sent)
                self.side_sends(hops, way, origin_z, sent)

            self.each(hops, go)


def gather_scratch():
    sem = pltpu.SemaphoreType.DMA
    return [sem((2, 16, 4)), sem((2, 16)), sem((2,))]


def gather_kernel(tokens_in, gain, w_gate_inner, w_state_io, w_step, tokens_out, full, pack, low, ss, rs, ls, xs, xr, xl):
    here = Place()
    half = lax.axis_index("tensor")
    rows = tokens_in.shape[0]
    units, cols = w_gate_inner.shape[2], full.shape[1]
    pack[:, :units] = w_gate_inner[1]
    pack[:, units : units + BW] = w_state_io[...]
    pack[:, units + BW :] = mm(w_step[...], as_places(w_step.shape[1])).astype(bf16)
    greet(here, True)
    cut = cols // 256 * 128
    moves = [
        Gather(here, pack.at[:, c], full, ss, rs, ls, n, c) for n, c in enumerate((slice(0, cut), slice(cut, cols)))
    ]
    for move in moves:
        move.start()
    part = rows // 4
    across, local = [], []
    for n in range(4):
        piece = slice(n * part, n * part + part)
        v = tokens_in[piece].astype(f32)
        scale = lax.rsqrt(jnp.mean(v * v, axis=1, keepdims=True) + norm_eps)
        low[piece] = (v * scale * gain[0:1]).astype(bf16)
        slot = tokens_out.at[pl.ds(pl.multiple_of(half * rows + n * part, part), part)]
        across.append(remote(low.at[piece], slot, xs.at[n], xr.at[n], tensor=1 - half))
        across[-1].start()
        local.append(pltpu.make_async_copy(low.at[piece], slot, xl.at[n]))
        local[-1].start()
    for hops in range(1, 5):
        for move in moves:
            if hops < 4:
                move.hop(hops)
            move.sides(hops - 1)
    for n in range(4):
        local[n].wait()
        across[n].wait()
    for move in moves:
        move.finish()


def gather_rows(tokens_in, gain, w_gate_inner, w_state_io, w_step, ways, collective_id):
    rows, width = tokens_in.shape
    _, own, units = w_gate_inner.shape
    cols = units + BW + 128
    vmem = pl.BlockSpec(memory_space=pltpu.VMEM)
    hbm = pl.BlockSpec(memory_space=pl.ANY)
    sem = pltpu.SemaphoreType.DMA
    return pl.pallas_call(
        gather_kernel,
        name="gather_rows",
        in_specs=[vmem] * 5,
        out_specs=[hbm, hbm],
        out_shape=[sds((2 * rows, width), bf16), sds((ways * own, cols), bf16)],
        scratch_shapes=[
            pltpu.VMEM((own, cols), bf16), pltpu.VMEM((rows, width), bf16), *gather_scratch(),
            sem((4,)), sem((4,)), sem((4,)),
        ],
        compiler_params=pltpu.CompilerParams(
            collective_id=collective_id, has_side_effects=True, vmem_limit_bytes=60 * 1024 * 1024
        ),
    )(tokens_in, gain, w_gate_inner, w_state_io, w_step)


class Reduce:
    def __init__(self, here, grads, out, bufs, sems):
        self.here, self.grads, self.out = here, grads, out
        self.held, self.buf_a, self.buf_b, self.buf_up, self.buf_dn = bufs
        self.local, self.send_a, self.recv_a, self.send_b, self.recv_b, self.send_c, self.recv_up, self.recv_dn = sems
        self.parts, self.rows = out.shape[:2]
        z = here.z
        self.order = (3 * (1 - z // 2), (3 * z + 2) % 5, 1 + z % 2, z)

    def spot(self, z, y, c):
        if self.grads is None:
            return z, (y * 2 + c) * self.rows
        return z * 2 + y, 0

    def own(self, z, y, c=None):
        at, base = self.spot(z, y, self.here.c if c is None else c)
        return self.held.at[at, :, pl.ds(pl.multiple_of(base, 16), self.rows)]

    def block(self, z, y, c):
        if self.grads is None:
            return self.own(z, y, c)
        at = pl.multiple_of(self.here.at(z, y, c) * self.rows, self.rows)
        return self.grads.at[:, pl.ds(at, self.rows)]

    def copy_a(self, z, y):
        here, at = self.here, z * 2 + y
        return remote(self.block(z, y, 1 - here.c), self.buf_a.at[at], self.send_a.at[at], self.recv_a.at[at], dp=here.core())

    def take(self, z, y):
        return pltpu.make_async_copy(self.block(z, y, self.here.c), self.own(z, y), self.local.at[z * 2 + y])

    def copy_b(self, z):
        here = self.here
        return remote(self.own(z, 1 - here.y), self.buf_b.at[z], self.send_b.at[z], self.recv_b.at[z], dp=here.side())

    def copy_up(self, z):
        return remote(self.own(z, self.here.y), self.buf_up.at[z], self.send_c.at[z], self.recv_up.at[z], dp=self.here.up())

    def copy_dn(self, z):
        return remote(self.own(z, self.here.y), self.buf_dn.at[z], self.send_c.at[z], self.recv_dn.at[z], dp=self.here.down())

    def add(self, z, y, buf, slot):
        at, base = self.spot(z, y, self.here.c)

        def rows(n, carry):
            piece = pl.ds(pl.multiple_of(n * 16, 16), 16)
            held = pl.ds(pl.multiple_of(base + n * 16, 16), 16)
            for part in range(self.parts):
                total = self.held[at, part, held].astype(f32) + buf[slot, part, piece].astype(f32)
                self.held[at, part, held] = total.astype(bf16)
            return carry

        lax.fori_loop(0, self.rows // 16, rows, 0)

    def start(self):
        here = self.here
        for side in (1 - here.y, here.y):
            for z in self.order:
                self.copy_a(z, side).start()
                self.take(z, side).start()

    def join(self, z, y):
        if self.grads is not None:
            self.take(z, y).wait()
        self.copy_a(z, y).wait_recv()
        self.add(z, y, self.buf_a, z * 2 + y)

    def cores(self, z):
        self.join(z, 1 - self.here.y)
        self.copy_b(z).start()

    def stay(self, z):
        self.join(z, self.here.y)

    def sides(self, z):
        self.copy_b(z).wait_recv()
        self.add(z, self.here.y, self.buf_b, z)

    def pass_on(self, z):
        here = self.here

        def up():
            def below():
                self.copy_up(z).wait_recv()
                self.add(z, here.y, self.buf_up, z)

            pl.when(here.z > 0)(below)
            self.copy_up(z).start()

        def down():
            def above():
                self.copy_dn(z).wait_recv()
                self.add(z, here.y, self.buf_dn, z)

            pl.when(here.z < 3)(above)
            self.copy_dn(z).start()

        pl.when(z > here.z)(up)
        pl.when(z < here.z)(down)

    def finish(self):
        here = self.here
        z = here.z
        at, base = self.spot(z, here.y, here.c)
        pl.when(z > 0)(lambda: self.copy_up(z).wait_recv())
        pl.when(z < 3)(lambda: self.copy_dn(z).wait_recv())

        def rows(n, carry):
            piece = pl.ds(pl.multiple_of(n * 16, 16), 16)
            held = pl.ds(pl.multiple_of(base + n * 16, 16), 16)
            for part in range(self.parts):
                below = jnp.where(z > 0, self.buf_up[z, part, piece].astype(f32), 0.0)
                above = jnp.where(z < 3, self.buf_dn[z, part, piece].astype(f32), 0.0)
                self.out[part, piece] = self.held[at, part, held].astype(f32) + below + above
            return carry

        lax.fori_loop(0, self.rows // 16, rows, 0)
        for zn in self.order:
            self.copy_a(zn, 0).wait_send()
            self.copy_a(zn, 1).wait_send()
            self.copy_b(zn).wait_send()
            pl.when(zn > z)(lambda zn=zn: self.copy_up(zn).wait_send())
            pl.when(zn < z)(lambda zn=zn: self.copy_dn(zn).wait_send())


def reduce_scratch(parts, rows, cols, by_z=False):
    sem = pltpu.SemaphoreType.DMA
    block = (parts, rows, cols)
    held = (4, parts, 4 * rows, cols) if by_z else (8,) + block
    return [
        pltpu.VMEM(held, bf16), pltpu.VMEM((8,) + block, bf16), pltpu.VMEM((4,) + block, bf16),
        pltpu.VMEM((4,) + block, bf16), pltpu.VMEM((4,) + block, bf16),
        sem((8,)), sem((8,)), sem((8,)), sem((4,)), sem((4,)), sem((4,)), sem((4,)), sem((4,)),
    ]


def tail_kernel(
    normed_t, dinner, dsd, dgate, wb, wa, gk, ggg, gks, hs, norm_gain, w_gate_inner, w_state_io, w_step, gate_grads,
    gn_out, inner_out, step_out, both_out, small_out, shard_out, give, got, send_g, recv_g, nt_v, dinner_v, dsd_v, dgate_v, wg_v, wa_v, away, came, total, landed, loads, send_x, recv_x, send, recv, *scratch,
):
    here = Place()
    half = lax.axis_index("tensor")
    units = dgate.shape[1]
    sources = (normed_t, dinner, dsd, dgate, wb.at[:, :units], wa)
    pending = [
        pltpu.make_async_copy(src, dst, loads.at[n])
        for n, (src, dst) in enumerate(zip(sources, (nt_v, dinner_v, dsd_v, dgate_v, wg_v, wa_v)))
    ]
    for copy in pending:
        copy.start()
    far = pltpu.get_barrier_semaphore()
    partners = [here.me + bit - 2 * bit * ((here.me // bit) % 2) for bit in (2, 4, 8, 1)]
    for partner in partners:
        pl.semaphore_signal(far, 1, device_id={"dp": partner}, device_id_type=MESH)
    pl.semaphore_signal(far, 1, device_id={"tensor": 1 - half}, device_id_type=MESH)
    middle = (here.z == 1) | (here.z == 2)
    pl.when(here.z == 1)(lambda: pl.semaphore_signal(far, 1, device_id={"dp": here.up()}, device_id_type=MESH))
    pl.when(here.z == 2)(lambda: pl.semaphore_signal(far, 1, device_id={"dp": here.down()}, device_id_type=MESH))
    pl.semaphore_wait(far, 5 + middle.astype(jnp.int32))
    work = Reduce(here, None, shard_out, scratch[:5], scratch[5:])
    order = work.order
    rows = gn_out.shape[0]
    chunks, _, wide = away.shape

    def swap(k):
        return remote(total.at[k], landed.at[k], send.at[k], recv.at[k], dp=partners[k])

    def swapped(k):
        swap(k).wait()
        total[k + 1] = total[k] + landed[k]
        if k < 3:
            swap(k + 1).start()

    def across(n):
        return remote(away.at[n], came.at[n], send_x.at[n], recv_x.at[n], tensor=1 - half)

    def pulled(which, n):
        mine = pl.ds(pl.multiple_of(which * rows, rows), rows)
        at = pl.ds(pl.multiple_of(n * wide, wide), wide)
        return (
            mm(dgate_v[mine], wg_v[at], 1, 1)
            + mm(dinner_v[mine], wa_v[at, :units], 1, 1)
            + mm(dsd_v[mine], wa_v[at, units:], 1, 1)
        )

    def far_chunk(n, carry):
        away[n] = pulled(1 - half, n).astype(bf16)
        across(n).start()
        return carry

    def near_chunk(n, carry):
        gn_out[:, pl.ds(pl.multiple_of(n * wide, wide), wide)] = pulled(half, n)
        return carry

    def grads(n, carry):
        z = jnp.where(n == 0, order[0], jnp.where(n == 1, order[1], jnp.where(n == 2, order[2], order[3])))
        count = 4 * work.rows
        left = nt_v[pl.ds(pl.multiple_of(z * count, count), count)]
        work.held[z, 0, :, :units] = mm(left, dinner_v[...]).astype(bf16)
        work.held[z, 0, :, units:] = mm(left, dsd_v[...]).astype(bf16)
        work.copy_a(z, 1 - here.y).start()
        work.copy_a(z, here.y).start()

        @pl.when(n == 0)
        def _():
            for copy in pending[3:]:
                copy.wait()

        far_chunk(n, carry)
        work.cores(z)
        return carry

    total[0, 0:6] = gk[0:6]
    total[0, 6:7] = ggg[0:1]
    for k in range(5):
        total[0, 7:8, k * BW : k * BW + BW] = gks[k : k + 1]
    for k in range(2):
        total[0, 7:8, 5 * BW + k * 128 : 5 * BW + k * 128 + 128] = hs[k : k + 1]
    swap(0).start()
    for copy in pending[:3]:
        copy.wait()
    swapped(0)
    lax.fori_loop(0, 4, grads, 0)
    swapped(1)
    work.stay(order[0])
    work.sides(order[0])
    pl.when(~middle)(lambda: work.pass_on(order[0]))
    lax.fori_loop(4, chunks, far_chunk, 0)
    swapped(2)
    for n in range(1, 4):
        work.stay(order[n])
    work.sides(order[1])
    pl.when(~middle)(lambda: work.pass_on(order[1]))
    lax.fori_loop(0, 3, near_chunk, 0)
    pl.when(middle)(lambda: work.pass_on(order[0]))
    work.sides(order[2])
    pl.when(~middle)(lambda: work.pass_on(order[2]))
    lax.fori_loop(3, chunks, near_chunk, 0)
    swapped(3)
    small_out[...] = total[4]
    pl.when(middle)(lambda: work.pass_on(order[1]))
    work.sides(order[3])
    pl.when(middle)(lambda: work.pass_on(order[2]))
    work.finish()

    def arrive(n, carry):
        across(n).wait()
        at = pl.ds(pl.multiple_of(n * wide, wide), wide)
        gn_out[:, at] = gn_out[:, at] + came[n].astype(f32)
        return carry

    inner_out[0] = gate_grads[0]
    inner_out[1] = shard_out[0, :, :units]
    step_out[...] = shard_out[0, :, units + BW :]
    count = work.rows
    part = shard_out[0, :, units + BW :] * mm(w_step[...], as_places(w_step.shape[1]))
    for c in range(2):
        at = slice(units + c * 128, units + c * 128 + 128)
        part = part + shard_out[0, :, at] * w_state_io[:, c * 128 : c * 128 + 128].astype(f32)
    for c in range(units // 128):
        at = slice(c * 128, c * 128 + 128)
        part = part + gate_grads[0, :, at] * w_gate_inner[0, :, at].astype(f32)
        part = part + shard_out[0, :, at] * w_gate_inner[1, :, at].astype(f32)
    part = jnp.concatenate([part, jnp.zeros((128 - count, 128), f32)], axis=0)
    row = jnp.sum(jnp.transpose(part), axis=0, keepdims=True)
    shape = (norm_gain.shape[1], 128)
    pick = (iota(shape, 0) == iota(shape, 1) + here.me * count) & (iota(shape, 1) < count)
    gain = lay(norm_gain[...], pick.astype(f32).astype(bf16))[0:1]
    row = row / jnp.where(iota((1, 128), 1) < count, gain, 1.0)
    low = pltpu.roll(row, 128 - count // 2, 1)
    first = half == 0

    def share(at, a, b):
        both_out[at] = jnp.where(first, a, b)
        give[at] = jnp.where(first, b, a)

    share(slice(0, count), shard_out[0, :, units : units + 128], shard_out[0, :, units + 128 : units + 256])
    for k in range(5):
        pair = [small_out[7:8, k * BW + c * 128 : k * BW + c * 128 + 128] for c in range(2)]
        share(slice(count + k, count + k + 1), *pair)
    share(slice(count + 5, count + 6), row, low)
    share(slice(count + 6, count + 8), jnp.zeros((2, 128), f32), jnp.zeros((2, 128), f32))
    last = remote(give, got, send_g, recv_g, tensor=1 - half)
    last.start()
    lax.fori_loop(0, chunks, arrive, 0)
    last.wait()
    both_out[...] = both_out[...] + got[...]


def reduce_tail(normed_t, dinner, dsd, dgate, wb, wa, sums, weights, ways, collective_id):
    width, tokens = normed_t.shape
    small = sums[0]
    units, cols, rows = dgate.shape[1], wa.shape[1], width // ways
    chunks = width // BW
    vmem = pl.BlockSpec(memory_space=pltpu.VMEM)
    hbm = pl.BlockSpec(memory_space=pl.ANY)
    sem = pltpu.SemaphoreType.DMA
    return pl.pallas_call(
        tail_kernel, name="tail", in_specs=[hbm] * 6 + [vmem] * 9, out_specs=[vmem] * 5,
        out_shape=[
            sds((tokens // 2, width)), sds((2, rows, units)), sds((rows, 128)), sds((rows + 8, 128)), sds(small.shape),
        ],
        scratch_shapes=[
            pltpu.VMEM((1, rows, cols), f32), pltpu.VMEM((rows + 8, 128), f32), pltpu.VMEM((rows + 8, 128), f32), sem, sem,
            pltpu.VMEM(normed_t.shape, bf16), pltpu.VMEM(dinner.shape, bf16), pltpu.VMEM(dsd.shape, bf16),
            pltpu.VMEM(dgate.shape, bf16), pltpu.VMEM((width, units), bf16), pltpu.VMEM(wa.shape, bf16),
            pltpu.VMEM((chunks, tokens // 2, BW), bf16), pltpu.VMEM((chunks, tokens // 2, BW), bf16),
            pltpu.VMEM((5,) + small.shape, f32), pltpu.VMEM((4,) + small.shape, f32),
            sem((6,)), sem((chunks,)), sem((chunks,)), sem((4,)), sem((4,)),
        ] + reduce_scratch(1, rows, cols, True),
        compiler_params=pltpu.CompilerParams(
            collective_id=collective_id, has_side_effects=True, vmem_limit_bytes=62 * 1024 * 1024
        ),
    )(normed_t, dinner, dsd, dgate, wb, wa, *sums, *weights)


def swap(v):
    return lax.ppermute(v, "tensor", [(0, 1), (1, 0)])


def halves(v, axis):
    size = v.shape[axis] // 2
    me = lax.axis_index("tensor")
    return (
        lax.dynamic_slice_in_dim(v, me * size, size, axis),
        lax.dynamic_slice_in_dim(v, (1 - me) * size, size, axis),
    )


def once(shape, at=None):
    where = at or (0,) * len(shape)
    return pl.BlockSpec(shape, lambda i: where, pipeline_mode=pl.Buffered(1))


def by_cols(rows, offset=0):
    return pl.BlockSpec((rows, BW), lambda i: (0, i + offset))


def params(collective_id=None):
    return pltpu.CompilerParams(
        dimension_semantics=("arbitrary",), vmem_limit_bytes=60 * 1024 * 1024,
        collective_id=collective_id, has_side_effects=collective_id is not None,
    )


def spread(v):
    lead = v.shape[:-1]
    v = v.reshape(lead + (v.shape[-1] // HB, HB))
    v = jnp.pad(v, [(0, 0)] * len(lead) + [(0, 0), (0, 8 - HB)]).reshape(lead + (-1,))
    return jnp.pad(v, [(0, 0)] * len(lead) + [(0, 128 - v.shape[-1])])


def gathered_heads(v, heads):
    return v[..., : heads * 2].reshape(v.shape[:-1] + (heads // HB, 8))[..., :HB].reshape(v.shape[:-1] + (heads,))


def sds(shape, dtype=f32):
    return jax.ShapeDtypeStruct(shape, dtype)


def on_device(
    residual, norm_gain, w_gate_inner, w_state_io, w_step, conv_inner, conv_state,
    step_bias, decay_log, skip_gain, gate_gain, w_output, cotangent,
):
    width = residual.shape[1]
    units = w_gate_inner.shape[2]
    heads = w_step.shape[1]
    blocks = units // BW
    unit_total = units * lax.axis_size("tensor")
    ways = lax.axis_size("dp")
    own_links = ways == 16
    rows_in = residual.astype(f32)
    rstd_in = lax.rsqrt(jnp.mean(rows_in * rows_in, axis=1, keepdims=True) + norm_eps)
    scaled = rows_in * rstd_in
    pack_a = jnp.concatenate([w_gate_inner[1], w_state_io, spread(w_step)], axis=1)
    w_output_t = w_output.T
    gain_in = jnp.broadcast_to(norm_gain[None], (8, width))
    if own_links:
        normed, wa = gather_rows(residual, gain_in, w_gate_inner, w_state_io, w_step, ways, 1)
    else:
        wa = lax.all_gather(pack_a, "dp", axis=0, tiled=True)
        normed = lax.all_gather((scaled * norm_gain).astype(bf16), "tensor", axis=0, tiled=True)
    tokens = normed.shape[0]
    spans = tokens // Q
    gain8 = jnp.broadcast_to(gate_gain[None], (8, units))

    hbm = pl.BlockSpec(memory_space=pl.ANY)
    sem = pltpu.SemaphoreType.DMA
    def stage(rows, first):
        return pl.BlockSpec((rows, BW), lambda i: (0, jnp.clip(i - first, 0, blocks - 1)))

    inner, ssd, states, cst, bc, step, cum, step_t, cum_t, pre_t, *sent = pl.pallas_call(
        functools.partial(mixer_forward, own_links),
        name="mixer_forward",
        grid=(blocks * (3 if own_links else 1),),
        in_specs=[
            once((tokens, width)), stage(width, 0), once((width, 384), (0, units // 384)),
            stage(5, 0), once((5, BW)), once((heads,)), once((heads,)), once((heads,)),
        ] + ([once(v.shape) for v in (cotangent, w_gate_inner, w_output_t)] + [stage(8, 2 * blocks)]) * own_links,
        out_specs=[
            stage(tokens, 0), stage(tokens, 0), pl.BlockSpec((spans, BW, 128), lambda i: (0, jnp.clip(i, 0, blocks - 1), 0)),
            once((tokens, BW)), once((tokens, BW)), once((tokens, 128)), once((tokens, 128)),
            once((48, tokens)), once((48, tokens)), once((48, tokens)),
        ] + [hbm, hbm, stage(tokens, blocks), stage(tokens, 2 * blocks), once((8, tokens))] * own_links,
        out_shape=[
            sds((tokens, units)), sds((tokens, units)), sds((spans, units, 128)),
            sds((tokens, BW)), sds((tokens, BW), bf16), sds((tokens, 128)), sds((tokens, 128)),
            sds((48, tokens)), sds((48, tokens)), sds((48, tokens)),
        ] + [
            sds((tokens, width), bf16), sds((width, 2 * units), bf16), sds((tokens, units)), sds((tokens, units)),
            sds((8, tokens)),
        ] * own_links,
        scratch_shapes=[
            pltpu.VMEM((tokens + 8, BW), f32), pltpu.VMEM((spans, Q, Q), f32),
            pltpu.VMEM((tokens, 128), f32), pltpu.VMEM((tokens, 128), f32), pltpu.VMEM((8, tokens), f32),
            pltpu.VMEM((Q, HB * Q), bf16), pltpu.VMEM((HB * Q, BW), bf16), pltpu.VMEM((BW, 128), f32),
        ] + ([
            pltpu.VMEM((blocks + 1, tokens, BW), f32), pltpu.VMEM((blocks, width, BW), bf16), pltpu.VMEM((tokens, width), bf16),
            pltpu.VMEM((tokens, 128), f32), pltpu.VMEM((tokens, 128), f32), pltpu.VMEM((8, tokens), f32),
            pltpu.VMEM((8, tokens), f32), sem((blocks,)), sem((3,)),
        ] + gather_scratch() + [sem, sem, sem]) * own_links,
        compiler_params=params(2 if own_links else None),
        cost_estimate=pl.CostEstimate(flops=2 * tokens * width * (units + 384) + 4 * tokens * 256 * units, bytes_accessed=30_000_000, transcendentals=heads * spans * Q * Q),
    )(
        normed, wa, wa, conv_inner, conv_state, step_bias, decay_log, skip_gain,
        *[cotangent, w_gate_inner, w_output_t, gain8] * own_links,
    )

    if own_links:
        cot, wb, gate, ggo, stats = sent
    else:
        wb = lax.all_gather(jnp.concatenate([w_gate_inner[0], w_output_t], axis=1), "dp", axis=0, tiled=True)
        cot = lax.all_gather(cotangent, "tensor", axis=0, tiled=True)
        gate, ggo, stats = pl.pallas_call(
            gate_forward,
            name="gate_forward",
            grid=(blocks,),
            in_specs=[
                once((tokens, width)), once((tokens, width)), by_cols(width), by_cols(width, blocks),
                by_cols(tokens), by_cols(8),
            ],
            out_specs=[by_cols(tokens), by_cols(tokens), once((8, tokens))],
            out_shape=[sds((tokens, units)), sds((tokens, units)), sds((8, tokens))],
            scratch_shapes=[pltpu.VMEM((tokens, 128), f32), pltpu.VMEM((tokens, 128), f32)],
            compiler_params=params(),
            cost_estimate=pl.CostEstimate(flops=4 * tokens * width * units, bytes_accessed=35_000_000, transcendentals=tokens * units),
        )(normed, cot, wb, wb, ssd, gain8)
        stats = stats + swap(stats)

    dy, dgate, ng, ggg, grad_b, normed_t = pl.pallas_call(
        functools.partial(gate_backward, float(unit_total)),
        name="gate_backward",
        grid=(blocks,),
        in_specs=[
            once((8, tokens)), by_cols(tokens), by_cols(tokens), by_cols(tokens), by_cols(8),
            once((tokens, width)), once((tokens, width)),
        ],
        out_specs=[
            by_cols(tokens), by_cols(tokens), by_cols(tokens), by_cols(8),
            pl.BlockSpec((2, width, BW), lambda i: (0, 0, i)), once((width, tokens)),
        ],
        out_shape=[
            sds((tokens, units), bf16), sds((tokens, units), bf16), sds((tokens, units), bf16), sds((8, units)),
            sds((2, width, units), bf16), sds((width, tokens), bf16),
        ],
        scratch_shapes=[pltpu.VMEM((tokens, 128), f32), pltpu.VMEM((width, tokens), bf16)],
        compiler_params=params(),
        cost_estimate=pl.CostEstimate(flops=4 * tokens * units * width, bytes_accessed=45_000_000, transcendentals=tokens * units),
    )(stats, gate, ssd, ggo, gain8, normed, cot)

    mixed = mm(ng, wb[:, units:], 1, 1).astype(bf16)
    mixed_near, mixed_far = halves(mixed, 0)

    dinner, gk, dsd, gks, hs, *sent = pl.pallas_call(
        functools.partial(mixer_backward, own_links),
        name="mixer_backward",
        grid=(blocks,),
        in_specs=[
            by_cols(tokens), by_cols(tokens), pl.BlockSpec((spans, BW, 128), lambda i: (0, i, 0)),
            by_cols(5), once((5, BW)), once((heads,)), once((heads,)),
            once((tokens, BW)), once((tokens, BW)), once((tokens, 128)), once((tokens, 128)),
            once((48, tokens)), once((48, tokens)), once((48, tokens)),
        ] + [hbm, hbm] * own_links,
        out_specs=[by_cols(tokens), by_cols(8), once((tokens, 384)), once((8, BW)), once((8, 128))]
        + [hbm, once((2, width // ways, units))] * own_links,
        out_shape=[sds((tokens, units), bf16), sds((8, units)), sds((tokens, 384), bf16), sds((8, BW)), sds((8, 128))]
        + [sds((tokens // 2, width), bf16), sds((2, width // ways, units))] * own_links,
        scratch_shapes=[
            pltpu.VMEM((tokens + 8, BW), f32), pltpu.VMEM((tokens + 8, BW), f32),
            pltpu.VMEM((spans, Q, Q), f32), pltpu.VMEM((spans, Q, Q), f32),
            pltpu.VMEM((tokens, 128), f32), pltpu.VMEM((tokens, 128), f32),
            pltpu.VMEM((tokens, 128), f32), pltpu.VMEM((tokens, 128), f32), pltpu.VMEM((8, tokens), f32),
            pltpu.VMEM((HB * Q, Q), bf16), pltpu.VMEM((HB * Q, BW), bf16), pltpu.VMEM((HB * Q, Q), f32),
            pltpu.VMEM((BW, 128), f32),
            pltpu.VMEM((48, tokens), f32), pltpu.VMEM((48, tokens), f32), pltpu.VMEM((48, tokens), f32),
            pltpu.VMEM((48, tokens), f32), pltpu.VMEM((48, 128), f32), pltpu.VMEM((8, BW), f32),
        ] + ([sem, sem] + reduce_scratch(2, width // ways, units)) * own_links,
        compiler_params=params(4 if own_links else None),
        cost_estimate=pl.CostEstimate(flops=40_000_000_000, bytes_accessed=30_000_000, transcendentals=heads * spans * Q * Q),
    )(
        inner, dy, states, conv_inner, conv_state, decay_log, skip_gain, cst, bc, step, cum, step_t, cum_t, pre_t,
        *[mixed, grad_b] * own_links,
    )
    if own_links:
        mixed_got, wb_shard = sent
    else:
        mixed_got = swap(mixed_far)
        wb_shard = lax.psum_scatter(grad_b, "dp", scatter_dimension=1, tiled=True).astype(f32)
    output = (rows_in + mixed_near.astype(f32) + mixed_got.astype(f32)).astype(bf16)

    if own_links:
        weights = (gain_in, w_gate_inner, w_state_io, w_step, wb_shard)
        sums = (gk, ggg, gks, hs)
        grad_normed, inner_grads, step_grads, both, small = reduce_tail(
            normed_t, dinner, dsd, dgate, wb, wa, sums, weights, ways, 5
        )
    else:
        last = jnp.concatenate([gks[:5].reshape(-1), hs[0], hs[1]])
        small = jnp.concatenate([gk[:6], ggg[:1], last[None]], axis=0)
        grad_a = jnp.concatenate([mm(normed_t, dinner).astype(bf16), mm(normed_t, dsd).astype(bf16)], axis=1)
        pulled = mm(dgate, wb[:, :units], 1, 1) + mm(dinner, wa[:, :units], 1, 1) + mm(dsd, wa[:, units:], 1, 1)
        near, far = halves(pulled.astype(bf16), 0)
        wa_shard = lax.psum_scatter(grad_a, "dp", scatter_dimension=0, tiled=True).astype(f32)
        small = lax.psum(small, "dp")
        grad_normed = near.astype(f32) + swap(far).astype(f32)
    grad_v = grad_normed * norm_gain
    grad_residual = cotangent.astype(f32) + rstd_in * (
        grad_v - scaled * jnp.mean(grad_v * scaled, axis=1, keepdims=True)
    )

    bias_sum = gathered_heads(small[7, 5 * BW : 5 * BW + 128], heads)
    decay_sum = gathered_heads(small[7, 5 * BW + 128 : 5 * BW + 256], heads)
    skip_sum = jnp.sum(small[5].reshape(heads, HEAD), axis=1)

    count = width // ways
    if own_links:
        gain_part = both[count + 5, : count // 2]
    else:
        conv_state_sum = small[7, : 5 * BW].reshape(5, BW)
        gain_rows = jnp.sum(wb_shard[0] * w_gate_inner[0].astype(f32), axis=1) + jnp.sum(
            wa_shard * pack_a.astype(f32), axis=1
        )
        gain_own = gain_rows / lax.dynamic_slice_in_dim(norm_gain, lax.axis_index("dp") * count, count)
        near_s, far_s = halves(jnp.concatenate([wa_shard[:, units : units + BW], conv_state_sum], axis=0), 1)
        near_g, far_g = halves(gain_own, 0)
        far_all = jnp.concatenate([far_s.reshape(-1), far_g])
        got = swap(far_all)
        both = near_s + got[: far_s.size].reshape(far_s.shape)
        gain_part = near_g + got[far_s.size :]
        inner_grads = jnp.stack([wb_shard[0], wa_shard[:, :units]])
        step_grads = wa_shard[:, units + BW :]
    return (
        output,
        grad_residual,
        gain_part,
        inner_grads,
        both[:count],
        gathered_heads(step_grads, heads),
        small[0:5],
        both[count : count + 5],
        bias_sum,
        decay_sum,
        skip_sum,
        small[6],
        wb_shard[1].T,
    )


def solution(mesh):
    return jax.shard_map(
        on_device,
        mesh=mesh,
        in_specs=(
            P(("dp", "tensor"), None),
            P(),
            P(None, "dp", "tensor"),
            P("dp", None),
            P("dp", "tensor"),
            P(None, "tensor"),
            P(),
            P("tensor"),
            P("tensor"),
            P("tensor"),
            P("tensor"),
            P("tensor", "dp"),
            P(("dp", "tensor"), None),
        ),
        out_specs=(
            P(("dp", "tensor"), None),
            P(("dp", "tensor"), None),
            P(("dp", "tensor")),
            P(None, "dp", "tensor"),
            P("dp", "tensor"),
            P("dp", "tensor"),
            P(None, "tensor"),
            P(None, "tensor"),
            P("tensor"),
            P("tensor"),
            P("tensor"),
            P("tensor"),
            P("tensor", "dp"),
        ),
        check_vma=False,
    )
```

```python
import functools

import jax
import jax.numpy as jnp
from jax import lax
from jax.experimental import pallas as pl
from jax.experimental.pallas import tpu as pltpu
from jax.sharding import PartitionSpec as P

Q = 256
LEN = 1024
HEAD = 64
BW = 256
HB = BW // HEAD
LOG2E = 1.4426950408889634
FAR = -1e30
norm_eps = 1e-05
MESH = pl.DeviceIdType.MESH
f32 = jnp.float32
bf16 = jnp.bfloat16


def mm(a, b, ca=1, cb=0):
    return lax.dot_general(a, b, (((ca,), (cb,)), ((), ())), preferred_element_type=f32)


def sigmoid(v):
    return 1.0 / (1.0 + jnp.exp(-v))


def split3(a):
    hi = a.astype(bf16)
    rest = a - hi.astype(f32)
    mid = rest.astype(bf16)
    low = (rest - mid.astype(f32)).astype(bf16)
    return hi, mid, low


def split2(a):
    hi = a.astype(bf16)
    return hi, (a - hi.astype(f32)).astype(bf16)


def iota(shape, axis):
    return lax.broadcasted_iota(jnp.int32, shape, axis)


def expand(cols):
    rows = cols.shape[0]
    left = iota((rows, 128), 1) < HEAD
    return jnp.concatenate(
        [jnp.where(left, cols[:, 2 * q : 2 * q + 1], cols[:, 2 * q + 1 : 2 * q + 2]) for q in range(2)],
        axis=1,
    )


def conv_taps(window, kernel):
    out = kernel[4:5] + kernel[3:4] * window[8:]
    for k in range(3):
        out = out + kernel[k : k + 1] * pltpu.roll(window, 3 - k, 0)[8:]
    return out


def head_row(ref):
    return jnp.broadcast_to(ref[...][None, :], (8, ref.shape[0]))


def lay(rows, pick):
    parts = split3(rows)
    return mm(parts[0], pick) + mm(parts[1], pick) + mm(parts[2], pick)


def as_places(heads):
    lane = iota((heads, 128), 1)
    place = lane % 8
    return ((lane // 8 * HB + place == iota((heads, 128), 0)) & (place < HB)).astype(f32).astype(bf16)


def as_units(heads, block):
    return (iota((heads, BW), 1) // HEAD + HB * block == iota((heads, BW), 0)).astype(f32).astype(bf16)


def head_masks():
    lane = iota((1, BW), 1) // HEAD
    return [(lane == j).astype(f32).astype(bf16) for j in range(HB)]


def quads():
    for r in range(0, Q, 64):
        for half in range(2):
            if half * 128 <= r:
                yield r, half, r < half * 128 + 128


def decay_chunk(col, row, r, half, diag):
    gap = col[r : r + 64] - row[:, half * 128 : half * 128 + 128]
    if diag:
        keep = iota((64, 128), 0) + (r - half * 128) >= iota((64, 128), 1)
        gap = jnp.where(keep, gap, FAR)
    return jnp.exp2(gap)


def mixer_forward(links, normed, wi, wsx, kin, kst, bias, log_rate, skip_in, *refs):
    refs = list(refs)
    if links:
        sent = refs[:3] + refs[14:16]
        gain, gate_refs = refs[3], refs[16:19]
        refs = refs[4:14] + refs[19:]
    inner_out, ssd_out, states_out, cst_out, bc_out, step_out, cum_out, stepT_out, cumT_out, preT_out = refs[:10]
    buf, gram, colc, cols, rowp, mst, xst, state = refs[10:18]
    i = pl.program_id(0)
    tokens = normed.shape[0]
    spans = tokens // Q
    blocks = inner_out.shape[1] // BW
    if links:
        work = BesideForward(*sent, *refs[27:])
        ssd_v, *gate_scratch = refs[18:27]
        blocks = ssd_v.shape[0] - 1
    heads = bias.shape[0]
    skip = lay(head_row(skip_in), as_units(heads, i))[0:1]

    if links:
        pl.when(i == 0)(work.start)

    @pl.when(i == 0)
    def _():
        proj = mm(normed[...], wsx[...])
        buf[0:8] = jnp.zeros((8, BW), f32)
        cst_out[...] = proj[:, :BW]
        buf[8 : 8 + tokens] = proj[:, :BW]
        tri = (iota((Q, Q), 0) >= iota((Q, Q), 1)).astype(f32).astype(bf16)
        places = as_places(heads)
        pre = proj[:, BW:] + lay(head_row(bias), places)[0:1]
        step = jnp.maximum(pre, 0.0) + jnp.log1p(jnp.exp(-jnp.abs(pre)))
        step_out[...] = step
        scaled = step * (lay(-jnp.exp(head_row(log_rate)), places)[0:1] * LOG2E)
        for s in range(spans):
            parts = split3(scaled[s * Q : s * Q + Q])
            cum_out[s * Q : s * Q + Q] = mm(tri, parts[0]) + mm(tri, parts[1]) + mm(tri, parts[2])
            conv = conv_taps(buf[s * Q : s * Q + Q + 8], kst[...])
            bc = (conv * sigmoid(conv)).astype(bf16)
            bc_out[s * Q : s * Q + Q] = bc
            gram[s] = mm(bc[:, 128:], bc[:, :128], 1, 1)
        preT_out[...] = jnp.transpose(pre)[:48]
        stepT_out[...] = jnp.transpose(step)[:48]
        cumT_out[...] = jnp.transpose(cum_out[...])[:48]
        mst[...] = jnp.zeros(mst.shape, bf16)

    def mix():
        inner = mm(normed[...], wi[...])
        inner_out[...] = inner
        buf[8 : 8 + tokens] = inner
        turn = lax.rem(128 - 8 * i, 128)
        colc[...] = pltpu.roll(cum_out[...], turn, 1)
        cols[...] = pltpu.roll(step_out[...], turn, 1)
        rows8 = pl.ds(pl.multiple_of(8 * i, 8), 8)
        rowp[...] = cumT_out[rows8] - jnp.log2(stepT_out[rows8])
        state[...] = jnp.zeros(state.shape, f32)
        masks = head_masks()

        def span(s, carry):
            at = pl.multiple_of(s * Q, Q)
            rows = pl.ds(at, Q)
            conv = conv_taps(buf[pl.ds(at, Q + 8)], kin[...])
            xs = conv * sigmoid(conv)
            x_low = xs.astype(bf16)
            col = colc[rows]
            total = col[Q - 1 : Q]
            growth = expand(jnp.exp2(col[:, :8]))
            weight = expand(jnp.exp2(total[:, :8] - col[:, :8]) * cols[rows][:, :8])
            xw_low = (xs * weight).astype(bf16)
            for j in range(HB):
                xst[j * Q : j * Q + Q] = x_low * masks[j]
                row = rowp[j : j + 1, rows]
                for r, half, diag in quads():
                    part = gram[s, r : r + 64, half * 128 : half * 128 + 128]
                    dec = decay_chunk(col[:, j : j + 1], row, r, half, diag)
                    mst[r : r + 64, j * Q + half * 128 : j * Q + half * 128 + 128] = (part * dec).astype(bf16)
            intra = mm(mst[...], xst[...])
            state_in = state[...]
            states_out[s] = state_in
            bc = bc_out[rows]
            readout = mm(bc[:, 128:], state_in.astype(bf16), 1, 1)
            ssd = intra + growth * readout + skip * xs
            ssd_out[rows] = ssd
            if links:
                ssd_v[blocks, rows] = ssd
            local = mm(xw_low, bc[:, :128], 0, 0)
            fade = jnp.exp2(total)
            for j in range(HB):
                at_j = slice(j * HEAD, j * HEAD + HEAD)
                state[at_j] = fade[:, j : j + 1] * state_in[at_j] + local[at_j]
            if links:
                work.step(i * spans + s)
            return carry

        lax.fori_loop(0, spans, span, 0)

    if not links:
        mix()
        return
    pl.when(i < blocks)(mix)

    @pl.when(i < blocks)
    def _():
        ssd_v[i] = ssd_v[blocks]

    gates = GateForward(i - blocks, blocks, normed, sent[3], sent[4], gain, ssd_v, *gate_refs, *gate_scratch)

    @pl.when(i == blocks)
    def _():
        work.first()
        gates.start(0)


    @pl.when((i >= blocks) & (i < 2 * blocks))
    def _():
        gates.gate()
        work.between(i - blocks)


    @pl.when(i == 2 * blocks)
    def _():
        work.finish()
        gates.start(1)

    pl.when(i >= 2 * blocks)(gates.pull)


class GateForward:
    def __init__(
        self, at, blocks, normed, cot, wb, gain, ssd_v, gate_out, ggo_out, stats_out, w_v, cot_v, sq, gi, mine, landed, wl, cl
    ):
        self.at, self.blocks, self.normed, self.cot, self.wb, self.gain, self.ssd_v = at, blocks, normed, cot, wb, gain, ssd_v
        self.gate_out, self.ggo_out, self.stats_out = gate_out, ggo_out, stats_out
        self.w_v, self.cot_v, self.sq, self.gi, self.mine, self.landed, self.wl, self.cl = w_v, cot_v, sq, gi, mine, landed, wl, cl

    def load(self, which, n):
        cols = slice((which * self.blocks + n) * BW, (which * self.blocks + n + 1) * BW)
        return pltpu.make_async_copy(self.wb.at[:, cols], self.w_v.at[n], self.wl.at[n])

    def tokens(self):
        return pltpu.make_async_copy(self.cot, self.cot_v, self.cl.at[0])

    def start(self, which):
        if not which:
            self.tokens().start()
        for n in range(self.blocks):
            self.load(which, n).start()
        if which:
            self.tokens().wait()
        total = self.gi if which else self.sq
        total[...] = jnp.zeros(total.shape, f32)

    def gate(self):
        b = self.at
        pltpu.make_async_copy(self.wb.at[:, :BW], self.w_v.at[b], self.wl.at[b]).wait()
        gate = mm(self.normed[...], self.w_v[b])
        self.gate_out[...] = gate
        gated = self.ssd_v[b] * (gate * sigmoid(gate))
        self.ssd_v[b] = gated
        squares = gated * gated
        self.sq[...] += squares[:, :128] + squares[:, 128:]

    def pull(self):
        b = self.at - self.blocks
        pltpu.make_async_copy(self.wb.at[:, :BW], self.w_v.at[b], self.wl.at[b]).wait()
        ggo = mm(self.cot_v[...], self.w_v[b])
        self.ggo_out[...] = ggo
        inner = ggo * self.gain[0:1] * self.ssd_v[b]
        self.gi[...] += inner[:, :128] + inner[:, 128:]
        pl.when(b == self.blocks - 1)(self.last)

    def last(self):
        self.mine[...] = token_sums(self.sq[...], self.gi[...])
        swap = remote(self.mine, self.landed, self.cl.at[1], self.cl.at[2], tensor=1 - lax.axis_index("tensor"))
        swap.start()
        swap.wait()
        self.stats_out[...] = self.mine[...] + self.landed[...]


def token_sums(sq, gi):
    lane = iota(sq.shape, 1)
    both = jnp.where(
        lane == 0,
        jnp.sum(sq, axis=1, keepdims=True),
        jnp.where(lane == 1, jnp.sum(gi, axis=1, keepdims=True), 0.0),
    )
    return jnp.transpose(both)[:8]


class BesideForward:
    def __init__(self, cot, w_gate_inner, w_output_t, cot_out, wb, ss, rs, ls, xs, xr, xl):
        self.here = Place()
        units = w_output_t.shape[1]
        self.moves = [
            Gather(self.here, own, wb, ss, rs, ls, n, slice(n * units, n * units + units))
            for n, own in enumerate((w_gate_inner.at[0], w_output_t))
        ]
        half = lax.axis_index("tensor")
        rows = cot.shape[0]
        slot = cot_out.at[pl.ds(pl.multiple_of(half * rows, rows), rows)]
        self.across = remote(cot, slot, xs, xr, tensor=1 - half)
        self.local = pltpu.make_async_copy(cot, slot, xl)

    def start(self):
        greet(self.here, True)
        for move in self.moves:
            move.start()
        self.across.start()
        self.local.start()

    def step(self, at):
        for when, chunk, hops in ((6, 0, 1), (10, 1, 1), (14, 0, 2), (18, 1, 2), (22, 0, 3)):

            def go(move=self.moves[chunk], hops=hops):
                move.hop(hops)
                move.sides(hops - 1)

            pl.when(at == when)(go)

    def first(self):
        self.moves[0].sides(3)
        self.moves[1].hop(3)
        self.moves[0].finish()
        self.local.wait()
        self.across.wait()

    def between(self, at):
        pl.when(at == 1)(lambda: self.moves[1].sides(2))

    def finish(self):
        move = self.moves[1]
        move.sides(3)
        move.finish()


def gate_forward(normed, cot, wg, wo, ssd, gain, gate_out, ggo_out, stats_out, sq, gi):
    i = pl.program_id(0)

    @pl.when(i == 0)
    def _():
        sq[...] = jnp.zeros(sq.shape, f32)
        gi[...] = jnp.zeros(gi.shape, f32)

    gate = mm(normed[...], wg[...])
    gate_out[...] = gate
    ggo = mm(cot[...], wo[...])
    ggo_out[...] = ggo
    gated = ssd[...] * (gate * sigmoid(gate))
    squares = gated * gated
    sq[...] += squares[:, :128] + squares[:, 128:]
    inner = ggo * gain[0:1] * gated
    gi[...] += inner[:, :128] + inner[:, 128:]

    @pl.when(i == pl.num_programs(0) - 1)
    def _():
        stats_out[...] = token_sums(sq[...], gi[...])


def gate_backward(
    unit_total, stats, gate, ssd, ggo, gain, normed, cot, dy_out, dgate_out, ng_out, gg_out, grads_out, normed_t, cols, cot_t
):
    @pl.when(pl.program_id(0) == 0)
    def _():
        full = jnp.concatenate([stats[...], jnp.zeros((120, stats.shape[1]), f32)], axis=0)
        cols[...] = jnp.transpose(full)

        def turn(n, carry):
            here = pl.ds(pl.multiple_of(n * 128, 128), 128)
            normed_t[here] = jnp.transpose(normed[:, here])
            cot_t[here] = jnp.transpose(cot[:, here])
            return carry

        lax.fori_loop(0, normed.shape[1] // 128, turn, 0)

    rstd = lax.rsqrt(cols[:, 0:1] / unit_total + norm_eps)
    pull = rstd * rstd * rstd * (cols[:, 1:2] / unit_total)
    v = gate[...]
    sig = sigmoid(v)
    act = v * sig
    y = ssd[...]
    gated = y * act
    scaled = gated * rstd
    ng = (scaled * gain[0:1]).astype(bf16)
    ng_out[...] = ng
    grads_out[1] = mm(cot_t[...], ng).astype(bf16)
    gg = ggo[...]
    gg_out[...] = jnp.broadcast_to(jnp.sum(gg * scaled, axis=0, keepdims=True), gg_out.shape)
    grad = rstd * (gg * gain[0:1]) - gated * pull
    dy_out[...] = (grad * act).astype(bf16)
    dgate = (grad * y * (sig * (1.0 + v * (1.0 - sig)))).astype(bf16)
    dgate_out[...] = dgate
    grads_out[0] = mm(normed_t[...], dgate).astype(bf16)


class BesideBackward:
    def __init__(self, mixed, grads, far_out, shard_out, scratch):
        self.here = Place()
        half = lax.axis_index("tensor")
        rows = far_out.shape[0]
        other = mixed.at[pl.ds(pl.multiple_of((1 - half) * rows, rows), rows)]
        self.across = remote(other, far_out, scratch[0], scratch[1], tensor=1 - half)
        self.sum = Reduce(self.here, grads, shard_out, scratch[2:7], scratch[7:15])

    def start(self):
        greet(self.here, True)
        self.sum.start()
        self.across.start()

    def step(self, at):
        total = self.sum
        z = self.here.z
        ends = (z == 0) | (z == 3)
        for n, block in enumerate(total.order):
            pl.when(at == n)(lambda z=block: total.cores(z))
            pl.when(at == (4, 5, 7, 8)[n])(lambda z=block: total.stay(z))
            pl.when(at == (6, 11, 17, 22)[n])(lambda z=block: total.sides(z))
        for n, block in enumerate(total.order[:3]):
            when = jnp.where(ends, (6, 11, 17)[n], (12, 18, 19)[n])
            pl.when(at == when)(lambda z=block: total.pass_on(z))

    def finish(self):
        self.sum.finish()
        self.across.wait()


def mixer_backward(links, inner, dy, states, kin, kst, log_rate, skip_in, cst, bc_in, step_in, cum_in, stepT, cumT, preT, *refs):
    refs = list(refs)
    if links:
        beside = refs[:2] + refs[7:9]
        refs = refs[2:7] + refs[9:]
        work = BesideBackward(*beside, refs[24:])
    dinner_out, gk_out, dsd_out, gks_out, hs_out = refs[:5]
    buf, dbuf, gram, gg, gb, gc, colc, cols, rowp, mst, dyst, gmix, sgrad = refs[5:18]
    rs_t, cs_t, dr_t, wg_t, gt_t, gtaps = refs[18:24]
    i = pl.program_id(0)
    if links:
        pl.when(i == 0)(work.start)
    heads = log_rate.shape[0]
    skip = lay(head_row(skip_in), as_units(heads, i))[0:1]
    tokens = inner.shape[0]
    spans = tokens // Q
    masks = head_masks()

    @pl.when(i == 0)
    def _():
        buf[0:8] = jnp.zeros((8, BW), f32)
        dbuf[tokens : tokens + 8] = jnp.zeros((8, BW), f32)
        for s in range(spans):
            bc = bc_in[s * Q : s * Q + Q]
            gram[s] = mm(bc[:, 128:], bc[:, :128], 1, 1)
        for ref in (gg, gb, gc, rs_t, cs_t, dr_t, wg_t, gt_t):
            ref[...] = jnp.zeros(ref.shape, f32)
        mst[...] = jnp.zeros(mst.shape, bf16)

    buf[8 : 8 + tokens] = inner[...]
    turn = lax.rem(128 - 8 * i, 128)
    colc[...] = pltpu.roll(cum_in[...], turn, 1)
    cols[...] = pltpu.roll(step_in[...], turn, 1)
    rows8 = pl.ds(pl.multiple_of(8 * i, 8), 8)
    rowp[...] = cumT[rows8] - jnp.log2(stepT[rows8])
    sgrad[...] = jnp.zeros(sgrad.shape, f32)
    gtaps[...] = jnp.zeros(gtaps.shape, f32)
    pick = (iota((8, BW), 1) // HEAD == iota((8, BW), 0)).astype(f32).astype(bf16)

    def conv_rows(at, kernel, grad_act, conv, sig):
        gco = grad_act * (sig * (1.0 + conv * (1.0 - sig)))
        dbuf[pl.ds(at, Q)] = gco
        into = buf[pl.ds(pl.multiple_of(at + 8, 8), Q)]
        gtaps[4:5] += jnp.sum(gco, axis=0, keepdims=True)
        after = dbuf[pl.ds(at, Q + 8)]
        grad_in = kernel[3:4] * gco
        gtaps[3:4] += jnp.sum(gco * into, axis=0, keepdims=True)
        for k in range(3):
            later = pltpu.roll(after, Q + 8 - (3 - k), 0)[:Q]
            gtaps[k : k + 1] += jnp.sum(later * into, axis=0, keepdims=True)
            grad_in = grad_in + kernel[k : k + 1] * later
        return grad_in

    def span(back, carry):
        s = spans - 1 - back
        at = pl.multiple_of(s * Q, Q)
        rows = pl.ds(at, Q)
        conv = conv_taps(buf[pl.ds(at, Q + 8)], kin[...])
        sig = sigmoid(conv)
        xs = conv * sig
        x_low = xs.astype(bf16)
        dy_s = dy[rows]
        dy_f = dy_s.astype(f32)
        bc = bc_in[rows]
        b_low, c_low = bc[:, :128], bc[:, 128:]
        col = colc[rows]
        total = col[Q - 1 : Q]
        for j in range(HB):
            dyst[j * Q : j * Q + Q] = dy_s * masks[j]
        gmix[...] = mm(dyst[...], x_low, 1, 1)
        lane = iota((Q, 128), 1)
        row_sums = jnp.zeros((Q, 128), f32)
        for j in range(HB):
            row = rowp[j : j + 1, rows]
            col_sum = [jnp.zeros((1, 128), f32), jnp.zeros((1, 128), f32)]
            row_parts = []
            for r, half, diag in quads():
                here = slice(half * 128, half * 128 + 128)
                dec = decay_chunk(col[:, j : j + 1], row, r, half, diag)
                part = gram[s, r : r + 64, here]
                p = gmix[j * Q + r : j * Q + r + 64, here] * dec
                gg[s, r : r + 64, here] += p
                q = p * part
                mst[j * Q + r : j * Q + r + 64, here] = (part * dec).astype(bf16)
                col_sum[half] = col_sum[half] + jnp.sum(q, axis=0, keepdims=True)
                if half == 0:
                    row_parts.append(q)
                else:
                    row_parts[-1] = row_parts[-1] + q
            sums = jnp.concatenate([jnp.sum(q, axis=1, keepdims=True) for q in row_parts], axis=0)
            row_sums = jnp.where(lane == j, sums, row_sums)
            cs_t[pl.ds(8 * i + j, 1), rows] = jnp.concatenate(col_sum, axis=1)
        rs_t[rows8, rows] = jnp.transpose(row_sums)[:8]
        grad_xs = mm(mst[...], dyst[...], 0, 0) + skip * dy_f

        growth = expand(jnp.exp2(col[:, :8]))
        weight = expand(jnp.exp2(total[:, :8] - col[:, :8]) * cols[rows][:, :8])
        state_in = states[s]
        state_low = state_in.astype(bf16)
        state_grad = sgrad[...]
        carry_low = state_grad.astype(bf16)
        readout = mm(c_low, state_low, 1, 1)
        read_low = (dy_f * growth).astype(bf16)
        hi, low = split2(dy_f * readout)
        dr_t[rows8, rows] = mm(pick, hi, 1, 1) + mm(pick, low, 1, 1)
        gc[rows] += mm(read_low, state_low)
        grad_xw = mm(b_low, carry_low, 1, 1)
        xw_low = (xs * weight).astype(bf16)
        gb[rows] += mm(xw_low, carry_low)
        hi, low = split2(grad_xw * xs)
        wg_t[rows8, rows] = mm(pick, hi, 1, 1) + mm(pick, low, 1, 1)
        hi, low = split2(state_grad * state_in)
        sums = jnp.sum(mm(pick, hi) + mm(pick, low), axis=1, keepdims=True)
        gt_t[rows8] = jnp.where(iota((8, 128), 1) == s, sums, gt_t[rows8])
        grad_xs = grad_xs + grad_xw * weight
        local = mm(read_low, c_low, 0, 0)
        fade = jnp.exp2(total)
        for j in range(HB):
            at_j = slice(j * HEAD, j * HEAD + HEAD)
            sgrad[at_j] = fade[:, j : j + 1] * state_grad[at_j] + local[at_j]
        gtaps[5:6] += jnp.sum(dy_f * xs, axis=0, keepdims=True)
        dinner_out[rows] = conv_rows(at, kin[...], grad_xs, conv, sig).astype(bf16)
        if links:
            work.step(i * spans + back)
        return carry

    lax.fori_loop(0, spans, span, 0)
    gk_out[...] = gtaps[...]

    @pl.when(i == pl.num_programs(0) - 1)
    def _():
        buf[8 : 8 + tokens] = cst[...]
        gtaps[...] = jnp.zeros(gtaps.shape, f32)
        rates = lay(-jnp.exp(head_row(log_rate)), as_places(heads))[0:1]
        rate = jnp.transpose(jnp.broadcast_to(rates, (128, 128)))[:48, 0:1]
        later = (iota((Q, Q), 0) >= iota((Q, Q), 1)).astype(f32).astype(bf16)
        last = iota((48, Q), 1) == Q - 1
        bias_sum = jnp.zeros((48, 1), f32)
        decay_sum = jnp.zeros((48, 1), f32)
        for back in range(spans):
            s = spans - 1 - back
            rows = slice(s * Q, s * Q + Q)
            bc = bc_in[rows]
            gl = gg[s].astype(bf16)
            grad_c = gc[rows] + mm(gl, bc[:, :128])
            grad_b = gb[rows] + mm(gl, bc[:, 128:], 0, 0)
            both = jnp.concatenate([grad_b, grad_c], axis=1)
            conv = conv_taps(buf[s * Q : s * Q + Q + 8], kst[...])
            dsd_out[rows, :BW] = conv_rows(s * Q, kst[...], both, conv, sigmoid(conv)).astype(bf16)

            cum, step, pre = cumT[:, rows], stepT[:, rows], preT[:, rows]
            total = cum[:, Q - 1 : Q]
            rate_w = jnp.exp2(total - cum)
            wg = wg_t[:, rows]
            cs = cs_t[:, rows]
            moved = wg * (rate_w * step)
            grad_cum = rs_t[:, rows] - cs + jnp.exp2(cum) * dr_t[:, rows] - moved
            grad_total = jnp.exp2(total) * gt_t[:, s : s + 1] + jnp.sum(moved, axis=1, keepdims=True)
            grad_cum = grad_cum + jnp.where(last, grad_total, 0.0)
            parts = split3(grad_cum)
            grad_rate = mm(parts[0], later) + mm(parts[1], later) + mm(parts[2], later)
            sig = sigmoid(pre)
            ratio = jnp.where(pre < -15.0, 1.0, sig / step)
            grad_pre = (wg * rate_w + grad_rate * rate) * sig + cs * ratio
            bias_sum = bias_sum + jnp.sum(grad_pre, axis=1, keepdims=True)
            decay_sum = decay_sum + jnp.sum(grad_rate * step, axis=1, keepdims=True)
            full = jnp.concatenate([grad_pre, jnp.zeros((80, Q), f32)], axis=0)
            dsd_out[rows, BW:] = jnp.transpose(full).astype(bf16)
        gks_out[...] = gtaps[...]
        lane = iota((48, 128), 1)
        both = jnp.where(lane == 0, bias_sum, jnp.where(lane == 1, decay_sum * rate, 0.0))
        hs_out[...] = jnp.transpose(jnp.concatenate([both, jnp.zeros((80, 128), f32)], axis=0))[:8]
        if links:
            work.finish()


class Place:
    def __init__(self):
        me = lax.axis_index("dp")
        self.me = me
        self.c, self.y, self.z = me % 2, (me // 2) % 2, me // 4

    def at(self, z, y, c):
        return (z * 2 + y) * 2 + c

    def core(self):
        return self.at(self.z, self.y, 1 - self.c)

    def side(self):
        return self.at(self.z, 1 - self.y, self.c)

    def up(self):
        return self.me + 4

    def down(self):
        return self.me - 4


def greet(here, across):
    barrier = pltpu.get_barrier_semaphore()

    def signal(**device):
        pl.semaphore_signal(barrier, 1, device_id=device, device_id_type=MESH)

    signal(dp=here.core())
    signal(dp=here.side())
    pl.when(here.z < 3)(lambda: signal(dp=here.up()))
    pl.when(here.z > 0)(lambda: signal(dp=here.down()))
    if across:
        signal(tensor=1 - lax.axis_index("tensor"))
    ends = (here.z == 0).astype(jnp.int32) + (here.z == 3).astype(jnp.int32)
    pl.semaphore_wait(barrier, 4 + int(across) - ends)


def remote(src, dst, send_sem, recv_sem, **device):
    return pltpu.make_async_remote_copy(
        src_ref=src, dst_ref=dst, send_sem=send_sem, recv_sem=recv_sem, device_id=device, device_id_type=MESH
    )


class Gather:
    def __init__(self, here, own, full, ss, rs, ls, chunk, cols):
        self.here, self.full, self.ss, self.rs, self.chunk, self.cols = here, full, ss, rs, chunk, cols
        self.rows = own.shape[0]
        self.own = own
        self.lift = chunk == 0
        self.local = pltpu.make_async_copy(own, self.slot(here.me), ls.at[chunk])

    def slot(self, origin):
        return self.full.at[pl.ds(pl.multiple_of(origin * self.rows, self.rows), self.rows), self.cols]

    def copy(self, origin, way, src=None):
        here = self.here
        target = (here.up, here.down, here.side, here.core)[way]()
        slot = self.slot(origin)
        sems = self.ss.at[self.chunk, origin, way], self.rs.at[self.chunk, origin]
        return remote(slot if src is None else src, slot, *sems, dp=target)

    def arrived(self, origin):
        self.copy(origin, 3).wait_recv()

    def ways(self, hops):
        z = self.here.z
        return ((0, z),) if hops == 0 else ((0, z - hops), (1, z + hops))

    def onward(self, way):
        return (self.here.z < 3) if way == 0 else (self.here.z > 0)

    def own_sends(self, hops, way, origin_z, act):
        here = self.here
        origin = here.at(origin_z, here.y, here.c)
        for along in (0, 1) if hops == 0 else (way,):
            pl.when(self.onward(along))(lambda along=along: act(origin, along))
        if hops and self.lift:
            pl.when((origin_z != 0) & (origin_z != 3))(lambda: act(origin, 2))
        else:
            act(origin, 2)
        act(origin, 3)

    def side_sends(self, hops, way, origin_z, act):
        here = self.here
        origin = here.at(origin_z, 1 - here.y, here.c)
        act(origin, 3)
        if self.lift and hops == 0:
            pl.when(here.z == 0)(lambda: act(origin, 0))
            pl.when(here.z == 3)(lambda: act(origin, 1))
        elif self.lift:
            pl.when((origin_z == 3 * way) & self.onward(way))(lambda: act(origin, way))

    def each(self, hops, act):
        for way, origin_z in self.ways(hops):
            if hops == 0:
                act(way, origin_z)
            else:
                pl.when((origin_z >= 0) & (origin_z <= 3))(lambda way=way, origin_z=origin_z: act(way, origin_z))

    def send(self, origin, way):
        self.copy(origin, way).start()

    def start(self):
        self.own_sends(0, 0, self.here.z, lambda origin, way: self.copy(origin, way, self.own).start())
        self.local.start()

    def hop(self, hops):
        def go(way, origin_z):
            self.arrived(self.here.at(origin_z, self.here.y, self.here.c))
            self.own_sends(hops, way, origin_z, self.send)

        self.each(hops, go)

    def sides(self, hops):
        def go(way, origin_z):
            self.arrived(self.here.at(origin_z, 1 - self.here.y, self.here.c))
            self.side_sends(hops, way, origin_z, self.send)

        self.each(hops, go)

    def finish(self):
        here = self.here
        self.local.wait()
        for z in range(4):
            for y in range(2):
                self.arrived(here.at(z, y, 1 - here.c))

        def sent(origin, way):
            self.copy(origin, way).wait_send()

        for hops in range(4):

            def go(way, origin_z, hops=hops):
                self.own_sends(hops, way, origin_z, sent)
                self.side_sends(hops, way, origin_z, sent)

            self.each(hops, go)


def gather_scratch():
    sem = pltpu.SemaphoreType.DMA
    return [sem((2, 16, 4)), sem((2, 16)), sem((2,))]


def gather_kernel(tokens_in, gain, w_gate_inner, w_state_io, w_step, tokens_out, full, pack, low, ss, rs, ls, xs, xr, xl):
    here = Place()
    half = lax.axis_index("tensor")
    rows = tokens_in.shape[0]
    units, cols = w_gate_inner.shape[2], full.shape[1]
    pack[:, :units] = w_gate_inner[1]
    pack[:, units : units + BW] = w_state_io[...]
    pack[:, units + BW :] = mm(w_step[...], as_places(w_step.shape[1])).astype(bf16)
    greet(here, True)
    cut = cols // 256 * 128
    moves = [
        Gather(here, pack.at[:, c], full, ss, rs, ls, n, c) for n, c in enumerate((slice(0, cut), slice(cut, cols)))
    ]
    for move in moves:
        move.start()
    part = rows // 4
    across, local = [], []
    for n in range(4):
        piece = slice(n * part, n * part + part)
        v = tokens_in[piece].astype(f32)
        scale = lax.rsqrt(jnp.mean(v * v, axis=1, keepdims=True) + norm_eps)
        low[piece] = (v * scale * gain[0:1]).astype(bf16)
        slot = tokens_out.at[pl.ds(pl.multiple_of(half * rows + n * part, part), part)]
        across.append(remote(low.at[piece], slot, xs.at[n], xr.at[n], tensor=1 - half))
        across[-1].start()
        local.append(pltpu.make_async_copy(low.at[piece], slot, xl.at[n]))
        local[-1].start()
    for hops in range(1, 5):
        for move in moves:
            if hops < 4:
                move.hop(hops)
            move.sides(hops - 1)
    for n in range(4):
        local[n].wait()
        across[n].wait()
    for move in moves:
        move.finish()


def gather_rows(tokens_in, gain, w_gate_inner, w_state_io, w_step, ways, collective_id):
    rows, width = tokens_in.shape
    _, own, units = w_gate_inner.shape
    cols = units + BW + 128
    vmem = pl.BlockSpec(memory_space=pltpu.VMEM)
    hbm = pl.BlockSpec(memory_space=pl.ANY)
    sem = pltpu.SemaphoreType.DMA
    return pl.pallas_call(
        gather_kernel,
        name="gather_rows",
        in_specs=[vmem] * 5,
        out_specs=[hbm, hbm],
        out_shape=[sds((2 * rows, width), bf16), sds((ways * own, cols), bf16)],
        scratch_shapes=[
            pltpu.VMEM((own, cols), bf16), pltpu.VMEM((rows, width), bf16), *gather_scratch(),
            sem((4,)), sem((4,)), sem((4,)),
        ],
        compiler_params=pltpu.CompilerParams(
            collective_id=collective_id, has_side_effects=True, vmem_limit_bytes=60 * 1024 * 1024
        ),
    )(tokens_in, gain, w_gate_inner, w_state_io, w_step)


class Reduce:
    def __init__(self, here, grads, out, bufs, sems):
        self.here, self.grads, self.out = here, grads, out
        self.held, self.buf_a, self.buf_b, self.buf_up, self.buf_dn = bufs
        self.local, self.send_a, self.recv_a, self.send_b, self.recv_b, self.send_c, self.recv_up, self.recv_dn = sems
        self.parts, self.rows = out.shape[:2]
        z = here.z
        self.order = (3 * (1 - z // 2), (3 * z + 2) % 5, 1 + z % 2, z)

    def spot(self, z, y, c):
        if self.grads is None:
            return z, (y * 2 + c) * self.rows
        return z * 2 + y, 0

    def own(self, z, y, c=None):
        at, base = self.spot(z, y, self.here.c if c is None else c)
        return self.held.at[at, :, pl.ds(pl.multiple_of(base, 16), self.rows)]

    def block(self, z, y, c):
        if self.grads is None:
            return self.own(z, y, c)
        at = pl.multiple_of(self.here.at(z, y, c) * self.rows, self.rows)
        return self.grads.at[:, pl.ds(at, self.rows)]

    def copy_a(self, z, y):
        here, at = self.here, z * 2 + y
        return remote(self.block(z, y, 1 - here.c), self.buf_a.at[at], self.send_a.at[at], self.recv_a.at[at], dp=here.core())

    def take(self, z, y):
        return pltpu.make_async_copy(self.block(z, y, self.here.c), self.own(z, y), self.local.at[z * 2 + y])

    def copy_b(self, z):
        here = self.here
        return remote(self.own(z, 1 - here.y), self.buf_b.at[z], self.send_b.at[z], self.recv_b.at[z], dp=here.side())

    def copy_up(self, z):
        return remote(self.own(z, self.here.y), self.buf_up.at[z], self.send_c.at[z], self.recv_up.at[z], dp=self.here.up())

    def copy_dn(self, z):
        return remote(self.own(z, self.here.y), self.buf_dn.at[z], self.send_c.at[z], self.recv_dn.at[z], dp=self.here.down())

    def add(self, z, y, buf, slot):
        at, base = self.spot(z, y, self.here.c)

        def rows(n, carry):
            piece = pl.ds(pl.multiple_of(n * 16, 16), 16)
            held = pl.ds(pl.multiple_of(base + n * 16, 16), 16)
            for part in range(self.parts):
                total = self.held[at, part, held].astype(f32) + buf[slot, part, piece].astype(f32)
                self.held[at, part, held] = total.astype(bf16)
            return carry

        lax.fori_loop(0, self.rows // 16, rows, 0)

    def start(self):
        here = self.here
        for side in (1 - here.y, here.y):
            for z in self.order:
                self.copy_a(z, side).start()
                self.take(z, side).start()

    def join(self, z, y):
        if self.grads is not None:
            self.take(z, y).wait()
        self.copy_a(z, y).wait_recv()
        self.add(z, y, self.buf_a, z * 2 + y)

    def cores(self, z):
        self.join(z, 1 - self.here.y)
        self.copy_b(z).start()

    def stay(self, z):
        self.join(z, self.here.y)

    def sides(self, z):
        self.copy_b(z).wait_recv()
        self.add(z, self.here.y, self.buf_b, z)

    def pass_on(self, z):
        here = self.here

        def up():
            def below():
                self.copy_up(z).wait_recv()
                self.add(z, here.y, self.buf_up, z)

            pl.when(here.z > 0)(below)
            self.copy_up(z).start()

        def down():
            def above():
                self.copy_dn(z).wait_recv()
                self.add(z, here.y, self.buf_dn, z)

            pl.when(here.z < 3)(above)
            self.copy_dn(z).start()

        pl.when(z > here.z)(up)
        pl.when(z < here.z)(down)

    def finish(self):
        here = self.here
        z = here.z
        at, base = self.spot(z, here.y, here.c)
        pl.when(z > 0)(lambda: self.copy_up(z).wait_recv())
        pl.when(z < 3)(lambda: self.copy_dn(z).wait_recv())

        def rows(n, carry):
            piece = pl.ds(pl.multiple_of(n * 16, 16), 16)
            held = pl.ds(pl.multiple_of(base + n * 16, 16), 16)
            for part in range(self.parts):
                below = jnp.where(z > 0, self.buf_up[z, part, piece].astype(f32), 0.0)
                above = jnp.where(z < 3, self.buf_dn[z, part, piece].astype(f32), 0.0)
                self.out[part, piece] = self.held[at, part, held].astype(f32) + below + above
            return carry

        lax.fori_loop(0, self.rows // 16, rows, 0)
        for zn in self.order:
            self.copy_a(zn, 0).wait_send()
            self.copy_a(zn, 1).wait_send()
            self.copy_b(zn).wait_send()
            pl.when(zn > z)(lambda zn=zn: self.copy_up(zn).wait_send())
            pl.when(zn < z)(lambda zn=zn: self.copy_dn(zn).wait_send())


def reduce_scratch(parts, rows, cols, by_z=False):
    sem = pltpu.SemaphoreType.DMA
    block = (parts, rows, cols)
    held = (4, parts, 4 * rows, cols) if by_z else (8,) + block
    return [
        pltpu.VMEM(held, bf16), pltpu.VMEM((8,) + block, bf16), pltpu.VMEM((4,) + block, bf16),
        pltpu.VMEM((4,) + block, bf16), pltpu.VMEM((4,) + block, bf16),
        sem((8,)), sem((8,)), sem((8,)), sem((4,)), sem((4,)), sem((4,)), sem((4,)), sem((4,)),
    ]


def tail_kernel(
    normed_t, dinner, dsd, dgate, wb, wa, gk, ggg, gks, hs, norm_gain, w_gate_inner, w_state_io, w_step, gate_grads,
    gn_out, inner_out, step_out, both_out, small_out, shard_out, give, got, send_g, recv_g, nt_v, dinner_v, dsd_v, dgate_v, wg_v, wa_v, away, came, total, landed, loads, send_x, recv_x, send, recv, *scratch,
):
    here = Place()
    half = lax.axis_index("tensor")
    units = dgate.shape[1]
    sources = (normed_t, dinner, dsd, dgate, wb.at[:, :units], wa)
    pending = [
        pltpu.make_async_copy(src, dst, loads.at[n])
        for n, (src, dst) in enumerate(zip(sources, (nt_v, dinner_v, dsd_v, dgate_v, wg_v, wa_v)))
    ]
    for copy in pending[:3]:
        copy.start()
    far = pltpu.get_barrier_semaphore()
    partners = [here.me + bit - 2 * bit * ((here.me // bit) % 2) for bit in (2, 4, 8, 1)]
    for partner in partners:
        pl.semaphore_signal(far, 1, device_id={"dp": partner}, device_id_type=MESH)
    pl.semaphore_signal(far, 1, device_id={"tensor": 1 - half}, device_id_type=MESH)
    middle = (here.z == 1) | (here.z == 2)
    pl.when(here.z == 1)(lambda: pl.semaphore_signal(far, 1, device_id={"dp": here.up()}, device_id_type=MESH))
    pl.when(here.z == 2)(lambda: pl.semaphore_signal(far, 1, device_id={"dp": here.down()}, device_id_type=MESH))
    pl.semaphore_wait(far, 5 + middle.astype(jnp.int32))
    work = Reduce(here, None, shard_out, scratch[:5], scratch[5:])
    order = work.order
    rows = gn_out.shape[0]
    chunks, _, wide = away.shape

    def swap(k):
        return remote(total.at[k], landed.at[k], send.at[k], recv.at[k], dp=partners[k])

    def swapped(k):
        swap(k).wait()
        total[k + 1] = total[k] + landed[k]
        if k < 3:
            swap(k + 1).start()

    def across(n):
        return remote(away.at[n], came.at[n], send_x.at[n], recv_x.at[n], tensor=1 - half)

    def pulled(which, n):
        mine = pl.ds(pl.multiple_of(which * rows, rows), rows)
        at = pl.ds(pl.multiple_of(n * wide, wide), wide)
        return (
            mm(dgate_v[mine], wg_v[at], 1, 1)
            + mm(dinner_v[mine], wa_v[at, :units], 1, 1)
            + mm(dsd_v[mine], wa_v[at, units:], 1, 1)
        )

    def far_chunk(n, carry):
        away[n] = pulled(1 - half, n).astype(bf16)
        across(n).start()
        return carry

    def near_chunk(n, carry):
        gn_out[:, pl.ds(pl.multiple_of(n * wide, wide), wide)] = pulled(half, n)
        return carry

    def grads(n, carry):
        z = jnp.where(n == 0, order[0], jnp.where(n == 1, order[1], jnp.where(n == 2, order[2], order[3])))
        count = 4 * work.rows
        left = nt_v[pl.ds(pl.multiple_of(z * count, count), count)]
        work.held[z, 0, :, :units] = mm(left, dinner_v[...]).astype(bf16)
        work.held[z, 0, :, units:] = mm(left, dsd_v[...]).astype(bf16)
        work.copy_a(z, 1 - here.y).start()
        work.copy_a(z, here.y).start()

        @pl.when(n == 1)
        def _():
            for copy in pending[3:]:
                copy.wait()

        @pl.when(n > 0)
        def _():
            far_chunk(n - 1, carry)

        work.cores(z)
        return carry

    total[0, 0:6] = gk[0:6]
    total[0, 6:7] = ggg[0:1]
    for k in range(5):
        total[0, 7:8, k * BW : k * BW + BW] = gks[k : k + 1]
    for k in range(2):
        total[0, 7:8, 5 * BW + k * 128 : 5 * BW + k * 128 + 128] = hs[k : k + 1]
    swap(0).start()
    for copy in pending[:3]:
        copy.wait()
    for copy in pending[3:]:
        copy.start()
    swapped(0)
    lax.fori_loop(0, 4, grads, 0)
    swapped(1)
    work.stay(order[0])
    work.sides(order[0])
    pl.when(~middle)(lambda: work.pass_on(order[0]))
    lax.fori_loop(3, chunks, far_chunk, 0)
    swapped(2)
    for n in range(1, 4):
        work.stay(order[n])
    work.sides(order[1])
    pl.when(~middle)(lambda: work.pass_on(order[1]))
    lax.fori_loop(0, 3, near_chunk, 0)
    pl.when(middle)(lambda: work.pass_on(order[0]))
    work.sides(order[2])
    pl.when(~middle)(lambda: work.pass_on(order[2]))
    lax.fori_loop(3, chunks, near_chunk, 0)
    swapped(3)
    small_out[...] = total[4]
    pl.when(middle)(lambda: work.pass_on(order[1]))
    work.sides(order[3])
    pl.when(middle)(lambda: work.pass_on(order[2]))
    work.finish()

    def arrive(n, carry):
        across(n).wait()
        at = pl.ds(pl.multiple_of(n * wide, wide), wide)
        gn_out[:, at] = gn_out[:, at] + came[n].astype(f32)
        return carry

    inner_out[0] = gate_grads[0]
    inner_out[1] = shard_out[0, :, :units]
    step_out[...] = shard_out[0, :, units + BW :]
    count = work.rows
    part = shard_out[0, :, units + BW :] * mm(w_step[...], as_places(w_step.shape[1]))
    for c in range(2):
        at = slice(units + c * 128, units + c * 128 + 128)
        part = part + shard_out[0, :, at] * w_state_io[:, c * 128 : c * 128 + 128].astype(f32)
    for c in range(units // 128):
        at = slice(c * 128, c * 128 + 128)
        part = part + gate_grads[0, :, at] * w_gate_inner[0, :, at].astype(f32)
        part = part + shard_out[0, :, at] * w_gate_inner[1, :, at].astype(f32)
    part = jnp.concatenate([part, jnp.zeros((128 - count, 128), f32)], axis=0)
    row = jnp.sum(jnp.transpose(part), axis=0, keepdims=True)
    shape = (norm_gain.shape[1], 128)
    pick = (iota(shape, 0) == iota(shape, 1) + here.me * count) & (iota(shape, 1) < count)
    gain = lay(norm_gain[...], pick.astype(f32).astype(bf16))[0:1]
    row = row / jnp.where(iota((1, 128), 1) < count, gain, 1.0)
    low = pltpu.roll(row, 128 - count // 2, 1)
    first = half == 0

    def share(at, a, b):
        both_out[at] = jnp.where(first, a, b)
        give[at] = jnp.where(first, b, a)

    share(slice(0, count), shard_out[0, :, units : units + 128], shard_out[0, :, units + 128 : units + 256])
    for k in range(5):
        pair = [small_out[7:8, k * BW + c * 128 : k * BW + c * 128 + 128] for c in range(2)]
        share(slice(count + k, count + k + 1), *pair)
    share(slice(count + 5, count + 6), row, low)
    share(slice(count + 6, count + 8), jnp.zeros((2, 128), f32), jnp.zeros((2, 128), f32))
    last = remote(give, got, send_g, recv_g, tensor=1 - half)
    last.start()
    lax.fori_loop(0, chunks, arrive, 0)
    last.wait()
    both_out[...] = both_out[...] + got[...]


def reduce_tail(normed_t, dinner, dsd, dgate, wb, wa, sums, weights, ways, collective_id):
    width, tokens = normed_t.shape
    small = sums[0]
    units, cols, rows = dgate.shape[1], wa.shape[1], width // ways
    chunks = width // BW
    vmem = pl.BlockSpec(memory_space=pltpu.VMEM)
    hbm = pl.BlockSpec(memory_space=pl.ANY)
    sem = pltpu.SemaphoreType.DMA
    return pl.pallas_call(
        tail_kernel, name="tail", in_specs=[hbm] * 6 + [vmem] * 9, out_specs=[vmem] * 5,
        out_shape=[
            sds((tokens // 2, width)), sds((2, rows, units)), sds((rows, 128)), sds((rows + 8, 128)), sds(small.shape),
        ],
        scratch_shapes=[
            pltpu.VMEM((1, rows, cols), f32), pltpu.VMEM((rows + 8, 128), f32), pltpu.VMEM((rows + 8, 128), f32), sem, sem,
            pltpu.VMEM(normed_t.shape, bf16), pltpu.VMEM(dinner.shape, bf16), pltpu.VMEM(dsd.shape, bf16),
            pltpu.VMEM(dgate.shape, bf16), pltpu.VMEM((width, units), bf16), pltpu.VMEM(wa.shape, bf16),
            pltpu.VMEM((chunks, tokens // 2, BW), bf16), pltpu.VMEM((chunks, tokens // 2, BW), bf16),
            pltpu.VMEM((5,) + small.shape, f32), pltpu.VMEM((4,) + small.shape, f32),
            sem((6,)), sem((chunks,)), sem((chunks,)), sem((4,)), sem((4,)),
        ] + reduce_scratch(1, rows, cols, True),
        compiler_params=pltpu.CompilerParams(
            collective_id=collective_id, has_side_effects=True, vmem_limit_bytes=62 * 1024 * 1024
        ),
    )(normed_t, dinner, dsd, dgate, wb, wa, *sums, *weights)


def swap(v):
    return lax.ppermute(v, "tensor", [(0, 1), (1, 0)])


def halves(v, axis):
    size = v.shape[axis] // 2
    me = lax.axis_index("tensor")
    return (
        lax.dynamic_slice_in_dim(v, me * size, size, axis),
        lax.dynamic_slice_in_dim(v, (1 - me) * size, size, axis),
    )


def once(shape, at=None):
    where = at or (0,) * len(shape)
    return pl.BlockSpec(shape, lambda i: where, pipeline_mode=pl.Buffered(1))


def by_cols(rows, offset=0):
    return pl.BlockSpec((rows, BW), lambda i: (0, i + offset))


def params(collective_id=None):
    return pltpu.CompilerParams(
        dimension_semantics=("arbitrary",), vmem_limit_bytes=60 * 1024 * 1024,
        collective_id=collective_id, has_side_effects=collective_id is not None,
    )


def spread(v):
    lead = v.shape[:-1]
    v = v.reshape(lead + (v.shape[-1] // HB, HB))
    v = jnp.pad(v, [(0, 0)] * len(lead) + [(0, 0), (0, 8 - HB)]).reshape(lead + (-1,))
    return jnp.pad(v, [(0, 0)] * len(lead) + [(0, 128 - v.shape[-1])])


def gathered_heads(v, heads):
    return v[..., : heads * 2].reshape(v.shape[:-1] + (heads // HB, 8))[..., :HB].reshape(v.shape[:-1] + (heads,))


def sds(shape, dtype=f32):
    return jax.ShapeDtypeStruct(shape, dtype)


def on_device(
    residual, norm_gain, w_gate_inner, w_state_io, w_step, conv_inner, conv_state,
    step_bias, decay_log, skip_gain, gate_gain, w_output, cotangent,
):
    width = residual.shape[1]
    units = w_gate_inner.shape[2]
    heads = w_step.shape[1]
    blocks = units // BW
    unit_total = units * lax.axis_size("tensor")
    ways = lax.axis_size("dp")
    own_links = ways == 16
    rows_in = residual.astype(f32)
    rstd_in = lax.rsqrt(jnp.mean(rows_in * rows_in, axis=1, keepdims=True) + norm_eps)
    scaled = rows_in * rstd_in
    pack_a = jnp.concatenate([w_gate_inner[1], w_state_io, spread(w_step)], axis=1)
    w_output_t = w_output.T
    gain_in = jnp.broadcast_to(norm_gain[None], (8, width))
    if own_links:
        normed, wa = gather_rows(residual, gain_in, w_gate_inner, w_state_io, w_step, ways, 1)
    else:
        wa = lax.all_gather(pack_a, "dp", axis=0, tiled=True)
        normed = lax.all_gather((scaled * norm_gain).astype(bf16), "tensor", axis=0, tiled=True)
    tokens = normed.shape[0]
    spans = tokens // Q
    gain8 = jnp.broadcast_to(gate_gain[None], (8, units))

    hbm = pl.BlockSpec(memory_space=pl.ANY)
    sem = pltpu.SemaphoreType.DMA
    def stage(rows, first):
        return pl.BlockSpec((rows, BW), lambda i: (0, jnp.clip(i - first, 0, blocks - 1)))

    inner, ssd, states, cst, bc, step, cum, step_t, cum_t, pre_t, *sent = pl.pallas_call(
        functools.partial(mixer_forward, own_links),
        name="mixer_forward",
        grid=(blocks * (3 if own_links else 1),),
        in_specs=[
            once((tokens, width)), stage(width, 0), once((width, 384), (0, units // 384)),
            stage(5, 0), once((5, BW)), once((heads,)), once((heads,)), once((heads,)),
        ] + ([once(v.shape) for v in (cotangent, w_gate_inner, w_output_t)] + [stage(8, 2 * blocks)]) * own_links,
        out_specs=[
            stage(tokens, 0), stage(tokens, 0), pl.BlockSpec((spans, BW, 128), lambda i: (0, jnp.clip(i, 0, blocks - 1), 0)),
            once((tokens, BW)), once((tokens, BW)), once((tokens, 128)), once((tokens, 128)),
            once((48, tokens)), once((48, tokens)), once((48, tokens)),
        ] + [hbm, hbm, stage(tokens, blocks), stage(tokens, 2 * blocks), once((8, tokens))] * own_links,
        out_shape=[
            sds((tokens, units)), sds((tokens, units)), sds((spans, units, 128)),
            sds((tokens, BW)), sds((tokens, BW), bf16), sds((tokens, 128)), sds((tokens, 128)),
            sds((48, tokens)), sds((48, tokens)), sds((48, tokens)),
        ] + [
            sds((tokens, width), bf16), sds((width, 2 * units), bf16), sds((tokens, units)), sds((tokens, units)),
            sds((8, tokens)),
        ] * own_links,
        scratch_shapes=[
            pltpu.VMEM((tokens + 8, BW), f32), pltpu.VMEM((spans, Q, Q), f32),
            pltpu.VMEM((tokens, 128), f32), pltpu.VMEM((tokens, 128), f32), pltpu.VMEM((8, tokens), f32),
            pltpu.VMEM((Q, HB * Q), bf16), pltpu.VMEM((HB * Q, BW), bf16), pltpu.VMEM((BW, 128), f32),
        ] + ([
            pltpu.VMEM((blocks + 1, tokens, BW), f32), pltpu.VMEM((blocks, width, BW), bf16), pltpu.VMEM((tokens, width), bf16),
            pltpu.VMEM((tokens, 128), f32), pltpu.VMEM((tokens, 128), f32), pltpu.VMEM((8, tokens), f32),
            pltpu.VMEM((8, tokens), f32), sem((blocks,)), sem((3,)),
        ] + gather_scratch() + [sem, sem, sem]) * own_links,
        compiler_params=params(2 if own_links else None),
        cost_estimate=pl.CostEstimate(flops=2 * tokens * width * (units + 384) + 4 * tokens * 256 * units, bytes_accessed=30_000_000, transcendentals=heads * spans * Q * Q),
    )(
        normed, wa, wa, conv_inner, conv_state, step_bias, decay_log, skip_gain,
        *[cotangent, w_gate_inner, w_output_t, gain8] * own_links,
    )

    if own_links:
        cot, wb, gate, ggo, stats = sent
    else:
        wb = lax.all_gather(jnp.concatenate([w_gate_inner[0], w_output_t], axis=1), "dp", axis=0, tiled=True)
        cot = lax.all_gather(cotangent, "tensor", axis=0, tiled=True)
        gate, ggo, stats = pl.pallas_call(
            gate_forward,
            name="gate_forward",
            grid=(blocks,),
            in_specs=[
                once((tokens, width)), once((tokens, width)), by_cols(width), by_cols(width, blocks),
                by_cols(tokens), by_cols(8),
            ],
            out_specs=[by_cols(tokens), by_cols(tokens), once((8, tokens))],
            out_shape=[sds((tokens, units)), sds((tokens, units)), sds((8, tokens))],
            scratch_shapes=[pltpu.VMEM((tokens, 128), f32), pltpu.VMEM((tokens, 128), f32)],
            compiler_params=params(),
            cost_estimate=pl.CostEstimate(flops=4 * tokens * width * units, bytes_accessed=35_000_000, transcendentals=tokens * units),
        )(normed, cot, wb, wb, ssd, gain8)
        stats = stats + swap(stats)

    dy, dgate, ng, ggg, grad_b, normed_t = pl.pallas_call(
        functools.partial(gate_backward, float(unit_total)),
        name="gate_backward",
        grid=(blocks,),
        in_specs=[
            once((8, tokens)), by_cols(tokens), by_cols(tokens), by_cols(tokens), by_cols(8),
            once((tokens, width)), once((tokens, width)),
        ],
        out_specs=[
            by_cols(tokens), by_cols(tokens), by_cols(tokens), by_cols(8),
            pl.BlockSpec((2, width, BW), lambda i: (0, 0, i)), once((width, tokens)),
        ],
        out_shape=[
            sds((tokens, units), bf16), sds((tokens, units), bf16), sds((tokens, units), bf16), sds((8, units)),
            sds((2, width, units), bf16), sds((width, tokens), bf16),
        ],
        scratch_shapes=[pltpu.VMEM((tokens, 128), f32), pltpu.VMEM((width, tokens), bf16)],
        compiler_params=params(),
        cost_estimate=pl.CostEstimate(flops=4 * tokens * units * width, bytes_accessed=45_000_000, transcendentals=tokens * units),
    )(stats, gate, ssd, ggo, gain8, normed, cot)

    mixed = mm(ng, wb[:, units:], 1, 1).astype(bf16)
    mixed_near, mixed_far = halves(mixed, 0)

    dinner, gk, dsd, gks, hs, *sent = pl.pallas_call(
        functools.partial(mixer_backward, own_links),
        name="mixer_backward",
        grid=(blocks,),
        in_specs=[
            by_cols(tokens), by_cols(tokens), pl.BlockSpec((spans, BW, 128), lambda i: (0, i, 0)),
            by_cols(5), once((5, BW)), once((heads,)), once((heads,)),
            once((tokens, BW)), once((tokens, BW)), once((tokens, 128)), once((tokens, 128)),
            once((48, tokens)), once((48, tokens)), once((48, tokens)),
        ] + [hbm, hbm] * own_links,
        out_specs=[by_cols(tokens), by_cols(8), once((tokens, 384)), once((8, BW)), once((8, 128))]
        + [hbm, once((2, width // ways, units))] * own_links,
        out_shape=[sds((tokens, units), bf16), sds((8, units)), sds((tokens, 384), bf16), sds((8, BW)), sds((8, 128))]
        + [sds((tokens // 2, width), bf16), sds((2, width // ways, units))] * own_links,
        scratch_shapes=[
            pltpu.VMEM((tokens + 8, BW), f32), pltpu.VMEM((tokens + 8, BW), f32),
            pltpu.VMEM((spans, Q, Q), f32), pltpu.VMEM((spans, Q, Q), f32),
            pltpu.VMEM((tokens, 128), f32), pltpu.VMEM((tokens, 128), f32),
            pltpu.VMEM((tokens, 128), f32), pltpu.VMEM((tokens, 128), f32), pltpu.VMEM((8, tokens), f32),
            pltpu.VMEM((HB * Q, Q), bf16), pltpu.VMEM((HB * Q, BW), bf16), pltpu.VMEM((HB * Q, Q), f32),
            pltpu.VMEM((BW, 128), f32),
            pltpu.VMEM((48, tokens), f32), pltpu.VMEM((48, tokens), f32), pltpu.VMEM((48, tokens), f32),
            pltpu.VMEM((48, tokens), f32), pltpu.VMEM((48, 128), f32), pltpu.VMEM((8, BW), f32),
        ] + ([sem, sem] + reduce_scratch(2, width // ways, units)) * own_links,
        compiler_params=params(4 if own_links else None),
        cost_estimate=pl.CostEstimate(flops=40_000_000_000, bytes_accessed=30_000_000, transcendentals=heads * spans * Q * Q),
    )(
        inner, dy, states, conv_inner, conv_state, decay_log, skip_gain, cst, bc, step, cum, step_t, cum_t, pre_t,
        *[mixed, grad_b] * own_links,
    )
    if own_links:
        mixed_got, wb_shard = sent
    else:
        mixed_got = swap(mixed_far)
        wb_shard = lax.psum_scatter(grad_b, "dp", scatter_dimension=1, tiled=True).astype(f32)
    output = (rows_in + mixed_near.astype(f32) + mixed_got.astype(f32)).astype(bf16)

    if own_links:
        weights = (gain_in, w_gate_inner, w_state_io, w_step, wb_shard)
        sums = (gk, ggg, gks, hs)
        grad_normed, inner_grads, step_grads, both, small = reduce_tail(
            normed_t, dinner, dsd, dgate, wb, wa, sums, weights, ways, 5
        )
    else:
        last = jnp.concatenate([gks[:5].reshape(-1), hs[0], hs[1]])
        small = jnp.concatenate([gk[:6], ggg[:1], last[None]], axis=0)
        grad_a = jnp.concatenate([mm(normed_t, dinner).astype(bf16), mm(normed_t, dsd).astype(bf16)], axis=1)
        pulled = mm(dgate, wb[:, :units], 1, 1) + mm(dinner, wa[:, :units], 1, 1) + mm(dsd, wa[:, units:], 1, 1)
        near, far = halves(pulled.astype(bf16), 0)
        wa_shard = lax.psum_scatter(grad_a, "dp", scatter_dimension=0, tiled=True).astype(f32)
        small = lax.psum(small, "dp")
        grad_normed = near.astype(f32) + swap(far).astype(f32)
    grad_v = grad_normed * norm_gain
    grad_residual = cotangent.astype(f32) + rstd_in * (
        grad_v - scaled * jnp.mean(grad_v * scaled, axis=1, keepdims=True)
    )

    bias_sum = gathered_heads(small[7, 5 * BW : 5 * BW + 128], heads)
    decay_sum = gathered_heads(small[7, 5 * BW + 128 : 5 * BW + 256], heads)
    skip_sum = jnp.sum(small[5].reshape(heads, HEAD), axis=1)

    count = width // ways
    if own_links:
        gain_part = both[count + 5, : count // 2]
    else:
        conv_state_sum = small[7, : 5 * BW].reshape(5, BW)
        gain_rows = jnp.sum(wb_shard[0] * w_gate_inner[0].astype(f32), axis=1) + jnp.sum(
            wa_shard * pack_a.astype(f32), axis=1
        )
        gain_own = gain_rows / lax.dynamic_slice_in_dim(norm_gain, lax.axis_index("dp") * count, count)
        near_s, far_s = halves(jnp.concatenate([wa_shard[:, units : units + BW], conv_state_sum], axis=0), 1)
        near_g, far_g = halves(gain_own, 0)
        far_all = jnp.concatenate([far_s.reshape(-1), far_g])
        got = swap(far_all)
        both = near_s + got[: far_s.size].reshape(far_s.shape)
        gain_part = near_g + got[far_s.size :]
        inner_grads = jnp.stack([wb_shard[0], wa_shard[:, :units]])
        step_grads = wa_shard[:, units + BW :]
    return (
        output,
        grad_residual,
        gain_part,
        inner_grads,
        both[:count],
        gathered_heads(step_grads, heads),
        small[0:5],
        both[count : count + 5],
        bias_sum,
        decay_sum,
        skip_sum,
        small[6],
        wb_shard[1].T,
    )


def solution(mesh):
    return jax.shard_map(
        on_device,
        mesh=mesh,
        in_specs=(
            P(("dp", "tensor"), None),
            P(),
            P(None, "dp", "tensor"),
            P("dp", None),
            P("dp", "tensor"),
            P(None, "tensor"),
            P(),
            P("tensor"),
            P("tensor"),
            P("tensor"),
            P("tensor"),
            P("tensor", "dp"),
            P(("dp", "tensor"), None),
        ),
        out_specs=(
            P(("dp", "tensor"), None),
            P(("dp", "tensor"), None),
            P(("dp", "tensor")),
            P(None, "dp", "tensor"),
            P("dp", "tensor"),
            P("dp", "tensor"),
            P(None, "tensor"),
            P(None, "tensor"),
            P("tensor"),
            P("tensor"),
            P("tensor"),
            P("tensor"),
            P("tensor", "dp"),
        ),
        check_vma=False,
    )
```

```python
import functools

import jax
import jax.numpy as jnp
from jax import lax
from jax.experimental import pallas as pl
from jax.experimental.pallas import tpu as pltpu
from jax.sharding import PartitionSpec as P

Q = 256
LEN = 1024
HEAD = 64
BW = 256
HB = BW // HEAD
LOG2E = 1.4426950408889634
FAR = -1e30
norm_eps = 1e-05
MESH = pl.DeviceIdType.MESH
f32 = jnp.float32
bf16 = jnp.bfloat16


def mm(a, b, ca=1, cb=0):
    return lax.dot_general(a, b, (((ca,), (cb,)), ((), ())), preferred_element_type=f32)


def sigmoid(v):
    return 1.0 / (1.0 + jnp.exp(-v))


def split3(a):
    hi = a.astype(bf16)
    rest = a - hi.astype(f32)
    mid = rest.astype(bf16)
    low = (rest - mid.astype(f32)).astype(bf16)
    return hi, mid, low


def split2(a):
    hi = a.astype(bf16)
    return hi, (a - hi.astype(f32)).astype(bf16)


def iota(shape, axis):
    return lax.broadcasted_iota(jnp.int32, shape, axis)


def expand(cols):
    rows = cols.shape[0]
    left = iota((rows, 128), 1) < HEAD
    return jnp.concatenate(
        [jnp.where(left, cols[:, 2 * q : 2 * q + 1], cols[:, 2 * q + 1 : 2 * q + 2]) for q in range(2)],
        axis=1,
    )


def conv_taps(window, kernel):
    out = kernel[4:5] + kernel[3:4] * window[8:]
    for k in range(3):
        out = out + kernel[k : k + 1] * pltpu.roll(window, 3 - k, 0)[8:]
    return out


def head_row(ref):
    return jnp.broadcast_to(ref[...][None, :], (8, ref.shape[0]))


def lay(rows, pick):
    parts = split3(rows)
    return mm(parts[0], pick) + mm(parts[1], pick) + mm(parts[2], pick)


def as_places(heads):
    lane = iota((heads, 128), 1)
    place = lane % 8
    return ((lane // 8 * HB + place == iota((heads, 128), 0)) & (place < HB)).astype(f32).astype(bf16)


def as_units(heads, block):
    return (iota((heads, BW), 1) // HEAD + HB * block == iota((heads, BW), 0)).astype(f32).astype(bf16)


def head_masks():
    lane = iota((1, BW), 1) // HEAD
    return [(lane == j).astype(f32).astype(bf16) for j in range(HB)]


def quads():
    for r in range(0, Q, 64):
        for half in range(2):
            if half * 128 <= r:
                yield r, half, r < half * 128 + 128


def decay_chunk(col, row, r, half, diag):
    gap = col[r : r + 64] - row[:, half * 128 : half * 128 + 128]
    if diag:
        keep = iota((64, 128), 0) + (r - half * 128) >= iota((64, 128), 1)
        gap = jnp.where(keep, gap, FAR)
    return jnp.exp2(gap)


def mixer_forward(links, normed, wi, wsx, kin, kst, bias, log_rate, skip_in, *refs):
    refs = list(refs)
    if links:
        sent = refs[:3] + refs[14:16]
        gain, gate_refs = refs[3], refs[16:19]
        refs = refs[4:14] + refs[19:]
    inner_out, ssd_out, states_out, cst_out, bc_out, step_out, cum_out, stepT_out, cumT_out, preT_out = refs[:10]
    buf, gram, colc, cols, rowp, mst, xst, state = refs[10:18]
    i = pl.program_id(0)
    tokens = normed.shape[0]
    spans = tokens // Q
    blocks = inner_out.shape[1] // BW
    if links:
        work = BesideForward(*sent, *refs[27:])
        ssd_v, *gate_scratch = refs[18:27]
        blocks = ssd_v.shape[0] - 1
    heads = bias.shape[0]
    skip = lay(head_row(skip_in), as_units(heads, i))[0:1]

    if links:
        pl.when(i == 0)(work.start)

    @pl.when(i == 0)
    def _():
        proj = mm(normed[...], wsx[...])
        buf[0:8] = jnp.zeros((8, BW), f32)
        cst_out[...] = proj[:, :BW]
        buf[8 : 8 + tokens] = proj[:, :BW]
        tri = (iota((Q, Q), 0) >= iota((Q, Q), 1)).astype(f32).astype(bf16)
        places = as_places(heads)
        pre = proj[:, BW:] + lay(head_row(bias), places)[0:1]
        step = jnp.maximum(pre, 0.0) + jnp.log1p(jnp.exp(-jnp.abs(pre)))
        step_out[...] = step
        scaled = step * (lay(-jnp.exp(head_row(log_rate)), places)[0:1] * LOG2E)
        for s in range(spans):
            parts = split3(scaled[s * Q : s * Q + Q])
            cum_out[s * Q : s * Q + Q] = mm(tri, parts[0]) + mm(tri, parts[1]) + mm(tri, parts[2])
            conv = conv_taps(buf[s * Q : s * Q + Q + 8], kst[...])
            bc = (conv * sigmoid(conv)).astype(bf16)
            bc_out[s * Q : s * Q + Q] = bc
            gram[s] = mm(bc[:, 128:], bc[:, :128], 1, 1)
        preT_out[...] = jnp.transpose(pre)[:48]
        stepT_out[...] = jnp.transpose(step)[:48]
        cumT_out[...] = jnp.transpose(cum_out[...])[:48]
        mst[...] = jnp.zeros(mst.shape, bf16)

    def mix():
        inner = mm(normed[...], wi[...])
        inner_out[...] = inner
        buf[8 : 8 + tokens] = inner
        turn = lax.rem(128 - 8 * i, 128)
        colc[...] = pltpu.roll(cum_out[...], turn, 1)
        cols[...] = pltpu.roll(step_out[...], turn, 1)
        rows8 = pl.ds(pl.multiple_of(8 * i, 8), 8)
        rowp[...] = cumT_out[rows8] - jnp.log2(stepT_out[rows8])
        state[...] = jnp.zeros(state.shape, f32)
        masks = head_masks()

        def span(s, carry):
            at = pl.multiple_of(s * Q, Q)
            rows = pl.ds(at, Q)
            conv = conv_taps(buf[pl.ds(at, Q + 8)], kin[...])
            xs = conv * sigmoid(conv)
            x_low = xs.astype(bf16)
            col = colc[rows]
            total = col[Q - 1 : Q]
            growth = expand(jnp.exp2(col[:, :8]))
            weight = expand(jnp.exp2(total[:, :8] - col[:, :8]) * cols[rows][:, :8])
            xw_low = (xs * weight).astype(bf16)
            for j in range(HB):
                xst[j * Q : j * Q + Q] = x_low * masks[j]
                row = rowp[j : j + 1, rows]
                for r, half, diag in quads():
                    part = gram[s, r : r + 64, half * 128 : half * 128 + 128]
                    dec = decay_chunk(col[:, j : j + 1], row, r, half, diag)
                    mst[r : r + 64, j * Q + half * 128 : j * Q + half * 128 + 128] = (part * dec).astype(bf16)
            intra = mm(mst[...], xst[...])
            state_in = state[...]
            states_out[s] = state_in
            bc = bc_out[rows]
            readout = mm(bc[:, 128:], state_in.astype(bf16), 1, 1)
            ssd = intra + growth * readout + skip * xs
            ssd_out[rows] = ssd
            if links:
                ssd_v[blocks, rows] = ssd
            local = mm(xw_low, bc[:, :128], 0, 0)
            fade = jnp.exp2(total)
            for j in range(HB):
                at_j = slice(j * HEAD, j * HEAD + HEAD)
                state[at_j] = fade[:, j : j + 1] * state_in[at_j] + local[at_j]
            if links:
                work.step(i * spans + s)
            return carry

        lax.fori_loop(0, spans, span, 0)

    if not links:
        mix()
        return
    pl.when(i < blocks)(mix)

    @pl.when(i < blocks)
    def _():
        ssd_v[i] = ssd_v[blocks]

    gates = GateForward(i - blocks, blocks, normed, sent[3], sent[4], gain, ssd_v, *gate_refs, *gate_scratch)

    @pl.when(i == blocks)
    def _():
        work.first()
        gates.start(0)


    pl.when((i >= blocks) & (i < 2 * blocks))(gates.gate)

    @pl.when(i == 2 * blocks)
    def _():
        work.finish()
        gates.start(1)

    pl.when(i >= 2 * blocks)(gates.pull)


class GateForward:
    def __init__(
        self, at, blocks, normed, cot, wb, gain, ssd_v, gate_out, ggo_out, stats_out, w_v, cot_v, sq, gi, mine, landed, wl, cl
    ):
        self.at, self.blocks, self.normed, self.cot, self.wb, self.gain, self.ssd_v = at, blocks, normed, cot, wb, gain, ssd_v
        self.gate_out, self.ggo_out, self.stats_out = gate_out, ggo_out, stats_out
        self.w_v, self.cot_v, self.sq, self.gi, self.mine, self.landed, self.wl, self.cl = w_v, cot_v, sq, gi, mine, landed, wl, cl

    def load(self, which, n):
        cols = slice((which * self.blocks + n) * BW, (which * self.blocks + n + 1) * BW)
        return pltpu.make_async_copy(self.wb.at[:, cols], self.w_v.at[n], self.wl.at[n])

    def tokens(self):
        return pltpu.make_async_copy(self.cot, self.cot_v, self.cl.at[0])

    def start(self, which):
        if not which:
            self.tokens().start()
        for n in range(self.blocks):
            self.load(which, n).start()
        if which:
            self.tokens().wait()
        total = self.gi if which else self.sq
        total[...] = jnp.zeros(total.shape, f32)

    def gate(self):
        b = self.at
        pltpu.make_async_copy(self.wb.at[:, :BW], self.w_v.at[b], self.wl.at[b]).wait()
        gate = mm(self.normed[...], self.w_v[b])
        self.gate_out[...] = gate
        gated = self.ssd_v[b] * (gate * sigmoid(gate))
        self.ssd_v[b] = gated
        squares = gated * gated
        self.sq[...] += squares[:, :128] + squares[:, 128:]

    def pull(self):
        b = self.at - self.blocks
        pltpu.make_async_copy(self.wb.at[:, :BW], self.w_v.at[b], self.wl.at[b]).wait()
        ggo = mm(self.cot_v[...], self.w_v[b])
        self.ggo_out[...] = ggo
        inner = ggo * self.gain[0:1] * self.ssd_v[b]
        self.gi[...] += inner[:, :128] + inner[:, 128:]
        pl.when(b == self.blocks - 1)(self.last)

    def last(self):
        self.mine[...] = token_sums(self.sq[...], self.gi[...])
        swap = remote(self.mine, self.landed, self.cl.at[1], self.cl.at[2], tensor=1 - lax.axis_index("tensor"))
        swap.start()
        swap.wait()
        self.stats_out[...] = self.mine[...] + self.landed[...]


def token_sums(sq, gi):
    lane = iota(sq.shape, 1)
    both = jnp.where(
        lane == 0,
        jnp.sum(sq, axis=1, keepdims=True),
        jnp.where(lane == 1, jnp.sum(gi, axis=1, keepdims=True), 0.0),
    )
    return jnp.transpose(both)[:8]


class BesideForward:
    def __init__(self, cot, w_gate_inner, w_output_t, cot_out, wb, ss, rs, ls, xs, xr, xl):
        self.here = Place()
        units = w_output_t.shape[1]
        self.moves = [
            Gather(self.here, own, wb, ss, rs, ls, n, slice(n * units, n * units + units))
            for n, own in enumerate((w_gate_inner.at[0], w_output_t))
        ]
        half = lax.axis_index("tensor")
        rows = cot.shape[0]
        slot = cot_out.at[pl.ds(pl.multiple_of(half * rows, rows), rows)]
        self.across = remote(cot, slot, xs, xr, tensor=1 - half)
        self.local = pltpu.make_async_copy(cot, slot, xl)

    def start(self):
        greet(self.here, True)
        for move in self.moves:
            move.start()
        self.across.start()
        self.local.start()

    def step(self, at):
        for when, chunk, hops in ((5, 0, 1), (9, 1, 1), (13, 0, 2), (16, 1, 2), (20, 0, 3), (23, 1, 3)):

            def go(move=self.moves[chunk], hops=hops):
                move.hop(hops)
                move.sides(hops - 1)

            pl.when(at == when)(go)

    def first(self):
        self.moves[0].sides(3)
        self.moves[0].finish()
        self.local.wait()
        self.across.wait()

    def finish(self):
        move = self.moves[1]
        move.sides(3)
        move.finish()


def gate_forward(normed, cot, wg, wo, ssd, gain, gate_out, ggo_out, stats_out, sq, gi):
    i = pl.program_id(0)

    @pl.when(i == 0)
    def _():
        sq[...] = jnp.zeros(sq.shape, f32)
        gi[...] = jnp.zeros(gi.shape, f32)

    gate = mm(normed[...], wg[...])
    gate_out[...] = gate
    ggo = mm(cot[...], wo[...])
    ggo_out[...] = ggo
    gated = ssd[...] * (gate * sigmoid(gate))
    squares = gated * gated
    sq[...] += squares[:, :128] + squares[:, 128:]
    inner = ggo * gain[0:1] * gated
    gi[...] += inner[:, :128] + inner[:, 128:]

    @pl.when(i == pl.num_programs(0) - 1)
    def _():
        stats_out[...] = token_sums(sq[...], gi[...])


def gate_backward(
    unit_total, stats, gate, ssd, ggo, gain, normed, cot, dy_out, dgate_out, ng_out, gg_out, grads_out, normed_t, cols, cot_t
):
    @pl.when(pl.program_id(0) == 0)
    def _():
        full = jnp.concatenate([stats[...], jnp.zeros((120, stats.shape[1]), f32)], axis=0)
        cols[...] = jnp.transpose(full)

        def turn(n, carry):
            here = pl.ds(pl.multiple_of(n * 128, 128), 128)
            normed_t[here] = jnp.transpose(normed[:, here])
            cot_t[here] = jnp.transpose(cot[:, here])
            return carry

        lax.fori_loop(0, normed.shape[1] // 128, turn, 0)

    rstd = lax.rsqrt(cols[:, 0:1] / unit_total + norm_eps)
    pull = rstd * rstd * rstd * (cols[:, 1:2] / unit_total)
    v = gate[...]
    sig = sigmoid(v)
    act = v * sig
    y = ssd[...]
    gated = y * act
    scaled = gated * rstd
    ng = (scaled * gain[0:1]).astype(bf16)
    ng_out[...] = ng
    grads_out[1] = mm(cot_t[...], ng).astype(bf16)
    gg = ggo[...]
    gg_out[...] = jnp.broadcast_to(jnp.sum(gg * scaled, axis=0, keepdims=True), gg_out.shape)
    grad = rstd * (gg * gain[0:1]) - gated * pull
    dy_out[...] = (grad * act).astype(bf16)
    dgate = (grad * y * (sig * (1.0 + v * (1.0 - sig)))).astype(bf16)
    dgate_out[...] = dgate
    grads_out[0] = mm(normed_t[...], dgate).astype(bf16)


class BesideBackward:
    def __init__(self, mixed, grads, far_out, shard_out, scratch):
        self.here = Place()
        half = lax.axis_index("tensor")
        rows = far_out.shape[0]
        other = mixed.at[pl.ds(pl.multiple_of((1 - half) * rows, rows), rows)]
        self.across = remote(other, far_out, scratch[0], scratch[1], tensor=1 - half)
        self.sum = Reduce(self.here, grads, shard_out, scratch[2:7], scratch[7:15])

    def start(self):
        greet(self.here, True)
        self.sum.start()
        self.across.start()

    def step(self, at):
        total = self.sum
        z = self.here.z
        ends = (z == 0) | (z == 3)
        for n, block in enumerate(total.order):
            pl.when(at == n)(lambda z=block: total.cores(z))
            pl.when(at == (4, 5, 7, 8)[n])(lambda z=block: total.stay(z))
            pl.when(at == (6, 11, 17, 22)[n])(lambda z=block: total.sides(z))
        for n, block in enumerate(total.order[:3]):
            when = jnp.where(ends, (6, 11, 17)[n], (12, 18, 19)[n])
            pl.when(at == when)(lambda z=block: total.pass_on(z))

    def finish(self):
        self.sum.finish()
        self.across.wait()


def mixer_backward(links, inner, dy, states, kin, kst, log_rate, skip_in, cst, bc_in, step_in, cum_in, stepT, cumT, preT, *refs):
    refs = list(refs)
    if links:
        beside = refs[:2] + refs[7:9]
        refs = refs[2:7] + refs[9:]
        work = BesideBackward(*beside, refs[24:])
    dinner_out, gk_out, dsd_out, gks_out, hs_out = refs[:5]
    buf, dbuf, gram, gg, gb, gc, colc, cols, rowp, mst, dyst, gmix, sgrad = refs[5:18]
    rs_t, cs_t, dr_t, wg_t, gt_t, gtaps = refs[18:24]
    i = pl.program_id(0)
    if links:
        pl.when(i == 0)(work.start)
    heads = log_rate.shape[0]
    skip = lay(head_row(skip_in), as_units(heads, i))[0:1]
    tokens = inner.shape[0]
    spans = tokens // Q
    masks = head_masks()

    @pl.when(i == 0)
    def _():
        buf[0:8] = jnp.zeros((8, BW), f32)
        dbuf[tokens : tokens + 8] = jnp.zeros((8, BW), f32)
        for s in range(spans):
            bc = bc_in[s * Q : s * Q + Q]
            gram[s] = mm(bc[:, 128:], bc[:, :128], 1, 1)
        for ref in (gg, gb, gc, rs_t, cs_t, dr_t, wg_t, gt_t):
            ref[...] = jnp.zeros(ref.shape, f32)
        mst[...] = jnp.zeros(mst.shape, bf16)

    buf[8 : 8 + tokens] = inner[...]
    turn = lax.rem(128 - 8 * i, 128)
    colc[...] = pltpu.roll(cum_in[...], turn, 1)
    cols[...] = pltpu.roll(step_in[...], turn, 1)
    rows8 = pl.ds(pl.multiple_of(8 * i, 8), 8)
    rowp[...] = cumT[rows8] - jnp.log2(stepT[rows8])
    sgrad[...] = jnp.zeros(sgrad.shape, f32)
    gtaps[...] = jnp.zeros(gtaps.shape, f32)
    pick = (iota((8, BW), 1) // HEAD == iota((8, BW), 0)).astype(f32).astype(bf16)

    def conv_rows(at, kernel, grad_act, conv, sig):
        gco = grad_act * (sig * (1.0 + conv * (1.0 - sig)))
        dbuf[pl.ds(at, Q)] = gco
        into = buf[pl.ds(pl.multiple_of(at + 8, 8), Q)]
        gtaps[4:5] += jnp.sum(gco, axis=0, keepdims=True)
        after = dbuf[pl.ds(at, Q + 8)]
        grad_in = kernel[3:4] * gco
        gtaps[3:4] += jnp.sum(gco * into, axis=0, keepdims=True)
        for k in range(3):
            later = pltpu.roll(after, Q + 8 - (3 - k), 0)[:Q]
            gtaps[k : k + 1] += jnp.sum(later * into, axis=0, keepdims=True)
            grad_in = grad_in + kernel[k : k + 1] * later
        return grad_in

    def span(back, carry):
        s = spans - 1 - back
        at = pl.multiple_of(s * Q, Q)
        rows = pl.ds(at, Q)
        conv = conv_taps(buf[pl.ds(at, Q + 8)], kin[...])
        sig = sigmoid(conv)
        xs = conv * sig
        x_low = xs.astype(bf16)
        dy_s = dy[rows]
        dy_f = dy_s.astype(f32)
        bc = bc_in[rows]
        b_low, c_low = bc[:, :128], bc[:, 128:]
        col = colc[rows]
        total = col[Q - 1 : Q]
        for j in range(HB):
            dyst[j * Q : j * Q + Q] = dy_s * masks[j]
        gmix[...] = mm(dyst[...], x_low, 1, 1)
        lane = iota((Q, 128), 1)
        row_sums = jnp.zeros((Q, 128), f32)
        for j in range(HB):
            row = rowp[j : j + 1, rows]
            col_sum = [jnp.zeros((1, 128), f32), jnp.zeros((1, 128), f32)]
            row_parts = []
            for r, half, diag in quads():
                here = slice(half * 128, half * 128 + 128)
                dec = decay_chunk(col[:, j : j + 1], row, r, half, diag)
                part = gram[s, r : r + 64, here]
                p = gmix[j * Q + r : j * Q + r + 64, here] * dec
                gg[s, r : r + 64, here] += p
                q = p * part
                mst[j * Q + r : j * Q + r + 64, here] = (part * dec).astype(bf16)
                col_sum[half] = col_sum[half] + jnp.sum(q, axis=0, keepdims=True)
                if half == 0:
                    row_parts.append(q)
                else:
                    row_parts[-1] = row_parts[-1] + q
            sums = jnp.concatenate([jnp.sum(q, axis=1, keepdims=True) for q in row_parts], axis=0)
            row_sums = jnp.where(lane == j, sums, row_sums)
            cs_t[pl.ds(8 * i + j, 1), rows] = jnp.concatenate(col_sum, axis=1)
        rs_t[rows8, rows] = jnp.transpose(row_sums)[:8]
        grad_xs = mm(mst[...], dyst[...], 0, 0) + skip * dy_f

        growth = expand(jnp.exp2(col[:, :8]))
        weight = expand(jnp.exp2(total[:, :8] - col[:, :8]) * cols[rows][:, :8])
        state_in = states[s]
        state_low = state_in.astype(bf16)
        state_grad = sgrad[...]
        carry_low = state_grad.astype(bf16)
        readout = mm(c_low, state_low, 1, 1)
        read_low = (dy_f * growth).astype(bf16)
        hi, low = split2(dy_f * readout)
        dr_t[rows8, rows] = mm(pick, hi, 1, 1) + mm(pick, low, 1, 1)
        gc[rows] += mm(read_low, state_low)
        grad_xw = mm(b_low, carry_low, 1, 1)
        xw_low = (xs * weight).astype(bf16)
        gb[rows] += mm(xw_low, carry_low)
        hi, low = split2(grad_xw * xs)
        wg_t[rows8, rows] = mm(pick, hi, 1, 1) + mm(pick, low, 1, 1)
        hi, low = split2(state_grad * state_in)
        sums = jnp.sum(mm(pick, hi) + mm(pick, low), axis=1, keepdims=True)
        gt_t[rows8] = jnp.where(iota((8, 128), 1) == s, sums, gt_t[rows8])
        grad_xs = grad_xs + grad_xw * weight
        local = mm(read_low, c_low, 0, 0)
        fade = jnp.exp2(total)
        for j in range(HB):
            at_j = slice(j * HEAD, j * HEAD + HEAD)
            sgrad[at_j] = fade[:, j : j + 1] * state_grad[at_j] + local[at_j]
        gtaps[5:6] += jnp.sum(dy_f * xs, axis=0, keepdims=True)
        dinner_out[rows] = conv_rows(at, kin[...], grad_xs, conv, sig).astype(bf16)
        if links:
            work.step(i * spans + back)
        return carry

    lax.fori_loop(0, spans, span, 0)
    gk_out[...] = gtaps[...]

    @pl.when(i == pl.num_programs(0) - 1)
    def _():
        buf[8 : 8 + tokens] = cst[...]
        gtaps[...] = jnp.zeros(gtaps.shape, f32)
        rates = lay(-jnp.exp(head_row(log_rate)), as_places(heads))[0:1]
        rate = jnp.transpose(jnp.broadcast_to(rates, (128, 128)))[:48, 0:1]
        later = (iota((Q, Q), 0) >= iota((Q, Q), 1)).astype(f32).astype(bf16)
        last = iota((48, Q), 1) == Q - 1
        bias_sum = jnp.zeros((48, 1), f32)
        decay_sum = jnp.zeros((48, 1), f32)
        for back in range(spans):
            s = spans - 1 - back
            rows = slice(s * Q, s * Q + Q)
            bc = bc_in[rows]
            gl = gg[s].astype(bf16)
            grad_c = gc[rows] + mm(gl, bc[:, :128])
            grad_b = gb[rows] + mm(gl, bc[:, 128:], 0, 0)
            both = jnp.concatenate([grad_b, grad_c], axis=1)
            conv = conv_taps(buf[s * Q : s * Q + Q + 8], kst[...])
            dsd_out[rows, :BW] = conv_rows(s * Q, kst[...], both, conv, sigmoid(conv)).astype(bf16)

            cum, step, pre = cumT[:, rows], stepT[:, rows], preT[:, rows]
            total = cum[:, Q - 1 : Q]
            rate_w = jnp.exp2(total - cum)
            wg = wg_t[:, rows]
            cs = cs_t[:, rows]
            moved = wg * (rate_w * step)
            grad_cum = rs_t[:, rows] - cs + jnp.exp2(cum) * dr_t[:, rows] - moved
            grad_total = jnp.exp2(total) * gt_t[:, s : s + 1] + jnp.sum(moved, axis=1, keepdims=True)
            grad_cum = grad_cum + jnp.where(last, grad_total, 0.0)
            parts = split3(grad_cum)
            grad_rate = mm(parts[0], later) + mm(parts[1], later) + mm(parts[2], later)
            sig = sigmoid(pre)
            ratio = jnp.where(pre < -15.0, 1.0, sig / step)
            grad_pre = (wg * rate_w + grad_rate * rate) * sig + cs * ratio
            bias_sum = bias_sum + jnp.sum(grad_pre, axis=1, keepdims=True)
            decay_sum = decay_sum + jnp.sum(grad_rate * step, axis=1, keepdims=True)
            full = jnp.concatenate([grad_pre, jnp.zeros((80, Q), f32)], axis=0)
            dsd_out[rows, BW:] = jnp.transpose(full).astype(bf16)
        gks_out[...] = gtaps[...]
        lane = iota((48, 128), 1)
        both = jnp.where(lane == 0, bias_sum, jnp.where(lane == 1, decay_sum * rate, 0.0))
        hs_out[...] = jnp.transpose(jnp.concatenate([both, jnp.zeros((80, 128), f32)], axis=0))[:8]
        if links:
            work.finish()


class Place:
    def __init__(self):
        me = lax.axis_index("dp")
        self.me = me
        self.c, self.y, self.z = me % 2, (me // 2) % 2, me // 4

    def at(self, z, y, c):
        return (z * 2 + y) * 2 + c

    def core(self):
        return self.at(self.z, self.y, 1 - self.c)

    def side(self):
        return self.at(self.z, 1 - self.y, self.c)

    def up(self):
        return self.me + 4

    def down(self):
        return self.me - 4


def greet(here, across):
    barrier = pltpu.get_barrier_semaphore()

    def signal(**device):
        pl.semaphore_signal(barrier, 1, device_id=device, device_id_type=MESH)

    signal(dp=here.core())
    signal(dp=here.side())
    pl.when(here.z < 3)(lambda: signal(dp=here.up()))
    pl.when(here.z > 0)(lambda: signal(dp=here.down()))
    if across:
        signal(tensor=1 - lax.axis_index("tensor"))
    ends = (here.z == 0).astype(jnp.int32) + (here.z == 3).astype(jnp.int32)
    pl.semaphore_wait(barrier, 4 + int(across) - ends)


def remote(src, dst, send_sem, recv_sem, **device):
    return pltpu.make_async_remote_copy(
        src_ref=src, dst_ref=dst, send_sem=send_sem, recv_sem=recv_sem, device_id=device, device_id_type=MESH
    )


class Gather:
    def __init__(self, here, own, full, ss, rs, ls, chunk, cols):
        self.here, self.full, self.ss, self.rs, self.chunk, self.cols = here, full, ss, rs, chunk, cols
        self.rows = own.shape[0]
        self.own = own
        self.lift = chunk == 0
        self.local = pltpu.make_async_copy(own, self.slot(here.me), ls.at[chunk])

    def slot(self, origin):
        return self.full.at[pl.ds(pl.multiple_of(origin * self.rows, self.rows), self.rows), self.cols]

    def copy(self, origin, way, src=None):
        here = self.here
        target = (here.up, here.down, here.side, here.core)[way]()
        slot = self.slot(origin)
        sems = self.ss.at[self.chunk, origin, way], self.rs.at[self.chunk, origin]
        return remote(slot if src is None else src, slot, *sems, dp=target)

    def arrived(self, origin):
        self.copy(origin, 3).wait_recv()

    def ways(self, hops):
        z = self.here.z
        return ((0, z),) if hops == 0 else ((0, z - hops), (1, z + hops))

    def onward(self, way):
        return (self.here.z < 3) if way == 0 else (self.here.z > 0)

    def own_sends(self, hops, way, origin_z, act):
        here = self.here
        origin = here.at(origin_z, here.y, here.c)
        for along in (0, 1) if hops == 0 else (way,):
            pl.when(self.onward(along))(lambda along=along: act(origin, along))
        if hops and self.lift:
            pl.when((origin_z != 0) & (origin_z != 3))(lambda: act(origin, 2))
        else:
            act(origin, 2)
        act(origin, 3)

    def side_sends(self, hops, way, origin_z, act):
        here = self.here
        origin = here.at(origin_z, 1 - here.y, here.c)
        act(origin, 3)
        if self.lift and hops == 0:
            pl.when(here.z == 0)(lambda: act(origin, 0))
            pl.when(here.z == 3)(lambda: act(origin, 1))
        elif self.lift:
            pl.when((origin_z == 3 * way) & self.onward(way))(lambda: act(origin, way))

    def each(self, hops, act):
        for way, origin_z in self.ways(hops):
            if hops == 0:
                act(way, origin_z)
            else:
                pl.when((origin_z >= 0) & (origin_z <= 3))(lambda way=way, origin_z=origin_z: act(way, origin_z))

    def send(self, origin, way):
        self.copy(origin, way).start()

    def start(self):
        self.own_sends(0, 0, self.here.z, lambda origin, way: self.copy(origin, way, self.own).start())
        self.local.start()

    def hop(self, hops):
        def go(way, origin_z):
            self.arrived(self.here.at(origin_z, self.here.y, self.here.c))
            self.own_sends(hops, way, origin_z, self.send)

        self.each(hops, go)

    def sides(self, hops):
        def go(way, origin_z):
            self.arrived(self.here.at(origin_z, 1 - self.here.y, self.here.c))
            self.side_sends(hops, way, origin_z, self.send)

        self.each(hops, go)

    def finish(self):
        here = self.here
        self.local.wait()
        for z in range(4):
            for y in range(2):
                self.arrived(here.at(z, y, 1 - here.c))

        def sent(origin, way):
            self.copy(origin, way).wait_send()

        for hops in range(4):

            def go(way, origin_z, hops=hops):
                self.own_sends(hops, way, origin_z, sent)
                self.side_sends(hops, way, origin_z, sent)

            self.each(hops, go)


def gather_scratch():
    sem = pltpu.SemaphoreType.DMA
    return [sem((2, 16, 4)), sem((2, 16)), sem((2,))]


def gather_kernel(tokens_in, gain, w_gate_inner, w_state_io, w_step, tokens_out, full, pack, low, ss, rs, ls, xs, xr, xl):
    here = Place()
    half = lax.axis_index("tensor")
    rows = tokens_in.shape[0]
    units, cols = w_gate_inner.shape[2], full.shape[1]
    pack[:, :units] = w_gate_inner[1]
    pack[:, units : units + BW] = w_state_io[...]
    pack[:, units + BW :] = mm(w_step[...], as_places(w_step.shape[1])).astype(bf16)
    greet(here, True)
    cut = cols // 256 * 128
    moves = [
        Gather(here, pack.at[:, c], full, ss, rs, ls, n, c) for n, c in enumerate((slice(0, cut), slice(cut, cols)))
    ]
    for move in moves:
        move.start()
    part = rows // 4
    across, local = [], []
    for n in range(4):
        piece = slice(n * part, n * part + part)
        v = tokens_in[piece].astype(f32)
        scale = lax.rsqrt(jnp.mean(v * v, axis=1, keepdims=True) + norm_eps)
        low[piece] = (v * scale * gain[0:1]).astype(bf16)
        slot = tokens_out.at[pl.ds(pl.multiple_of(half * rows + n * part, part), part)]
        across.append(remote(low.at[piece], slot, xs.at[n], xr.at[n], tensor=1 - half))
        across[-1].start()
        local.append(pltpu.make_async_copy(low.at[piece], slot, xl.at[n]))
        local[-1].start()
    for hops in range(1, 5):
        for move in moves:
            if hops < 4:
                move.hop(hops)
            move.sides(hops - 1)
    for n in range(4):
        local[n].wait()
        across[n].wait()
    for move in moves:
        move.finish()


def gather_rows(tokens_in, gain, w_gate_inner, w_state_io, w_step, ways, collective_id):
    rows, width = tokens_in.shape
    _, own, units = w_gate_inner.shape
    cols = units + BW + 128
    vmem = pl.BlockSpec(memory_space=pltpu.VMEM)
    hbm = pl.BlockSpec(memory_space=pl.ANY)
    sem = pltpu.SemaphoreType.DMA
    return pl.pallas_call(
        gather_kernel,
        name="gather_rows",
        in_specs=[vmem] * 5,
        out_specs=[hbm, hbm],
        out_shape=[sds((2 * rows, width), bf16), sds((ways * own, cols), bf16)],
        scratch_shapes=[
            pltpu.VMEM((own, cols), bf16), pltpu.VMEM((rows, width), bf16), *gather_scratch(),
            sem((4,)), sem((4,)), sem((4,)),
        ],
        compiler_params=pltpu.CompilerParams(
            collective_id=collective_id, has_side_effects=True, vmem_limit_bytes=60 * 1024 * 1024
        ),
    )(tokens_in, gain, w_gate_inner, w_state_io, w_step)


class Reduce:
    def __init__(self, here, grads, out, bufs, sems):
        self.here, self.grads, self.out = here, grads, out
        self.held, self.buf_a, self.buf_b, self.buf_up, self.buf_dn = bufs
        self.local, self.send_a, self.recv_a, self.send_b, self.recv_b, self.send_c, self.recv_up, self.recv_dn = sems
        self.parts, self.rows = out.shape[:2]
        z = here.z
        self.order = (3 * (1 - z // 2), (3 * z + 2) % 5, 1 + z % 2, z)

    def spot(self, z, y, c):
        if self.grads is None:
            return z, (y * 2 + c) * self.rows
        return z * 2 + y, 0

    def own(self, z, y, c=None):
        at, base = self.spot(z, y, self.here.c if c is None else c)
        return self.held.at[at, :, pl.ds(pl.multiple_of(base, 16), self.rows)]

    def block(self, z, y, c):
        if self.grads is None:
            return self.own(z, y, c)
        at = pl.multiple_of(self.here.at(z, y, c) * self.rows, self.rows)
        return self.grads.at[:, pl.ds(at, self.rows)]

    def copy_a(self, z, y):
        here, at = self.here, z * 2 + y
        return remote(self.block(z, y, 1 - here.c), self.buf_a.at[at], self.send_a.at[at], self.recv_a.at[at], dp=here.core())

    def take(self, z, y):
        return pltpu.make_async_copy(self.block(z, y, self.here.c), self.own(z, y), self.local.at[z * 2 + y])

    def copy_b(self, z):
        here = self.here
        return remote(self.own(z, 1 - here.y), self.buf_b.at[z], self.send_b.at[z], self.recv_b.at[z], dp=here.side())

    def copy_up(self, z):
        return remote(self.own(z, self.here.y), self.buf_up.at[z], self.send_c.at[z], self.recv_up.at[z], dp=self.here.up())

    def copy_dn(self, z):
        return remote(self.own(z, self.here.y), self.buf_dn.at[z], self.send_c.at[z], self.recv_dn.at[z], dp=self.here.down())

    def add(self, z, y, buf, slot):
        at, base = self.spot(z, y, self.here.c)

        def rows(n, carry):
            piece = pl.ds(pl.multiple_of(n * 16, 16), 16)
            held = pl.ds(pl.multiple_of(base + n * 16, 16), 16)
            for part in range(self.parts):
                total = self.held[at, part, held].astype(f32) + buf[slot, part, piece].astype(f32)
                self.held[at, part, held] = total.astype(bf16)
            return carry

        lax.fori_loop(0, self.rows // 16, rows, 0)

    def start(self):
        here = self.here
        for side in (1 - here.y, here.y):
            for z in self.order:
                self.copy_a(z, side).start()
                self.take(z, side).start()

    def join(self, z, y):
        if self.grads is not None:
            self.take(z, y).wait()
        self.copy_a(z, y).wait_recv()
        self.add(z, y, self.buf_a, z * 2 + y)

    def cores(self, z):
        self.join(z, 1 - self.here.y)
        self.copy_b(z).start()

    def stay(self, z):
        self.join(z, self.here.y)

    def sides(self, z):
        self.copy_b(z).wait_recv()
        self.add(z, self.here.y, self.buf_b, z)

    def pass_on(self, z):
        here = self.here

        def up():
            def below():
                self.copy_up(z).wait_recv()
                self.add(z, here.y, self.buf_up, z)

            pl.when(here.z > 0)(below)
            self.copy_up(z).start()

        def down():
            def above():
                self.copy_dn(z).wait_recv()
                self.add(z, here.y, self.buf_dn, z)

            pl.when(here.z < 3)(above)
            self.copy_dn(z).start()

        pl.when(z > here.z)(up)
        pl.when(z < here.z)(down)

    def finish(self):
        here = self.here
        z = here.z
        at, base = self.spot(z, here.y, here.c)
        pl.when(z > 0)(lambda: self.copy_up(z).wait_recv())
        pl.when(z < 3)(lambda: self.copy_dn(z).wait_recv())

        def rows(n, carry):
            piece = pl.ds(pl.multiple_of(n * 16, 16), 16)
            held = pl.ds(pl.multiple_of(base + n * 16, 16), 16)
            for part in range(self.parts):
                below = jnp.where(z > 0, self.buf_up[z, part, piece].astype(f32), 0.0)
                above = jnp.where(z < 3, self.buf_dn[z, part, piece].astype(f32), 0.0)
                self.out[part, piece] = self.held[at, part, held].astype(f32) + below + above
            return carry

        lax.fori_loop(0, self.rows // 16, rows, 0)
        for zn in self.order:
            self.copy_a(zn, 0).wait_send()
            self.copy_a(zn, 1).wait_send()
            self.copy_b(zn).wait_send()
            pl.when(zn > z)(lambda zn=zn: self.copy_up(zn).wait_send())
            pl.when(zn < z)(lambda zn=zn: self.copy_dn(zn).wait_send())


def reduce_scratch(parts, rows, cols, by_z=False):
    sem = pltpu.SemaphoreType.DMA
    block = (parts, rows, cols)
    held = (4, parts, 4 * rows, cols) if by_z else (8,) + block
    return [
        pltpu.VMEM(held, bf16), pltpu.VMEM((8,) + block, bf16), pltpu.VMEM((4,) + block, bf16),
        pltpu.VMEM((4,) + block, bf16), pltpu.VMEM((4,) + block, bf16),
        sem((8,)), sem((8,)), sem((8,)), sem((4,)), sem((4,)), sem((4,)), sem((4,)), sem((4,)),
    ]


def tail_kernel(
    normed_t, dinner, dsd, dgate, wb, wa, gk, ggg, gks, hs, norm_gain, w_gate_inner, w_state_io, w_step, gate_grads,
    gn_out, inner_out, step_out, both_out, small_out, shard_out, give, got, send_g, recv_g, nt_v, dinner_v, dsd_v, dgate_v, wg_v, wa_v, away, came, total, landed, loads, send_x, recv_x, send, recv, *scratch,
):
    here = Place()
    half = lax.axis_index("tensor")
    units = dgate.shape[1]
    sources = (normed_t, dinner, dsd, dgate, wb.at[:, :units], wa)
    pending = [
        pltpu.make_async_copy(src, dst, loads.at[n])
        for n, (src, dst) in enumerate(zip(sources, (nt_v, dinner_v, dsd_v, dgate_v, wg_v, wa_v)))
    ]
    for copy in pending:
        copy.start()
    far = pltpu.get_barrier_semaphore()
    partners = [here.me + bit - 2 * bit * ((here.me // bit) % 2) for bit in (2, 4, 8, 1)]
    for partner in partners:
        pl.semaphore_signal(far, 1, device_id={"dp": partner}, device_id_type=MESH)
    pl.semaphore_signal(far, 1, device_id={"tensor": 1 - half}, device_id_type=MESH)
    middle = (here.z == 1) | (here.z == 2)
    pl.when(here.z == 1)(lambda: pl.semaphore_signal(far, 1, device_id={"dp": here.up()}, device_id_type=MESH))
    pl.when(here.z == 2)(lambda: pl.semaphore_signal(far, 1, device_id={"dp": here.down()}, device_id_type=MESH))
    pl.semaphore_wait(far, 5 + middle.astype(jnp.int32))
    work = Reduce(here, None, shard_out, scratch[:5], scratch[5:])
    order = work.order
    rows = gn_out.shape[0]
    chunks, _, wide = away.shape

    def swap(k):
        return remote(total.at[k], landed.at[k], send.at[k], recv.at[k], dp=partners[k])

    def swapped(k):
        swap(k).wait()
        total[k + 1] = total[k] + landed[k]
        if k < 3:
            swap(k + 1).start()

    def across(n):
        return remote(away.at[n], came.at[n], send_x.at[n], recv_x.at[n], tensor=1 - half)

    def pulled(which, n):
        mine = pl.ds(pl.multiple_of(which * rows, rows), rows)
        at = pl.ds(pl.multiple_of(n * wide, wide), wide)
        return (
            mm(dgate_v[mine], wg_v[at], 1, 1)
            + mm(dinner_v[mine], wa_v[at, :units], 1, 1)
            + mm(dsd_v[mine], wa_v[at, units:], 1, 1)
        )

    def far_chunk(n, carry):
        away[n] = pulled(1 - half, n).astype(bf16)
        across(n).start()
        return carry

    def near_chunk(n, carry):
        gn_out[:, pl.ds(pl.multiple_of(n * wide, wide), wide)] = pulled(half, n)
        return carry

    def grads(n, carry):
        z = jnp.where(n == 0, order[0], jnp.where(n == 1, order[1], jnp.where(n == 2, order[2], order[3])))
        count = 4 * work.rows
        left = nt_v[pl.ds(pl.multiple_of(z * count, count), count)]
        work.held[z, 0, :, :units] = mm(left, dinner_v[...]).astype(bf16)
        work.held[z, 0, :, units:] = mm(left, dsd_v[...]).astype(bf16)
        work.copy_a(z, 1 - here.y).start()
        work.copy_a(z, here.y).start()

        @pl.when(n == 0)
        def _():
            for copy in pending[3:]:
                copy.wait()

        far_chunk(n, carry)
        work.cores(z)
        return carry

    total[0, 0:6] = gk[0:6]
    total[0, 6:7] = ggg[0:1]
    for k in range(5):
        total[0, 7:8, k * BW : k * BW + BW] = gks[k : k + 1]
    for k in range(2):
        total[0, 7:8, 5 * BW + k * 128 : 5 * BW + k * 128 + 128] = hs[k : k + 1]
    swap(0).start()
    for copy in pending[:3]:
        copy.wait()
    swapped(0)
    lax.fori_loop(0, 4, grads, 0)
    swapped(1)
    work.stay(order[0])
    work.sides(order[0])
    pl.when(~middle)(lambda: work.pass_on(order[0]))
    lax.fori_loop(4, chunks, far_chunk, 0)
    swapped(2)
    for n in range(1, 4):
        work.stay(order[n])
    work.sides(order[1])
    pl.when(~middle)(lambda: work.pass_on(order[1]))
    lax.fori_loop(0, 3, near_chunk, 0)
    pl.when(middle)(lambda: work.pass_on(order[0]))
    work.sides(order[2])
    pl.when(~middle)(lambda: work.pass_on(order[2]))
    lax.fori_loop(3, chunks, near_chunk, 0)
    swapped(3)
    small_out[...] = total[4]
    pl.when(middle)(lambda: work.pass_on(order[1]))
    work.sides(order[3])
    pl.when(middle)(lambda: work.pass_on(order[2]))
    work.finish()

    def arrive(n, carry):
        across(n).wait()
        at = pl.ds(pl.multiple_of(n * wide, wide), wide)
        gn_out[:, at] = gn_out[:, at] + came[n].astype(f32)
        return carry

    inner_out[0] = gate_grads[0]
    inner_out[1] = shard_out[0, :, :units]
    step_out[...] = shard_out[0, :, units + BW :]
    count = work.rows
    part = shard_out[0, :, units + BW :] * mm(w_step[...], as_places(w_step.shape[1]))
    for c in range(2):
        at = slice(units + c * 128, units + c * 128 + 128)
        part = part + shard_out[0, :, at] * w_state_io[:, c * 128 : c * 128 + 128].astype(f32)
    for c in range(units // 128):
        at = slice(c * 128, c * 128 + 128)
        part = part + gate_grads[0, :, at] * w_gate_inner[0, :, at].astype(f32)
        part = part + shard_out[0, :, at] * w_gate_inner[1, :, at].astype(f32)
    part = jnp.concatenate([part, jnp.zeros((128 - count, 128), f32)], axis=0)
    row = jnp.sum(jnp.transpose(part), axis=0, keepdims=True)
    shape = (norm_gain.shape[1], 128)
    pick = (iota(shape, 0) == iota(shape, 1) + here.me * count) & (iota(shape, 1) < count)
    gain = lay(norm_gain[...], pick.astype(f32).astype(bf16))[0:1]
    row = row / jnp.where(iota((1, 128), 1) < count, gain, 1.0)
    low = pltpu.roll(row, 128 - count // 2, 1)
    first = half == 0

    def share(at, a, b):
        both_out[at] = jnp.where(first, a, b)
        give[at] = jnp.where(first, b, a)

    share(slice(0, count), shard_out[0, :, units : units + 128], shard_out[0, :, units + 128 : units + 256])
    for k in range(5):
        pair = [small_out[7:8, k * BW + c * 128 : k * BW + c * 128 + 128] for c in range(2)]
        share(slice(count + k, count + k + 1), *pair)
    share(slice(count + 5, count + 6), row, low)
    share(slice(count + 6, count + 8), jnp.zeros((2, 128), f32), jnp.zeros((2, 128), f32))
    last = remote(give, got, send_g, recv_g, tensor=1 - half)
    last.start()
    lax.fori_loop(0, chunks, arrive, 0)
    last.wait()
    both_out[...] = both_out[...] + got[...]


def reduce_tail(normed_t, dinner, dsd, dgate, wb, wa, sums, weights, ways, collective_id):
    width, tokens = normed_t.shape
    small = sums[0]
    units, cols, rows = dgate.shape[1], wa.shape[1], width // ways
    chunks = width // BW
    vmem = pl.BlockSpec(memory_space=pltpu.VMEM)
    hbm = pl.BlockSpec(memory_space=pl.ANY)
    sem = pltpu.SemaphoreType.DMA
    return pl.pallas_call(
        tail_kernel, name="tail", in_specs=[hbm] * 6 + [vmem] * 9, out_specs=[vmem] * 5,
        out_shape=[
            sds((tokens // 2, width)), sds((2, rows, units)), sds((rows, 128)), sds((rows + 8, 128)), sds(small.shape),
        ],
        scratch_shapes=[
            pltpu.VMEM((1, rows, cols), f32), pltpu.VMEM((rows + 8, 128), f32), pltpu.VMEM((rows + 8, 128), f32), sem, sem,
            pltpu.VMEM(normed_t.shape, bf16), pltpu.VMEM(dinner.shape, bf16), pltpu.VMEM(dsd.shape, bf16),
            pltpu.VMEM(dgate.shape, bf16), pltpu.VMEM((width, units), bf16), pltpu.VMEM(wa.shape, bf16),
            pltpu.VMEM((chunks, tokens // 2, BW), bf16), pltpu.VMEM((chunks, tokens // 2, BW), bf16),
            pltpu.VMEM((5,) + small.shape, f32), pltpu.VMEM((4,) + small.shape, f32),
            sem((6,)), sem((chunks,)), sem((chunks,)), sem((4,)), sem((4,)),
        ] + reduce_scratch(1, rows, cols, True),
        compiler_params=pltpu.CompilerParams(
            collective_id=collective_id, has_side_effects=True, vmem_limit_bytes=62 * 1024 * 1024
        ),
    )(normed_t, dinner, dsd, dgate, wb, wa, *sums, *weights)


def swap(v):
    return lax.ppermute(v, "tensor", [(0, 1), (1, 0)])


def halves(v, axis):
    size = v.shape[axis] // 2
    me = lax.axis_index("tensor")
    return (
        lax.dynamic_slice_in_dim(v, me * size, size, axis),
        lax.dynamic_slice_in_dim(v, (1 - me) * size, size, axis),
    )


def once(shape, at=None):
    where = at or (0,) * len(shape)
    return pl.BlockSpec(shape, lambda i: where, pipeline_mode=pl.Buffered(1))


def by_cols(rows, offset=0):
    return pl.BlockSpec((rows, BW), lambda i: (0, i + offset))


def params(collective_id=None):
    return pltpu.CompilerParams(
        dimension_semantics=("arbitrary",), vmem_limit_bytes=60 * 1024 * 1024,
        collective_id=collective_id, has_side_effects=collective_id is not None,
    )


def spread(v):
    lead = v.shape[:-1]
    v = v.reshape(lead + (v.shape[-1] // HB, HB))
    v = jnp.pad(v, [(0, 0)] * len(lead) + [(0, 0), (0, 8 - HB)]).reshape(lead + (-1,))
    return jnp.pad(v, [(0, 0)] * len(lead) + [(0, 128 - v.shape[-1])])


def gathered_heads(v, heads):
    return v[..., : heads * 2].reshape(v.shape[:-1] + (heads // HB, 8))[..., :HB].reshape(v.shape[:-1] + (heads,))


def sds(shape, dtype=f32):
    return jax.ShapeDtypeStruct(shape, dtype)


def on_device(
    residual, norm_gain, w_gate_inner, w_state_io, w_step, conv_inner, conv_state,
    step_bias, decay_log, skip_gain, gate_gain, w_output, cotangent,
):
    width = residual.shape[1]
    units = w_gate_inner.shape[2]
    heads = w_step.shape[1]
    blocks = units // BW
    unit_total = units * lax.axis_size("tensor")
    ways = lax.axis_size("dp")
    own_links = ways == 16
    rows_in = residual.astype(f32)
    rstd_in = lax.rsqrt(jnp.mean(rows_in * rows_in, axis=1, keepdims=True) + norm_eps)
    scaled = rows_in * rstd_in
    pack_a = jnp.concatenate([w_gate_inner[1], w_state_io, spread(w_step)], axis=1)
    w_output_t = w_output.T
    gain_in = jnp.broadcast_to(norm_gain[None], (8, width))
    if own_links:
        normed, wa = gather_rows(residual, gain_in, w_gate_inner, w_state_io, w_step, ways, 1)
    else:
        wa = lax.all_gather(pack_a, "dp", axis=0, tiled=True)
        normed = lax.all_gather((scaled * norm_gain).astype(bf16), "tensor", axis=0, tiled=True)
    tokens = normed.shape[0]
    spans = tokens // Q
    gain8 = jnp.broadcast_to(gate_gain[None], (8, units))

    hbm = pl.BlockSpec(memory_space=pl.ANY)
    sem = pltpu.SemaphoreType.DMA
    def stage(rows, first):
        return pl.BlockSpec((rows, BW), lambda i: (0, jnp.clip(i - first, 0, blocks - 1)))

    inner, ssd, states, cst, bc, step, cum, step_t, cum_t, pre_t, *sent = pl.pallas_call(
        functools.partial(mixer_forward, own_links),
        name="mixer_forward",
        grid=(blocks * (3 if own_links else 1),),
        in_specs=[
            once((tokens, width)), stage(width, 0), once((width, 384), (0, units // 384)),
            stage(5, 0), once((5, BW)), once((heads,)), once((heads,)), once((heads,)),
        ] + ([once(v.shape) for v in (cotangent, w_gate_inner, w_output_t)] + [stage(8, 2 * blocks)]) * own_links,
        out_specs=[
            stage(tokens, 0), stage(tokens, 0), pl.BlockSpec((spans, BW, 128), lambda i: (0, jnp.clip(i, 0, blocks - 1), 0)),
            once((tokens, BW)), once((tokens, BW)), once((tokens, 128)), once((tokens, 128)),
            once((48, tokens)), once((48, tokens)), once((48, tokens)),
        ] + [hbm, hbm, stage(tokens, blocks), stage(tokens, 2 * blocks), once((8, tokens))] * own_links,
        out_shape=[
            sds((tokens, units)), sds((tokens, units)), sds((spans, units, 128)),
            sds((tokens, BW)), sds((tokens, BW), bf16), sds((tokens, 128)), sds((tokens, 128)),
            sds((48, tokens)), sds((48, tokens)), sds((48, tokens)),
        ] + [
            sds((tokens, width), bf16), sds((width, 2 * units), bf16), sds((tokens, units)), sds((tokens, units)),
            sds((8, tokens)),
        ] * own_links,
        scratch_shapes=[
            pltpu.VMEM((tokens + 8, BW), f32), pltpu.VMEM((spans, Q, Q), f32),
            pltpu.VMEM((tokens, 128), f32), pltpu.VMEM((tokens, 128), f32), pltpu.VMEM((8, tokens), f32),
            pltpu.VMEM((Q, HB * Q), bf16), pltpu.VMEM((HB * Q, BW), bf16), pltpu.VMEM((BW, 128), f32),
        ] + ([
            pltpu.VMEM((blocks + 1, tokens, BW), f32), pltpu.VMEM((blocks, width, BW), bf16), pltpu.VMEM((tokens, width), bf16),
            pltpu.VMEM((tokens, 128), f32), pltpu.VMEM((tokens, 128), f32), pltpu.VMEM((8, tokens), f32),
            pltpu.VMEM((8, tokens), f32), sem((blocks,)), sem((3,)),
        ] + gather_scratch() + [sem, sem, sem]) * own_links,
        compiler_params=params(2 if own_links else None),
        cost_estimate=pl.CostEstimate(flops=2 * tokens * width * (units + 384) + 4 * tokens * 256 * units, bytes_accessed=30_000_000, transcendentals=heads * spans * Q * Q),
    )(
        normed, wa, wa, conv_inner, conv_state, step_bias, decay_log, skip_gain,
        *[cotangent, w_gate_inner, w_output_t, gain8] * own_links,
    )

    if own_links:
        cot, wb, gate, ggo, stats = sent
    else:
        wb = lax.all_gather(jnp.concatenate([w_gate_inner[0], w_output_t], axis=1), "dp", axis=0, tiled=True)
        cot = lax.all_gather(cotangent, "tensor", axis=0, tiled=True)
        gate, ggo, stats = pl.pallas_call(
            gate_forward,
            name="gate_forward",
            grid=(blocks,),
            in_specs=[
                once((tokens, width)), once((tokens, width)), by_cols(width), by_cols(width, blocks),
                by_cols(tokens), by_cols(8),
            ],
            out_specs=[by_cols(tokens), by_cols(tokens), once((8, tokens))],
            out_shape=[sds((tokens, units)), sds((tokens, units)), sds((8, tokens))],
            scratch_shapes=[pltpu.VMEM((tokens, 128), f32), pltpu.VMEM((tokens, 128), f32)],
            compiler_params=params(),
            cost_estimate=pl.CostEstimate(flops=4 * tokens * width * units, bytes_accessed=35_000_000, transcendentals=tokens * units),
        )(normed, cot, wb, wb, ssd, gain8)
        stats = stats + swap(stats)

    dy, dgate, ng, ggg, grad_b, normed_t = pl.pallas_call(
        functools.partial(gate_backward, float(unit_total)),
        name="gate_backward",
        grid=(blocks,),
        in_specs=[
            once((8, tokens)), by_cols(tokens), by_cols(tokens), by_cols(tokens), by_cols(8),
            once((tokens, width)), once((tokens, width)),
        ],
        out_specs=[
            by_cols(tokens), by_cols(tokens), by_cols(tokens), by_cols(8),
            pl.BlockSpec((2, width, BW), lambda i: (0, 0, i)), once((width, tokens)),
        ],
        out_shape=[
            sds((tokens, units), bf16), sds((tokens, units), bf16), sds((tokens, units), bf16), sds((8, units)),
            sds((2, width, units), bf16), sds((width, tokens), bf16),
        ],
        scratch_shapes=[pltpu.VMEM((tokens, 128), f32), pltpu.VMEM((width, tokens), bf16)],
        compiler_params=params(),
        cost_estimate=pl.CostEstimate(flops=4 * tokens * units * width, bytes_accessed=45_000_000, transcendentals=tokens * units),
    )(stats, gate, ssd, ggo, gain8, normed, cot)

    mixed = mm(ng, wb[:, units:], 1, 1).astype(bf16)
    mixed_near, mixed_far = halves(mixed, 0)

    dinner, gk, dsd, gks, hs, *sent = pl.pallas_call(
        functools.partial(mixer_backward, own_links),
        name="mixer_backward",
        grid=(blocks,),
        in_specs=[
            by_cols(tokens), by_cols(tokens), pl.BlockSpec((spans, BW, 128), lambda i: (0, i, 0)),
            by_cols(5), once((5, BW)), once((heads,)), once((heads,)),
            once((tokens, BW)), once((tokens, BW)), once((tokens, 128)), once((tokens, 128)),
            once((48, tokens)), once((48, tokens)), once((48, tokens)),
        ] + [hbm, hbm] * own_links,
        out_specs=[by_cols(tokens), by_cols(8), once((tokens, 384)), once((8, BW)), once((8, 128))]
        + [hbm, once((2, width // ways, units))] * own_links,
        out_shape=[sds((tokens, units), bf16), sds((8, units)), sds((tokens, 384), bf16), sds((8, BW)), sds((8, 128))]
        + [sds((tokens // 2, width), bf16), sds((2, width // ways, units))] * own_links,
        scratch_shapes=[
            pltpu.VMEM((tokens + 8, BW), f32), pltpu.VMEM((tokens + 8, BW), f32),
            pltpu.VMEM((spans, Q, Q), f32), pltpu.VMEM((spans, Q, Q), f32),
            pltpu.VMEM((tokens, 128), f32), pltpu.VMEM((tokens, 128), f32),
            pltpu.VMEM((tokens, 128), f32), pltpu.VMEM((tokens, 128), f32), pltpu.VMEM((8, tokens), f32),
            pltpu.VMEM((HB * Q, Q), bf16), pltpu.VMEM((HB * Q, BW), bf16), pltpu.VMEM((HB * Q, Q), f32),
            pltpu.VMEM((BW, 128), f32),
            pltpu.VMEM((48, tokens), f32), pltpu.VMEM((48, tokens), f32), pltpu.VMEM((48, tokens), f32),
            pltpu.VMEM((48, tokens), f32), pltpu.VMEM((48, 128), f32), pltpu.VMEM((8, BW), f32),
        ] + ([sem, sem] + reduce_scratch(2, width // ways, units)) * own_links,
        compiler_params=params(4 if own_links else None),
        cost_estimate=pl.CostEstimate(flops=40_000_000_000, bytes_accessed=30_000_000, transcendentals=heads * spans * Q * Q),
    )(
        inner, dy, states, conv_inner, conv_state, decay_log, skip_gain, cst, bc, step, cum, step_t, cum_t, pre_t,
        *[mixed, grad_b] * own_links,
    )
    if own_links:
        mixed_got, wb_shard = sent
    else:
        mixed_got = swap(mixed_far)
        wb_shard = lax.psum_scatter(grad_b, "dp", scatter_dimension=1, tiled=True).astype(f32)
    output = (rows_in + mixed_near.astype(f32) + mixed_got.astype(f32)).astype(bf16)

    if own_links:
        weights = (gain_in, w_gate_inner, w_state_io, w_step, wb_shard)
        sums = (gk, ggg, gks, hs)
        grad_normed, inner_grads, step_grads, both, small = reduce_tail(
            normed_t, dinner, dsd, dgate, wb, wa, sums, weights, ways, 5
        )
    else:
        last = jnp.concatenate([gks[:5].reshape(-1), hs[0], hs[1]])
        small = jnp.concatenate([gk[:6], ggg[:1], last[None]], axis=0)
        grad_a = jnp.concatenate([mm(normed_t, dinner).astype(bf16), mm(normed_t, dsd).astype(bf16)], axis=1)
        pulled = mm(dgate, wb[:, :units], 1, 1) + mm(dinner, wa[:, :units], 1, 1) + mm(dsd, wa[:, units:], 1, 1)
        near, far = halves(pulled.astype(bf16), 0)
        wa_shard = lax.psum_scatter(grad_a, "dp", scatter_dimension=0, tiled=True).astype(f32)
        small = lax.psum(small, "dp")
        grad_normed = near.astype(f32) + swap(far).astype(f32)
    grad_v = grad_normed * norm_gain
    grad_residual = cotangent.astype(f32) + rstd_in * (
        grad_v - scaled * jnp.mean(grad_v * scaled, axis=1, keepdims=True)
    )

    bias_sum = gathered_heads(small[7, 5 * BW : 5 * BW + 128], heads)
    decay_sum = gathered_heads(small[7, 5 * BW + 128 : 5 * BW + 256], heads)
    skip_sum = jnp.sum(small[5].reshape(heads, HEAD), axis=1)

    count = width // ways
    if own_links:
        gain_part = both[count + 5, : count // 2]
    else:
        conv_state_sum = small[7, : 5 * BW].reshape(5, BW)
        gain_rows = jnp.sum(wb_shard[0] * w_gate_inner[0].astype(f32), axis=1) + jnp.sum(
            wa_shard * pack_a.astype(f32), axis=1
        )
        gain_own = gain_rows / lax.dynamic_slice_in_dim(norm_gain, lax.axis_index("dp") * count, count)
        near_s, far_s = halves(jnp.concatenate([wa_shard[:, units : units + BW], conv_state_sum], axis=0), 1)
        near_g, far_g = halves(gain_own, 0)
        far_all = jnp.concatenate([far_s.reshape(-1), far_g])
        got = swap(far_all)
        both = near_s + got[: far_s.size].reshape(far_s.shape)
        gain_part = near_g + got[far_s.size :]
        inner_grads = jnp.stack([wb_shard[0], wa_shard[:, :units]])
        step_grads = wa_shard[:, units + BW :]
    return (
        output,
        grad_residual,
        gain_part,
        inner_grads,
        both[:count],
        gathered_heads(step_grads, heads),
        small[0:5],
        both[count : count + 5],
        bias_sum,
        decay_sum,
        skip_sum,
        small[6],
        wb_shard[1].T,
    )


def solution(mesh):
    return jax.shard_map(
        on_device,
        mesh=mesh,
        in_specs=(
            P(("dp", "tensor"), None),
            P(),
            P(None, "dp", "tensor"),
            P("dp", None),
            P("dp", "tensor"),
            P(None, "tensor"),
            P(),
            P("tensor"),
            P("tensor"),
            P("tensor"),
            P("tensor"),
            P("tensor", "dp"),
            P(("dp", "tensor"), None),
        ),
        out_specs=(
            P(("dp", "tensor"), None),
            P(("dp", "tensor"), None),
            P(("dp", "tensor")),
            P(None, "dp", "tensor"),
            P("dp", "tensor"),
            P("dp", "tensor"),
            P(None, "tensor"),
            P(None, "tensor"),
            P("tensor"),
            P("tensor"),
            P("tensor"),
            P("tensor"),
            P("tensor", "dp"),
        ),
        check_vma=False,
    )
```
